32 devices in a mesh: batch: 4 (over y, core), seq: 8 (over z, x).
Axes of the slice: x: 2, y: 2, z: 4, core: 2. Of those that a mesh axis runs over, the one named last changes fastest.
Arguments:
- tokens: bfloat16 [4, 1024, 2048], P('batch', 'seq'), may hold values from -6 to 6
- lengths: int32 [4], P('batch'), may hold values from 256 to 1024, as said below
- norm_gain: bfloat16 [2048], P(('batch', 'seq')), may hold values from 0.5 to 1.5
- in_proj: bfloat16 [2048, 8192], P(('batch', 'seq')), may hold values from -0.125 to 0.125
- conv_weight: bfloat16 [4, 4096], P(None, ('batch', 'seq')), may hold values from -3 to 3
- conv_bias: bfloat16 [4096], P(('batch', 'seq')), may hold values from -3 to 3
- x_proj: bfloat16 [4096, 160], P(('batch', 'seq')), may hold values from -0.09375 to 0.09375
- dt_proj: bfloat16 [128, 4096], P(None, ('batch', 'seq')), may hold values from -0.25 to 0.25
- dt_bias: bfloat16 [4096], P(('batch', 'seq')), may hold values from -12 to 0
- a_log: bfloat16 [4096, 16], P(('batch', 'seq')), may hold values from 0 to 2.6875
- skip: bfloat16 [4096], P(('batch', 'seq')), may hold values from 0.5 to 1.5
- out_proj: bfloat16 [4096, 2048], P(('batch', 'seq')), may hold values from -0.375 to 0.375
- cotangent: bfloat16 [4, 1024, 2048], P('batch', 'seq'), may hold values from -6 to 6
Outputs:
- block_out: float32 [4, 1024, 2048], P('batch', 'seq')
- grad_tokens: float32 [4, 1024, 2048], P('batch', 'seq')
- grad_norm_gain: float32 [2048], P(('batch', 'seq'))
- grad_in_proj: float32 [2048, 8192], P(('batch', 'seq'))
- grad_conv_weight: float32 [4, 4096], P(None, ('batch', 'seq'))
- grad_conv_bias: float32 [4096], P(('batch', 'seq'))
- grad_x_proj: float32 [4096, 160], P(('batch', 'seq'))
- grad_dt_proj: float32 [128, 4096], P(None, ('batch', 'seq'))
- grad_dt_bias: float32 [4096], P(('batch', 'seq'))
- grad_a_log: float32 [4096, 16], P(('batch', 'seq'))
- grad_skip: float32 [4096], P(('batch', 'seq'))
- grad_out_proj: float32 [4096, 2048], P(('batch', 'seq'))
The draws below stay inside these ranges and needn't reach their ends.
Inputs may be any that keep to these rules, and one draw needn't show every extreme that they name: Slots below lengths[i] of sequence i hold tokens, the rest are padding; in every draw one sequence has exactly 1024 slots and one exactly a quarter of 1024.
All inputs are finite; a program needn't handle non-finite values.
Results may differ from the reference program's by a relative error of at most 0.012.
Values may be sent and summed in bfloat16 or wider, within the bound.
No kernel may reach another device: no remote copies, remote signals or barrier semaphores. Data moves between devices by JAX's collectives and lax.ppermute only.
A program may use at most 448 MiB of HBM per device.

```python
import math
import jax
import jax.numpy as jnp
from jax import lax

D = 2048
DI = 4096
NST = 16
RANK = 128
KW = 4
LEN_DEV = 128
SEQUENCES = 4
LENGTH = 1024


def draw_lengths(key, part):
    first_key, second_key = jax.random.split(key)
    values = jax.random.randint(first_key, (SEQUENCES,), LENGTH // 4, LENGTH + 1)
    order = jax.random.permutation(second_key, SEQUENCES)
    values = values.at[order[0]].set(LENGTH)
    values = values.at[order[1]].set(LENGTH // 4)
    return values.astype(jnp.int32)


def draw_dt_bias(key, part):
    pick_key, slow_key, fast_key = jax.random.split(key, 3)
    share = 0.5
    is_slow = jax.random.uniform(pick_key, (DI,)) < share
    slow_rate = jnp.exp(jax.random.uniform(slow_key, (DI,), minval=math.log(0.5 / LENGTH), maxval=math.log(2.0 / LENGTH)))
    fast_rate = jnp.exp(jax.random.uniform(fast_key, (DI,), minval=math.log(0.005), maxval=math.log(0.05)))
    rate = jnp.where(is_slow, slow_rate, fast_rate).astype(jnp.float32)
    return (rate + jnp.log(-jnp.expm1(-rate))).astype(jnp.bfloat16)


def steps_of(key, extent, shards, least, high):
    gain, own = 1.0, jax.random.fold_in(key, 6)
    for dim, shards_of in shards:
        steps = jnp.exp(jax.random.uniform(jax.random.fold_in(own, dim), (shards_of,), jnp.float32, least / len(shards), high / len(shards)))
        gain = gain * jnp.repeat(steps, extent[dim] // shards_of).reshape([-1 if axis == dim else 1 for axis in range(len(extent))])
    return gain


def noise(stream_key, shape, width, most, cuts=(), kind=jnp.bfloat16):
    array = width * jax.random.normal(stream_key, shape, jnp.float32)
    if cuts:
        array = array * steps_of(stream_key, shape, cuts, -0.22, 0.18)
    return jnp.clip(array, -most, most).astype(kind)


def setup_inputs(seed: int = 0) -> dict:
    keys = jax.random.split(jax.random.key(seed), 14)
    return {
        "tokens": noise(keys[0], (SEQUENCES, LENGTH, D), 1.0, 6.0, ((0, 4), (1, 8))),
        "lengths": draw_lengths(jax.random.fold_in(keys[13], 71), 0),
        "norm_gain": jnp.clip(1.0 + 0.1 * jax.random.normal(keys[2], (D,), jnp.float32), 0.5, 1.5).astype(jnp.bfloat16),
        "in_proj": noise(keys[3], (D, 2 * DI), D ** -0.5, 0.125, ((0, 32),)),
        "conv_weight": noise(keys[4], (KW, DI), KW ** -0.5, 3.0, ((1, 32),)),
        "conv_bias": noise(keys[5], (DI,), 0.5, 3.0, ((0, 32),)),
        "x_proj": noise(keys[6], (DI, RANK + 2 * NST), DI ** -0.5, 0.09375, ((0, 32),)),
        "dt_proj": noise(keys[7], (RANK, DI), (4 * RANK) ** -0.5, 0.25, ((1, 32),)),
        "dt_bias": draw_dt_bias(jax.random.fold_in(keys[13], 71), 0),
        "a_log": jnp.clip(2.6875 * jax.random.uniform(keys[9], (DI, NST), jnp.float32) ** steps_of(keys[9], (DI, NST), ((0, 32),), -0.2, 0.2), 0.0, 2.6875).astype(jnp.bfloat16),
        "skip": jnp.clip(0.5 + 1.0 * jax.random.uniform(keys[10], (DI,), jnp.float32) ** steps_of(keys[10], (DI,), ((0, 32),), -0.2, 0.2), 0.5, 1.5).astype(jnp.bfloat16),
        "out_proj": noise(keys[11], (DI, D), (DI // 16) ** -0.5, 0.375, ((0, 32),)),
        "cotangent": noise(keys[12], (SEQUENCES, LENGTH, D), 1.0, 6.0, ((0, 4), (1, 8))),
    }


@jax.custom_vjp
def low(v):
    return lax.optimization_barrier(v.astype(jnp.bfloat16)).astype(jnp.float32)

@jax.custom_vjp
def low_back(v):
    return v

def low_keep(v):
    return (low(v), None)

def low_pass(kept, grad):
    return (grad,)

def back_keep(v):
    return (v, None)

def back_low(kept, grad):
    return (low(grad),)
low.defvjp(low_keep, low_pass)
low_back.defvjp(back_keep, back_low)
epsilon = 1e-05
highest = lax.Precision.HIGHEST

def forward(params, stream, length):
    norm_scale, input_weight, conv_taps, conv_shift, select_weight, delta_weight, delta_shift, decay_logs, skip_gain, output_weight = params
    positions = jnp.arange(LENGTH, dtype=jnp.int32)
    keep_mask = (positions < length).astype(jnp.float32)[:, None]
    scale = lax.rsqrt(lax.optimization_barrier(jnp.mean(stream * stream, axis=-1, keepdims=True)) + epsilon)
    normalized_input = low(stream * scale * norm_scale)
    projected_input = low(low_back(jnp.dot(normalized_input, input_weight, precision=highest)))
    inner_x = projected_input[:, :DI]
    gate_z = projected_input[:, DI:]
    padded = jnp.concatenate([jnp.zeros((KW - 1, DI), jnp.float32), inner_x], axis=0)
    conv_out = conv_shift + jnp.zeros((LENGTH, DI), jnp.float32)
    for tap_index in range(KW):
        conv_out = conv_out + conv_taps[tap_index] * padded[tap_index:tap_index + LENGTH]
    conv_out = low_back(conv_out)
    active = low(jax.nn.silu(conv_out))
    select = low_back(jnp.dot(active, select_weight, precision=highest))
    delta_low = low(select[:, :RANK])
    b_proj = select[:, RANK:RANK + NST]
    c_proj = select[:, RANK + NST:]
    delta = jax.nn.softplus(low_back(jnp.dot(delta_low, delta_weight, precision=highest)) + delta_shift)
    decay = -jnp.exp(decay_logs)

    def step(state, inputs):
        delta_row, active_row, b_row, c_row = inputs
        state = jnp.exp(delta_row[:, None] * decay) * state + (delta_row * active_row)[:, None] * b_row[None, :]
        return (state, lax.optimization_barrier(jnp.sum(state * c_row[None, :], axis=1)))

    def block_scan(state, inputs):
        return lax.scan(step, state, inputs)
    block_count = LENGTH // LEN_DEV
    packed = tuple((column.reshape(block_count, LEN_DEV, column.shape[-1]) for column in (delta, active, b_proj, c_proj)))
    final_state, outputs = lax.scan(jax.checkpoint(block_scan), jnp.zeros((DI, NST), jnp.float32), packed)
    mixed = outputs.reshape(LENGTH, DI) + skip_gain * active
    gated_values = low(mixed * jax.nn.silu(gate_z))
    branch_output = low_back(jnp.dot(gated_values, output_weight, precision=highest))
    return keep_mask * (stream + branch_output)

def reference(tokens, lengths, norm_gain, in_proj, conv_weight, conv_bias, x_proj, dt_proj, dt_bias, a_log, skip, out_proj, cotangent):
    params = tuple((weight.astype(jnp.float32) for weight in (norm_gain, in_proj, conv_weight, conv_bias, x_proj, dt_proj, dt_bias, a_log, skip, out_proj)))
    totals_init = tuple((jnp.zeros(weight.shape, jnp.float32) for weight in params))

    def one_sequence(totals, item):
        stream, length, upstream_gradient = item
        result, pullback = jax.vjp(lambda values, inputs_seq: forward(values, inputs_seq, length), params, stream.astype(jnp.float32))
        grads, d_stream = pullback(upstream_gradient.astype(jnp.float32))
        totals = jax.tree.map(jnp.add, totals, grads)
        return (totals, (result, d_stream))
    totals, (outputs, d_tokens) = lax.scan(one_sequence, totals_init, (tokens, lengths, cotangent))
    return (outputs, d_tokens, totals[0], totals[1], totals[2], totals[3], totals[4], totals[5], totals[6], totals[7], totals[8], totals[9])
```

```python
import functools

import jax
import jax.numpy as jnp
from jax import lax
from jax.experimental import pallas as pl
from jax.experimental.pallas import tpu as pltpu
from jax.sharding import PartitionSpec as P

bf16, f32 = jnp.bfloat16, jnp.float32
NT = (((1,), (1,)), ((), ()))
LANES = 128
GROUP = 32
BLOCK = 128
epsilon = 1e-05
LOG2E = 1.4426950408889634


def spread(tile, row, lanes, states):
    return jnp.broadcast_to(tile[row : row + 1, lanes], (states, LANES))


def selectors(select, states):
    low = select.shape[1] - 4 * states
    middle = low + 2 * states
    block = select[:, low:middle].astype(f32) + select[:, middle:].astype(f32)
    return jnp.transpose(block), block[:, :states], block[:, states:]


def block_diagonal(values, step):
    rows, states = values.shape
    wide = step * states
    spread_out = (
        lax.broadcasted_iota(jnp.int32, (states, wide), 1) % states
        == lax.broadcasted_iota(jnp.int32, (states, wide), 0)
    ).astype(bf16)
    value = jnp.dot(values.astype(bf16), spread_out, preferred_element_type=f32)
    place = lax.broadcasted_iota(jnp.int32, (rows, wide), 0) % step
    owner = lax.broadcasted_iota(jnp.int32, (rows, wide), 1) // states
    return jnp.where(place == owner, value, 0.0).astype(bf16)


def forward_body(tiles, step, delta, active, select, rate, mixed, kept, state, drive, columns):
    rows, states = delta.shape[0], rate.shape[0]
    wide = step * states

    @pl.when(pl.program_id(0) == 0)
    def _():
        state[...] = jnp.zeros_like(state)

    turned, _, c_block = selectors(select[...], states)
    columns[...] = turned[:states]
    drive[...] = delta[...] * active[...].astype(f32)
    rates = [rate[:, k * LANES : (k + 1) * LANES] for k in range(tiles)]

    def group(number, held):
        held = list(held)
        base = pl.multiple_of(number * GROUP, GROUP)
        delta_now, drive_now = delta.at[pl.ds(base, GROUP), :], drive.at[pl.ds(base, GROUP), :]
        b_now = pltpu.roll(columns[...], rows - base, 1)
        for j in range(GROUP):
            b_wide = jnp.broadcast_to(b_now[:, j : j + 1], (states, LANES))
            for k in range(tiles):
                lanes = slice(k * LANES, (k + 1) * LANES)
                decay = jnp.exp2(spread(delta_now, j, lanes, states) * rates[k])
                held[k] = decay * held[k] + spread(drive_now, j, lanes, states) * b_wide
                at = pl.ds(pl.multiple_of((base + j) * states, states), states)
                kept[at, lanes] = held[k].astype(bf16)
        return tuple(held)

    held = lax.fori_loop(
        0,
        rows // GROUP,
        group,
        tuple(state[:, k * LANES : (k + 1) * LANES] for k in range(tiles)),
    )
    for k in range(tiles):
        state[:, k * LANES : (k + 1) * LANES] = held[k]
    c_diag = block_diagonal(c_block, step)
    for q in range(rows // step):
        part = kept[q * wide : (q + 1) * wide, :]
        spot = slice(q * step, (q + 1) * step)
        mixed[spot, :] = jnp.dot(c_diag[spot, :], part, preferred_element_type=f32)


def scan_forward(delta, active, select, rate, block, step):
    length, width = delta.shape
    states = rate.shape[0]
    tiles = width // LANES
    return pl.pallas_call(
        functools.partial(forward_body, tiles, step),
        grid=(length // block,),
        in_specs=[
            pl.BlockSpec((block, width), lambda i: (i, 0)),
            pl.BlockSpec((block, width), lambda i: (i, 0)),
            pl.BlockSpec((block, select.shape[1]), lambda i: (i, 0)),
            pl.BlockSpec((states, width), lambda i: (0, 0)),
        ],
        out_specs=[
            pl.BlockSpec((block, width), lambda i: (i, 0)),
            pl.BlockSpec((block * states, width), lambda i: (i, 0)),
        ],
        out_shape=[
            jax.ShapeDtypeStruct((length, width), f32),
            jax.ShapeDtypeStruct((length * states, width), bf16),
        ],
        scratch_shapes=[
            pltpu.VMEM((states, width), f32),
            pltpu.VMEM((block, width), f32),
            pltpu.VMEM((states, block), f32),
        ],
        compiler_params=pltpu.CompilerParams(vmem_limit_bytes=48 << 20),
        cost_estimate=pl.CostEstimate(
            flops=8 * length * width * states,
            transcendentals=length * width * states,
            bytes_accessed=length * width * (2 * states + 10),
        ),
        name="scan_forward",
    )(delta, active, select, rate)


FEW = 4


def backward_body(
    tiles, step, delta, active, d_mixed, select, rate, decay_rate, kept, kept_before,
    d_delta, d_active, d_bc, d_log, push, drive, columns, grads, rated, timed, folding,
):
    rows, states = delta.shape[0], rate.shape[0]
    blocks = pl.num_programs(0)
    first = pl.program_id(0) == blocks - 1
    wide = step * states

    @pl.when(pl.program_id(0) == 0)
    def _():
        push[...] = jnp.zeros_like(push)
        d_log[...] = jnp.zeros_like(d_log)

    turned, b_block, _ = selectors(select[...], states)
    columns[...] = turned[states:]
    drive[...] = delta[...] * active[...].astype(f32)
    rates = [rate[:, k * LANES : (k + 1) * LANES] for k in range(tiles)]
    own_rates = [decay_rate[:, k * LANES : (k + 1) * LANES].astype(bf16) for k in range(tiles)]

    def group(step_number, carry):
        carry = list(carry)
        number = rows // GROUP - 1 - step_number
        base = pl.multiple_of(number * GROUP, GROUP)
        delta_now = delta.at[pl.ds(base, GROUP), :]
        mixed_now = d_mixed.at[pl.ds(base, GROUP), :]
        c_now = pltpu.roll(columns[...], rows - base, 1)
        sums = [None] * tiles
        for j in reversed(range(GROUP)):
            c_wide = jnp.broadcast_to(c_now[:, j : j + 1], (states, LANES))
            at = pl.ds(pl.multiple_of((base + j) * states, states), states)
            for k in range(tiles):
                lanes = slice(k * LANES, (k + 1) * LANES)
                if j:
                    prior = pl.ds(pl.multiple_of((base + j - 1) * states, states), states)
                    before = kept[prior, lanes]
                else:
                    prior = pl.ds(
                        pl.multiple_of(jnp.maximum(base - 1, 0) * states, states), states
                    )
                    edge = jnp.where(first, jnp.zeros((), bf16), kept_before[:, lanes])
                    before = jnp.where(number == 0, edge, kept[prior, lanes])
                step_size = spread(delta_now, j, lanes, states)
                grad = spread(mixed_now, j, lanes, states) * c_wide + carry[k]
                carry[k] = jnp.exp2(step_size * rates[k]) * grad
                grads[at, lanes] = grad.astype(bf16)
                rated_now = carry[k].astype(bf16) * before * own_rates[k]
                rated[at, lanes] = rated_now
                timed_now = rated_now * step_size.astype(bf16)
                sums[k] = timed_now if sums[k] is None else sums[k] + timed_now
                if j % FEW == 0:
                    spot = pl.multiple_of((base // FEW + j // FEW) * states, states)
                    timed[pl.ds(spot, states), lanes] = sums[k]
                    sums[k] = None
        return tuple(carry)

    carry = lax.fori_loop(
        0,
        rows // GROUP,
        group,
        tuple(push[:, k * LANES : (k + 1) * LANES] for k in range(tiles)),
    )
    for k in range(tiles):
        push[:, k * LANES : (k + 1) * LANES] = carry[k]

    place = lax.broadcasted_iota(jnp.int32, (step, wide), 0)
    owner = lax.broadcasted_iota(jnp.int32, (step, wide), 1) // states
    ones_diag = (place == owner).astype(bf16)
    diag = (place == owner).astype(f32)
    b_diag = block_diagonal(b_block, step)
    for q in range(rows // step):
        spot = slice(q * step, (q + 1) * step)
        tall = slice(q * wide, (q + 1) * wide)
        through = jnp.dot(b_diag[spot, :], grads[tall, :], preferred_element_type=f32)
        summed = jnp.dot(ones_diag, rated[tall, :], preferred_element_type=f32)
        d_delta[spot, :] = summed + active[spot, :].astype(f32) * through
        d_active[spot, :] = delta[spot, :] * through
        d_b = lax.dot_general(
            drive[spot, :].astype(bf16), grads[tall, :], NT, preferred_element_type=f32
        )
        d_c = lax.dot_general(
            d_mixed[spot, :].astype(bf16), kept[tall, :], NT, preferred_element_type=f32
        )
        folding[spot, :wide] = d_b * diag
        folding[spot, wide:] = d_c * diag
    fold = (
        lax.broadcasted_iota(jnp.int32, (wide, states), 0) % states
        == lax.broadcasted_iota(jnp.int32, (wide, states), 1)
    ).astype(bf16)
    for number in range(2):
        value = folding[:, number * wide : (number + 1) * wide]
        high = value.astype(bf16)
        low = (value - high.astype(f32)).astype(bf16)
        d_bc[:, number * states : (number + 1) * states] = jnp.dot(
            high, fold, preferred_element_type=f32
        ) + jnp.dot(low, fold, preferred_element_type=f32)
    span = rows // FEW * states
    pick = (
        lax.broadcasted_iota(jnp.int32, (states, span), 1) % states
        == lax.broadcasted_iota(jnp.int32, (states, span), 0)
    ).astype(bf16)
    d_log[...] += jnp.dot(pick, timed[...], preferred_element_type=f32)


def scan_backward(delta, active, d_mixed, select, rate, decay_rate, kept, block, step):
    length, width = delta.shape
    states = rate.shape[0]
    tiles = width // LANES
    blocks = length // block
    back = lambda i: (blocks - 1 - i, 0)
    return pl.pallas_call(
        functools.partial(backward_body, tiles, step),
        grid=(blocks,),
        in_specs=[
            pl.BlockSpec((block, width), back),
            pl.BlockSpec((block, width), back),
            pl.BlockSpec((block, width), back),
            pl.BlockSpec((block, select.shape[1]), back),
            pl.BlockSpec((states, width), lambda i: (0, 0)),
            pl.BlockSpec((states, width), lambda i: (0, 0)),
            pl.BlockSpec((block * states, width), back),
            pl.BlockSpec(
                (states, width), lambda i: (jnp.maximum((blocks - 1 - i) * block - 1, 0), 0)
            ),
        ],
        out_specs=[
            pl.BlockSpec((block, width), back),
            pl.BlockSpec((block, width), back),
            pl.BlockSpec((block, 2 * states), back),
            pl.BlockSpec((states, width), lambda i: (0, 0)),
        ],
        out_shape=[
            jax.ShapeDtypeStruct((length, width), f32),
            jax.ShapeDtypeStruct((length, width), f32),
            jax.ShapeDtypeStruct((length, 2 * states), f32),
            jax.ShapeDtypeStruct((states, width), f32),
        ],
        scratch_shapes=[
            pltpu.VMEM((states, width), f32),
            pltpu.VMEM((block, width), f32),
            pltpu.VMEM((states, block), f32),
            pltpu.VMEM((block * states, width), bf16),
            pltpu.VMEM((block * states, width), bf16),
            pltpu.VMEM((block // FEW * states, width), bf16),
            pltpu.VMEM((block, 2 * step * states), f32),
        ],
        compiler_params=pltpu.CompilerParams(vmem_limit_bytes=48 << 20),
        cost_estimate=pl.CostEstimate(
            flops=20 * length * width * states,
            transcendentals=length * width * states,
            bytes_accessed=length * width * (2 * states + 20),
        ),
        name="scan_backward",
    )(delta, active, d_mixed, select, rate, decay_rate, kept, kept)


def after(values, *others):
    return lax.optimization_barrier((values, *others))[0]


def inner_swap(value, axis):
    count = lax.axis_size(axis)
    return lax.ppermute(value, axis, [(i, i ^ 1) for i in range(count)])


def outer_shift(value, axis, steps):
    count = lax.axis_size(axis)
    half = count // 2
    pairs = [(i, (i // 2 + steps) % half * 2 + i % 2) for i in range(count)]
    return lax.ppermute(value, axis, pairs)


def shift_order(half):
    return sorted(range(1, half), key=lambda k: (-min(k, half - k), k))


def pieces_of_all(own, axis):
    count = lax.axis_size(axis)
    place = lax.axis_index(axis)
    half = count // 2
    outer, inner = place // 2, place % 2
    yield place, own
    arrived = {k: outer_shift(own, axis, k) for k in shift_order(half)}
    yield outer * 2 + 1 - inner, inner_swap(own, axis)
    for k, piece in arrived.items():
        origin = (outer - k + half) % half
        yield origin * 2 + inner, piece
    for k, piece in arrived.items():
        origin = (outer - k + half) % half
        yield origin * 2 + 1 - inner, inner_swap(piece, axis)


def gathered(own, axis, dim=0):
    count, size = lax.axis_size(axis), own.shape[dim]
    whole = jnp.zeros(own.shape[:dim] + (count * size,) + own.shape[dim + 1 :], own.dtype)
    for place, piece in pieces_of_all(own, axis):
        whole = lax.dynamic_update_slice_in_dim(whole, piece, place * size, dim)
    return whole


def hop(value, axis, moves):
    pairs = [(a * 2 + i, b * 2 + i) for a, b in moves for i in (0, 1)]
    return lax.ppermute(value, axis, pairs)


def swap_at(value, axis, spots):
    pairs = [(a * 2 + i, a * 2 + 1 - i) for a in spots for i in (0, 1)]
    return lax.ppermute(value, axis, pairs)


UP, DOWN = [(0, 1), (1, 2), (2, 3)], [(1, 0), (2, 1), (3, 2)]


def line_gathered(own, axis, first=()):
    if lax.axis_size(axis) != 8:
        return lax.all_gather(own, axis, axis=0, tiled=True)
    place = lax.axis_index(axis)
    z, x = place // 2, place % 2
    rows = own.shape[0]
    upper, edge = z >= 2, (z == 0) | (z == 3)
    across = jnp.where(upper, z - 2, z + 2)
    far = jnp.where(z == 3, 0, 3)

    def put(whole, piece, spot, side):
        return lax.dynamic_update_slice_in_dim(whole, piece, (spot * 2 + side) * rows, 0)

    def put_far(whole, piece, side):
        held = lax.dynamic_slice_in_dim(whole, (far * 2 + side) * rows, rows, 0)
        return put(whole, jnp.where(edge, piece, held), far, side)

    whole = jnp.zeros((8 * rows,) + own.shape[1:], own.dtype)
    up, down, other = hop(own, axis, UP), hop(own, axis, DOWN), swap_at(own, axis, range(4))
    up_two, down_two = hop(up, axis, UP[1:]), hop(down, axis, DOWN[:2])
    other_up, other_down = swap_at(up, axis, (1, 2, 3)), swap_at(down, axis, (0, 1, 2))
    whole = put(put(whole, own, z, x), other, z, 1 - x)
    whole = put(put(whole, up, (z + 3) % 4, x), down, (z + 1) % 4, x)
    two = after(jnp.where(upper, up_two, down_two), *first)
    three = hop(two, axis, [(2, 3), (1, 0)])
    other_two = swap_at(two, axis, range(4))
    whole = put(put(whole, other_up, (z + 3) % 4, 1 - x), other_down, (z + 1) % 4, 1 - x)
    whole = put(whole, two, across, x)
    other_three = swap_at(three, axis, (0, 3))
    whole = put(whole, other_two, across, 1 - x)
    return put_far(put_far(whole, three, x), other_three, 1 - x)


def line_summed(part_of, axis):
    if lax.axis_size(axis) != 8:
        return (scattered_sum(part_of, axis),)
    place = lax.axis_index(axis)
    z, x = place // 2, place % 2
    upper, edge = z >= 2, (z == 0) | (z == 3)
    across = jnp.where(upper, z - 2, z + 2)
    far = jnp.where(z == 0, 3, 0)
    above, below = jnp.minimum(z + 1, 3), jnp.maximum(z - 1, 0)

    def swapped(spot, spots):
        return swap_at(part_of(spot * 2 + 1 - x), axis, spots)

    def added(spot, given):
        return part_of(spot * 2 + x).astype(f32) + given.astype(f32)

    given_far = swapped(far, (0, 3))
    given_across = swapped(across, range(4))
    given_above, given_below = swapped(above, (0, 1, 2)), swapped(below, (1, 2, 3))
    given_own = swapped(z, range(4))
    three = hop(added(far, given_far).astype(bf16), axis, [(0, 1), (3, 2)])
    two = added(across, given_across) + jnp.where(edge, 0.0, three.astype(f32))
    two = two.astype(bf16)
    two_up, two_down = hop(two, axis, UP[:2]), hop(two, axis, DOWN[1:])
    one_up = (added(above, given_above) + two_up.astype(f32)).astype(bf16)
    one_down = (added(below, given_below) + two_down.astype(f32)).astype(bf16)
    up, down = hop(one_up, axis, UP), hop(one_down, axis, DOWN)
    return added(z, given_own), up, down


def scattered_sum(part_of, axis):
    count = lax.axis_size(axis)
    place = lax.axis_index(axis)
    half = count // 2
    outer, inner = place // 2, place % 2
    total = None
    for k in shift_order(half) + [0]:
        target = (outer + k) % half
        given = inner_swap(part_of(target * 2 + 1 - inner), axis)
        piece = part_of(target * 2 + inner).astype(f32) + given.astype(f32)
        if k:
            piece = outer_shift(piece.astype(bf16), axis, k).astype(f32)
        total = piece if total is None else total + piece
    return total


def rows_of(value, rows):
    return lambda place: lax.dynamic_slice_in_dim(value, place * rows, rows, 0)


def summed_over_seq(part, change):
    count = lax.axis_size("seq")
    length, columns = part.shape
    part = part.astype(bf16).reshape(count, length // count, columns)
    own = change(jnp.sum(lax.all_to_all(part, "seq", 0, 0).astype(f32), axis=0))
    return shared(own, "seq").reshape(length, own.shape[1])


def two_terms(value):
    high = value.astype(bf16)
    return [high, (value - high.astype(f32)).astype(bf16)]


def shared(own, axis):
    wide = jnp.broadcast_to(own[None], (lax.axis_size(axis),) + own.shape)
    return lax.all_to_all(wide, axis, 0, 0)


def matmul(a, b, dims=(((1,), (0,)), ((), ()))):
    return lax.dot_general(a, b, dims, preferred_element_type=f32)


TN = (((0,), (0,)), ((), ()))


def on_device(
    tokens,
    lengths,
    norm_gain,
    in_proj,
    conv_weight,
    conv_bias,
    x_proj,
    dt_proj,
    dt_bias,
    a_log,
    skip,
    out_proj,
    cotangent,
):
    batch, seq = lax.axis_size("batch"), lax.axis_size("seq")
    place = lax.axis_index("seq")
    span, model = tokens.shape[1:]
    length = span * seq
    in_rows = in_proj.shape[0]
    own = skip.shape[0]
    taps = conv_weight.shape[0]
    rank = dt_proj.shape[0]
    states = a_log.shape[1]
    width = own * batch

    halves = in_proj.reshape(in_rows, 2, batch, seq, own).transpose(1, 3, 0, 2, 4)
    halves = halves.reshape(2, seq, in_rows, width)
    columns = lax.all_to_all(halves[0], "seq", 0, 0)
    gate_columns = lax.all_to_all(after(halves[1], columns), "seq", 0, 0)
    conv_weight = after(conv_weight, halves)
    small = jnp.concatenate(
        [
            dt_proj,
            x_proj.T,
            a_log.T,
            conv_weight,
            conv_bias[None],
            dt_bias[None],
            skip[None],
            jnp.pad(norm_gain, (0, own - in_rows))[None],
        ],
        axis=0,
    )
    small = gathered(small, "batch", 1)
    cuts = [rank, 2 * rank + 2 * states, 2 * rank + 3 * states]
    cuts = cuts + [cuts[2] + taps + i for i in range(4)]
    delta_weight, select_weight, decay_logs, conv_taps, conv_shift, delta_shift, skip_gain, gain = (
        jnp.split(small, cuts, axis=0)
    )
    conv_taps, conv_shift = conv_taps.astype(f32), conv_shift.astype(f32)
    delta_shift, skip_gain = delta_shift.astype(f32), skip_gain.astype(f32)
    decay = -jnp.exp(decay_logs.astype(f32))
    gain = gain.reshape(batch, own)[:, :in_rows]
    gain = shared(after(gain, gate_columns), "seq").transpose(1, 0, 2).reshape(model).astype(f32)

    input_weight = gathered(columns.reshape(seq * in_rows, width), "batch")
    output_weight = gathered(out_proj, "batch")

    def normed(rows):
        rows = rows.astype(f32)
        scale = lax.rsqrt(jnp.mean(rows * rows, axis=-1, keepdims=True) + epsilon)
        return (rows * scale * gain).astype(bf16)

    stream = line_gathered(tokens[0], "seq", (columns,))
    gate_weight = gathered(gate_columns.reshape(seq * in_rows, width), "batch")
    normalized = normed(stream)
    upstream = lax.all_gather(cotangent[0], "seq", axis=0, tiled=True)

    valid = (jnp.arange(length, dtype=jnp.int32) < lengths[0])[:, None]
    inner = matmul(normalized, input_weight).astype(bf16)
    padded = jnp.pad(inner, ((taps - 1, 0), (0, 0)))
    conv_out = conv_shift + jnp.zeros((length, width), f32)
    for tap in range(taps):
        conv_out = conv_out + conv_taps[tap] * padded[tap : tap + length].astype(f32)
    active = jax.nn.silu(conv_out).astype(bf16)
    active_f = active.astype(f32)

    partial = matmul(active, select_weight, NT)
    select = summed_over_seq(
        partial,
        lambda s: jnp.concatenate([s[:, :rank].astype(bf16)] + two_terms(s[:, rank:]), axis=1),
    )
    gate = matmul(after(normalized, partial), gate_weight).astype(bf16).astype(f32)
    delta_low = select[:, :rank]
    delta_raw = matmul(delta_low, delta_weight) + delta_shift
    delta = jax.nn.softplus(delta_raw)

    block = min(BLOCK, length)
    step = 256 // states
    rate = decay * LOG2E
    mixed, kept = scan_forward(delta, active, select, rate, block, step)
    mixed = mixed + skip_gain * active_f
    gate_sig = jax.nn.sigmoid(gate)
    gated = (mixed * gate * gate_sig).astype(bf16)
    branch = matmul(gated, output_weight).astype(bf16)
    upstream, branch = lax.optimization_barrier((upstream, branch))
    upstream = jnp.where(valid, upstream, 0).astype(bf16)
    branch = lax.psum_scatter(branch, "seq", scatter_dimension=0, tiled=True)
    own_valid = lax.dynamic_slice_in_dim(valid, place * span, span, 0)
    own_stream = tokens[0].astype(f32)
    block_out = jnp.where(own_valid, own_stream + branch.astype(f32), 0.0)

    d_gated = matmul(upstream, output_weight, NT)
    d_mixed = d_gated * gate * gate_sig
    d_gate = d_gated * mixed * gate_sig * (1.0 + gate * (1.0 - gate_sig))
    grad_skip = jnp.sum(d_mixed * active_f, axis=0, keepdims=True)

    d_gate_low = d_gate.astype(bf16)
    d_delta, d_active, d_bc, grad_log = scan_backward(
        delta, active, d_mixed, select, rate, decay, kept, block, step
    )
    d_raw = d_delta * jax.nn.sigmoid(delta_raw)
    grad_dt_bias = jnp.sum(d_raw, axis=0, keepdims=True)
    d_raw_low = d_raw.astype(bf16)
    grad_dt_proj = matmul(delta_low, d_raw_low, TN)
    partial = jnp.concatenate([matmul(d_raw_low, delta_weight, NT), d_bc], axis=1)
    d_select = summed_over_seq(partial, lambda s: s.astype(bf16))
    gated, d_gate_low = after((gated, d_gate_low), partial)
    grad_output = scattered_sum(rows_of(matmul(gated, upstream, TN).astype(bf16), own), "batch")
    grad_gate = scattered_sum(
        rows_of(matmul(normalized, d_gate_low, TN).astype(bf16), model // batch), "batch"
    )
    d_select, branch = lax.optimization_barrier((d_select, branch))
    grad_x_proj = matmul(d_select, active, TN)
    d_active = d_active + d_mixed * skip_gain + matmul(d_select, select_weight)
    conv_sig = jax.nn.sigmoid(conv_out)
    d_conv = (d_active * conv_sig * (1.0 + conv_out * (1.0 - conv_sig))).astype(bf16)
    d_conv_f = d_conv.astype(f32)
    grad_conv_bias = jnp.sum(d_conv_f, axis=0, keepdims=True)
    grad_conv = jnp.stack(
        [
            jnp.sum(d_conv_f * padded[tap : tap + length].astype(f32), axis=0)
            for tap in range(taps)
        ]
    )
    extended = jnp.pad(d_conv, ((0, taps - 1), (0, 0)))
    d_inner = jnp.zeros((length, width), f32)
    for tap in range(taps):
        offset = taps - 1 - tap
        d_inner = d_inner + conv_taps[tap] * extended[offset : offset + length].astype(f32)
    d_inner = d_inner.astype(bf16)
    d_normalized = matmul(
        jnp.concatenate([d_inner, d_gate_low], axis=1),
        jnp.concatenate([input_weight, gate_weight], axis=1),
        NT,
    ).astype(bf16)
    d_inner, d_normalized = lax.optimization_barrier((d_inner, d_normalized))
    d_normalized, *last_terms = line_summed(rows_of(d_normalized, span), "seq")
    grad_inner = scattered_sum(
        rows_of(matmul(normalized, d_inner, TN).astype(bf16), model // batch), "batch"
    )

    both = jnp.concatenate([grad_inner, grad_gate], axis=1).astype(bf16)
    both = lax.all_to_all(both.reshape(seq, in_rows, 2 * width), "seq", 0, 0)
    both = both.reshape(seq, in_rows, 2, batch, own).transpose(1, 2, 3, 0, 4)
    grad_input = both.reshape(in_rows, 2 * batch * seq * own).astype(f32)

    small_grads = jnp.concatenate(
        [grad_dt_proj, grad_x_proj, grad_log, grad_conv, grad_conv_bias, grad_dt_bias, grad_skip],
        axis=0,
    )
    small_grads = lax.psum_scatter(small_grads, "batch", scatter_dimension=1, tiled=True)
    g_dt_proj, g_x_proj, g_log, g_conv, g_conv_bias, g_dt_bias, g_skip = jnp.split(
        small_grads, cuts[:-1], axis=0
    )

    own_upstream = jnp.where(own_valid, cotangent[0].astype(f32), 0.0)
    own_scale = lax.rsqrt(jnp.mean(own_stream * own_stream, axis=-1, keepdims=True) + epsilon)
    grad_gain = jnp.sum(grad_input * in_proj.astype(f32), axis=1) / norm_gain.astype(f32)
    d_normalized = after(d_normalized, g_x_proj, g_log, g_conv, g_skip, grad_input, grad_gain)
    for term in last_terms:
        d_normalized = d_normalized + term.astype(f32)
    d_hat = d_normalized * gain
    grad_tokens = (
        own_scale * d_hat
        - own_stream
        * own_scale
        * own_scale
        * own_scale
        * jnp.mean(d_hat * own_stream, axis=-1, keepdims=True)
        + own_upstream
    )
    return (
        block_out[None],
        grad_tokens[None],
        grad_gain,
        grad_input,
        g_conv,
        g_conv_bias[0],
        g_x_proj.T,
        g_dt_proj,
        g_dt_bias[0],
        g_log.T,
        g_skip[0],
        grad_output,
    )


def solution(mesh):
    placed = (
        P("batch", "seq", None),
        P("batch"),
        P(("batch", "seq")),
        P(("batch", "seq"), None),
        P(None, ("batch", "seq")),
        P(("batch", "seq")),
        P(("batch", "seq"), None),
        P(None, ("batch", "seq")),
        P(("batch", "seq")),
        P(("batch", "seq"), None),
        P(("batch", "seq")),
        P(("batch", "seq"), None),
        P("batch", "seq", None),
    )
    return jax.shard_map(
        on_device,
        mesh=mesh,
        in_specs=placed,
        out_specs=(
            P("batch", "seq", None),
            P("batch", "seq", None),
            P(("batch", "seq")),
            P(("batch", "seq"), None),
            P(None, ("batch", "seq")),
            P(("batch", "seq")),
            P(("batch", "seq"), None),
            P(None, ("batch", "seq")),
            P(("batch", "seq")),
            P(("batch", "seq"), None),
            P(("batch", "seq")),
            P(("batch", "seq"), None),
        ),
        check_vma=False,
    )
```

```python
import functools

import jax
import jax.numpy as jnp
from jax import lax
from jax.experimental import pallas as pl
from jax.experimental.pallas import tpu as pltpu
from jax.sharding import PartitionSpec as P

bf16, f32 = jnp.bfloat16, jnp.float32
NT = (((1,), (1,)), ((), ()))
LANES = 128
GROUP = 32
BLOCK = 128
epsilon = 1e-05
LOG2E = 1.4426950408889634


def spread(tile, row, lanes, states):
    return jnp.broadcast_to(tile[row : row + 1, lanes], (states, LANES))


def selectors(select, states):
    low = select.shape[1] - 4 * states
    middle = low + 2 * states
    block = select[:, low:middle].astype(f32) + select[:, middle:].astype(f32)
    return jnp.transpose(block), block[:, :states], block[:, states:]


def block_diagonal(values, step):
    rows, states = values.shape
    wide = step * states
    spread_out = (
        lax.broadcasted_iota(jnp.int32, (states, wide), 1) % states
        == lax.broadcasted_iota(jnp.int32, (states, wide), 0)
    ).astype(bf16)
    value = jnp.dot(values.astype(bf16), spread_out, preferred_element_type=f32)
    place = lax.broadcasted_iota(jnp.int32, (rows, wide), 0) % step
    owner = lax.broadcasted_iota(jnp.int32, (rows, wide), 1) // states
    return jnp.where(place == owner, value, 0.0).astype(bf16)


def forward_body(tiles, step, delta, active, select, rate, mixed, kept, state, drive, columns):
    rows, states = delta.shape[0], rate.shape[0]
    wide = step * states

    @pl.when(pl.program_id(0) == 0)
    def _():
        state[...] = jnp.zeros_like(state)

    turned, _, c_block = selectors(select[...], states)
    columns[...] = turned[:states]
    drive[...] = delta[...] * active[...].astype(f32)
    rates = [rate[:, k * LANES : (k + 1) * LANES] for k in range(tiles)]

    def group(number, held):
        held = list(held)
        base = pl.multiple_of(number * GROUP, GROUP)
        delta_now, drive_now = delta.at[pl.ds(base, GROUP), :], drive.at[pl.ds(base, GROUP), :]
        b_now = pltpu.roll(columns[...], rows - base, 1)
        for j in range(GROUP):
            b_wide = jnp.broadcast_to(b_now[:, j : j + 1], (states, LANES))
            for k in range(tiles):
                lanes = slice(k * LANES, (k + 1) * LANES)
                decay = jnp.exp2(spread(delta_now, j, lanes, states) * rates[k])
                held[k] = decay * held[k] + spread(drive_now, j, lanes, states) * b_wide
                at = pl.ds(pl.multiple_of((base + j) * states, states), states)
                kept[at, lanes] = held[k].astype(bf16)
        return tuple(held)

    held = lax.fori_loop(
        0,
        rows // GROUP,
        group,
        tuple(state[:, k * LANES : (k + 1) * LANES] for k in range(tiles)),
    )
    for k in range(tiles):
        state[:, k * LANES : (k + 1) * LANES] = held[k]
    c_diag = block_diagonal(c_block, step)
    for q in range(rows // step):
        part = kept[q * wide : (q + 1) * wide, :]
        spot = slice(q * step, (q + 1) * step)
        mixed[spot, :] = jnp.dot(c_diag[spot, :], part, preferred_element_type=f32)


def scan_forward(delta, active, select, rate, block, step):
    length, width = delta.shape
    states = rate.shape[0]
    tiles = width // LANES
    return pl.pallas_call(
        functools.partial(forward_body, tiles, step),
        grid=(length // block,),
        in_specs=[
            pl.BlockSpec((block, width), lambda i: (i, 0)),
            pl.BlockSpec((block, width), lambda i: (i, 0)),
            pl.BlockSpec((block, select.shape[1]), lambda i: (i, 0)),
            pl.BlockSpec((states, width), lambda i: (0, 0)),
        ],
        out_specs=[
            pl.BlockSpec((block, width), lambda i: (i, 0)),
            pl.BlockSpec((block * states, width), lambda i: (i, 0)),
        ],
        out_shape=[
            jax.ShapeDtypeStruct((length, width), f32),
            jax.ShapeDtypeStruct((length * states, width), bf16),
        ],
        scratch_shapes=[
            pltpu.VMEM((states, width), f32),
            pltpu.VMEM((block, width), f32),
            pltpu.VMEM((states, block), f32),
        ],
        compiler_params=pltpu.CompilerParams(vmem_limit_bytes=48 << 20),
        cost_estimate=pl.CostEstimate(
            flops=8 * length * width * states,
            transcendentals=length * width * states,
            bytes_accessed=length * width * (2 * states + 10),
        ),
        name="scan_forward",
    )(delta, active, select, rate)


FEW = 4


def backward_body(
    tiles, step, delta, active, d_mixed, select, rate, decay_rate, kept, kept_before,
    d_delta, d_active, d_bc, d_log, push, drive, columns, grads, rated, timed, folding,
):
    rows, states = delta.shape[0], rate.shape[0]
    blocks = pl.num_programs(0)
    first = pl.program_id(0) == blocks - 1
    wide = step * states

    @pl.when(pl.program_id(0) == 0)
    def _():
        push[...] = jnp.zeros_like(push)
        d_log[...] = jnp.zeros_like(d_log)

    turned, b_block, _ = selectors(select[...], states)
    columns[...] = turned[states:]
    drive[...] = delta[...] * active[...].astype(f32)
    rates = [rate[:, k * LANES : (k + 1) * LANES] for k in range(tiles)]
    own_rates = [decay_rate[:, k * LANES : (k + 1) * LANES].astype(bf16) for k in range(tiles)]

    def group(step_number, carry):
        carry = list(carry)
        number = rows // GROUP - 1 - step_number
        base = pl.multiple_of(number * GROUP, GROUP)
        delta_now = delta.at[pl.ds(base, GROUP), :]
        mixed_now = d_mixed.at[pl.ds(base, GROUP), :]
        c_now = pltpu.roll(columns[...], rows - base, 1)
        sums = [None] * tiles
        for j in reversed(range(GROUP)):
            c_wide = jnp.broadcast_to(c_now[:, j : j + 1], (states, LANES))
            at = pl.ds(pl.multiple_of((base + j) * states, states), states)
            for k in range(tiles):
                lanes = slice(k * LANES, (k + 1) * LANES)
                if j:
                    prior = pl.ds(pl.multiple_of((base + j - 1) * states, states), states)
                    before = kept[prior, lanes]
                else:
                    prior = pl.ds(
                        pl.multiple_of(jnp.maximum(base - 1, 0) * states, states), states
                    )
                    edge = jnp.where(first, jnp.zeros((), bf16), kept_before[:, lanes])
                    before = jnp.where(number == 0, edge, kept[prior, lanes])
                step_size = spread(delta_now, j, lanes, states)
                grad = spread(mixed_now, j, lanes, states) * c_wide + carry[k]
                carry[k] = jnp.exp2(step_size * rates[k]) * grad
                grads[at, lanes] = grad.astype(bf16)
                rated_now = carry[k].astype(bf16) * before * own_rates[k]
                rated[at, lanes] = rated_now
                timed_now = rated_now * step_size.astype(bf16)
                sums[k] = timed_now if sums[k] is None else sums[k] + timed_now
                if j % FEW == 0:
                    spot = pl.multiple_of((base // FEW + j // FEW) * states, states)
                    timed[pl.ds(spot, states), lanes] = sums[k]
                    sums[k] = None
        return tuple(carry)

    carry = lax.fori_loop(
        0,
        rows // GROUP,
        group,
        tuple(push[:, k * LANES : (k + 1) * LANES] for k in range(tiles)),
    )
    for k in range(tiles):
        push[:, k * LANES : (k + 1) * LANES] = carry[k]

    place = lax.broadcasted_iota(jnp.int32, (step, wide), 0)
    owner = lax.broadcasted_iota(jnp.int32, (step, wide), 1) // states
    ones_diag = (place == owner).astype(bf16)
    diag = (place == owner).astype(f32)
    b_diag = block_diagonal(b_block, step)
    for q in range(rows // step):
        spot = slice(q * step, (q + 1) * step)
        tall = slice(q * wide, (q + 1) * wide)
        through = jnp.dot(b_diag[spot, :], grads[tall, :], preferred_element_type=f32)
        summed = jnp.dot(ones_diag, rated[tall, :], preferred_element_type=f32)
        d_delta[spot, :] = summed + active[spot, :].astype(f32) * through
        d_active[spot, :] = delta[spot, :] * through
        d_b = lax.dot_general(
            drive[spot, :].astype(bf16), grads[tall, :], NT, preferred_element_type=f32
        )
        d_c = lax.dot_general(
            d_mixed[spot, :].astype(bf16), kept[tall, :], NT, preferred_element_type=f32
        )
        folding[spot, :wide] = d_b * diag
        folding[spot, wide:] = d_c * diag
    fold = (
        lax.broadcasted_iota(jnp.int32, (wide, states), 0) % states
        == lax.broadcasted_iota(jnp.int32, (wide, states), 1)
    ).astype(bf16)
    for number in range(2):
        value = folding[:, number * wide : (number + 1) * wide]
        high = value.astype(bf16)
        low = (value - high.astype(f32)).astype(bf16)
        d_bc[:, number * states : (number + 1) * states] = jnp.dot(
            high, fold, preferred_element_type=f32
        ) + jnp.dot(low, fold, preferred_element_type=f32)
    span = rows // FEW * states
    pick = (
        lax.broadcasted_iota(jnp.int32, (states, span), 1) % states
        == lax.broadcasted_iota(jnp.int32, (states, span), 0)
    ).astype(bf16)
    d_log[...] += jnp.dot(pick, timed[...], preferred_element_type=f32)


def scan_backward(delta, active, d_mixed, select, rate, decay_rate, kept, block, step):
    length, width = delta.shape
    states = rate.shape[0]
    tiles = width // LANES
    blocks = length // block
    back = lambda i: (blocks - 1 - i, 0)
    return pl.pallas_call(
        functools.partial(backward_body, tiles, step),
        grid=(blocks,),
        in_specs=[
            pl.BlockSpec((block, width), back),
            pl.BlockSpec((block, width), back),
            pl.BlockSpec((block, width), back),
            pl.BlockSpec((block, select.shape[1]), back),
            pl.BlockSpec((states, width), lambda i: (0, 0)),
            pl.BlockSpec((states, width), lambda i: (0, 0)),
            pl.BlockSpec((block * states, width), back),
            pl.BlockSpec(
                (states, width), lambda i: (jnp.maximum((blocks - 1 - i) * block - 1, 0), 0)
            ),
        ],
        out_specs=[
            pl.BlockSpec((block, width), back),
            pl.BlockSpec((block, width), back),
            pl.BlockSpec((block, 2 * states), back),
            pl.BlockSpec((states, width), lambda i: (0, 0)),
        ],
        out_shape=[
            jax.ShapeDtypeStruct((length, width), f32),
            jax.ShapeDtypeStruct((length, width), f32),
            jax.ShapeDtypeStruct((length, 2 * states), f32),
            jax.ShapeDtypeStruct((states, width), f32),
        ],
        scratch_shapes=[
            pltpu.VMEM((states, width), f32),
            pltpu.VMEM((block, width), f32),
            pltpu.VMEM((states, block), f32),
            pltpu.VMEM((block * states, width), bf16),
            pltpu.VMEM((block * states, width), bf16),
            pltpu.VMEM((block // FEW * states, width), bf16),
            pltpu.VMEM((block, 2 * step * states), f32),
        ],
        compiler_params=pltpu.CompilerParams(vmem_limit_bytes=48 << 20),
        cost_estimate=pl.CostEstimate(
            flops=20 * length * width * states,
            transcendentals=length * width * states,
            bytes_accessed=length * width * (2 * states + 20),
        ),
        name="scan_backward",
    )(delta, active, d_mixed, select, rate, decay_rate, kept, kept)


def after(values, *others):
    return lax.optimization_barrier((values, *others))[0]


def inner_swap(value, axis):
    count = lax.axis_size(axis)
    return lax.ppermute(value, axis, [(i, i ^ 1) for i in range(count)])


def outer_shift(value, axis, steps):
    count = lax.axis_size(axis)
    half = count // 2
    pairs = [(i, (i // 2 + steps) % half * 2 + i % 2) for i in range(count)]
    return lax.ppermute(value, axis, pairs)


def shift_order(half):
    return sorted(range(1, half), key=lambda k: (-min(k, half - k), k))


def pieces_of_all(own, axis):
    count = lax.axis_size(axis)
    place = lax.axis_index(axis)
    half = count // 2
    outer, inner = place // 2, place % 2
    yield place, own
    arrived = {k: outer_shift(own, axis, k) for k in shift_order(half)}
    yield outer * 2 + 1 - inner, inner_swap(own, axis)
    for k, piece in arrived.items():
        origin = (outer - k + half) % half
        yield origin * 2 + inner, piece
    for k, piece in arrived.items():
        origin = (outer - k + half) % half
        yield origin * 2 + 1 - inner, inner_swap(piece, axis)


def gathered(own, axis, dim=0):
    count, size = lax.axis_size(axis), own.shape[dim]
    whole = jnp.zeros(own.shape[:dim] + (count * size,) + own.shape[dim + 1 :], own.dtype)
    for place, piece in pieces_of_all(own, axis):
        whole = lax.dynamic_update_slice_in_dim(whole, piece, place * size, dim)
    return whole


def hop(value, axis, moves):
    pairs = [(a * 2 + i, b * 2 + i) for a, b in moves for i in (0, 1)]
    return lax.ppermute(value, axis, pairs)


def swap_at(value, axis, spots):
    pairs = [(a * 2 + i, a * 2 + 1 - i) for a in spots for i in (0, 1)]
    return lax.ppermute(value, axis, pairs)


UP, DOWN = [(0, 1), (1, 2), (2, 3)], [(1, 0), (2, 1), (3, 2)]


def line_gathered(own, axis, first=()):
    if lax.axis_size(axis) != 8:
        return lax.all_gather(own, axis, axis=0, tiled=True)
    place = lax.axis_index(axis)
    z, x = place // 2, place % 2
    rows = own.shape[0]
    upper, edge = z >= 2, (z == 0) | (z == 3)
    across = jnp.where(upper, z - 2, z + 2)
    far = jnp.where(z == 3, 0, 3)

    def put(whole, piece, spot, side):
        return lax.dynamic_update_slice_in_dim(whole, piece, (spot * 2 + side) * rows, 0)

    def put_far(whole, piece, side):
        held = lax.dynamic_slice_in_dim(whole, (far * 2 + side) * rows, rows, 0)
        return put(whole, jnp.where(edge, piece, held), far, side)

    whole = jnp.zeros((8 * rows,) + own.shape[1:], own.dtype)
    up, down, other = hop(own, axis, UP), hop(own, axis, DOWN), swap_at(own, axis, range(4))
    up_two, down_two = hop(up, axis, UP[1:]), hop(down, axis, DOWN[:2])
    other_up, other_down = swap_at(up, axis, (1, 2, 3)), swap_at(down, axis, (0, 1, 2))
    whole = put(put(whole, own, z, x), other, z, 1 - x)
    whole = put(put(whole, up, (z + 3) % 4, x), down, (z + 1) % 4, x)
    two = after(jnp.where(upper, up_two, down_two), *first)
    three = hop(two, axis, [(2, 3), (1, 0)])
    other_two = swap_at(two, axis, range(4))
    whole = put(put(whole, other_up, (z + 3) % 4, 1 - x), other_down, (z + 1) % 4, 1 - x)
    whole = put(whole, two, across, x)
    other_three = swap_at(three, axis, (0, 3))
    whole = put(whole, other_two, across, 1 - x)
    return put_far(put_far(whole, three, x), other_three, 1 - x)


def line_summed(part_of, axis):
    if lax.axis_size(axis) != 8:
        return (scattered_sum(part_of, axis),)
    place = lax.axis_index(axis)
    z, x = place // 2, place % 2
    upper, edge = z >= 2, (z == 0) | (z == 3)
    across = jnp.where(upper, z - 2, z + 2)
    far = jnp.where(z == 0, 3, 0)
    above, below = jnp.minimum(z + 1, 3), jnp.maximum(z - 1, 0)

    def swapped(spot, spots):
        return swap_at(part_of(spot * 2 + 1 - x), axis, spots)

    def added(spot, given):
        return part_of(spot * 2 + x).astype(f32) + given.astype(f32)

    given_far = swapped(far, (0, 3))
    given_across = swapped(across, range(4))
    given_above, given_below = swapped(above, (0, 1, 2)), swapped(below, (1, 2, 3))
    given_own = swapped(z, range(4))
    sent = added(far, given_far).astype(bf16)
    three = hop(sent, axis, [(0, 1), (3, 2)])
    given_across, given_above, given_below, given_own, _ = lax.optimization_barrier(
        (given_across, given_above, given_below, given_own, sent)
    )
    two = added(across, given_across) + jnp.where(edge, 0.0, three.astype(f32))
    near_up, near_down = added(above, given_above), added(below, given_below)
    own = added(z, given_own)
    two, near_up, near_down, own = lax.optimization_barrier(
        (two.astype(bf16), near_up, near_down, own)
    )
    two_up, two_down = hop(two, axis, UP[:2]), hop(two, axis, DOWN[1:])
    one_up = (near_up + two_up.astype(f32)).astype(bf16)
    one_down = (near_down + two_down.astype(f32)).astype(bf16)
    return own, hop(one_up, axis, UP), hop(one_down, axis, DOWN)


def scattered_sum(part_of, axis):
    count = lax.axis_size(axis)
    place = lax.axis_index(axis)
    half = count // 2
    outer, inner = place // 2, place % 2
    total = None
    for k in shift_order(half) + [0]:
        target = (outer + k) % half
        given = inner_swap(part_of(target * 2 + 1 - inner), axis)
        piece = part_of(target * 2 + inner).astype(f32) + given.astype(f32)
        if k:
            piece = outer_shift(piece.astype(bf16), axis, k).astype(f32)
        total = piece if total is None else total + piece
    return total


def rows_of(value, rows):
    return lambda place: lax.dynamic_slice_in_dim(value, place * rows, rows, 0)


def summed_over_seq(part, change):
    count = lax.axis_size("seq")
    length, columns = part.shape
    part = part.astype(bf16).reshape(count, length // count, columns)
    own = change(jnp.sum(lax.all_to_all(part, "seq", 0, 0).astype(f32), axis=0))
    return shared(own, "seq").reshape(length, own.shape[1])


def two_terms(value):
    high = value.astype(bf16)
    return [high, (value - high.astype(f32)).astype(bf16)]


def shared(own, axis):
    wide = jnp.broadcast_to(own[None], (lax.axis_size(axis),) + own.shape)
    return lax.all_to_all(wide, axis, 0, 0)


def matmul(a, b, dims=(((1,), (0,)), ((), ()))):
    return lax.dot_general(a, b, dims, preferred_element_type=f32)


TN = (((0,), (0,)), ((), ()))


def on_device(
    tokens,
    lengths,
    norm_gain,
    in_proj,
    conv_weight,
    conv_bias,
    x_proj,
    dt_proj,
    dt_bias,
    a_log,
    skip,
    out_proj,
    cotangent,
):
    batch, seq = lax.axis_size("batch"), lax.axis_size("seq")
    place = lax.axis_index("seq")
    span, model = tokens.shape[1:]
    length = span * seq
    in_rows = in_proj.shape[0]
    own = skip.shape[0]
    taps = conv_weight.shape[0]
    rank = dt_proj.shape[0]
    states = a_log.shape[1]
    width = own * batch

    halves = in_proj.reshape(in_rows, 2, batch, seq, own).transpose(1, 3, 0, 2, 4)
    halves = halves.reshape(2, seq, in_rows, width)
    columns = lax.all_to_all(halves[0], "seq", 0, 0)
    conv_weight = after(conv_weight, halves)
    small = jnp.concatenate(
        [
            dt_proj,
            x_proj.T,
            a_log.T,
            conv_weight,
            conv_bias[None],
            dt_bias[None],
            skip[None],
            jnp.pad(norm_gain, (0, own - in_rows))[None],
        ],
        axis=0,
    )
    small = gathered(small, "batch", 1)
    cuts = [rank, 2 * rank + 2 * states, 2 * rank + 3 * states]
    cuts = cuts + [cuts[2] + taps + i for i in range(4)]
    delta_weight, select_weight, decay_logs, conv_taps, conv_shift, delta_shift, skip_gain, gain = (
        jnp.split(small, cuts, axis=0)
    )
    conv_taps, conv_shift = conv_taps.astype(f32), conv_shift.astype(f32)
    delta_shift, skip_gain = delta_shift.astype(f32), skip_gain.astype(f32)
    decay = -jnp.exp(decay_logs.astype(f32))
    gain = gain.reshape(batch, own)[:, :in_rows]
    gain = shared(after(gain, columns), "seq")
    gate_columns = lax.all_to_all(after(halves[1], gain), "seq", 0, 0)
    gain = gain.transpose(1, 0, 2).reshape(model).astype(f32)

    input_weight = gathered(columns.reshape(seq * in_rows, width), "batch")
    output_weight = gathered(out_proj, "batch")

    def normed(rows):
        rows = rows.astype(f32)
        scale = lax.rsqrt(jnp.mean(rows * rows, axis=-1, keepdims=True) + epsilon)
        return (rows * scale * gain).astype(bf16)

    stream = line_gathered(tokens[0], "seq", (columns,))
    gate_weight = gathered(gate_columns.reshape(seq * in_rows, width), "batch")
    normalized = normed(stream)
    upstream = lax.all_gather(cotangent[0], "seq", axis=0, tiled=True)

    valid = (jnp.arange(length, dtype=jnp.int32) < lengths[0])[:, None]
    inner = matmul(normalized, input_weight).astype(bf16)
    padded = jnp.pad(inner, ((taps - 1, 0), (0, 0)))
    conv_out = conv_shift + jnp.zeros((length, width), f32)
    for tap in range(taps):
        conv_out = conv_out + conv_taps[tap] * padded[tap : tap + length].astype(f32)
    active = jax.nn.silu(conv_out).astype(bf16)
    active_f = active.astype(f32)

    partial = matmul(active, select_weight, NT)
    select = summed_over_seq(
        partial,
        lambda s: jnp.concatenate([s[:, :rank].astype(bf16)] + two_terms(s[:, rank:]), axis=1),
    )
    gate = matmul(after(normalized, partial), gate_weight).astype(bf16).astype(f32)
    delta_low = select[:, :rank]
    delta_raw = matmul(delta_low, delta_weight) + delta_shift
    delta = jax.nn.softplus(delta_raw)

    block = min(BLOCK, length)
    step = 256 // states
    rate = decay * LOG2E
    mixed, kept = scan_forward(delta, active, select, rate, block, step)
    mixed = mixed + skip_gain * active_f
    gate_sig = jax.nn.sigmoid(gate)
    gated = (mixed * gate * gate_sig).astype(bf16)
    branch = matmul(gated, output_weight).astype(bf16)
    upstream, branch = lax.optimization_barrier((upstream, branch))
    upstream = jnp.where(valid, upstream, 0).astype(bf16)
    branch = lax.psum_scatter(branch, "seq", scatter_dimension=0, tiled=True)
    own_valid = lax.dynamic_slice_in_dim(valid, place * span, span, 0)
    own_stream = tokens[0].astype(f32)
    block_out = jnp.where(own_valid, own_stream + branch.astype(f32), 0.0)

    d_gated = matmul(upstream, output_weight, NT)
    d_mixed = d_gated * gate * gate_sig
    d_gate = d_gated * mixed * gate_sig * (1.0 + gate * (1.0 - gate_sig))
    grad_skip = jnp.sum(d_mixed * active_f, axis=0, keepdims=True)

    d_gate_low = d_gate.astype(bf16)
    d_delta, d_active, d_bc, grad_log = scan_backward(
        delta, active, d_mixed, select, rate, decay, kept, block, step
    )
    d_raw = d_delta * jax.nn.sigmoid(delta_raw)
    grad_dt_bias = jnp.sum(d_raw, axis=0, keepdims=True)
    d_raw_low = d_raw.astype(bf16)
    grad_dt_proj = matmul(delta_low, d_raw_low, TN)
    partial = jnp.concatenate([matmul(d_raw_low, delta_weight, NT), d_bc], axis=1)
    d_select = summed_over_seq(partial, lambda s: s.astype(bf16))
    gated, d_gate_low = after((gated, d_gate_low), partial)
    grad_output = scattered_sum(rows_of(matmul(gated, upstream, TN).astype(bf16), own), "batch")
    grad_gate = scattered_sum(
        rows_of(matmul(normalized, d_gate_low, TN).astype(bf16), model // batch), "batch"
    )
    d_select, branch, grad_output, grad_gate = lax.optimization_barrier(
        (d_select, branch, grad_output, grad_gate)
    )
    grad_x_proj = matmul(d_select, active, TN)
    d_active = d_active + d_mixed * skip_gain + matmul(d_select, select_weight)
    conv_sig = jax.nn.sigmoid(conv_out)
    d_conv = (d_active * conv_sig * (1.0 + conv_out * (1.0 - conv_sig))).astype(bf16)
    d_conv_f = d_conv.astype(f32)
    grad_conv_bias = jnp.sum(d_conv_f, axis=0, keepdims=True)
    grad_conv = jnp.stack(
        [
            jnp.sum(d_conv_f * padded[tap : tap + length].astype(f32), axis=0)
            for tap in range(taps)
        ]
    )
    extended = jnp.pad(d_conv, ((0, taps - 1), (0, 0)))
    d_inner = jnp.zeros((length, width), f32)
    for tap in range(taps):
        offset = taps - 1 - tap
        d_inner = d_inner + conv_taps[tap] * extended[offset : offset + length].astype(f32)
    d_inner = d_inner.astype(bf16)
    grad_inner = matmul(normalized, d_inner, TN).astype(bf16)
    d_inner, grad_inner = lax.optimization_barrier((d_inner, grad_inner))
    d_normalized = matmul(
        jnp.concatenate([d_inner, d_gate_low], axis=1),
        jnp.concatenate([input_weight, gate_weight], axis=1),
        NT,
    ).astype(bf16)
    grad_inner = scattered_sum(rows_of(grad_inner, model // batch), "batch")
    d_normalized, *last_terms = line_summed(rows_of(d_normalized, span), "seq")

    both = jnp.concatenate([grad_inner, grad_gate], axis=1).astype(bf16)
    both = lax.all_to_all(both.reshape(seq, in_rows, 2 * width), "seq", 0, 0)
    both = both.reshape(seq, in_rows, 2, batch, own).transpose(1, 2, 3, 0, 4)
    grad_input = both.reshape(in_rows, 2 * batch * seq * own).astype(f32)

    small_grads = jnp.concatenate(
        [grad_dt_proj, grad_x_proj, grad_log, grad_conv, grad_conv_bias, grad_dt_bias, grad_skip],
        axis=0,
    )
    small_grads = lax.psum_scatter(small_grads, "batch", scatter_dimension=1, tiled=True)
    g_dt_proj, g_x_proj, g_log, g_conv, g_conv_bias, g_dt_bias, g_skip = jnp.split(
        small_grads, cuts[:-1], axis=0
    )

    own_upstream = jnp.where(own_valid, cotangent[0].astype(f32), 0.0)
    own_scale = lax.rsqrt(jnp.mean(own_stream * own_stream, axis=-1, keepdims=True) + epsilon)
    grad_gain = jnp.sum(grad_input * in_proj.astype(f32), axis=1) / norm_gain.astype(f32)
    d_normalized = after(d_normalized, g_x_proj, g_log, g_conv, g_skip, grad_input, grad_gain)
    for term in last_terms:
        d_normalized = d_normalized + term.astype(f32)
    d_hat = d_normalized * gain
    grad_tokens = (
        own_scale * d_hat
        - own_stream
        * own_scale
        * own_scale
        * own_scale
        * jnp.mean(d_hat * own_stream, axis=-1, keepdims=True)
        + own_upstream
    )
    return (
        block_out[None],
        grad_tokens[None],
        grad_gain,
        grad_input,
        g_conv,
        g_conv_bias[0],
        g_x_proj.T,
        g_dt_proj,
        g_dt_bias[0],
        g_log.T,
        g_skip[0],
        grad_output,
    )


def solution(mesh):
    placed = (
        P("batch", "seq", None),
        P("batch"),
        P(("batch", "seq")),
        P(("batch", "seq"), None),
        P(None, ("batch", "seq")),
        P(("batch", "seq")),
        P(("batch", "seq"), None),
        P(None, ("batch", "seq")),
        P(("batch", "seq")),
        P(("batch", "seq"), None),
        P(("batch", "seq")),
        P(("batch", "seq"), None),
        P("batch", "seq", None),
    )
    return jax.shard_map(
        on_device,
        mesh=mesh,
        in_specs=placed,
        out_specs=(
            P("batch", "seq", None),
            P("batch", "seq", None),
            P(("batch", "seq")),
            P(("batch", "seq"), None),
            P(None, ("batch", "seq")),
            P(("batch", "seq")),
            P(("batch", "seq"), None),
            P(None, ("batch", "seq")),
            P(("batch", "seq")),
            P(("batch", "seq"), None),
            P(("batch", "seq")),
            P(("batch", "seq"), None),
        ),
        check_vma=False,
    )
```

```python
import functools

import jax
import jax.numpy as jnp
from jax import lax
from jax.experimental import pallas as pl
from jax.experimental.pallas import tpu as pltpu
from jax.sharding import PartitionSpec as P

bf16, f32 = jnp.bfloat16, jnp.float32
NT = (((1,), (1,)), ((), ()))
LANES = 128
GROUP = 32
BLOCK = 128
epsilon = 1e-05
LOG2E = 1.4426950408889634


def spread(tile, row, lanes, states):
    return jnp.broadcast_to(tile[row : row + 1, lanes], (states, LANES))


def selectors(select, states):
    low = select.shape[1] - 4 * states
    middle = low + 2 * states
    block = select[:, low:middle].astype(f32) + select[:, middle:].astype(f32)
    return jnp.transpose(block), block[:, :states], block[:, states:]


def block_diagonal(values, step):
    rows, states = values.shape
    wide = step * states
    spread_out = (
        lax.broadcasted_iota(jnp.int32, (states, wide), 1) % states
        == lax.broadcasted_iota(jnp.int32, (states, wide), 0)
    ).astype(bf16)
    value = jnp.dot(values.astype(bf16), spread_out, preferred_element_type=f32)
    place = lax.broadcasted_iota(jnp.int32, (rows, wide), 0) % step
    owner = lax.broadcasted_iota(jnp.int32, (rows, wide), 1) // states
    return jnp.where(place == owner, value, 0.0).astype(bf16)


def forward_body(tiles, step, delta, active, select, rate, mixed, kept, state, drive, columns):
    rows, states = delta.shape[0], rate.shape[0]
    wide = step * states

    @pl.when(pl.program_id(0) == 0)
    def _():
        state[...] = jnp.zeros_like(state)

    turned, _, c_block = selectors(select[...], states)
    columns[...] = turned[:states]
    drive[...] = delta[...] * active[...].astype(f32)
    rates = [rate[:, k * LANES : (k + 1) * LANES] for k in range(tiles)]

    def group(number, held):
        held = list(held)
        base = pl.multiple_of(number * GROUP, GROUP)
        delta_now, drive_now = delta.at[pl.ds(base, GROUP), :], drive.at[pl.ds(base, GROUP), :]
        b_now = pltpu.roll(columns[...], rows - base, 1)
        for j in range(GROUP):
            b_wide = jnp.broadcast_to(b_now[:, j : j + 1], (states, LANES))
            for k in range(tiles):
                lanes = slice(k * LANES, (k + 1) * LANES)
                decay = jnp.exp2(spread(delta_now, j, lanes, states) * rates[k])
                held[k] = decay * held[k] + spread(drive_now, j, lanes, states) * b_wide
                at = pl.ds(pl.multiple_of((base + j) * states, states), states)
                kept[at, lanes] = held[k].astype(bf16)
        return tuple(held)

    held = lax.fori_loop(
        0,
        rows // GROUP,
        group,
        tuple(state[:, k * LANES : (k + 1) * LANES] for k in range(tiles)),
    )
    for k in range(tiles):
        state[:, k * LANES : (k + 1) * LANES] = held[k]
    c_diag = block_diagonal(c_block, step)
    for q in range(rows // step):
        part = kept[q * wide : (q + 1) * wide, :]
        spot = slice(q * step, (q + 1) * step)
        mixed[spot, :] = jnp.dot(c_diag[spot, :], part, preferred_element_type=f32)


def scan_forward(delta, active, select, rate, block, step):
    length, width = delta.shape
    states = rate.shape[0]
    tiles = width // LANES
    return pl.pallas_call(
        functools.partial(forward_body, tiles, step),
        grid=(length // block,),
        in_specs=[
            pl.BlockSpec((block, width), lambda i: (i, 0)),
            pl.BlockSpec((block, width), lambda i: (i, 0)),
            pl.BlockSpec((block, select.shape[1]), lambda i: (i, 0)),
            pl.BlockSpec((states, width), lambda i: (0, 0)),
        ],
        out_specs=[
            pl.BlockSpec((block, width), lambda i: (i, 0)),
            pl.BlockSpec((block * states, width), lambda i: (i, 0)),
        ],
        out_shape=[
            jax.ShapeDtypeStruct((length, width), f32),
            jax.ShapeDtypeStruct((length * states, width), bf16),
        ],
        scratch_shapes=[
            pltpu.VMEM((states, width), f32),
            pltpu.VMEM((block, width), f32),
            pltpu.VMEM((states, block), f32),
        ],
        compiler_params=pltpu.CompilerParams(vmem_limit_bytes=48 << 20),
        cost_estimate=pl.CostEstimate(
            flops=8 * length * width * states,
            transcendentals=length * width * states,
            bytes_accessed=length * width * (2 * states + 10),
        ),
        name="scan_forward",
    )(delta, active, select, rate)


FEW = 4


def backward_body(
    tiles, step, delta, active, d_mixed, select, rate, decay_rate, kept, kept_before,
    d_delta, d_active, d_bc, d_log, push, drive, columns, grads, rated, timed, folding,
):
    rows, states = delta.shape[0], rate.shape[0]
    blocks = pl.num_programs(0)
    first = pl.program_id(0) == blocks - 1
    wide = step * states

    @pl.when(pl.program_id(0) == 0)
    def _():
        push[...] = jnp.zeros_like(push)
        d_log[...] = jnp.zeros_like(d_log)

    turned, b_block, _ = selectors(select[...], states)
    columns[...] = turned[states:]
    drive[...] = delta[...] * active[...].astype(f32)
    rates = [rate[:, k * LANES : (k + 1) * LANES] for k in range(tiles)]
    own_rates = [decay_rate[:, k * LANES : (k + 1) * LANES].astype(bf16) for k in range(tiles)]

    def group(step_number, carry):
        carry = list(carry)
        number = rows // GROUP - 1 - step_number
        base = pl.multiple_of(number * GROUP, GROUP)
        delta_now = delta.at[pl.ds(base, GROUP), :]
        mixed_now = d_mixed.at[pl.ds(base, GROUP), :]
        c_now = pltpu.roll(columns[...], rows - base, 1)
        sums = [None] * tiles
        for j in reversed(range(GROUP)):
            c_wide = jnp.broadcast_to(c_now[:, j : j + 1], (states, LANES))
            at = pl.ds(pl.multiple_of((base + j) * states, states), states)
            for k in range(tiles):
                lanes = slice(k * LANES, (k + 1) * LANES)
                if j:
                    prior = pl.ds(pl.multiple_of((base + j - 1) * states, states), states)
                    before = kept[prior, lanes]
                else:
                    prior = pl.ds(
                        pl.multiple_of(jnp.maximum(base - 1, 0) * states, states), states
                    )
                    edge = jnp.where(first, jnp.zeros((), bf16), kept_before[:, lanes])
                    before = jnp.where(number == 0, edge, kept[prior, lanes])
                step_size = spread(delta_now, j, lanes, states)
                grad = spread(mixed_now, j, lanes, states) * c_wide + carry[k]
                carry[k] = jnp.exp2(step_size * rates[k]) * grad
                grads[at, lanes] = grad.astype(bf16)
                rated_now = carry[k].astype(bf16) * before * own_rates[k]
                rated[at, lanes] = rated_now
                timed_now = rated_now * step_size.astype(bf16)
                sums[k] = timed_now if sums[k] is None else sums[k] + timed_now
                if j % FEW == 0:
                    spot = pl.multiple_of((base // FEW + j // FEW) * states, states)
                    timed[pl.ds(spot, states), lanes] = sums[k]
                    sums[k] = None
        return tuple(carry)

    carry = lax.fori_loop(
        0,
        rows // GROUP,
        group,
        tuple(push[:, k * LANES : (k + 1) * LANES] for k in range(tiles)),
    )
    for k in range(tiles):
        push[:, k * LANES : (k + 1) * LANES] = carry[k]

    place = lax.broadcasted_iota(jnp.int32, (step, wide), 0)
    owner = lax.broadcasted_iota(jnp.int32, (step, wide), 1) // states
    ones_diag = (place == owner).astype(bf16)
    diag = (place == owner).astype(f32)
    b_diag = block_diagonal(b_block, step)
    for q in range(rows // step):
        spot = slice(q * step, (q + 1) * step)
        tall = slice(q * wide, (q + 1) * wide)
        through = jnp.dot(b_diag[spot, :], grads[tall, :], preferred_element_type=f32)
        summed = jnp.dot(ones_diag, rated[tall, :], preferred_element_type=f32)
        d_delta[spot, :] = summed + active[spot, :].astype(f32) * through
        d_active[spot, :] = delta[spot, :] * through
        d_b = lax.dot_general(
            drive[spot, :].astype(bf16), grads[tall, :], NT, preferred_element_type=f32
        )
        d_c = lax.dot_general(
            d_mixed[spot, :].astype(bf16), kept[tall, :], NT, preferred_element_type=f32
        )
        folding[spot, :wide] = d_b * diag
        folding[spot, wide:] = d_c * diag
    fold = (
        lax.broadcasted_iota(jnp.int32, (wide, states), 0) % states
        == lax.broadcasted_iota(jnp.int32, (wide, states), 1)
    ).astype(bf16)
    for number in range(2):
        value = folding[:, number * wide : (number + 1) * wide]
        high = value.astype(bf16)
        low = (value - high.astype(f32)).astype(bf16)
        d_bc[:, number * states : (number + 1) * states] = jnp.dot(
            high, fold, preferred_element_type=f32
        ) + jnp.dot(low, fold, preferred_element_type=f32)
    span = rows // FEW * states
    pick = (
        lax.broadcasted_iota(jnp.int32, (states, span), 1) % states
        == lax.broadcasted_iota(jnp.int32, (states, span), 0)
    ).astype(bf16)
    d_log[...] += jnp.dot(pick, timed[...], preferred_element_type=f32)


def scan_backward(delta, active, d_mixed, select, rate, decay_rate, kept, block, step):
    length, width = delta.shape
    states = rate.shape[0]
    tiles = width // LANES
    blocks = length // block
    back = lambda i: (blocks - 1 - i, 0)
    return pl.pallas_call(
        functools.partial(backward_body, tiles, step),
        grid=(blocks,),
        in_specs=[
            pl.BlockSpec((block, width), back),
            pl.BlockSpec((block, width), back),
            pl.BlockSpec((block, width), back),
            pl.BlockSpec((block, select.shape[1]), back),
            pl.BlockSpec((states, width), lambda i: (0, 0)),
            pl.BlockSpec((states, width), lambda i: (0, 0)),
            pl.BlockSpec((block * states, width), back),
            pl.BlockSpec(
                (states, width), lambda i: (jnp.maximum((blocks - 1 - i) * block - 1, 0), 0)
            ),
        ],
        out_specs=[
            pl.BlockSpec((block, width), back),
            pl.BlockSpec((block, width), back),
            pl.BlockSpec((block, 2 * states), back),
            pl.BlockSpec((states, width), lambda i: (0, 0)),
        ],
        out_shape=[
            jax.ShapeDtypeStruct((length, width), f32),
            jax.ShapeDtypeStruct((length, width), f32),
            jax.ShapeDtypeStruct((length, 2 * states), f32),
            jax.ShapeDtypeStruct((states, width), f32),
        ],
        scratch_shapes=[
            pltpu.VMEM((states, width), f32),
            pltpu.VMEM((block, width), f32),
            pltpu.VMEM((states, block), f32),
            pltpu.VMEM((block * states, width), bf16),
            pltpu.VMEM((block * states, width), bf16),
            pltpu.VMEM((block // FEW * states, width), bf16),
            pltpu.VMEM((block, 2 * step * states), f32),
        ],
        compiler_params=pltpu.CompilerParams(vmem_limit_bytes=48 << 20),
        cost_estimate=pl.CostEstimate(
            flops=20 * length * width * states,
            transcendentals=length * width * states,
            bytes_accessed=length * width * (2 * states + 20),
        ),
        name="scan_backward",
    )(delta, active, d_mixed, select, rate, decay_rate, kept, kept)


together = lax.optimization_barrier


def inner_swap(value, axis):
    count = lax.axis_size(axis)
    return lax.ppermute(value, axis, [(i, i ^ 1) for i in range(count)])


def outer_shift(value, axis, steps):
    count = lax.axis_size(axis)
    half = count // 2
    pairs = [(i, (i // 2 + steps) % half * 2 + i % 2) for i in range(count)]
    return lax.ppermute(value, axis, pairs)


def shift_order(half):
    return sorted(range(1, half), key=lambda k: (-min(k, half - k), k))


def pieces_of_all(own, axis):
    count = lax.axis_size(axis)
    place = lax.axis_index(axis)
    half = count // 2
    outer, inner = place // 2, place % 2
    yield place, own
    arrived = {k: outer_shift(own, axis, k) for k in shift_order(half)}
    yield outer * 2 + 1 - inner, inner_swap(own, axis)
    for k, piece in arrived.items():
        origin = (outer - k + half) % half
        yield origin * 2 + inner, piece
    for k, piece in arrived.items():
        origin = (outer - k + half) % half
        yield origin * 2 + 1 - inner, inner_swap(piece, axis)


def gathered(own, axis, dim=0):
    count, size = lax.axis_size(axis), own.shape[dim]
    whole = jnp.zeros(own.shape[:dim] + (count * size,) + own.shape[dim + 1 :], own.dtype)
    for place, piece in pieces_of_all(own, axis):
        whole = lax.dynamic_update_slice_in_dim(whole, piece, place * size, dim)
    return whole


def hop(value, axis, moves):
    pairs = [(a * 2 + i, b * 2 + i) for a, b in moves for i in (0, 1)]
    return lax.ppermute(value, axis, pairs)


def swap_at(value, axis, spots):
    pairs = [(a * 2 + i, a * 2 + 1 - i) for a in spots for i in (0, 1)]
    return lax.ppermute(value, axis, pairs)


UP, DOWN = [(0, 1), (1, 2), (2, 3)], [(1, 0), (2, 1), (3, 2)]


def line_gathered(own, axis):
    if lax.axis_size(axis) != 8:
        return lax.all_gather(own, axis, axis=0, tiled=True)
    place = lax.axis_index(axis)
    z, x = place // 2, place % 2
    rows = own.shape[0]
    upper, edge = z >= 2, (z == 0) | (z == 3)
    across = jnp.where(upper, z - 2, z + 2)
    far = jnp.where(z == 3, 0, 3)

    def put(whole, piece, spot, side):
        return lax.dynamic_update_slice_in_dim(whole, piece, (spot * 2 + side) * rows, 0)

    def put_far(whole, piece, side):
        held = lax.dynamic_slice_in_dim(whole, (far * 2 + side) * rows, rows, 0)
        return put(whole, jnp.where(edge, piece, held), far, side)

    whole = jnp.zeros((8 * rows,) + own.shape[1:], own.dtype)
    up, down, other = hop(own, axis, UP), hop(own, axis, DOWN), swap_at(own, axis, range(4))
    up_two, down_two = hop(up, axis, UP[1:]), hop(down, axis, DOWN[:2])
    other_up, other_down = swap_at(up, axis, (1, 2, 3)), swap_at(down, axis, (0, 1, 2))
    whole = put(put(whole, own, z, x), other, z, 1 - x)
    whole = put(put(whole, up, (z + 3) % 4, x), down, (z + 1) % 4, x)
    two = jnp.where(upper, up_two, down_two)
    three = hop(two, axis, [(2, 3), (1, 0)])
    other_two = swap_at(two, axis, range(4))
    whole = put(put(whole, other_up, (z + 3) % 4, 1 - x), other_down, (z + 1) % 4, 1 - x)
    whole = put(whole, two, across, x)
    other_three = swap_at(three, axis, (0, 3))
    whole = put(whole, other_two, across, 1 - x)
    return put_far(put_far(whole, three, x), other_three, 1 - x)


def line_summed(part_of, axis):
    if lax.axis_size(axis) != 8:
        return (scattered_sum(part_of, axis),)
    place = lax.axis_index(axis)
    z, x = place // 2, place % 2
    upper, edge = z >= 2, (z == 0) | (z == 3)
    across = jnp.where(upper, z - 2, z + 2)
    far = jnp.where(z == 0, 3, 0)
    above, below = jnp.minimum(z + 1, 3), jnp.maximum(z - 1, 0)

    def swapped(spot, spots):
        return swap_at(part_of(spot * 2 + 1 - x), axis, spots)

    def added(spot, given):
        return part_of(spot * 2 + x).astype(f32) + given.astype(f32)

    given_far = swapped(far, (0, 3))
    given_across = swapped(across, range(4))
    given_above, given_below = swapped(above, (0, 1, 2)), swapped(below, (1, 2, 3))
    given_own = swapped(z, range(4))
    three = hop(added(far, given_far).astype(bf16), axis, [(0, 1), (3, 2)])
    three, given_across, given_above, given_below = together(
        (three, given_across, given_above, given_below)
    )
    two = added(across, given_across) + jnp.where(edge, 0.0, three.astype(f32))
    two = two.astype(bf16)
    two_up, two_down, given_own = together(
        (hop(two, axis, UP[:2]), hop(two, axis, DOWN[1:]), given_own)
    )
    one_up = (added(above, given_above) + two_up.astype(f32)).astype(bf16)
    one_down = (added(below, given_below) + two_down.astype(f32)).astype(bf16)
    return added(z, given_own), hop(one_up, axis, UP), hop(one_down, axis, DOWN)


def scattered_sum(part_of, axis):
    count = lax.axis_size(axis)
    place = lax.axis_index(axis)
    half = count // 2
    outer, inner = place // 2, place % 2
    total = None
    for k in shift_order(half) + [0]:
        target = (outer + k) % half
        given = inner_swap(part_of(target * 2 + 1 - inner), axis)
        piece = part_of(target * 2 + inner).astype(f32) + given.astype(f32)
        if k:
            piece = outer_shift(piece.astype(bf16), axis, k).astype(f32)
        total = piece if total is None else total + piece
    return total


def rows_of(value, rows):
    return lambda place: lax.dynamic_slice_in_dim(value, place * rows, rows, 0)


def summed_over_seq(part, change):
    count = lax.axis_size("seq")
    length, columns = part.shape
    part = part.astype(bf16).reshape(count, length // count, columns)
    own = change(jnp.sum(lax.all_to_all(part, "seq", 0, 0).astype(f32), axis=0))
    return shared(own, "seq").reshape(length, own.shape[1])


def two_terms(value):
    high = value.astype(bf16)
    return [high, (value - high.astype(f32)).astype(bf16)]


def shared(own, axis):
    wide = jnp.broadcast_to(own[None], (lax.axis_size(axis),) + own.shape)
    return lax.all_to_all(wide, axis, 0, 0)


def matmul(a, b, dims=(((1,), (0,)), ((), ()))):
    return lax.dot_general(a, b, dims, preferred_element_type=f32)


TN = (((0,), (0,)), ((), ()))


def on_device(
    tokens,
    lengths,
    norm_gain,
    in_proj,
    conv_weight,
    conv_bias,
    x_proj,
    dt_proj,
    dt_bias,
    a_log,
    skip,
    out_proj,
    cotangent,
):
    batch, seq = lax.axis_size("batch"), lax.axis_size("seq")
    place = lax.axis_index("seq")
    span, model = tokens.shape[1:]
    length = span * seq
    in_rows = in_proj.shape[0]
    own = skip.shape[0]
    taps = conv_weight.shape[0]
    rank = dt_proj.shape[0]
    states = a_log.shape[1]
    width = own * batch

    halves = in_proj.reshape(in_rows, 2, batch, seq, own).transpose(1, 3, 0, 2, 4)
    halves = halves.reshape(2, seq, in_rows, width)
    columns = lax.all_to_all(halves[0], "seq", 0, 0)
    small = jnp.concatenate(
        [
            dt_proj,
            x_proj.T,
            a_log.T,
            conv_weight,
            conv_bias[None],
            dt_bias[None],
            skip[None],
            jnp.pad(norm_gain, (0, own - in_rows))[None],
        ],
        axis=0,
    )
    small = gathered(small, "batch", 1)
    cuts = [rank, 2 * rank + 2 * states, 2 * rank + 3 * states]
    cuts = cuts + [cuts[2] + taps + i for i in range(4)]
    delta_weight, select_weight, decay_logs, conv_taps, conv_shift, delta_shift, skip_gain, gain = (
        jnp.split(small, cuts, axis=0)
    )
    conv_taps, conv_shift = conv_taps.astype(f32), conv_shift.astype(f32)
    delta_shift, skip_gain = delta_shift.astype(f32), skip_gain.astype(f32)
    decay = -jnp.exp(decay_logs.astype(f32))
    gain = gain.reshape(batch, own)[:, :in_rows]
    columns, gain = together((columns, gain))
    gain = shared(gain, "seq")
    gate_columns, gain = together((halves[1], gain))
    gate_columns = lax.all_to_all(gate_columns, "seq", 0, 0)
    gain = gain.transpose(1, 0, 2).reshape(model).astype(f32)

    input_weight = gathered(columns.reshape(seq * in_rows, width), "batch")
    output_weight = gathered(out_proj, "batch")

    def normed(rows):
        rows = rows.astype(f32)
        scale = lax.rsqrt(jnp.mean(rows * rows, axis=-1, keepdims=True) + epsilon)
        return (rows * scale * gain).astype(bf16)

    stream = lax.all_gather(tokens[0], "seq", axis=0, tiled=True)
    gate_weight = gathered(gate_columns.reshape(seq * in_rows, width), "batch")
    normalized = normed(stream)
    upstream = line_gathered(cotangent[0], "seq")

    valid = (jnp.arange(length, dtype=jnp.int32) < lengths[0])[:, None]
    inner = matmul(normalized, input_weight).astype(bf16)
    padded = jnp.pad(inner, ((taps - 1, 0), (0, 0)))
    conv_out = conv_shift + jnp.zeros((length, width), f32)
    for tap in range(taps):
        conv_out = conv_out + conv_taps[tap] * padded[tap : tap + length].astype(f32)
    active = jax.nn.silu(conv_out).astype(bf16)
    active_f = active.astype(f32)

    partial, upstream = together((matmul(active, select_weight, NT), upstream))
    select = summed_over_seq(
        partial,
        lambda s: jnp.concatenate([s[:, :rank].astype(bf16)] + two_terms(s[:, rank:]), axis=1),
    )
    gate = matmul(normalized, gate_weight).astype(bf16).astype(f32)
    delta_low = select[:, :rank]
    delta_raw = matmul(delta_low, delta_weight) + delta_shift
    delta = jax.nn.softplus(delta_raw)

    block = min(BLOCK, length)
    step = 256 // states
    rate = decay * LOG2E
    mixed, kept = scan_forward(delta, active, select, rate, block, step)
    mixed = mixed + skip_gain * active_f
    gate_sig = jax.nn.sigmoid(gate)
    gated = (mixed * gate * gate_sig).astype(bf16)
    branch = matmul(gated, output_weight).astype(bf16)
    upstream, branch = together((upstream, branch))
    upstream = jnp.where(valid, upstream, 0).astype(bf16)
    branch = lax.psum_scatter(branch, "seq", scatter_dimension=0, tiled=True)
    own_valid = lax.dynamic_slice_in_dim(valid, place * span, span, 0)
    own_stream = tokens[0].astype(f32)
    block_out = jnp.where(own_valid, own_stream + branch.astype(f32), 0.0)

    d_gated = matmul(upstream, output_weight, NT)
    d_mixed = d_gated * gate * gate_sig
    d_gate = d_gated * mixed * gate_sig * (1.0 + gate * (1.0 - gate_sig))
    grad_skip = jnp.sum(d_mixed * active_f, axis=0, keepdims=True)

    d_gate_low = d_gate.astype(bf16)
    d_delta, d_active, d_bc, grad_log = scan_backward(
        delta, active, d_mixed, select, rate, decay, kept, block, step
    )
    d_raw = d_delta * jax.nn.sigmoid(delta_raw)
    grad_dt_bias = jnp.sum(d_raw, axis=0, keepdims=True)
    d_raw_low = d_raw.astype(bf16)
    grad_dt_proj = matmul(delta_low, d_raw_low, TN)
    partial = jnp.concatenate([matmul(d_raw_low, delta_weight, NT), d_bc], axis=1)
    d_select = summed_over_seq(partial, lambda s: s.astype(bf16))
    grad_output = scattered_sum(rows_of(matmul(gated, upstream, TN).astype(bf16), own), "batch")
    grad_gate = scattered_sum(
        rows_of(matmul(normalized, d_gate_low, TN).astype(bf16), model // batch), "batch"
    )
    d_select, branch, grad_output, grad_gate = together(
        (d_select, branch, grad_output, grad_gate)
    )
    grad_x_proj = matmul(d_select, active, TN)
    d_active = d_active + d_mixed * skip_gain + matmul(d_select, select_weight)
    conv_sig = jax.nn.sigmoid(conv_out)
    d_conv = (d_active * conv_sig * (1.0 + conv_out * (1.0 - conv_sig))).astype(bf16)
    d_conv_f = d_conv.astype(f32)
    grad_conv_bias = jnp.sum(d_conv_f, axis=0, keepdims=True)
    grad_conv = jnp.stack(
        [
            jnp.sum(d_conv_f * padded[tap : tap + length].astype(f32), axis=0)
            for tap in range(taps)
        ]
    )
    extended = jnp.pad(d_conv, ((0, taps - 1), (0, 0)))
    d_inner = jnp.zeros((length, width), f32)
    for tap in range(taps):
        offset = taps - 1 - tap
        d_inner = d_inner + conv_taps[tap] * extended[offset : offset + length].astype(f32)
    d_inner = d_inner.astype(bf16)
    grad_inner = matmul(normalized, d_inner, TN).astype(bf16)
    d_inner, grad_inner = together((d_inner, grad_inner))
    d_normalized = matmul(
        jnp.concatenate([d_inner, d_gate_low], axis=1),
        jnp.concatenate([input_weight, gate_weight], axis=1),
        NT,
    ).astype(bf16)
    grad_inner = scattered_sum(rows_of(grad_inner, model // batch), "batch")
    d_normalized, *last_terms = line_summed(rows_of(d_normalized, span), "seq")

    both = jnp.concatenate([grad_inner, grad_gate], axis=1).astype(bf16)
    both = lax.all_to_all(both.reshape(seq, in_rows, 2 * width), "seq", 0, 0)
    both = both.reshape(seq, in_rows, 2, batch, own).transpose(1, 2, 3, 0, 4)
    grad_input = both.reshape(in_rows, 2 * batch * seq * own).astype(f32)

    small_grads = jnp.concatenate(
        [grad_dt_proj, grad_x_proj, grad_log, grad_conv, grad_conv_bias, grad_dt_bias, grad_skip],
        axis=0,
    )
    small_grads = lax.psum_scatter(small_grads, "batch", scatter_dimension=1, tiled=True)
    g_dt_proj, g_x_proj, g_log, g_conv, g_conv_bias, g_dt_bias, g_skip = jnp.split(
        small_grads, cuts[:-1], axis=0
    )

    own_upstream = jnp.where(own_valid, cotangent[0].astype(f32), 0.0)
    own_scale = lax.rsqrt(jnp.mean(own_stream * own_stream, axis=-1, keepdims=True) + epsilon)
    grad_gain = jnp.sum(grad_input * in_proj.astype(f32), axis=1) / norm_gain.astype(f32)
    (
        d_normalized, g_dt_proj, g_x_proj, g_log, g_conv, g_conv_bias, g_dt_bias, g_skip,
        grad_input, grad_gain,
    ) = together(
        (
            d_normalized, g_dt_proj, g_x_proj, g_log, g_conv, g_conv_bias, g_dt_bias, g_skip,
            grad_input, grad_gain,
        )
    )
    for term in last_terms:
        d_normalized = d_normalized + term.astype(f32)
    d_hat = d_normalized * gain
    grad_tokens = (
        own_scale * d_hat
        - own_stream
        * own_scale
        * own_scale
        * own_scale
        * jnp.mean(d_hat * own_stream, axis=-1, keepdims=True)
        + own_upstream
    )
    return (
        block_out[None],
        grad_tokens[None],
        grad_gain,
        grad_input,
        g_conv,
        g_conv_bias[0],
        g_x_proj.T,
        g_dt_proj,
        g_dt_bias[0],
        g_log.T,
        g_skip[0],
        grad_output,
    )


def solution(mesh):
    placed = (
        P("batch", "seq", None),
        P("batch"),
        P(("batch", "seq")),
        P(("batch", "seq"), None),
        P(None, ("batch", "seq")),
        P(("batch", "seq")),
        P(("batch", "seq"), None),
        P(None, ("batch", "seq")),
        P(("batch", "seq")),
        P(("batch", "seq"), None),
        P(("batch", "seq")),
        P(("batch", "seq"), None),
        P("batch", "seq", None),
    )
    return jax.shard_map(
        on_device,
        mesh=mesh,
        in_specs=placed,
        out_specs=(
            P("batch", "seq", None),
            P("batch", "seq", None),
            P(("batch", "seq")),
            P(("batch", "seq"), None),
            P(None, ("batch", "seq")),
            P(("batch", "seq")),
            P(("batch", "seq"), None),
            P(None, ("batch", "seq")),
            P(("batch", "seq")),
            P(("batch", "seq"), None),
            P(("batch", "seq")),
            P(("batch", "seq"), None),
        ),
        check_vma=False,
    )
```

```python
import functools

import jax
import jax.numpy as jnp
from jax import lax
from jax.experimental import pallas as pl
from jax.experimental.pallas import tpu as pltpu
from jax.sharding import PartitionSpec as P

bf16, f32 = jnp.bfloat16, jnp.float32
NT = (((1,), (1,)), ((), ()))
LANES = 128
GROUP = 32
BLOCK = 128
epsilon = 1e-05
LOG2E = 1.4426950408889634


def spread(tile, row, lanes, states):
    return jnp.broadcast_to(tile[row : row + 1, lanes], (states, LANES))


def selectors(select, states):
    low = select.shape[1] - 4 * states
    middle = low + 2 * states
    block = select[:, low:middle].astype(f32) + select[:, middle:].astype(f32)
    return jnp.transpose(block), block[:, :states], block[:, states:]


def block_diagonal(values, step):
    rows, states = values.shape
    wide = step * states
    spread_out = (
        lax.broadcasted_iota(jnp.int32, (states, wide), 1) % states
        == lax.broadcasted_iota(jnp.int32, (states, wide), 0)
    ).astype(bf16)
    value = jnp.dot(values.astype(bf16), spread_out, preferred_element_type=f32)
    place = lax.broadcasted_iota(jnp.int32, (rows, wide), 0) % step
    owner = lax.broadcasted_iota(jnp.int32, (rows, wide), 1) // states
    return jnp.where(place == owner, value, 0.0).astype(bf16)


def forward_body(tiles, step, delta, active, select, rate, mixed, kept, state, drive, columns):
    rows, states = delta.shape[0], rate.shape[0]
    wide = step * states

    @pl.when(pl.program_id(0) == 0)
    def _():
        state[...] = jnp.zeros_like(state)

    turned, _, c_block = selectors(select[...], states)
    columns[...] = turned[:states]
    drive[...] = delta[...] * active[...].astype(f32)
    rates = [rate[:, k * LANES : (k + 1) * LANES] for k in range(tiles)]

    def group(number, held):
        held = list(held)
        base = pl.multiple_of(number * GROUP, GROUP)
        delta_now, drive_now = delta.at[pl.ds(base, GROUP), :], drive.at[pl.ds(base, GROUP), :]
        b_now = pltpu.roll(columns[...], rows - base, 1)
        for j in range(GROUP):
            b_wide = jnp.broadcast_to(b_now[:, j : j + 1], (states, LANES))
            for k in range(tiles):
                lanes = slice(k * LANES, (k + 1) * LANES)
                decay = jnp.exp2(spread(delta_now, j, lanes, states) * rates[k])
                held[k] = decay * held[k] + spread(drive_now, j, lanes, states) * b_wide
                at = pl.ds(pl.multiple_of((base + j) * states, states), states)
                kept[at, lanes] = held[k].astype(bf16)
        return tuple(held)

    held = lax.fori_loop(
        0,
        rows // GROUP,
        group,
        tuple(state[:, k * LANES : (k + 1) * LANES] for k in range(tiles)),
    )
    for k in range(tiles):
        state[:, k * LANES : (k + 1) * LANES] = held[k]
    c_diag = block_diagonal(c_block, step)
    for q in range(rows // step):
        part = kept[q * wide : (q + 1) * wide, :]
        spot = slice(q * step, (q + 1) * step)
        mixed[spot, :] = jnp.dot(c_diag[spot, :], part, preferred_element_type=f32)


def scan_forward(delta, active, select, rate, block, step):
    length, width = delta.shape
    states = rate.shape[0]
    tiles = width // LANES
    return pl.pallas_call(
        functools.partial(forward_body, tiles, step),
        grid=(length // block,),
        in_specs=[
            pl.BlockSpec((block, width), lambda i: (i, 0)),
            pl.BlockSpec((block, width), lambda i: (i, 0)),
            pl.BlockSpec((block, select.shape[1]), lambda i: (i, 0)),
            pl.BlockSpec((states, width), lambda i: (0, 0)),
        ],
        out_specs=[
            pl.BlockSpec((block, width), lambda i: (i, 0)),
            pl.BlockSpec((block * states, width), lambda i: (i, 0)),
        ],
        out_shape=[
            jax.ShapeDtypeStruct((length, width), f32),
            jax.ShapeDtypeStruct((length * states, width), bf16),
        ],
        scratch_shapes=[
            pltpu.VMEM((states, width), f32),
            pltpu.VMEM((block, width), f32),
            pltpu.VMEM((states, block), f32),
        ],
        compiler_params=pltpu.CompilerParams(vmem_limit_bytes=48 << 20),
        cost_estimate=pl.CostEstimate(
            flops=8 * length * width * states,
            transcendentals=length * width * states,
            bytes_accessed=length * width * (2 * states + 10),
        ),
        name="scan_forward",
    )(delta, active, select, rate)


FEW = 4


def backward_body(
    tiles, step, delta, active, d_mixed, select, rate, decay_rate, kept, kept_before,
    d_delta, d_active, d_bc, d_log, push, drive, columns, diagonals, folding, timed, *pairs,
):
    grads, rated = pairs[:2], pairs[2:]
    rows, states = delta.shape[0], rate.shape[0]
    blocks = pl.num_programs(0)
    first = pl.program_id(0) == blocks - 1
    wide = step * states

    @pl.when(pl.program_id(0) == 0)
    def _():
        push[...] = jnp.zeros_like(push)
        d_log[...] = jnp.zeros_like(d_log)

    turned, b_block, _ = selectors(select[...], states)
    columns[...] = turned[states:]
    drive[...] = delta[...] * active[...].astype(f32)
    rates = [rate[:, k * LANES : (k + 1) * LANES] for k in range(tiles)]
    own_rates = [decay_rate[:, k * LANES : (k + 1) * LANES].astype(bf16) for k in range(tiles)]

    place = lax.broadcasted_iota(jnp.int32, (step, wide), 0)
    owner = lax.broadcasted_iota(jnp.int32, (step, wide), 1) // states
    ones_diag = (place == owner).astype(bf16)
    diag = (place == owner).astype(f32)
    diagonals[...] = block_diagonal(b_block, step)

    def sums_of(number):
        held, through_of = number % 2, {}

        def spots(q):
            at = number * GROUP + q * step
            tall = slice(q * wide, (q + 1) * wide)
            return slice(at, at + step), tall

        def through(q):
            spot, tall = spots(q)
            value = jnp.dot(diagonals[spot, :], grads[held][tall, :], preferred_element_type=f32)
            d_active[spot, :] = delta[spot, :] * value
            through_of[q] = active[spot, :].astype(f32) * value

        def summed(q):
            spot, tall = spots(q)
            value = jnp.dot(ones_diag, rated[held][tall, :], preferred_element_type=f32)
            d_delta[spot, :] = value + through_of[q]

        def d_b(q):
            spot, tall = spots(q)
            folding[spot, :wide] = diag * lax.dot_general(
                drive[spot, :].astype(bf16), grads[held][tall, :], NT, preferred_element_type=f32
            )

        def d_c(q):
            spot, _ = spots(q)
            own = slice(spot.start * states, spot.stop * states)
            folding[spot, wide:] = diag * lax.dot_general(
                d_mixed[spot, :].astype(bf16), kept[own, :], NT, preferred_element_type=f32
            )

        return [
            functools.partial(part, q)
            for q in range(GROUP // step)
            for part in (through, summed, d_b, d_c)
        ]

    carry = [push[:, k * LANES : (k + 1) * LANES] for k in range(tiles)]
    waiting = []
    for number in reversed(range(rows // GROUP)):
        pace = GROUP // max(len(waiting), 1)
        sums = [None] * tiles
        held = number % 2
        for j in reversed(range(GROUP)):
            row = number * GROUP + j
            c_wide = jnp.broadcast_to(columns[:, row : row + 1], (states, LANES))
            at = slice(j * states, (j + 1) * states)
            for k in range(tiles):
                lanes = slice(k * LANES, (k + 1) * LANES)
                if row:
                    before = kept[(row - 1) * states : row * states, lanes]
                else:
                    before = jnp.where(first, jnp.zeros((), bf16), kept_before[:, lanes])
                step_size = spread(delta, row, lanes, states)
                grad = spread(d_mixed, row, lanes, states) * c_wide + carry[k]
                carry[k] = jnp.exp2(step_size * rates[k]) * grad
                grads[held][at, lanes] = grad.astype(bf16)
                rated_now = carry[k].astype(bf16) * before * own_rates[k]
                rated[held][at, lanes] = rated_now
                timed_now = rated_now * step_size.astype(bf16)
                sums[k] = timed_now if sums[k] is None else sums[k] + timed_now
                if j % FEW == 0:
                    spot = row // FEW * states
                    timed[spot : spot + states, lanes] = sums[k]
                    sums[k] = None
            if waiting and j % pace == 0:
                waiting.pop(0)()
        while waiting:
            waiting.pop(0)()
        waiting = sums_of(number)
    while waiting:
        waiting.pop(0)()
    for k in range(tiles):
        push[:, k * LANES : (k + 1) * LANES] = carry[k]
    fold = (
        lax.broadcasted_iota(jnp.int32, (wide, states), 0) % states
        == lax.broadcasted_iota(jnp.int32, (wide, states), 1)
    ).astype(bf16)
    for number in range(2):
        value = folding[:, number * wide : (number + 1) * wide]
        high = value.astype(bf16)
        d_bc[:, number * states : (number + 1) * states] = jnp.dot(
            high, fold, preferred_element_type=f32
        )
    span = rows // FEW * states
    pick = (
        lax.broadcasted_iota(jnp.int32, (states, span), 1) % states
        == lax.broadcasted_iota(jnp.int32, (states, span), 0)
    ).astype(bf16)
    d_log[...] += jnp.dot(pick, timed[...], preferred_element_type=f32)


def scan_backward(delta, active, d_mixed, select, rate, decay_rate, kept, block, step):
    length, width = delta.shape
    states = rate.shape[0]
    tiles = width // LANES
    blocks = length // block
    back = lambda i: (blocks - 1 - i, 0)
    return pl.pallas_call(
        functools.partial(backward_body, tiles, step),
        grid=(blocks,),
        in_specs=[
            pl.BlockSpec((block, width), back),
            pl.BlockSpec((block, width), back),
            pl.BlockSpec((block, width), back),
            pl.BlockSpec((block, select.shape[1]), back),
            pl.BlockSpec((states, width), lambda i: (0, 0)),
            pl.BlockSpec((states, width), lambda i: (0, 0)),
            pl.BlockSpec((block * states, width), back),
            pl.BlockSpec(
                (states, width), lambda i: (jnp.maximum((blocks - 1 - i) * block - 1, 0), 0)
            ),
        ],
        out_specs=[
            pl.BlockSpec((block, width), back),
            pl.BlockSpec((block, width), back),
            pl.BlockSpec((block, 2 * states), back),
            pl.BlockSpec((states, width), lambda i: (0, 0)),
        ],
        out_shape=[
            jax.ShapeDtypeStruct((length, width), f32),
            jax.ShapeDtypeStruct((length, width), f32),
            jax.ShapeDtypeStruct((length, 2 * states), f32),
            jax.ShapeDtypeStruct((states, width), f32),
        ],
        scratch_shapes=[
            pltpu.VMEM((states, width), f32),
            pltpu.VMEM((block, width), f32),
            pltpu.VMEM((states, block), f32),
            pltpu.VMEM((block, step * states), bf16),
            pltpu.VMEM((block, 2 * step * states), f32),
            pltpu.VMEM((block // FEW * states, width), bf16),
        ]
        + [pltpu.VMEM((GROUP * states, width), bf16)] * 4,
        compiler_params=pltpu.CompilerParams(vmem_limit_bytes=48 << 20),
        cost_estimate=pl.CostEstimate(
            flops=20 * length * width * states,
            transcendentals=length * width * states,
            bytes_accessed=length * width * (2 * states + 20),
        ),
        name="scan_backward",
    )(delta, active, d_mixed, select, rate, decay_rate, kept, kept)


together = lax.optimization_barrier


def inner_swap(value, axis):
    count = lax.axis_size(axis)
    return lax.ppermute(value, axis, [(i, i ^ 1) for i in range(count)])


def outer_shift(value, axis, steps):
    count = lax.axis_size(axis)
    half = count // 2
    pairs = [(i, (i // 2 + steps) % half * 2 + i % 2) for i in range(count)]
    return lax.ppermute(value, axis, pairs)


def shift_order(half):
    return sorted(range(1, half), key=lambda k: (-min(k, half - k), k))


def pieces_of_all(own, axis):
    count = lax.axis_size(axis)
    place = lax.axis_index(axis)
    half = count // 2
    outer, inner = place // 2, place % 2
    yield place, own
    arrived = {k: outer_shift(own, axis, k) for k in shift_order(half)}
    yield outer * 2 + 1 - inner, inner_swap(own, axis)
    for k, piece in arrived.items():
        origin = (outer - k + half) % half
        yield origin * 2 + inner, piece
    for k, piece in arrived.items():
        origin = (outer - k + half) % half
        yield origin * 2 + 1 - inner, inner_swap(piece, axis)


def gathered(own, axis, dim=0):
    count, size = lax.axis_size(axis), own.shape[dim]
    whole = jnp.zeros(own.shape[:dim] + (count * size,) + own.shape[dim + 1 :], own.dtype)
    for place, piece in pieces_of_all(own, axis):
        whole = lax.dynamic_update_slice_in_dim(whole, piece, place * size, dim)
    return whole


def hop(value, axis, moves):
    pairs = [(a * 2 + i, b * 2 + i) for a, b in moves for i in (0, 1)]
    return lax.ppermute(value, axis, pairs)


def swap_at(value, axis, spots):
    pairs = [(a * 2 + i, a * 2 + 1 - i) for a in spots for i in (0, 1)]
    return lax.ppermute(value, axis, pairs)


UP, DOWN = [(0, 1), (1, 2), (2, 3)], [(1, 0), (2, 1), (3, 2)]


def line_gathered(own, axis):
    if lax.axis_size(axis) != 8:
        return lax.all_gather(own, axis, axis=0, tiled=True)
    place = lax.axis_index(axis)
    z, x = place // 2, place % 2
    rows = own.shape[0]
    upper, edge = z >= 2, (z == 0) | (z == 3)
    across = jnp.where(upper, z - 2, z + 2)
    far = jnp.where(z == 3, 0, 3)

    def put(whole, piece, spot, side):
        return lax.dynamic_update_slice_in_dim(whole, piece, (spot * 2 + side) * rows, 0)

    def put_far(whole, piece, side):
        held = lax.dynamic_slice_in_dim(whole, (far * 2 + side) * rows, rows, 0)
        return put(whole, jnp.where(edge, piece, held), far, side)

    whole = jnp.zeros((8 * rows,) + own.shape[1:], own.dtype)
    up, down, other = hop(own, axis, UP), hop(own, axis, DOWN), swap_at(own, axis, range(4))
    up_two, down_two = hop(up, axis, UP[1:]), hop(down, axis, DOWN[:2])
    other_up, other_down = swap_at(up, axis, (1, 2, 3)), swap_at(down, axis, (0, 1, 2))
    whole = put(put(whole, own, z, x), other, z, 1 - x)
    whole = put(put(whole, up, (z + 3) % 4, x), down, (z + 1) % 4, x)
    two = jnp.where(upper, up_two, down_two)
    three = hop(two, axis, [(2, 3), (1, 0)])
    other_two = swap_at(two, axis, range(4))
    whole = put(put(whole, other_up, (z + 3) % 4, 1 - x), other_down, (z + 1) % 4, 1 - x)
    whole = put(whole, two, across, x)
    other_three = swap_at(three, axis, (0, 3))
    whole = put(whole, other_two, across, 1 - x)
    return put_far(put_far(whole, three, x), other_three, 1 - x)


def line_summed(part_of, axis):
    if lax.axis_size(axis) != 8:
        return (scattered_sum(part_of, axis),)
    place = lax.axis_index(axis)
    z, x = place // 2, place % 2
    upper, edge = z >= 2, (z == 0) | (z == 3)
    across = jnp.where(upper, z - 2, z + 2)
    far = jnp.where(z == 0, 3, 0)
    above, below = jnp.minimum(z + 1, 3), jnp.maximum(z - 1, 0)

    def swapped(spot, spots):
        return swap_at(part_of(spot * 2 + 1 - x), axis, spots)

    def added(spot, given):
        return part_of(spot * 2 + x).astype(f32) + given.astype(f32)

    given_far = swapped(far, (0, 3))
    given_across = swapped(across, range(4))
    given_above, given_below = swapped(above, (0, 1, 2)), swapped(below, (1, 2, 3))
    given_own = swapped(z, range(4))
    three = hop(added(far, given_far).astype(bf16), axis, [(0, 1), (3, 2)])
    three, given_across, given_above, given_below = together(
        (three, given_across, given_above, given_below)
    )
    two = added(across, given_across) + jnp.where(edge, 0.0, three.astype(f32))
    two = two.astype(bf16)
    two_up, two_down, given_own = together(
        (hop(two, axis, UP[:2]), hop(two, axis, DOWN[1:]), given_own)
    )
    one_up = (added(above, given_above) + two_up.astype(f32)).astype(bf16)
    one_down = (added(below, given_below) + two_down.astype(f32)).astype(bf16)
    return added(z, given_own), hop(one_up, axis, UP), hop(one_down, axis, DOWN)


def scattered_sum(part_of, axis):
    count = lax.axis_size(axis)
    place = lax.axis_index(axis)
    half = count // 2
    outer, inner = place // 2, place % 2
    total = None
    for k in shift_order(half) + [0]:
        target = (outer + k) % half
        given = inner_swap(part_of(target * 2 + 1 - inner), axis)
        piece = part_of(target * 2 + inner).astype(f32) + given.astype(f32)
        if k:
            piece = outer_shift(piece.astype(bf16), axis, k).astype(f32)
        total = piece if total is None else total + piece
    return total


def rows_of(value, rows):
    return lambda place: lax.dynamic_slice_in_dim(value, place * rows, rows, 0)


def summed_over_seq(part, change):
    count = lax.axis_size("seq")
    length, columns = part.shape
    part = part.astype(bf16).reshape(count, length // count, columns)
    own = change(jnp.sum(lax.all_to_all(part, "seq", 0, 0).astype(f32), axis=0))
    return shared(own, "seq").reshape(length, own.shape[1])


def two_terms(value):
    high = value.astype(bf16)
    return [high, (value - high.astype(f32)).astype(bf16)]


def shared(own, axis):
    wide = jnp.broadcast_to(own[None], (lax.axis_size(axis),) + own.shape)
    return lax.all_to_all(wide, axis, 0, 0)


def matmul(a, b, dims=(((1,), (0,)), ((), ()))):
    return lax.dot_general(a, b, dims, preferred_element_type=f32)


TN = (((0,), (0,)), ((), ()))


def on_device(
    tokens,
    lengths,
    norm_gain,
    in_proj,
    conv_weight,
    conv_bias,
    x_proj,
    dt_proj,
    dt_bias,
    a_log,
    skip,
    out_proj,
    cotangent,
):
    batch, seq = lax.axis_size("batch"), lax.axis_size("seq")
    place = lax.axis_index("seq")
    span, model = tokens.shape[1:]
    length = span * seq
    in_rows = in_proj.shape[0]
    own = skip.shape[0]
    taps = conv_weight.shape[0]
    rank = dt_proj.shape[0]
    states = a_log.shape[1]
    width = own * batch

    halves = in_proj.reshape(in_rows, 2, batch, seq, own).transpose(1, 3, 0, 2, 4)
    halves = halves.reshape(2, seq, in_rows, width)
    columns = lax.all_to_all(halves[0], "seq", 0, 0)
    small = jnp.concatenate(
        [
            dt_proj,
            x_proj.T,
            a_log.T,
            conv_weight,
            conv_bias[None],
            dt_bias[None],
            skip[None],
            jnp.pad(norm_gain, (0, own - in_rows))[None],
        ],
        axis=0,
    )
    small = gathered(small, "batch", 1)
    cuts = [rank, 2 * rank + 2 * states, 2 * rank + 3 * states]
    cuts = cuts + [cuts[2] + taps + i for i in range(4)]
    delta_weight, select_weight, decay_logs, conv_taps, conv_shift, delta_shift, skip_gain, gain = (
        jnp.split(small, cuts, axis=0)
    )
    conv_taps, conv_shift = conv_taps.astype(f32), conv_shift.astype(f32)
    delta_shift, skip_gain = delta_shift.astype(f32), skip_gain.astype(f32)
    decay = -jnp.exp(decay_logs.astype(f32))
    gain = gain.reshape(batch, own)[:, :in_rows]
    columns, gain = together((columns, gain))
    gain = shared(gain, "seq")
    gate_columns, gain = together((halves[1], gain))
    gate_columns = lax.all_to_all(gate_columns, "seq", 0, 0)
    gain = gain.transpose(1, 0, 2).reshape(model).astype(f32)

    input_weight = gathered(columns.reshape(seq * in_rows, width), "batch")
    output_weight = gathered(out_proj, "batch")

    def normed(rows):
        rows = rows.astype(f32)
        scale = lax.rsqrt(jnp.mean(rows * rows, axis=-1, keepdims=True) + epsilon)
        return (rows * scale * gain).astype(bf16)

    stream = lax.all_gather(tokens[0], "seq", axis=0, tiled=True)
    gate_weight = gathered(gate_columns.reshape(seq * in_rows, width), "batch")
    normalized = normed(stream)
    upstream = line_gathered(cotangent[0], "seq")

    valid = (jnp.arange(length, dtype=jnp.int32) < lengths[0])[:, None]
    inner = matmul(normalized, input_weight).astype(bf16)
    padded = jnp.pad(inner, ((taps - 1, 0), (0, 0)))
    conv_out = conv_shift + jnp.zeros((length, width), f32)
    for tap in range(taps):
        conv_out = conv_out + conv_taps[tap] * padded[tap : tap + length].astype(f32)
    active = jax.nn.silu(conv_out).astype(bf16)
    active_f = active.astype(f32)

    partial, upstream = together((matmul(active, select_weight, NT), upstream))
    select = summed_over_seq(
        partial,
        lambda s: jnp.concatenate([s[:, :rank].astype(bf16)] + two_terms(s[:, rank:]), axis=1),
    )
    upstream = jnp.where(valid, upstream, 0).astype(bf16)
    gate_low = matmul(normalized, gate_weight).astype(bf16)
    d_gated = matmul(upstream, output_weight, NT)
    select, gate_low, d_gated = together((select, gate_low, d_gated))
    gate = gate_low.astype(f32)
    gate_sig = jax.nn.sigmoid(gate)
    delta_low = select[:, :rank]
    delta_raw = matmul(delta_low, delta_weight) + delta_shift
    delta = jax.nn.softplus(delta_raw)

    block = min(BLOCK, length)
    step = 256 // states
    rate = decay * LOG2E
    mixed, kept = scan_forward(delta, active, select, rate, block, step)
    mixed = mixed + skip_gain * active_f
    gated = (mixed * gate * gate_sig).astype(bf16)
    branch = matmul(gated, output_weight).astype(bf16)
    d_gated, branch = together((d_gated, branch))
    branch = lax.psum_scatter(branch, "seq", scatter_dimension=0, tiled=True)
    own_valid = lax.dynamic_slice_in_dim(valid, place * span, span, 0)
    own_stream = tokens[0].astype(f32)
    block_out = jnp.where(own_valid, own_stream + branch.astype(f32), 0.0)

    d_mixed = d_gated * gate * gate_sig
    d_gate = d_gated * mixed * gate_sig * (1.0 + gate * (1.0 - gate_sig))
    grad_skip = jnp.sum(d_mixed * active_f, axis=0, keepdims=True)
    d_gate_low = d_gate.astype(bf16)

    d_delta, d_active, d_bc, grad_log = scan_backward(
        delta, active, d_mixed, select, rate, decay, kept, block, step
    )
    d_raw = d_delta * jax.nn.sigmoid(delta_raw)
    grad_dt_bias = jnp.sum(d_raw, axis=0, keepdims=True)
    d_raw_low = d_raw.astype(bf16)
    grad_dt_proj = matmul(delta_low, d_raw_low, TN)
    partial = jnp.concatenate([matmul(d_raw_low, delta_weight, NT), d_bc], axis=1)
    d_select = summed_over_seq(partial, lambda s: s.astype(bf16))
    grad_gate = scattered_sum(
        rows_of(matmul(normalized, d_gate_low, TN).astype(bf16), model // batch), "batch"
    )
    d_select, branch, grad_gate = together((d_select, branch, grad_gate))
    grad_x_proj = matmul(d_select, active, TN)
    d_active = d_active + d_mixed * skip_gain + matmul(d_select, select_weight)
    conv_sig = jax.nn.sigmoid(conv_out)
    d_conv = (d_active * conv_sig * (1.0 + conv_out * (1.0 - conv_sig))).astype(bf16)
    d_conv_f = d_conv.astype(f32)
    grad_conv_bias = jnp.sum(d_conv_f, axis=0, keepdims=True)
    grad_conv = jnp.stack(
        [
            jnp.sum(d_conv_f * padded[tap : tap + length].astype(f32), axis=0)
            for tap in range(taps)
        ]
    )
    extended = jnp.pad(d_conv, ((0, taps - 1), (0, 0)))
    d_inner = jnp.zeros((length, width), f32)
    for tap in range(taps):
        offset = taps - 1 - tap
        d_inner = d_inner + conv_taps[tap] * extended[offset : offset + length].astype(f32)
    d_inner = d_inner.astype(bf16)
    grad_inner = matmul(normalized, d_inner, TN).astype(bf16)
    d_inner, grad_inner = together((d_inner, grad_inner))
    d_normalized = matmul(
        jnp.concatenate([d_inner, d_gate_low], axis=1),
        jnp.concatenate([input_weight, gate_weight], axis=1),
        NT,
    ).astype(bf16)
    grad_inner = scattered_sum(rows_of(grad_inner, model // batch), "batch")
    d_normalized, gated = together((d_normalized, gated))
    grad_output = lax.psum_scatter(
        matmul(gated, upstream, TN).astype(bf16), "batch", scatter_dimension=0, tiled=True
    ).astype(f32)
    d_normalized, *last_terms = line_summed(rows_of(d_normalized, span), "seq")

    both = jnp.concatenate([grad_inner, grad_gate], axis=1).astype(bf16)
    both = lax.all_to_all(both.reshape(seq, in_rows, 2 * width), "seq", 0, 0)
    both = both.reshape(seq, in_rows, 2, batch, own).transpose(1, 2, 3, 0, 4)
    grad_input = both.reshape(in_rows, 2 * batch * seq * own).astype(f32)

    small_grads = jnp.concatenate(
        [grad_dt_proj, grad_x_proj, grad_log, grad_conv, grad_conv_bias, grad_dt_bias, grad_skip],
        axis=0,
    )
    small_grads = lax.psum_scatter(small_grads, "batch", scatter_dimension=1, tiled=True)
    g_dt_proj, g_x_proj, g_log, g_conv, g_conv_bias, g_dt_bias, g_skip = jnp.split(
        small_grads, cuts[:-1], axis=0
    )

    own_upstream = jnp.where(own_valid, cotangent[0].astype(f32), 0.0)
    own_scale = lax.rsqrt(jnp.mean(own_stream * own_stream, axis=-1, keepdims=True) + epsilon)
    grad_gain = jnp.sum(grad_input * in_proj.astype(f32), axis=1) / norm_gain.astype(f32)
    (
        d_normalized, g_dt_proj, g_x_proj, g_log, g_conv, g_conv_bias, g_dt_bias, g_skip,
        grad_input, grad_gain,
    ) = together(
        (
            d_normalized, g_dt_proj, g_x_proj, g_log, g_conv, g_conv_bias, g_dt_bias, g_skip,
            grad_input, grad_gain,
        )
    )
    for term in last_terms:
        d_normalized = d_normalized + term.astype(f32)
    d_hat = d_normalized * gain
    grad_tokens = (
        own_scale * d_hat
        - own_stream
        * own_scale
        * own_scale
        * own_scale
        * jnp.mean(d_hat * own_stream, axis=-1, keepdims=True)
        + own_upstream
    )
    return (
        block_out[None],
        grad_tokens[None],
        grad_gain,
        grad_input,
        g_conv,
        g_conv_bias[0],
        g_x_proj.T,
        g_dt_proj,
        g_dt_bias[0],
        g_log.T,
        g_skip[0],
        grad_output,
    )


def solution(mesh):
    placed = (
        P("batch", "seq", None),
        P("batch"),
        P(("batch", "seq")),
        P(("batch", "seq"), None),
        P(None, ("batch", "seq")),
        P(("batch", "seq")),
        P(("batch", "seq"), None),
        P(None, ("batch", "seq")),
        P(("batch", "seq")),
        P(("batch", "seq"), None),
        P(("batch", "seq")),
        P(("batch", "seq"), None),
        P("batch", "seq", None),
    )
    return jax.shard_map(
        on_device,
        mesh=mesh,
        in_specs=placed,
        out_specs=(
            P("batch", "seq", None),
            P("batch", "seq", None),
            P(("batch", "seq")),
            P(("batch", "seq"), None),
            P(None, ("batch", "seq")),
            P(("batch", "seq")),
            P(("batch", "seq"), None),
            P(None, ("batch", "seq")),
            P(("batch", "seq")),
            P(("batch", "seq"), None),
            P(("batch", "seq")),
            P(("batch", "seq"), None),
        ),
        check_vma=False,
    )
```

```python
import functools

import jax
import jax.numpy as jnp
from jax import lax
from jax.experimental import pallas as pl
from jax.experimental.pallas import tpu as pltpu
from jax.sharding import PartitionSpec as P

bf16, f32 = jnp.bfloat16, jnp.float32
NT = (((1,), (1,)), ((), ()))
LANES = 128
GROUP = 32
BLOCK = 128
epsilon = 1e-05
LOG2E = 1.4426950408889634


def spread(tile, row, lanes, states):
    return jnp.broadcast_to(tile[row : row + 1, lanes], (states, LANES))


def selectors(select, states):
    low = select.shape[1] - 4 * states
    middle = low + 2 * states
    block = select[:, low:middle].astype(f32) + select[:, middle:].astype(f32)
    return jnp.transpose(block), block[:, :states], block[:, states:]


def block_diagonal(values, step):
    rows, states = values.shape
    wide = step * states
    spread_out = (
        lax.broadcasted_iota(jnp.int32, (states, wide), 1) % states
        == lax.broadcasted_iota(jnp.int32, (states, wide), 0)
    ).astype(bf16)
    value = jnp.dot(values.astype(bf16), spread_out, preferred_element_type=f32)
    place = lax.broadcasted_iota(jnp.int32, (rows, wide), 0) % step
    owner = lax.broadcasted_iota(jnp.int32, (rows, wide), 1) // states
    return jnp.where(place == owner, value, 0.0).astype(bf16)


def forward_body(tiles, step, delta, active, select, rate, mixed, kept, state, drive, columns):
    rows, states = delta.shape[0], rate.shape[0]
    wide = step * states

    @pl.when(pl.program_id(0) == 0)
    def _():
        state[...] = jnp.zeros_like(state)

    turned, _, c_block = selectors(select[...], states)
    columns[...] = turned[:states]
    drive[...] = delta[...] * active[...].astype(f32)
    rates = [rate[:, k * LANES : (k + 1) * LANES] for k in range(tiles)]

    def group(number, held):
        held = list(held)
        base = pl.multiple_of(number * GROUP, GROUP)
        delta_now, drive_now = delta.at[pl.ds(base, GROUP), :], drive.at[pl.ds(base, GROUP), :]
        b_now = pltpu.roll(columns[...], rows - base, 1)
        for j in range(GROUP):
            b_wide = jnp.broadcast_to(b_now[:, j : j + 1], (states, LANES))
            for k in range(tiles):
                lanes = slice(k * LANES, (k + 1) * LANES)
                decay = jnp.exp2(spread(delta_now, j, lanes, states) * rates[k])
                held[k] = decay * held[k] + spread(drive_now, j, lanes, states) * b_wide
                at = pl.ds(pl.multiple_of((base + j) * states, states), states)
                kept[at, lanes] = held[k].astype(bf16)
        return tuple(held)

    held = lax.fori_loop(
        0,
        rows // GROUP,
        group,
        tuple(state[:, k * LANES : (k + 1) * LANES] for k in range(tiles)),
    )
    for k in range(tiles):
        state[:, k * LANES : (k + 1) * LANES] = held[k]
    c_diag = block_diagonal(c_block, step)
    for q in range(rows // step):
        part = kept[q * wide : (q + 1) * wide, :]
        spot = slice(q * step, (q + 1) * step)
        mixed[spot, :] = jnp.dot(c_diag[spot, :], part, preferred_element_type=f32)


def scan_forward(delta, active, select, rate, block, step):
    length, width = delta.shape
    states = rate.shape[0]
    tiles = width // LANES
    return pl.pallas_call(
        functools.partial(forward_body, tiles, step),
        grid=(length // block,),
        in_specs=[
            pl.BlockSpec((block, width), lambda i: (i, 0)),
            pl.BlockSpec((block, width), lambda i: (i, 0)),
            pl.BlockSpec((block, select.shape[1]), lambda i: (i, 0)),
            pl.BlockSpec((states, width), lambda i: (0, 0)),
        ],
        out_specs=[
            pl.BlockSpec((block, width), lambda i: (i, 0)),
            pl.BlockSpec((block * states, width), lambda i: (i, 0)),
        ],
        out_shape=[
            jax.ShapeDtypeStruct((length, width), f32),
            jax.ShapeDtypeStruct((length * states, width), bf16),
        ],
        scratch_shapes=[
            pltpu.VMEM((states, width), f32),
            pltpu.VMEM((block, width), f32),
            pltpu.VMEM((states, block), f32),
        ],
        compiler_params=pltpu.CompilerParams(vmem_limit_bytes=48 << 20),
        cost_estimate=pl.CostEstimate(
            flops=8 * length * width * states,
            transcendentals=length * width * states,
            bytes_accessed=length * width * (2 * states + 10),
        ),
        name="scan_forward",
    )(delta, active, select, rate)


FEW = 4


def backward_body(
    tiles, step, delta, active, d_mixed, select, rate, decay_rate, kept, kept_before,
    d_delta, d_active, d_bc, d_log, push, drive, columns, diagonals, folding, timed, *pairs,
):
    grads, rated = pairs[:2], pairs[2:]
    rows, states = delta.shape[0], rate.shape[0]
    blocks = pl.num_programs(0)
    first = pl.program_id(0) == blocks - 1
    wide = step * states

    @pl.when(pl.program_id(0) == 0)
    def _():
        push[...] = jnp.zeros_like(push)
        d_log[...] = jnp.zeros_like(d_log)

    turned, b_block, _ = selectors(select[...], states)
    columns[...] = turned[states:]
    drive[...] = delta[...] * active[...].astype(f32)
    rates = [rate[:, k * LANES : (k + 1) * LANES] for k in range(tiles)]
    own_rates = [decay_rate[:, k * LANES : (k + 1) * LANES].astype(bf16) for k in range(tiles)]

    place = lax.broadcasted_iota(jnp.int32, (step, wide), 0)
    owner = lax.broadcasted_iota(jnp.int32, (step, wide), 1) // states
    ones_diag = (place == owner).astype(bf16)
    diag = (place == owner).astype(f32)
    diagonals[...] = block_diagonal(b_block, step)

    def sums_of(number):
        held, through_of = number % 2, {}

        def spots(q):
            at = number * GROUP + q * step
            tall = slice(q * wide, (q + 1) * wide)
            return slice(at, at + step), tall

        def through(q):
            spot, tall = spots(q)
            value = jnp.dot(diagonals[spot, :], grads[held][tall, :], preferred_element_type=f32)
            d_active[spot, :] = delta[spot, :] * value
            through_of[q] = active[spot, :].astype(f32) * value

        def summed(q):
            spot, tall = spots(q)
            value = jnp.dot(ones_diag, rated[held][tall, :], preferred_element_type=f32)
            d_delta[spot, :] = value + through_of[q]

        def d_b(q):
            spot, tall = spots(q)
            folding[spot, :wide] = diag * lax.dot_general(
                drive[spot, :].astype(bf16), grads[held][tall, :], NT, preferred_element_type=f32
            )

        def d_c(q):
            spot, _ = spots(q)
            own = slice(spot.start * states, spot.stop * states)
            folding[spot, wide:] = diag * lax.dot_general(
                d_mixed[spot, :].astype(bf16), kept[own, :], NT, preferred_element_type=f32
            )

        return [
            functools.partial(part, q)
            for q in range(GROUP // step)
            for part in (through, summed, d_b, d_c)
        ]

    carry = [push[:, k * LANES : (k + 1) * LANES] for k in range(tiles)]
    waiting = []
    for number in reversed(range(rows // GROUP)):
        pace = GROUP // max(len(waiting), 1)
        sums = [None] * tiles
        held = number % 2
        for j in reversed(range(GROUP)):
            row = number * GROUP + j
            c_wide = jnp.broadcast_to(columns[:, row : row + 1], (states, LANES))
            at = slice(j * states, (j + 1) * states)
            for k in range(tiles):
                lanes = slice(k * LANES, (k + 1) * LANES)
                if row:
                    before = kept[(row - 1) * states : row * states, lanes]
                else:
                    before = jnp.where(first, jnp.zeros((), bf16), kept_before[:, lanes])
                step_size = spread(delta, row, lanes, states)
                grad = spread(d_mixed, row, lanes, states) * c_wide + carry[k]
                carry[k] = jnp.exp2(step_size * rates[k]) * grad
                grads[held][at, lanes] = grad.astype(bf16)
                rated_now = carry[k].astype(bf16) * before * own_rates[k]
                rated[held][at, lanes] = rated_now
                timed_now = rated_now * step_size.astype(bf16)
                sums[k] = timed_now if sums[k] is None else sums[k] + timed_now
                if j % FEW == 0:
                    spot = row // FEW * states
                    timed[spot : spot + states, lanes] = sums[k]
                    sums[k] = None
            if waiting and j % pace == 0:
                waiting.pop(0)()
        while waiting:
            waiting.pop(0)()
        waiting = sums_of(number)
    while waiting:
        waiting.pop(0)()
    for k in range(tiles):
        push[:, k * LANES : (k + 1) * LANES] = carry[k]
    fold = (
        lax.broadcasted_iota(jnp.int32, (wide, states), 0) % states
        == lax.broadcasted_iota(jnp.int32, (wide, states), 1)
    ).astype(bf16)
    for number in range(2):
        value = folding[:, number * wide : (number + 1) * wide]
        high = value.astype(bf16)
        d_bc[:, number * states : (number + 1) * states] = jnp.dot(
            high, fold, preferred_element_type=f32
        )
    span = rows // FEW * states
    pick = (
        lax.broadcasted_iota(jnp.int32, (states, span), 1) % states
        == lax.broadcasted_iota(jnp.int32, (states, span), 0)
    ).astype(bf16)
    d_log[...] += jnp.dot(pick, timed[...], preferred_element_type=f32)


def scan_backward(delta, active, d_mixed, select, rate, decay_rate, kept, block, step):
    length, width = delta.shape
    states = rate.shape[0]
    tiles = width // LANES
    blocks = length // block
    back = lambda i: (blocks - 1 - i, 0)
    return pl.pallas_call(
        functools.partial(backward_body, tiles, step),
        grid=(blocks,),
        in_specs=[
            pl.BlockSpec((block, width), back),
            pl.BlockSpec((block, width), back),
            pl.BlockSpec((block, width), back),
            pl.BlockSpec((block, select.shape[1]), back),
            pl.BlockSpec((states, width), lambda i: (0, 0)),
            pl.BlockSpec((states, width), lambda i: (0, 0)),
            pl.BlockSpec((block * states, width), back),
            pl.BlockSpec(
                (states, width), lambda i: (jnp.maximum((blocks - 1 - i) * block - 1, 0), 0)
            ),
        ],
        out_specs=[
            pl.BlockSpec((block, width), back),
            pl.BlockSpec((block, width), back),
            pl.BlockSpec((block, 2 * states), back),
            pl.BlockSpec((states, width), lambda i: (0, 0)),
        ],
        out_shape=[
            jax.ShapeDtypeStruct((length, width), f32),
            jax.ShapeDtypeStruct((length, width), f32),
            jax.ShapeDtypeStruct((length, 2 * states), f32),
            jax.ShapeDtypeStruct((states, width), f32),
        ],
        scratch_shapes=[
            pltpu.VMEM((states, width), f32),
            pltpu.VMEM((block, width), f32),
            pltpu.VMEM((states, block), f32),
            pltpu.VMEM((block, step * states), bf16),
            pltpu.VMEM((block, 2 * step * states), f32),
            pltpu.VMEM((block // FEW * states, width), bf16),
        ]
        + [pltpu.VMEM((GROUP * states, width), bf16)] * 4,
        compiler_params=pltpu.CompilerParams(vmem_limit_bytes=48 << 20),
        cost_estimate=pl.CostEstimate(
            flops=20 * length * width * states,
            transcendentals=length * width * states,
            bytes_accessed=length * width * (2 * states + 20),
        ),
        name="scan_backward",
    )(delta, active, d_mixed, select, rate, decay_rate, kept, kept)


together = lax.optimization_barrier


def inner_swap(value, axis):
    count = lax.axis_size(axis)
    return lax.ppermute(value, axis, [(i, i ^ 1) for i in range(count)])


def outer_shift(value, axis, steps):
    count = lax.axis_size(axis)
    half = count // 2
    pairs = [(i, (i // 2 + steps) % half * 2 + i % 2) for i in range(count)]
    return lax.ppermute(value, axis, pairs)


def shift_order(half):
    return sorted(range(1, half), key=lambda k: (-min(k, half - k), k))


def pieces_of_all(own, axis):
    count = lax.axis_size(axis)
    place = lax.axis_index(axis)
    half = count // 2
    outer, inner = place // 2, place % 2
    yield place, own
    arrived = {k: outer_shift(own, axis, k) for k in shift_order(half)}
    yield outer * 2 + 1 - inner, inner_swap(own, axis)
    for k, piece in arrived.items():
        origin = (outer - k + half) % half
        yield origin * 2 + inner, piece
    for k, piece in arrived.items():
        origin = (outer - k + half) % half
        yield origin * 2 + 1 - inner, inner_swap(piece, axis)


def gathered(own, axis, dim=0):
    count, size = lax.axis_size(axis), own.shape[dim]
    whole = jnp.zeros(own.shape[:dim] + (count * size,) + own.shape[dim + 1 :], own.dtype)
    for place, piece in pieces_of_all(own, axis):
        whole = lax.dynamic_update_slice_in_dim(whole, piece, place * size, dim)
    return whole


def hop(value, axis, moves):
    pairs = [(a * 2 + i, b * 2 + i) for a, b in moves for i in (0, 1)]
    return lax.ppermute(value, axis, pairs)


def swap_at(value, axis, spots):
    pairs = [(a * 2 + i, a * 2 + 1 - i) for a in spots for i in (0, 1)]
    return lax.ppermute(value, axis, pairs)


UP, DOWN = [(0, 1), (1, 2), (2, 3)], [(1, 0), (2, 1), (3, 2)]


def line_gathered(own, axis, held):
    if lax.axis_size(axis) != 8:
        return lax.all_gather(own, axis, axis=0, tiled=True), held
    place = lax.axis_index(axis)
    z, x = place // 2, place % 2
    rows = own.shape[0]
    upper, edge = z >= 2, (z == 0) | (z == 3)
    across = jnp.where(upper, z - 2, z + 2)
    far = jnp.where(z == 3, 0, 3)

    def put(whole, piece, spot, side):
        return lax.dynamic_update_slice_in_dim(whole, piece, (spot * 2 + side) * rows, 0)

    def put_far(whole, piece, side):
        held = lax.dynamic_slice_in_dim(whole, (far * 2 + side) * rows, rows, 0)
        return put(whole, jnp.where(edge, piece, held), far, side)

    whole = jnp.zeros((8 * rows,) + own.shape[1:], own.dtype)
    up, down, other, held = together(
        (hop(own, axis, UP), hop(own, axis, DOWN), swap_at(own, axis, range(4)), held)
    )
    up_two, down_two = hop(up, axis, UP[1:]), hop(down, axis, DOWN[:2])
    other_up, other_down = swap_at(up, axis, (1, 2, 3)), swap_at(down, axis, (0, 1, 2))
    whole = put(put(whole, own, z, x), other, z, 1 - x)
    whole = put(put(whole, up, (z + 3) % 4, x), down, (z + 1) % 4, x)
    two = jnp.where(upper, up_two, down_two)
    three = hop(two, axis, [(2, 3), (1, 0)])
    other_two = swap_at(two, axis, range(4))
    whole = put(put(whole, other_up, (z + 3) % 4, 1 - x), other_down, (z + 1) % 4, 1 - x)
    whole = put(whole, two, across, x)
    other_three = swap_at(three, axis, (0, 3))
    whole = put(whole, other_two, across, 1 - x)
    return put_far(put_far(whole, three, x), other_three, 1 - x), held


def line_summed(part_of, axis):
    if lax.axis_size(axis) != 8:
        return (scattered_sum(part_of, axis),)
    place = lax.axis_index(axis)
    z, x = place // 2, place % 2
    upper, edge = z >= 2, (z == 0) | (z == 3)
    across = jnp.where(upper, z - 2, z + 2)
    far = jnp.where(z == 0, 3, 0)
    above, below = jnp.minimum(z + 1, 3), jnp.maximum(z - 1, 0)

    def swapped(spot, spots):
        return swap_at(part_of(spot * 2 + 1 - x), axis, spots)

    def added(spot, given):
        return part_of(spot * 2 + x).astype(f32) + given.astype(f32)

    given_far = swapped(far, (0, 3))
    given_across = swapped(across, range(4))
    given_above, given_below = swapped(above, (0, 1, 2)), swapped(below, (1, 2, 3))
    given_own = swapped(z, range(4))
    three = hop(added(far, given_far).astype(bf16), axis, [(0, 1), (3, 2)])
    three, given_across, given_above, given_below = together(
        (three, given_across, given_above, given_below)
    )
    two = added(across, given_across) + jnp.where(edge, 0.0, three.astype(f32))
    two = two.astype(bf16)
    two_up, two_down, given_own = together(
        (hop(two, axis, UP[:2]), hop(two, axis, DOWN[1:]), given_own)
    )
    one_up = (added(above, given_above) + two_up.astype(f32)).astype(bf16)
    one_down = (added(below, given_below) + two_down.astype(f32)).astype(bf16)
    return added(z, given_own), hop(one_up, axis, UP), hop(one_down, axis, DOWN)


def scattered_sum(part_of, axis):
    count = lax.axis_size(axis)
    place = lax.axis_index(axis)
    half = count // 2
    outer, inner = place // 2, place % 2
    total = None
    for k in shift_order(half) + [0]:
        target = (outer + k) % half
        given = inner_swap(part_of(target * 2 + 1 - inner), axis)
        piece = part_of(target * 2 + inner).astype(f32) + given.astype(f32)
        if k:
            piece = outer_shift(piece.astype(bf16), axis, k).astype(f32)
        total = piece if total is None else total + piece
    return total


def rows_of(value, rows):
    return lambda place: lax.dynamic_slice_in_dim(value, place * rows, rows, 0)


def summed_over_seq(part, change):
    count = lax.axis_size("seq")
    length, columns = part.shape
    part = part.astype(bf16).reshape(count, length // count, columns)
    own = change(jnp.sum(lax.all_to_all(part, "seq", 0, 0).astype(f32), axis=0))
    return shared(own, "seq").reshape(length, own.shape[1])


def two_terms(value):
    high = value.astype(bf16)
    return [high, (value - high.astype(f32)).astype(bf16)]


def shared(own, axis):
    wide = jnp.broadcast_to(own[None], (lax.axis_size(axis),) + own.shape)
    return lax.all_to_all(wide, axis, 0, 0)


def matmul(a, b, dims=(((1,), (0,)), ((), ()))):
    return lax.dot_general(a, b, dims, preferred_element_type=f32)


TN = (((0,), (0,)), ((), ()))


def on_device(
    tokens,
    lengths,
    norm_gain,
    in_proj,
    conv_weight,
    conv_bias,
    x_proj,
    dt_proj,
    dt_bias,
    a_log,
    skip,
    out_proj,
    cotangent,
):
    batch, seq = lax.axis_size("batch"), lax.axis_size("seq")
    place = lax.axis_index("seq")
    span, model = tokens.shape[1:]
    length = span * seq
    in_rows = in_proj.shape[0]
    own = skip.shape[0]
    taps = conv_weight.shape[0]
    rank = dt_proj.shape[0]
    states = a_log.shape[1]
    width = own * batch

    halves = in_proj.reshape(in_rows, 2, batch, seq, own).transpose(1, 3, 0, 2, 4)
    halves = halves.reshape(2, seq, in_rows, width)
    columns = lax.all_to_all(halves[0], "seq", 0, 0)
    small = jnp.concatenate(
        [
            dt_proj,
            x_proj.T,
            a_log.T,
            conv_weight,
            conv_bias[None],
            dt_bias[None],
            skip[None],
            jnp.pad(norm_gain, (0, own - in_rows))[None],
        ],
        axis=0,
    )
    small = gathered(small, "batch", 1)
    cuts = [rank, 2 * rank + 2 * states, 2 * rank + 3 * states]
    cuts = cuts + [cuts[2] + taps + i for i in range(4)]
    delta_weight, select_weight, decay_logs, conv_taps, conv_shift, delta_shift, skip_gain, gain = (
        jnp.split(small, cuts, axis=0)
    )
    conv_taps, conv_shift = conv_taps.astype(f32), conv_shift.astype(f32)
    delta_shift, skip_gain = delta_shift.astype(f32), skip_gain.astype(f32)
    decay = -jnp.exp(decay_logs.astype(f32))
    gain = gain.reshape(batch, own)[:, :in_rows]
    columns, gain = together((columns, gain))
    gain = shared(gain, "seq")
    gate_columns, gain = together((halves[1], gain))
    gate_columns = lax.all_to_all(gate_columns, "seq", 0, 0)
    gain = gain.transpose(1, 0, 2).reshape(model).astype(f32)

    input_weight = gathered(columns.reshape(seq * in_rows, width), "batch")

    def normed(rows):
        rows = rows.astype(f32)
        scale = lax.rsqrt(jnp.mean(rows * rows, axis=-1, keepdims=True) + epsilon)
        return (rows * scale * gain).astype(bf16)

    stream = lax.all_gather(tokens[0], "seq", axis=0, tiled=True)
    gate_weight = gathered(gate_columns.reshape(seq * in_rows, width), "batch")
    normalized = normed(stream)
    upstream, out_proj = line_gathered(cotangent[0], "seq", out_proj)
    output_weight = gathered(out_proj, "batch")

    valid = (jnp.arange(length, dtype=jnp.int32) < lengths[0])[:, None]
    inner = matmul(normalized, input_weight).astype(bf16)
    padded = jnp.pad(inner, ((taps - 1, 0), (0, 0)))
    conv_out = conv_shift + jnp.zeros((length, width), f32)
    for tap in range(taps):
        conv_out = conv_out + conv_taps[tap] * padded[tap : tap + length].astype(f32)
    active = jax.nn.silu(conv_out).astype(bf16)
    active_f = active.astype(f32)

    partial, upstream = together((matmul(active, select_weight, NT), upstream))
    select = summed_over_seq(
        partial,
        lambda s: jnp.concatenate([s[:, :rank].astype(bf16)] + two_terms(s[:, rank:]), axis=1),
    )
    upstream = jnp.where(valid, upstream, 0).astype(bf16)
    gate_low = matmul(normalized, gate_weight).astype(bf16)
    d_gated = matmul(upstream, output_weight, NT)
    select, gate_low, d_gated = together((select, gate_low, d_gated))
    gate = gate_low.astype(f32)
    gate_sig = jax.nn.sigmoid(gate)
    delta_low = select[:, :rank]
    delta_raw = matmul(delta_low, delta_weight) + delta_shift
    delta = jax.nn.softplus(delta_raw)

    block = min(BLOCK, length)
    step = 256 // states
    rate = decay * LOG2E
    mixed, kept = scan_forward(delta, active, select, rate, block, step)
    mixed = mixed + skip_gain * active_f
    gated = (mixed * gate * gate_sig).astype(bf16)
    branch = matmul(gated, output_weight).astype(bf16)
    d_gated, branch = together((d_gated, branch))
    branch = lax.psum_scatter(branch, "seq", scatter_dimension=0, tiled=True)
    own_valid = lax.dynamic_slice_in_dim(valid, place * span, span, 0)
    own_stream = tokens[0].astype(f32)

    d_mixed = d_gated * gate * gate_sig
    d_gate = d_gated * mixed * gate_sig * (1.0 + gate * (1.0 - gate_sig))
    grad_skip = jnp.sum(d_mixed * active_f, axis=0, keepdims=True)
    d_gate_low = d_gate.astype(bf16)

    d_delta, d_active, d_bc, grad_log = scan_backward(
        delta, active, d_mixed, select, rate, decay, kept, block, step
    )
    d_raw = d_delta * jax.nn.sigmoid(delta_raw)
    grad_dt_bias = jnp.sum(d_raw, axis=0, keepdims=True)
    d_raw_low = d_raw.astype(bf16)
    grad_dt_proj = matmul(delta_low, d_raw_low, TN)
    partial = jnp.concatenate([matmul(d_raw_low, delta_weight, NT), d_bc], axis=1)
    d_select = summed_over_seq(partial, lambda s: s.astype(bf16))
    grad_gate = scattered_sum(
        rows_of(matmul(normalized, d_gate_low, TN).astype(bf16), model // batch), "batch"
    )
    d_select, grad_gate = together((d_select, grad_gate))
    grad_x_proj = matmul(d_select, active, TN)
    d_active = d_active + d_mixed * skip_gain + matmul(d_select, select_weight)
    conv_sig = jax.nn.sigmoid(conv_out)
    d_conv = (d_active * conv_sig * (1.0 + conv_out * (1.0 - conv_sig))).astype(bf16)
    d_conv_f = d_conv.astype(f32)
    grad_conv_bias = jnp.sum(d_conv_f, axis=0, keepdims=True)
    grad_conv = jnp.stack(
        [
            jnp.sum(d_conv_f * padded[tap : tap + length].astype(f32), axis=0)
            for tap in range(taps)
        ]
    )
    extended = jnp.pad(d_conv, ((0, taps - 1), (0, 0)))
    d_inner = jnp.zeros((length, width), f32)
    for tap in range(taps):
        offset = taps - 1 - tap
        d_inner = d_inner + conv_taps[tap] * extended[offset : offset + length].astype(f32)
    d_inner = d_inner.astype(bf16)
    grad_inner = matmul(normalized, d_inner, TN).astype(bf16)
    d_inner, grad_inner, branch = together((d_inner, grad_inner, branch))
    d_normalized = matmul(
        jnp.concatenate([d_inner, d_gate_low], axis=1),
        jnp.concatenate([input_weight, gate_weight], axis=1),
        NT,
    ).astype(bf16)
    grad_inner = scattered_sum(rows_of(grad_inner, model // batch), "batch")
    grad_gate = grad_gate.astype(bf16).reshape(seq, in_rows, width)
    grad_gate = lax.all_to_all(grad_gate, "seq", 0, 0)
    d_normalized, gated, grad_gate = together((d_normalized, gated, grad_gate))
    grad_output = lax.psum_scatter(
        matmul(gated, upstream, TN).astype(bf16), "batch", scatter_dimension=0, tiled=True
    ).astype(f32)
    d_normalized, *last_terms = line_summed(rows_of(d_normalized, span), "seq")

    block_out = jnp.where(own_valid, own_stream + branch.astype(f32), 0.0)

    def columns_of(part):
        part = part.reshape(seq, in_rows, batch, own).transpose(1, 2, 0, 3)
        return part.reshape(in_rows, batch * seq * own).astype(f32)

    grad_inner = grad_inner.astype(bf16).reshape(seq, in_rows, width)
    grad_inner = lax.all_to_all(grad_inner, "seq", 0, 0)
    grad_input = jnp.concatenate([columns_of(grad_inner), columns_of(grad_gate)], axis=1)

    small_grads = jnp.concatenate(
        [grad_dt_proj, grad_x_proj, grad_log, grad_conv, grad_conv_bias, grad_dt_bias, grad_skip],
        axis=0,
    )
    small_grads = lax.psum_scatter(small_grads, "batch", scatter_dimension=1, tiled=True)
    g_dt_proj, g_x_proj, g_log, g_conv, g_conv_bias, g_dt_bias, g_skip = jnp.split(
        small_grads, cuts[:-1], axis=0
    )

    own_upstream = jnp.where(own_valid, cotangent[0].astype(f32), 0.0)
    own_scale = lax.rsqrt(jnp.mean(own_stream * own_stream, axis=-1, keepdims=True) + epsilon)
    grad_gain = jnp.sum(grad_input * in_proj.astype(f32), axis=1) / norm_gain.astype(f32)
    (
        d_normalized, g_dt_proj, g_x_proj, g_log, g_conv, g_conv_bias, g_dt_bias, g_skip,
        grad_input, grad_gain, grad_output,
    ) = together(
        (
            d_normalized, g_dt_proj, g_x_proj, g_log, g_conv, g_conv_bias, g_dt_bias, g_skip,
            grad_input, grad_gain, grad_output,
        )
    )
    for term in last_terms:
        d_normalized = d_normalized + term.astype(f32)
    d_hat = d_normalized * gain
    grad_tokens = (
        own_scale * d_hat
        - own_stream
        * own_scale
        * own_scale
        * own_scale
        * jnp.mean(d_hat * own_stream, axis=-1, keepdims=True)
        + own_upstream
    )
    return (
        block_out[None],
        grad_tokens[None],
        grad_gain,
        grad_input,
        g_conv,
        g_conv_bias[0],
        g_x_proj.T,
        g_dt_proj,
        g_dt_bias[0],
        g_log.T,
        g_skip[0],
        grad_output,
    )


def solution(mesh):
    placed = (
        P("batch", "seq", None),
        P("batch"),
        P(("batch", "seq")),
        P(("batch", "seq"), None),
        P(None, ("batch", "seq")),
        P(("batch", "seq")),
        P(("batch", "seq"), None),
        P(None, ("batch", "seq")),
        P(("batch", "seq")),
        P(("batch", "seq"), None),
        P(("batch", "seq")),
        P(("batch", "seq"), None),
        P("batch", "seq", None),
    )
    return jax.shard_map(
        on_device,
        mesh=mesh,
        in_specs=placed,
        out_specs=(
            P("batch", "seq", None),
            P("batch", "seq", None),
            P(("batch", "seq")),
            P(("batch", "seq"), None),
            P(None, ("batch", "seq")),
            P(("batch", "seq")),
            P(("batch", "seq"), None),
            P(None, ("batch", "seq")),
            P(("batch", "seq")),
            P(("batch", "seq"), None),
            P(("batch", "seq")),
            P(("batch", "seq"), None),
        ),
        check_vma=False,
    )
```

```python
import functools

import jax
import jax.numpy as jnp
from jax import lax
from jax.experimental import pallas as pl
from jax.experimental.pallas import tpu as pltpu
from jax.sharding import PartitionSpec as P

bf16, f32 = jnp.bfloat16, jnp.float32
NT = (((1,), (1,)), ((), ()))
LANES = 128
GROUP = 32
BLOCK = 128
epsilon = 1e-05
LOG2E = 1.4426950408889634


def spread(tile, row, lanes, states):
    return jnp.broadcast_to(tile[row : row + 1, lanes], (states, LANES))


def selectors(select, states):
    low = select.shape[1] - 4 * states
    middle = low + 2 * states
    block = select[:, low:middle].astype(f32) + select[:, middle:].astype(f32)
    return jnp.transpose(block), block[:, :states], block[:, states:]


def block_diagonal(values, step):
    rows, states = values.shape
    wide = step * states
    spread_out = (
        lax.broadcasted_iota(jnp.int32, (states, wide), 1) % states
        == lax.broadcasted_iota(jnp.int32, (states, wide), 0)
    ).astype(bf16)
    value = jnp.dot(values.astype(bf16), spread_out, preferred_element_type=f32)
    place = lax.broadcasted_iota(jnp.int32, (rows, wide), 0) % step
    owner = lax.broadcasted_iota(jnp.int32, (rows, wide), 1) // states
    return jnp.where(place == owner, value, 0.0).astype(bf16)


def forward_body(tiles, step, delta, active, select, rate, mixed, kept, state, drive, columns):
    rows, states = delta.shape[0], rate.shape[0]
    wide = step * states

    @pl.when(pl.program_id(0) == 0)
    def _():
        state[...] = jnp.zeros_like(state)

    turned, _, c_block = selectors(select[...], states)
    columns[...] = turned[:states]
    drive[...] = delta[...] * active[...].astype(f32)
    rates = [rate[:, k * LANES : (k + 1) * LANES] for k in range(tiles)]

    def group(number, held):
        held = list(held)
        base = pl.multiple_of(number * GROUP, GROUP)
        delta_now, drive_now = delta.at[pl.ds(base, GROUP), :], drive.at[pl.ds(base, GROUP), :]
        b_now = pltpu.roll(columns[...], rows - base, 1)
        for j in range(GROUP):
            b_wide = jnp.broadcast_to(b_now[:, j : j + 1], (states, LANES))
            for k in range(tiles):
                lanes = slice(k * LANES, (k + 1) * LANES)
                decay = jnp.exp2(spread(delta_now, j, lanes, states) * rates[k])
                held[k] = decay * held[k] + spread(drive_now, j, lanes, states) * b_wide
                at = pl.ds(pl.multiple_of((base + j) * states, states), states)
                kept[at, lanes] = held[k].astype(bf16)
        return tuple(held)

    held = lax.fori_loop(
        0,
        rows // GROUP,
        group,
        tuple(state[:, k * LANES : (k + 1) * LANES] for k in range(tiles)),
    )
    for k in range(tiles):
        state[:, k * LANES : (k + 1) * LANES] = held[k]
    c_diag = block_diagonal(c_block, step)
    for q in range(rows // step):
        part = kept[q * wide : (q + 1) * wide, :]
        spot = slice(q * step, (q + 1) * step)
        mixed[spot, :] = jnp.dot(c_diag[spot, :], part, preferred_element_type=f32)


def scan_forward(delta, active, select, rate, block, step):
    length, width = delta.shape
    states = rate.shape[0]
    tiles = width // LANES
    return pl.pallas_call(
        functools.partial(forward_body, tiles, step),
        grid=(length // block,),
        in_specs=[
            pl.BlockSpec((block, width), lambda i: (i, 0)),
            pl.BlockSpec((block, width), lambda i: (i, 0)),
            pl.BlockSpec((block, select.shape[1]), lambda i: (i, 0)),
            pl.BlockSpec((states, width), lambda i: (0, 0)),
        ],
        out_specs=[
            pl.BlockSpec((block, width), lambda i: (i, 0)),
            pl.BlockSpec((block * states, width), lambda i: (i, 0)),
        ],
        out_shape=[
            jax.ShapeDtypeStruct((length, width), f32),
            jax.ShapeDtypeStruct((length * states, width), bf16),
        ],
        scratch_shapes=[
            pltpu.VMEM((states, width), f32),
            pltpu.VMEM((block, width), f32),
            pltpu.VMEM((states, block), f32),
        ],
        compiler_params=pltpu.CompilerParams(vmem_limit_bytes=48 << 20),
        cost_estimate=pl.CostEstimate(
            flops=8 * length * width * states,
            transcendentals=length * width * states,
            bytes_accessed=length * width * (2 * states + 10),
        ),
        name="scan_forward",
    )(delta, active, select, rate)


FEW = 4


def backward_body(
    tiles, step, delta, active, d_mixed, select, rate, decay_rate, kept, kept_before,
    d_delta, d_active, d_bc, d_log, push, drive, columns, diagonals, folding, timed, *pairs,
):
    grads, rated = pairs[:2], pairs[2:]
    rows, states = delta.shape[0], rate.shape[0]
    blocks = pl.num_programs(0)
    first = pl.program_id(0) == blocks - 1
    wide = step * states

    @pl.when(pl.program_id(0) == 0)
    def _():
        push[...] = jnp.zeros_like(push)
        d_log[...] = jnp.zeros_like(d_log)

    turned, b_block, _ = selectors(select[...], states)
    columns[...] = turned[states:]
    drive[...] = delta[...] * active[...].astype(f32)
    rates = [rate[:, k * LANES : (k + 1) * LANES] for k in range(tiles)]
    own_rates = [decay_rate[:, k * LANES : (k + 1) * LANES].astype(bf16) for k in range(tiles)]

    place = lax.broadcasted_iota(jnp.int32, (step, wide), 0)
    owner = lax.broadcasted_iota(jnp.int32, (step, wide), 1) // states
    ones_diag = (place == owner).astype(bf16)
    diag = (place == owner).astype(f32)
    diagonals[...] = block_diagonal(b_block, step)

    def sums_of(number):
        held, through_of = number % 2, {}

        def spots(q):
            at = number * GROUP + q * step
            tall = slice(q * wide, (q + 1) * wide)
            return slice(at, at + step), tall

        def through(q):
            spot, tall = spots(q)
            value = jnp.dot(diagonals[spot, :], grads[held][tall, :], preferred_element_type=f32)
            d_active[spot, :] = delta[spot, :] * value
            through_of[q] = active[spot, :].astype(f32) * value

        def summed(q):
            spot, tall = spots(q)
            value = jnp.dot(ones_diag, rated[held][tall, :], preferred_element_type=f32)
            d_delta[spot, :] = value + through_of[q]

        def d_b(q):
            spot, tall = spots(q)
            folding[spot, :wide] = diag * lax.dot_general(
                drive[spot, :].astype(bf16), grads[held][tall, :], NT, preferred_element_type=f32
            )

        def d_c(q):
            spot, _ = spots(q)
            own = slice(spot.start * states, spot.stop * states)
            folding[spot, wide:] = diag * lax.dot_general(
                d_mixed[spot, :].astype(bf16), kept[own, :], NT, preferred_element_type=f32
            )

        return [
            functools.partial(part, q)
            for q in range(GROUP // step)
            for part in (through, summed, d_b, d_c)
        ]

    carry = [push[:, k * LANES : (k + 1) * LANES] for k in range(tiles)]
    waiting = []
    for number in reversed(range(rows // GROUP)):
        pace = GROUP // max(len(waiting), 1)
        sums = [None] * tiles
        held = number % 2
        for j in reversed(range(GROUP)):
            row = number * GROUP + j
            c_wide = jnp.broadcast_to(columns[:, row : row + 1], (states, LANES))
            at = slice(j * states, (j + 1) * states)
            for k in range(tiles):
                lanes = slice(k * LANES, (k + 1) * LANES)
                if row:
                    before = kept[(row - 1) * states : row * states, lanes]
                else:
                    before = jnp.where(first, jnp.zeros((), bf16), kept_before[:, lanes])
                step_size = spread(delta, row, lanes, states)
                grad = spread(d_mixed, row, lanes, states) * c_wide + carry[k]
                carry[k] = jnp.exp2(step_size * rates[k]) * grad
                grads[held][at, lanes] = grad.astype(bf16)
                rated_now = carry[k].astype(bf16) * before * own_rates[k]
                rated[held][at, lanes] = rated_now
                timed_now = rated_now * step_size.astype(bf16)
                sums[k] = timed_now if sums[k] is None else sums[k] + timed_now
                if j % FEW == 0:
                    spot = row // FEW * states
                    timed[spot : spot + states, lanes] = sums[k]
                    sums[k] = None
            if waiting and j % pace == 0:
                waiting.pop(0)()
        while waiting:
            waiting.pop(0)()
        waiting = sums_of(number)
    while waiting:
        waiting.pop(0)()
    for k in range(tiles):
        push[:, k * LANES : (k + 1) * LANES] = carry[k]
    fold = (
        lax.broadcasted_iota(jnp.int32, (wide, states), 0) % states
        == lax.broadcasted_iota(jnp.int32, (wide, states), 1)
    ).astype(bf16)
    for number in range(2):
        value = folding[:, number * wide : (number + 1) * wide]
        high = value.astype(bf16)
        d_bc[:, number * states : (number + 1) * states] = jnp.dot(
            high, fold, preferred_element_type=f32
        )
    span = rows // FEW * states
    pick = (
        lax.broadcasted_iota(jnp.int32, (states, span), 1) % states
        == lax.broadcasted_iota(jnp.int32, (states, span), 0)
    ).astype(bf16)
    d_log[...] += jnp.dot(pick, timed[...], preferred_element_type=f32)


def scan_backward(delta, active, d_mixed, select, rate, decay_rate, kept, block, step):
    length, width = delta.shape
    states = rate.shape[0]
    tiles = width // LANES
    blocks = length // block
    back = lambda i: (blocks - 1 - i, 0)
    return pl.pallas_call(
        functools.partial(backward_body, tiles, step),
        grid=(blocks,),
        in_specs=[
            pl.BlockSpec((block, width), back),
            pl.BlockSpec((block, width), back),
            pl.BlockSpec((block, width), back),
            pl.BlockSpec((block, select.shape[1]), back),
            pl.BlockSpec((states, width), lambda i: (0, 0)),
            pl.BlockSpec((states, width), lambda i: (0, 0)),
            pl.BlockSpec((block * states, width), back),
            pl.BlockSpec(
                (states, width), lambda i: (jnp.maximum((blocks - 1 - i) * block - 1, 0), 0)
            ),
        ],
        out_specs=[
            pl.BlockSpec((block, width), back),
            pl.BlockSpec((block, width), back),
            pl.BlockSpec((block, 2 * states), back),
            pl.BlockSpec((states, width), lambda i: (0, 0)),
        ],
        out_shape=[
            jax.ShapeDtypeStruct((length, width), f32),
            jax.ShapeDtypeStruct((length, width), f32),
            jax.ShapeDtypeStruct((length, 2 * states), f32),
            jax.ShapeDtypeStruct((states, width), f32),
        ],
        scratch_shapes=[
            pltpu.VMEM((states, width), f32),
            pltpu.VMEM((block, width), f32),
            pltpu.VMEM((states, block), f32),
            pltpu.VMEM((block, step * states), bf16),
            pltpu.VMEM((block, 2 * step * states), f32),
            pltpu.VMEM((block // FEW * states, width), bf16),
        ]
        + [pltpu.VMEM((GROUP * states, width), bf16)] * 4,
        compiler_params=pltpu.CompilerParams(vmem_limit_bytes=48 << 20),
        cost_estimate=pl.CostEstimate(
            flops=20 * length * width * states,
            transcendentals=length * width * states,
            bytes_accessed=length * width * (2 * states + 20),
        ),
        name="scan_backward",
    )(delta, active, d_mixed, select, rate, decay_rate, kept, kept)


together = lax.optimization_barrier


def inner_swap(value, axis):
    count = lax.axis_size(axis)
    return lax.ppermute(value, axis, [(i, i ^ 1) for i in range(count)])


def outer_shift(value, axis, steps):
    count = lax.axis_size(axis)
    half = count // 2
    pairs = [(i, (i // 2 + steps) % half * 2 + i % 2) for i in range(count)]
    return lax.ppermute(value, axis, pairs)


def shift_order(half):
    return sorted(range(1, half), key=lambda k: (-min(k, half - k), k))


def pieces_of_all(own, axis):
    count = lax.axis_size(axis)
    place = lax.axis_index(axis)
    half = count // 2
    outer, inner = place // 2, place % 2
    yield place, own
    arrived = {k: outer_shift(own, axis, k) for k in shift_order(half)}
    yield outer * 2 + 1 - inner, inner_swap(own, axis)
    for k, piece in arrived.items():
        origin = (outer - k + half) % half
        yield origin * 2 + inner, piece
    for k, piece in arrived.items():
        origin = (outer - k + half) % half
        yield origin * 2 + 1 - inner, inner_swap(piece, axis)


def gathered(own, axis, dim=0):
    count, size = lax.axis_size(axis), own.shape[dim]
    whole = jnp.zeros(own.shape[:dim] + (count * size,) + own.shape[dim + 1 :], own.dtype)
    for place, piece in pieces_of_all(own, axis):
        whole = lax.dynamic_update_slice_in_dim(whole, piece, place * size, dim)
    return whole


def hop(value, axis, moves):
    pairs = [(a * 2 + i, b * 2 + i) for a, b in moves for i in (0, 1)]
    return lax.ppermute(value, axis, pairs)


def swap_at(value, axis, spots):
    pairs = [(a * 2 + i, a * 2 + 1 - i) for a in spots for i in (0, 1)]
    return lax.ppermute(value, axis, pairs)


UP, DOWN = [(0, 1), (1, 2), (2, 3)], [(1, 0), (2, 1), (3, 2)]


def line_gathered(own, axis, held):
    if lax.axis_size(axis) != 8:
        return lax.all_gather(own, axis, axis=0, tiled=True), held
    place = lax.axis_index(axis)
    z, x = place // 2, place % 2
    rows = own.shape[0]
    upper, edge = z >= 2, (z == 0) | (z == 3)
    across = jnp.where(upper, z - 2, z + 2)
    far = jnp.where(z == 3, 0, 3)

    def put(whole, piece, spot, side):
        return lax.dynamic_update_slice_in_dim(whole, piece, (spot * 2 + side) * rows, 0)

    def put_far(whole, piece, side):
        held = lax.dynamic_slice_in_dim(whole, (far * 2 + side) * rows, rows, 0)
        return put(whole, jnp.where(edge, piece, held), far, side)

    whole = jnp.zeros((8 * rows,) + own.shape[1:], own.dtype)
    up, down, other, held = together(
        (hop(own, axis, UP), hop(own, axis, DOWN), swap_at(own, axis, range(4)), held)
    )
    up_two, down_two = hop(up, axis, UP[1:]), hop(down, axis, DOWN[:2])
    other_up, other_down = swap_at(up, axis, (1, 2, 3)), swap_at(down, axis, (0, 1, 2))
    whole = put(put(whole, own, z, x), other, z, 1 - x)
    whole = put(put(whole, up, (z + 3) % 4, x), down, (z + 1) % 4, x)
    two = jnp.where(upper, up_two, down_two)
    three = hop(two, axis, [(2, 3), (1, 0)])
    other_two = swap_at(two, axis, range(4))
    whole = put(put(whole, other_up, (z + 3) % 4, 1 - x), other_down, (z + 1) % 4, 1 - x)
    whole = put(whole, two, across, x)
    other_three = swap_at(three, axis, (0, 3))
    whole = put(whole, other_two, across, 1 - x)
    return put_far(put_far(whole, three, x), other_three, 1 - x), held


def line_summed(part_of, axis):
    if lax.axis_size(axis) != 8:
        return (scattered_sum(part_of, axis),)
    place = lax.axis_index(axis)
    z, x = place // 2, place % 2
    upper, edge = z >= 2, (z == 0) | (z == 3)
    across = jnp.where(upper, z - 2, z + 2)
    far = jnp.where(z == 0, 3, 0)
    above, below = jnp.minimum(z + 1, 3), jnp.maximum(z - 1, 0)

    def swapped(spot, spots):
        return swap_at(part_of(spot * 2 + 1 - x), axis, spots)

    def added(spot, given):
        return part_of(spot * 2 + x).astype(f32) + given.astype(f32)

    given_far = swapped(far, (0, 3))
    given_across = swapped(across, range(4))
    given_above, given_below = swapped(above, (0, 1, 2)), swapped(below, (1, 2, 3))
    given_own = swapped(z, range(4))
    three = hop(added(far, given_far).astype(bf16), axis, [(0, 1), (3, 2)])
    three, given_across, given_above, given_below = together(
        (three, given_across, given_above, given_below)
    )
    two = added(across, given_across) + jnp.where(edge, 0.0, three.astype(f32))
    two = two.astype(bf16)
    two_up, two_down, given_own = together(
        (hop(two, axis, UP[:2]), hop(two, axis, DOWN[1:]), given_own)
    )
    one_up = (added(above, given_above) + two_up.astype(f32)).astype(bf16)
    one_down = (added(below, given_below) + two_down.astype(f32)).astype(bf16)
    return added(z, given_own), hop(one_up, axis, UP), hop(one_down, axis, DOWN)


def scattered_sum(part_of, axis):
    count = lax.axis_size(axis)
    place = lax.axis_index(axis)
    half = count // 2
    outer, inner = place // 2, place % 2
    total = None
    for k in shift_order(half) + [0]:
        target = (outer + k) % half
        given = inner_swap(part_of(target * 2 + 1 - inner), axis)
        piece = part_of(target * 2 + inner).astype(f32) + given.astype(f32)
        if k:
            piece = outer_shift(piece.astype(bf16), axis, k).astype(f32)
        total = piece if total is None else total + piece
    return total


def rows_of(value, rows):
    return lambda place: lax.dynamic_slice_in_dim(value, place * rows, rows, 0)


def summed_over_seq(part, change):
    count = lax.axis_size("seq")
    length, columns = part.shape
    part = part.astype(bf16).reshape(count, length // count, columns)
    own = change(jnp.sum(lax.all_to_all(part, "seq", 0, 0).astype(f32), axis=0))
    return shared(own, "seq").reshape(length, own.shape[1])


def two_terms(value):
    high = value.astype(bf16)
    return [high, (value - high.astype(f32)).astype(bf16)]


def shared(own, axis):
    wide = jnp.broadcast_to(own[None], (lax.axis_size(axis),) + own.shape)
    return lax.all_to_all(wide, axis, 0, 0)


def matmul(a, b, dims=(((1,), (0,)), ((), ()))):
    return lax.dot_general(a, b, dims, preferred_element_type=f32)


TN = (((0,), (0,)), ((), ()))


def on_device(
    tokens,
    lengths,
    norm_gain,
    in_proj,
    conv_weight,
    conv_bias,
    x_proj,
    dt_proj,
    dt_bias,
    a_log,
    skip,
    out_proj,
    cotangent,
):
    batch, seq = lax.axis_size("batch"), lax.axis_size("seq")
    place = lax.axis_index("seq")
    span, model = tokens.shape[1:]
    length = span * seq
    in_rows = in_proj.shape[0]
    own = skip.shape[0]
    taps = conv_weight.shape[0]
    rank = dt_proj.shape[0]
    states = a_log.shape[1]
    width = own * batch

    own_gain = norm_gain.astype(f32)[:, None]
    scaled = (in_proj.astype(f32) * own_gain).astype(bf16)
    halves = scaled.reshape(in_rows, 2, batch, seq, own).transpose(1, 3, 0, 2, 4)
    halves = halves.reshape(2, seq, in_rows, width)
    columns = lax.all_to_all(halves[0], "seq", 0, 0)
    small = jnp.concatenate(
        [
            dt_proj,
            x_proj.T,
            a_log.T,
            conv_weight,
            conv_bias[None],
            dt_bias[None],
            skip[None],
        ],
        axis=0,
    )
    small = gathered(small, "batch", 1)
    cuts = [rank, 2 * rank + 2 * states, 2 * rank + 3 * states]
    cuts = cuts + [cuts[2] + taps + i for i in range(3)]
    delta_weight, select_weight, decay_logs, conv_taps, conv_shift, delta_shift, skip_gain = (
        jnp.split(small, cuts, axis=0)
    )
    conv_taps, conv_shift = conv_taps.astype(f32), conv_shift.astype(f32)
    delta_shift, skip_gain = delta_shift.astype(f32), skip_gain.astype(f32)
    decay = -jnp.exp(decay_logs.astype(f32))
    columns, gate_columns = together((columns, halves[1]))
    gate_columns = lax.all_to_all(gate_columns, "seq", 0, 0)

    input_weight = gathered(columns.reshape(seq * in_rows, width), "batch")

    def normed(rows):
        rows = rows.astype(f32)
        scale = lax.rsqrt(jnp.mean(rows * rows, axis=-1, keepdims=True) + epsilon)
        return (rows * scale).astype(bf16)

    stream = lax.all_gather(tokens[0], "seq", axis=0, tiled=True)
    gate_weight = gathered(gate_columns.reshape(seq * in_rows, width), "batch")
    normalized = normed(stream)
    upstream, out_proj = line_gathered(cotangent[0], "seq", out_proj)
    output_weight = gathered(out_proj, "batch")

    valid = (jnp.arange(length, dtype=jnp.int32) < lengths[0])[:, None]
    inner = matmul(normalized, input_weight).astype(bf16)
    padded = jnp.pad(inner, ((taps - 1, 0), (0, 0)))
    conv_out = conv_shift + jnp.zeros((length, width), f32)
    for tap in range(taps):
        conv_out = conv_out + conv_taps[tap] * padded[tap : tap + length].astype(f32)
    active = jax.nn.silu(conv_out).astype(bf16)
    active_f = active.astype(f32)

    partial, upstream = together((matmul(active, select_weight, NT), upstream))
    select = summed_over_seq(
        partial,
        lambda s: jnp.concatenate([s[:, :rank].astype(bf16)] + two_terms(s[:, rank:]), axis=1),
    )
    upstream = jnp.where(valid, upstream, 0).astype(bf16)
    gate_low = matmul(normalized, gate_weight).astype(bf16)
    d_gated = matmul(upstream, output_weight, NT)
    select, gate_low, d_gated = together((select, gate_low, d_gated))
    gate = gate_low.astype(f32)
    gate_sig = jax.nn.sigmoid(gate)
    delta_low = select[:, :rank]
    delta_raw = matmul(delta_low, delta_weight) + delta_shift
    delta = jax.nn.softplus(delta_raw)

    block = min(BLOCK, length)
    step = 256 // states
    rate = decay * LOG2E
    mixed, kept = scan_forward(delta, active, select, rate, block, step)
    mixed = mixed + skip_gain * active_f
    gated = (mixed * gate * gate_sig).astype(bf16)
    branch = matmul(gated, output_weight).astype(bf16)
    d_gated, branch = together((d_gated, branch))
    branch = lax.psum_scatter(branch, "seq", scatter_dimension=0, tiled=True)
    own_valid = lax.dynamic_slice_in_dim(valid, place * span, span, 0)
    own_stream = tokens[0].astype(f32)

    d_mixed = d_gated * gate * gate_sig
    d_gate = d_gated * mixed * gate_sig * (1.0 + gate * (1.0 - gate_sig))
    grad_skip = jnp.sum(d_mixed * active_f, axis=0, keepdims=True)
    d_gate_low = d_gate.astype(bf16)

    d_delta, d_active, d_bc, grad_log = scan_backward(
        delta, active, d_mixed, select, rate, decay, kept, block, step
    )
    d_raw = d_delta * jax.nn.sigmoid(delta_raw)
    grad_dt_bias = jnp.sum(d_raw, axis=0, keepdims=True)
    d_raw_low = d_raw.astype(bf16)
    grad_dt_proj = matmul(delta_low, d_raw_low, TN)
    partial = jnp.concatenate([matmul(d_raw_low, delta_weight, NT), d_bc], axis=1)
    d_select = summed_over_seq(partial, lambda s: s.astype(bf16))
    grad_gate = scattered_sum(
        rows_of(matmul(normalized, d_gate_low, TN).astype(bf16), model // batch), "batch"
    )
    d_select, grad_gate = together((d_select, grad_gate))
    grad_x_proj = matmul(d_select, active, TN)
    d_active = d_active + d_mixed * skip_gain + matmul(d_select, select_weight)
    conv_sig = jax.nn.sigmoid(conv_out)
    d_conv = (d_active * conv_sig * (1.0 + conv_out * (1.0 - conv_sig))).astype(bf16)
    d_conv_f = d_conv.astype(f32)
    grad_conv_bias = jnp.sum(d_conv_f, axis=0, keepdims=True)
    grad_conv = jnp.stack(
        [
            jnp.sum(d_conv_f * padded[tap : tap + length].astype(f32), axis=0)
            for tap in range(taps)
        ]
    )
    extended = jnp.pad(d_conv, ((0, taps - 1), (0, 0)))
    d_inner = jnp.zeros((length, width), f32)
    for tap in range(taps):
        offset = taps - 1 - tap
        d_inner = d_inner + conv_taps[tap] * extended[offset : offset + length].astype(f32)
    d_inner = d_inner.astype(bf16)
    grad_inner = matmul(normalized, d_inner, TN).astype(bf16)
    d_inner, grad_inner, branch = together((d_inner, grad_inner, branch))
    d_normalized = matmul(
        jnp.concatenate([d_inner, d_gate_low], axis=1),
        jnp.concatenate([input_weight, gate_weight], axis=1),
        NT,
    ).astype(bf16)
    grad_inner = scattered_sum(rows_of(grad_inner, model // batch), "batch")
    grad_gate = grad_gate.astype(bf16).reshape(seq, in_rows, width)
    grad_gate = lax.all_to_all(grad_gate, "seq", 0, 0)
    d_normalized, gated, grad_gate = together((d_normalized, gated, grad_gate))
    grad_output = lax.psum_scatter(
        matmul(gated, upstream, TN).astype(bf16), "batch", scatter_dimension=0, tiled=True
    ).astype(f32)
    d_normalized, *last_terms = line_summed(rows_of(d_normalized, span), "seq")

    block_out = jnp.where(own_valid, own_stream + branch.astype(f32), 0.0)

    def columns_of(part):
        part = part.reshape(seq, in_rows, batch, own).transpose(1, 2, 0, 3)
        return part.reshape(in_rows, batch * seq * own).astype(f32)

    grad_inner = grad_inner.astype(bf16).reshape(seq, in_rows, width)
    grad_inner = lax.all_to_all(grad_inner, "seq", 0, 0)
    grad_input = jnp.concatenate([columns_of(grad_inner), columns_of(grad_gate)], axis=1)

    small_grads = jnp.concatenate(
        [grad_dt_proj, grad_x_proj, grad_log, grad_conv, grad_conv_bias, grad_dt_bias, grad_skip],
        axis=0,
    )
    small_grads = lax.psum_scatter(small_grads, "batch", scatter_dimension=1, tiled=True)
    g_dt_proj, g_x_proj, g_log, g_conv, g_conv_bias, g_dt_bias, g_skip = jnp.split(
        small_grads, cuts, axis=0
    )

    own_upstream = jnp.where(own_valid, cotangent[0].astype(f32), 0.0)
    own_scale = lax.rsqrt(jnp.mean(own_stream * own_stream, axis=-1, keepdims=True) + epsilon)
    grad_gain = jnp.sum(grad_input * in_proj.astype(f32), axis=1)
    grad_input = grad_input * own_gain
    (
        d_normalized, g_dt_proj, g_x_proj, g_log, g_conv, g_conv_bias, g_dt_bias, g_skip,
        grad_input, grad_gain, grad_output,
    ) = together(
        (
            d_normalized, g_dt_proj, g_x_proj, g_log, g_conv, g_conv_bias, g_dt_bias, g_skip,
            grad_input, grad_gain, grad_output,
        )
    )
    for term in last_terms:
        d_normalized = d_normalized + term.astype(f32)
    d_hat = d_normalized
    grad_tokens = (
        own_scale * d_hat
        - own_stream
        * own_scale
        * own_scale
        * own_scale
        * jnp.mean(d_hat * own_stream, axis=-1, keepdims=True)
        + own_upstream
    )
    return (
        block_out[None],
        grad_tokens[None],
        grad_gain,
        grad_input,
        g_conv,
        g_conv_bias[0],
        g_x_proj.T,
        g_dt_proj,
        g_dt_bias[0],
        g_log.T,
        g_skip[0],
        grad_output,
    )


def solution(mesh):
    placed = (
        P("batch", "seq", None),
        P("batch"),
        P(("batch", "seq")),
        P(("batch", "seq"), None),
        P(None, ("batch", "seq")),
        P(("batch", "seq")),
        P(("batch", "seq"), None),
        P(None, ("batch", "seq")),
        P(("batch", "seq")),
        P(("batch", "seq"), None),
        P(("batch", "seq")),
        P(("batch", "seq"), None),
        P("batch", "seq", None),
    )
    return jax.shard_map(
        on_device,
        mesh=mesh,
        in_specs=placed,
        out_specs=(
            P("batch", "seq", None),
            P("batch", "seq", None),
            P(("batch", "seq")),
            P(("batch", "seq"), None),
            P(None, ("batch", "seq")),
            P(("batch", "seq")),
            P(("batch", "seq"), None),
            P(None, ("batch", "seq")),
            P(("batch", "seq")),
            P(("batch", "seq"), None),
            P(("batch", "seq")),
            P(("batch", "seq"), None),
        ),
        check_vma=False,
    )
```

```python
import functools

import jax
import jax.numpy as jnp
from jax import lax
from jax.experimental import pallas as pl
from jax.experimental.pallas import tpu as pltpu
from jax.sharding import PartitionSpec as P

bf16, f32 = jnp.bfloat16, jnp.float32
NT = (((1,), (1,)), ((), ()))
LANES = 128
GROUP = 32
BLOCK = 128
epsilon = 1e-05
LOG2E = 1.4426950408889634


def spread(tile, row, lanes, states):
    return jnp.broadcast_to(tile[row : row + 1, lanes], (states, LANES))


def selectors(select, states):
    low = select.shape[1] - 4 * states
    middle = low + 2 * states
    block = select[:, low:middle].astype(f32) + select[:, middle:].astype(f32)
    return jnp.transpose(block), block[:, :states], block[:, states:]


def block_diagonal(values, step):
    rows, states = values.shape
    wide = step * states
    spread_out = (
        lax.broadcasted_iota(jnp.int32, (states, wide), 1) % states
        == lax.broadcasted_iota(jnp.int32, (states, wide), 0)
    ).astype(bf16)
    value = jnp.dot(values.astype(bf16), spread_out, preferred_element_type=f32)
    place = lax.broadcasted_iota(jnp.int32, (rows, wide), 0) % step
    owner = lax.broadcasted_iota(jnp.int32, (rows, wide), 1) // states
    return jnp.where(place == owner, value, 0.0).astype(bf16)


def forward_body(tiles, step, delta, active, select, rate, mixed, kept, state, drive, columns):
    rows, states = delta.shape[0], rate.shape[0]
    wide = step * states

    @pl.when(pl.program_id(0) == 0)
    def _():
        state[...] = jnp.zeros_like(state)

    turned, _, c_block = selectors(select[...], states)
    columns[...] = turned[:states]
    drive[...] = delta[...] * active[...].astype(f32)
    rates = [rate[:, k * LANES : (k + 1) * LANES] for k in range(tiles)]

    def group(number, held):
        held = list(held)
        base = pl.multiple_of(number * GROUP, GROUP)
        delta_now, drive_now = delta.at[pl.ds(base, GROUP), :], drive.at[pl.ds(base, GROUP), :]
        b_now = pltpu.roll(columns[...], rows - base, 1)
        for j in range(GROUP):
            b_wide = jnp.broadcast_to(b_now[:, j : j + 1], (states, LANES))
            for k in range(tiles):
                lanes = slice(k * LANES, (k + 1) * LANES)
                decay = jnp.exp2(spread(delta_now, j, lanes, states) * rates[k])
                held[k] = decay * held[k] + spread(drive_now, j, lanes, states) * b_wide
                at = pl.ds(pl.multiple_of((base + j) * states, states), states)
                kept[at, lanes] = held[k].astype(bf16)
        return tuple(held)

    held = lax.fori_loop(
        0,
        rows // GROUP,
        group,
        tuple(state[:, k * LANES : (k + 1) * LANES] for k in range(tiles)),
    )
    for k in range(tiles):
        state[:, k * LANES : (k + 1) * LANES] = held[k]
    c_diag = block_diagonal(c_block, step)
    for q in range(rows // step):
        part = kept[q * wide : (q + 1) * wide, :]
        spot = slice(q * step, (q + 1) * step)
        mixed[spot, :] = jnp.dot(c_diag[spot, :], part, preferred_element_type=f32)


def scan_forward(delta, active, select, rate, block, step):
    length, width = delta.shape
    states = rate.shape[0]
    tiles = width // LANES
    return pl.pallas_call(
        functools.partial(forward_body, tiles, step),
        grid=(length // block,),
        in_specs=[
            pl.BlockSpec((block, width), lambda i: (i, 0)),
            pl.BlockSpec((block, width), lambda i: (i, 0)),
            pl.BlockSpec((block, select.shape[1]), lambda i: (i, 0)),
            pl.BlockSpec((states, width), lambda i: (0, 0)),
        ],
        out_specs=[
            pl.BlockSpec((block, width), lambda i: (i, 0)),
            pl.BlockSpec((block * states, width), lambda i: (i, 0)),
        ],
        out_shape=[
            jax.ShapeDtypeStruct((length, width), f32),
            jax.ShapeDtypeStruct((length * states, width), bf16),
        ],
        scratch_shapes=[
            pltpu.VMEM((states, width), f32),
            pltpu.VMEM((block, width), f32),
            pltpu.VMEM((states, block), f32),
        ],
        compiler_params=pltpu.CompilerParams(vmem_limit_bytes=48 << 20),
        cost_estimate=pl.CostEstimate(
            flops=8 * length * width * states,
            transcendentals=length * width * states,
            bytes_accessed=length * width * (2 * states + 10),
        ),
        name="scan_forward",
    )(delta, active, select, rate)


FEW = 4


def backward_body(
    tiles, step, delta, active, d_mixed, select, rate, decay_rate, kept, kept_before,
    d_delta, d_active, d_bc, d_log, push, drive, columns, diagonals, folding, timed, *pairs,
):
    grads, rated = pairs[:2], pairs[2:]
    rows, states = delta.shape[0], rate.shape[0]
    blocks = pl.num_programs(0)
    first = pl.program_id(0) == blocks - 1
    wide = step * states

    @pl.when(pl.program_id(0) == 0)
    def _():
        push[...] = jnp.zeros_like(push)
        d_log[...] = jnp.zeros_like(d_log)

    turned, b_block, _ = selectors(select[...], states)
    columns[...] = turned[states:]
    drive[...] = delta[...] * active[...].astype(f32)
    rates = [rate[:, k * LANES : (k + 1) * LANES] for k in range(tiles)]
    own_rates = [decay_rate[:, k * LANES : (k + 1) * LANES].astype(bf16) for k in range(tiles)]

    place = lax.broadcasted_iota(jnp.int32, (step, wide), 0)
    owner = lax.broadcasted_iota(jnp.int32, (step, wide), 1) // states
    ones_diag = (place == owner).astype(bf16)
    diag = (place == owner).astype(f32)
    diagonals[...] = block_diagonal(b_block, step)

    def sums_of(number):
        held, through_of = number % 2, {}

        def spots(q):
            at = number * GROUP + q * step
            tall = slice(q * wide, (q + 1) * wide)
            return slice(at, at + step), tall

        def through(q):
            spot, tall = spots(q)
            value = jnp.dot(diagonals[spot, :], grads[held][tall, :], preferred_element_type=f32)
            d_active[spot, :] = delta[spot, :] * value
            through_of[q] = active[spot, :].astype(f32) * value

        def summed(q):
            spot, tall = spots(q)
            value = jnp.dot(ones_diag, rated[held][tall, :], preferred_element_type=f32)
            d_delta[spot, :] = value + through_of[q]

        def d_b(q):
            spot, tall = spots(q)
            folding[spot, :wide] = diag * lax.dot_general(
                drive[spot, :].astype(bf16), grads[held][tall, :], NT, preferred_element_type=f32
            )

        def d_c(q):
            spot, _ = spots(q)
            own = slice(spot.start * states, spot.stop * states)
            folding[spot, wide:] = diag * lax.dot_general(
                d_mixed[spot, :].astype(bf16), kept[own, :], NT, preferred_element_type=f32
            )

        return [
            functools.partial(part, q)
            for q in range(GROUP // step)
            for part in (through, summed, d_b, d_c)
        ]

    carry = [push[:, k * LANES : (k + 1) * LANES] for k in range(tiles)]
    waiting = []
    for number in reversed(range(rows // GROUP)):
        pace = GROUP // max(len(waiting), 1)
        sums = [None] * tiles
        held = number % 2
        for j in reversed(range(GROUP)):
            row = number * GROUP + j
            c_wide = jnp.broadcast_to(columns[:, row : row + 1], (states, LANES))
            at = slice(j * states, (j + 1) * states)
            for k in range(tiles):
                lanes = slice(k * LANES, (k + 1) * LANES)
                if row:
                    before = kept[(row - 1) * states : row * states, lanes]
                else:
                    before = jnp.where(first, jnp.zeros((), bf16), kept_before[:, lanes])
                step_size = spread(delta, row, lanes, states)
                grad = spread(d_mixed, row, lanes, states) * c_wide + carry[k]
                carry[k] = jnp.exp2(step_size * rates[k]) * grad
                grads[held][at, lanes] = grad.astype(bf16)
                rated_now = carry[k].astype(bf16) * before * own_rates[k]
                rated[held][at, lanes] = rated_now
                timed_now = rated_now * step_size.astype(bf16)
                sums[k] = timed_now if sums[k] is None else sums[k] + timed_now
                if j % FEW == 0:
                    spot = row // FEW * states
                    timed[spot : spot + states, lanes] = sums[k]
                    sums[k] = None
            if waiting and j % pace == 0:
                waiting.pop(0)()
        while waiting:
            waiting.pop(0)()
        waiting = sums_of(number)
    while waiting:
        waiting.pop(0)()
    for k in range(tiles):
        push[:, k * LANES : (k + 1) * LANES] = carry[k]
    fold = (
        lax.broadcasted_iota(jnp.int32, (wide, states), 0) % states
        == lax.broadcasted_iota(jnp.int32, (wide, states), 1)
    ).astype(bf16)
    for number in range(2):
        value = folding[:, number * wide : (number + 1) * wide]
        high = value.astype(bf16)
        d_bc[:, number * states : (number + 1) * states] = jnp.dot(
            high, fold, preferred_element_type=f32
        )
    span = rows // FEW * states
    pick = (
        lax.broadcasted_iota(jnp.int32, (states, span), 1) % states
        == lax.broadcasted_iota(jnp.int32, (states, span), 0)
    ).astype(bf16)
    d_log[...] += jnp.dot(pick, timed[...], preferred_element_type=f32)


def scan_backward(delta, active, d_mixed, select, rate, decay_rate, kept, block, step):
    length, width = delta.shape
    states = rate.shape[0]
    tiles = width // LANES
    blocks = length // block
    back = lambda i: (blocks - 1 - i, 0)
    return pl.pallas_call(
        functools.partial(backward_body, tiles, step),
        grid=(blocks,),
        in_specs=[
            pl.BlockSpec((block, width), back),
            pl.BlockSpec((block, width), back),
            pl.BlockSpec((block, width), back),
            pl.BlockSpec((block, select.shape[1]), back),
            pl.BlockSpec((states, width), lambda i: (0, 0)),
            pl.BlockSpec((states, width), lambda i: (0, 0)),
            pl.BlockSpec((block * states, width), back),
            pl.BlockSpec(
                (states, width), lambda i: (jnp.maximum((blocks - 1 - i) * block - 1, 0), 0)
            ),
        ],
        out_specs=[
            pl.BlockSpec((block, width), back),
            pl.BlockSpec((block, width), back),
            pl.BlockSpec((block, 2 * states), back),
            pl.BlockSpec((states, width), lambda i: (0, 0)),
        ],
        out_shape=[
            jax.ShapeDtypeStruct((length, width), f32),
            jax.ShapeDtypeStruct((length, width), f32),
            jax.ShapeDtypeStruct((length, 2 * states), f32),
            jax.ShapeDtypeStruct((states, width), f32),
        ],
        scratch_shapes=[
            pltpu.VMEM((states, width), f32),
            pltpu.VMEM((block, width), f32),
            pltpu.VMEM((states, block), f32),
            pltpu.VMEM((block, step * states), bf16),
            pltpu.VMEM((block, 2 * step * states), f32),
            pltpu.VMEM((block // FEW * states, width), bf16),
        ]
        + [pltpu.VMEM((GROUP * states, width), bf16)] * 4,
        compiler_params=pltpu.CompilerParams(vmem_limit_bytes=48 << 20),
        cost_estimate=pl.CostEstimate(
            flops=20 * length * width * states,
            transcendentals=length * width * states,
            bytes_accessed=length * width * (2 * states + 20),
        ),
        name="scan_backward",
    )(delta, active, d_mixed, select, rate, decay_rate, kept, kept)


together = lax.optimization_barrier


def inner_swap(value, axis):
    count = lax.axis_size(axis)
    return lax.ppermute(value, axis, [(i, i ^ 1) for i in range(count)])


def outer_shift(value, axis, steps):
    count = lax.axis_size(axis)
    half = count // 2
    pairs = [(i, (i // 2 + steps) % half * 2 + i % 2) for i in range(count)]
    return lax.ppermute(value, axis, pairs)


def shift_order(half):
    return sorted(range(1, half), key=lambda k: (-min(k, half - k), k))


def pieces_of_all(own, axis):
    count = lax.axis_size(axis)
    place = lax.axis_index(axis)
    half = count // 2
    outer, inner = place // 2, place % 2
    yield place, own
    arrived = {k: outer_shift(own, axis, k) for k in shift_order(half)}
    yield outer * 2 + 1 - inner, inner_swap(own, axis)
    for k, piece in arrived.items():
        origin = (outer - k + half) % half
        yield origin * 2 + inner, piece
    for k, piece in arrived.items():
        origin = (outer - k + half) % half
        yield origin * 2 + 1 - inner, inner_swap(piece, axis)


def gathered(own, axis, dim=0):
    count, size = lax.axis_size(axis), own.shape[dim]
    whole = jnp.zeros(own.shape[:dim] + (count * size,) + own.shape[dim + 1 :], own.dtype)
    for place, piece in pieces_of_all(own, axis):
        whole = lax.dynamic_update_slice_in_dim(whole, piece, place * size, dim)
    return whole


def hop(value, axis, moves):
    pairs = [(a * 2 + i, b * 2 + i) for a, b in moves for i in (0, 1)]
    return lax.ppermute(value, axis, pairs)


def swap_at(value, axis, spots):
    pairs = [(a * 2 + i, a * 2 + 1 - i) for a in spots for i in (0, 1)]
    return lax.ppermute(value, axis, pairs)


UP, DOWN = [(0, 1), (1, 2), (2, 3)], [(1, 0), (2, 1), (3, 2)]


def line_gathered(own, axis):
    if lax.axis_size(axis) != 8:
        return lax.all_gather(own, axis, axis=0, tiled=True)
    place = lax.axis_index(axis)
    z, x = place // 2, place % 2
    rows = own.shape[0]
    upper, edge = z >= 2, (z == 0) | (z == 3)
    across = jnp.where(upper, z - 2, z + 2)
    far = jnp.where(z == 3, 0, 3)

    def put(whole, piece, spot, side):
        return lax.dynamic_update_slice_in_dim(whole, piece, (spot * 2 + side) * rows, 0)

    def put_far(whole, piece, side):
        held = lax.dynamic_slice_in_dim(whole, (far * 2 + side) * rows, rows, 0)
        return put(whole, jnp.where(edge, piece, held), far, side)

    whole = jnp.zeros((8 * rows,) + own.shape[1:], own.dtype)
    up, down, other = hop(own, axis, UP), hop(own, axis, DOWN), swap_at(own, axis, range(4))
    up_two, down_two = hop(up, axis, UP[1:]), hop(down, axis, DOWN[:2])
    other_up, other_down = swap_at(up, axis, (1, 2, 3)), swap_at(down, axis, (0, 1, 2))
    whole = put(put(whole, own, z, x), other, z, 1 - x)
    whole = put(put(whole, up, (z + 3) % 4, x), down, (z + 1) % 4, x)
    two = jnp.where(upper, up_two, down_two)
    three = hop(two, axis, [(2, 3), (1, 0)])
    other_two = swap_at(two, axis, range(4))
    whole = put(put(whole, other_up, (z + 3) % 4, 1 - x), other_down, (z + 1) % 4, 1 - x)
    whole = put(whole, two, across, x)
    other_three = swap_at(three, axis, (0, 3))
    whole = put(whole, other_two, across, 1 - x)
    return put_far(put_far(whole, three, x), other_three, 1 - x)


def line_summed(part_of, axis):
    if lax.axis_size(axis) != 8:
        return (scattered_sum(part_of, axis),)
    place = lax.axis_index(axis)
    z, x = place // 2, place % 2
    upper, edge = z >= 2, (z == 0) | (z == 3)
    across = jnp.where(upper, z - 2, z + 2)
    far = jnp.where(z == 0, 3, 0)
    above, below = jnp.minimum(z + 1, 3), jnp.maximum(z - 1, 0)

    def swapped(spot, spots):
        return swap_at(part_of(spot * 2 + 1 - x), axis, spots)

    def added(spot, given):
        return part_of(spot * 2 + x).astype(f32) + given.astype(f32)

    given_far = swapped(far, (0, 3))
    given_across = swapped(across, range(4))
    given_above, given_below = swapped(above, (0, 1, 2)), swapped(below, (1, 2, 3))
    given_own = swapped(z, range(4))
    three = hop(added(far, given_far).astype(bf16), axis, [(0, 1), (3, 2)])
    three, given_across, given_above, given_below = together(
        (three, given_across, given_above, given_below)
    )
    two = added(across, given_across) + jnp.where(edge, 0.0, three.astype(f32))
    two = two.astype(bf16)
    two_up, two_down, given_own = together(
        (hop(two, axis, UP[:2]), hop(two, axis, DOWN[1:]), given_own)
    )
    one_up = (added(above, given_above) + two_up.astype(f32)).astype(bf16)
    one_down = (added(below, given_below) + two_down.astype(f32)).astype(bf16)
    return added(z, given_own), hop(one_up, axis, UP), hop(one_down, axis, DOWN)


def scattered_sum(part_of, axis):
    count = lax.axis_size(axis)
    place = lax.axis_index(axis)
    half = count // 2
    outer, inner = place // 2, place % 2
    total = None
    for k in shift_order(half) + [0]:
        target = (outer + k) % half
        given = inner_swap(part_of(target * 2 + 1 - inner), axis)
        piece = part_of(target * 2 + inner).astype(f32) + given.astype(f32)
        if k:
            piece = outer_shift(piece.astype(bf16), axis, k).astype(f32)
        total = piece if total is None else total + piece
    return total


def rows_of(value, rows):
    return lambda place: lax.dynamic_slice_in_dim(value, place * rows, rows, 0)


def summed_over_seq(part, change):
    count = lax.axis_size("seq")
    length, columns = part.shape
    part = part.astype(bf16).reshape(count, length // count, columns)
    own = change(jnp.sum(lax.all_to_all(part, "seq", 0, 0).astype(f32), axis=0))
    return shared(own, "seq").reshape(length, own.shape[1])


def two_terms(value):
    high = value.astype(bf16)
    return [high, (value - high.astype(f32)).astype(bf16)]


def shared(own, axis):
    wide = jnp.broadcast_to(own[None], (lax.axis_size(axis),) + own.shape)
    return lax.all_to_all(wide, axis, 0, 0)


def matmul(a, b, dims=(((1,), (0,)), ((), ()))):
    return lax.dot_general(a, b, dims, preferred_element_type=f32)


TN = (((0,), (0,)), ((), ()))


def on_device(
    tokens,
    lengths,
    norm_gain,
    in_proj,
    conv_weight,
    conv_bias,
    x_proj,
    dt_proj,
    dt_bias,
    a_log,
    skip,
    out_proj,
    cotangent,
):
    batch, seq = lax.axis_size("batch"), lax.axis_size("seq")
    place = lax.axis_index("seq")
    span, model = tokens.shape[1:]
    length = span * seq
    in_rows = in_proj.shape[0]
    own = skip.shape[0]
    taps = conv_weight.shape[0]
    rank = dt_proj.shape[0]
    states = a_log.shape[1]
    width = own * batch

    columns = in_proj.reshape(in_rows, 2, batch, seq, own).transpose(3, 0, 1, 2, 4)
    columns = lax.all_to_all(columns.reshape(seq, in_rows, 2 * width), "seq", 0, 0)
    small = jnp.concatenate(
        [
            dt_proj,
            x_proj.T,
            a_log.T,
            conv_weight,
            conv_bias[None],
            dt_bias[None],
            skip[None],
            jnp.pad(norm_gain, (0, own - in_rows))[None],
        ],
        axis=0,
    )
    small = gathered(small, "batch", 1)
    cuts = [rank, 2 * rank + 2 * states, 2 * rank + 3 * states]
    cuts = cuts + [cuts[2] + taps + i for i in range(4)]
    delta_weight, select_weight, decay_logs, conv_taps, conv_shift, delta_shift, skip_gain, gain = (
        jnp.split(small, cuts, axis=0)
    )
    conv_taps, conv_shift = conv_taps.astype(f32), conv_shift.astype(f32)
    delta_shift, skip_gain = delta_shift.astype(f32), skip_gain.astype(f32)
    decay = -jnp.exp(decay_logs.astype(f32))
    gain = gain.reshape(batch, own)[:, :in_rows]
    columns, gain, out_proj = together((columns, gain, out_proj))
    gain = shared(gain, "seq").transpose(1, 0, 2).reshape(model).astype(f32)
    weight = gathered(columns.reshape(seq * in_rows, 2 * width), "batch")

    def normed(rows):
        rows = rows.astype(f32)
        scale = lax.rsqrt(jnp.mean(rows * rows, axis=-1, keepdims=True) + epsilon)
        return (rows * scale * gain).astype(bf16)

    stream = lax.all_gather(tokens[0], "seq", axis=0, tiled=True)
    normalized = normed(stream)
    upstream = line_gathered(cotangent[0], "seq")
    output_weight = gathered(out_proj, "batch")

    valid = (jnp.arange(length, dtype=jnp.int32) < lengths[0])[:, None]
    inner = matmul(normalized, weight[:, :width]).astype(bf16)
    padded = jnp.pad(inner, ((taps - 1, 0), (0, 0)))
    conv_out = conv_shift + jnp.zeros((length, width), f32)
    for tap in range(taps):
        conv_out = conv_out + conv_taps[tap] * padded[tap : tap + length].astype(f32)
    active = jax.nn.silu(conv_out).astype(bf16)
    active_f = active.astype(f32)

    partial, upstream = together((matmul(active, select_weight, NT), upstream))
    select = summed_over_seq(
        partial,
        lambda s: jnp.concatenate([s[:, :rank].astype(bf16)] + two_terms(s[:, rank:]), axis=1),
    )
    upstream = jnp.where(valid, upstream, 0).astype(bf16)
    gate_low = matmul(normalized, weight[:, width:]).astype(bf16)
    d_gated = matmul(upstream, output_weight, NT)
    select, gate_low, d_gated = together((select, gate_low, d_gated))
    gate = gate_low.astype(f32)
    gate_sig = jax.nn.sigmoid(gate)
    delta_low = select[:, :rank]
    delta_raw = matmul(delta_low, delta_weight) + delta_shift
    delta = jax.nn.softplus(delta_raw)

    block = min(BLOCK, length)
    step = 256 // states
    rate = decay * LOG2E
    mixed, kept = scan_forward(delta, active, select, rate, block, step)
    mixed = mixed + skip_gain * active_f
    gated = (mixed * gate * gate_sig).astype(bf16)
    branch = matmul(gated, output_weight).astype(bf16)
    d_gated, branch = together((d_gated, branch))
    branch = lax.psum_scatter(branch, "seq", scatter_dimension=0, tiled=True)
    own_valid = lax.dynamic_slice_in_dim(valid, place * span, span, 0)
    own_stream = tokens[0].astype(f32)

    d_mixed = d_gated * gate * gate_sig
    d_gate = d_gated * mixed * gate_sig * (1.0 + gate * (1.0 - gate_sig))
    grad_skip = jnp.sum(d_mixed * active_f, axis=0, keepdims=True)
    d_gate_low = d_gate.astype(bf16)

    d_delta, d_active, d_bc, grad_log = scan_backward(
        delta, active, d_mixed, select, rate, decay, kept, block, step
    )
    d_raw = d_delta * jax.nn.sigmoid(delta_raw)
    grad_dt_bias = jnp.sum(d_raw, axis=0, keepdims=True)
    d_raw_low = d_raw.astype(bf16)
    grad_dt_proj = matmul(delta_low, d_raw_low, TN)
    partial = jnp.concatenate([matmul(d_raw_low, delta_weight, NT), d_bc], axis=1)
    d_select = summed_over_seq(partial, lambda s: s.astype(bf16))
    grad_gate = scattered_sum(
        rows_of(matmul(normalized, d_gate_low, TN).astype(bf16), model // batch), "batch"
    )
    d_select, grad_gate = together((d_select, grad_gate))
    grad_x_proj = matmul(d_select, active, TN)
    d_active = d_active + d_mixed * skip_gain + matmul(d_select, select_weight)
    conv_sig = jax.nn.sigmoid(conv_out)
    d_conv = (d_active * conv_sig * (1.0 + conv_out * (1.0 - conv_sig))).astype(bf16)
    d_conv_f = d_conv.astype(f32)
    grad_conv_bias = jnp.sum(d_conv_f, axis=0, keepdims=True)
    grad_conv = jnp.stack(
        [
            jnp.sum(d_conv_f * padded[tap : tap + length].astype(f32), axis=0)
            for tap in range(taps)
        ]
    )
    extended = jnp.pad(d_conv, ((0, taps - 1), (0, 0)))
    d_inner = jnp.zeros((length, width), f32)
    for tap in range(taps):
        offset = taps - 1 - tap
        d_inner = d_inner + conv_taps[tap] * extended[offset : offset + length].astype(f32)
    d_inner = d_inner.astype(bf16)
    grad_inner = matmul(normalized, d_inner, TN).astype(bf16)
    d_inner, grad_inner, branch = together((d_inner, grad_inner, branch))
    d_normalized = matmul(
        jnp.concatenate([d_inner, d_gate_low], axis=1),
        weight,
        NT,
    ).astype(bf16)
    grad_inner = scattered_sum(rows_of(grad_inner, model // batch), "batch")
    grad_gate = grad_gate.astype(bf16).reshape(seq, in_rows, width)
    grad_gate = lax.all_to_all(grad_gate, "seq", 0, 0)
    d_normalized, gated, grad_gate = together((d_normalized, gated, grad_gate))
    grad_output = lax.psum_scatter(
        matmul(gated, upstream, TN).astype(bf16), "batch", scatter_dimension=0, tiled=True
    ).astype(f32)
    d_normalized, *last_terms = line_summed(rows_of(d_normalized, span), "seq")

    block_out = jnp.where(own_valid, own_stream + branch.astype(f32), 0.0)

    def columns_of(part):
        part = part.reshape(seq, in_rows, batch, own).transpose(1, 2, 0, 3)
        return part.reshape(in_rows, batch * seq * own).astype(f32)

    grad_inner = grad_inner.astype(bf16).reshape(seq, in_rows, width)
    grad_inner = lax.all_to_all(grad_inner, "seq", 0, 0)
    grad_input = jnp.concatenate([columns_of(grad_inner), columns_of(grad_gate)], axis=1)

    small_grads = jnp.concatenate(
        [grad_dt_proj, grad_x_proj, grad_log, grad_conv, grad_conv_bias, grad_dt_bias, grad_skip],
        axis=0,
    )
    small_grads = lax.psum_scatter(small_grads, "batch", scatter_dimension=1, tiled=True)
    g_dt_proj, g_x_proj, g_log, g_conv, g_conv_bias, g_dt_bias, g_skip = jnp.split(
        small_grads, cuts[:-1], axis=0
    )

    own_upstream = jnp.where(own_valid, cotangent[0].astype(f32), 0.0)
    own_scale = lax.rsqrt(jnp.mean(own_stream * own_stream, axis=-1, keepdims=True) + epsilon)
    grad_gain = jnp.sum(grad_input * in_proj.astype(f32), axis=1) / norm_gain.astype(f32)
    (
        d_normalized, g_dt_proj, g_x_proj, g_log, g_conv, g_conv_bias, g_dt_bias, g_skip,
        grad_input, grad_gain, grad_output,
    ) = together(
        (
            d_normalized, g_dt_proj, g_x_proj, g_log, g_conv, g_conv_bias, g_dt_bias, g_skip,
            grad_input, grad_gain, grad_output,
        )
    )
    for term in last_terms:
        d_normalized = d_normalized + term.astype(f32)
    d_hat = d_normalized * gain
    grad_tokens = (
        own_scale * d_hat
        - own_stream
        * own_scale
        * own_scale
        * own_scale
        * jnp.mean(d_hat * own_stream, axis=-1, keepdims=True)
        + own_upstream
    )
    return (
        block_out[None],
        grad_tokens[None],
        grad_gain,
        grad_input,
        g_conv,
        g_conv_bias[0],
        g_x_proj.T,
        g_dt_proj,
        g_dt_bias[0],
        g_log.T,
        g_skip[0],
        grad_output,
    )


def solution(mesh):
    placed = (
        P("batch", "seq", None),
        P("batch"),
        P(("batch", "seq")),
        P(("batch", "seq"), None),
        P(None, ("batch", "seq")),
        P(("batch", "seq")),
        P(("batch", "seq"), None),
        P(None, ("batch", "seq")),
        P(("batch", "seq")),
        P(("batch", "seq"), None),
        P(("batch", "seq")),
        P(("batch", "seq"), None),
        P("batch", "seq", None),
    )
    return jax.shard_map(
        on_device,
        mesh=mesh,
        in_specs=placed,
        out_specs=(
            P("batch", "seq", None),
            P("batch", "seq", None),
            P(("batch", "seq")),
            P(("batch", "seq"), None),
            P(None, ("batch", "seq")),
            P(("batch", "seq")),
            P(("batch", "seq"), None),
            P(None, ("batch", "seq")),
            P(("batch", "seq")),
            P(("batch", "seq"), None),
            P(("batch", "seq")),
            P(("batch", "seq"), None),
        ),
        check_vma=False,
    )
```

```python
import functools

import jax
import jax.numpy as jnp
from jax import lax
from jax.experimental import pallas as pl
from jax.experimental.pallas import tpu as pltpu
from jax.sharding import PartitionSpec as P

bf16, f32 = jnp.bfloat16, jnp.float32
NT = (((1,), (1,)), ((), ()))
LANES = 128
GROUP = 32
BLOCK = 128
epsilon = 1e-05
LOG2E = 1.4426950408889634


def spread(tile, row, lanes, states):
    return jnp.broadcast_to(tile[row : row + 1, lanes], (states, LANES))


def selectors(select, states):
    low = select.shape[1] - 4 * states
    middle = low + 2 * states
    block = select[:, low:middle].astype(f32) + select[:, middle:].astype(f32)
    return jnp.transpose(block), block[:, :states], block[:, states:]


def block_diagonal(values, step):
    rows, states = values.shape
    wide = step * states
    spread_out = (
        lax.broadcasted_iota(jnp.int32, (states, wide), 1) % states
        == lax.broadcasted_iota(jnp.int32, (states, wide), 0)
    ).astype(bf16)
    value = jnp.dot(values.astype(bf16), spread_out, preferred_element_type=f32)
    place = lax.broadcasted_iota(jnp.int32, (rows, wide), 0) % step
    owner = lax.broadcasted_iota(jnp.int32, (rows, wide), 1) // states
    return jnp.where(place == owner, value, 0.0).astype(bf16)


def forward_body(tiles, step, delta, active, select, rate, mixed, kept, state, drive, columns):
    rows, states = delta.shape[0], rate.shape[0]
    wide = step * states

    @pl.when(pl.program_id(0) == 0)
    def _():
        state[...] = jnp.zeros_like(state)

    turned, _, c_block = selectors(select[...], states)
    columns[...] = turned[:states]
    drive[...] = delta[...] * active[...].astype(f32)
    rates = [rate[:, k * LANES : (k + 1) * LANES] for k in range(tiles)]

    def group(number, held):
        held = list(held)
        base = pl.multiple_of(number * GROUP, GROUP)
        delta_now, drive_now = delta.at[pl.ds(base, GROUP), :], drive.at[pl.ds(base, GROUP), :]
        b_now = pltpu.roll(columns[...], rows - base, 1)
        for j in range(GROUP):
            b_wide = jnp.broadcast_to(b_now[:, j : j + 1], (states, LANES))
            for k in range(tiles):
                lanes = slice(k * LANES, (k + 1) * LANES)
                decay = jnp.exp2(spread(delta_now, j, lanes, states) * rates[k])
                held[k] = decay * held[k] + spread(drive_now, j, lanes, states) * b_wide
                at = pl.ds(pl.multiple_of((base + j) * states, states), states)
                kept[at, lanes] = held[k].astype(bf16)
        return tuple(held)

    held = lax.fori_loop(
        0,
        rows // GROUP,
        group,
        tuple(state[:, k * LANES : (k + 1) * LANES] for k in range(tiles)),
    )
    for k in range(tiles):
        state[:, k * LANES : (k + 1) * LANES] = held[k]
    c_diag = block_diagonal(c_block, step)
    for q in range(rows // step):
        part = kept[q * wide : (q + 1) * wide, :]
        spot = slice(q * step, (q + 1) * step)
        mixed[spot, :] = jnp.dot(c_diag[spot, :], part, preferred_element_type=f32)


def scan_forward(delta, active, select, rate, block, step):
    length, width = delta.shape
    states = rate.shape[0]
    tiles = width // LANES
    return pl.pallas_call(
        functools.partial(forward_body, tiles, step),
        grid=(length // block,),
        in_specs=[
            pl.BlockSpec((block, width), lambda i: (i, 0)),
            pl.BlockSpec((block, width), lambda i: (i, 0)),
            pl.BlockSpec((block, select.shape[1]), lambda i: (i, 0)),
            pl.BlockSpec((states, width), lambda i: (0, 0)),
        ],
        out_specs=[
            pl.BlockSpec((block, width), lambda i: (i, 0)),
            pl.BlockSpec((block * states, width), lambda i: (i, 0)),
        ],
        out_shape=[
            jax.ShapeDtypeStruct((length, width), f32),
            jax.ShapeDtypeStruct((length * states, width), bf16),
        ],
        scratch_shapes=[
            pltpu.VMEM((states, width), f32),
            pltpu.VMEM((block, width), f32),
            pltpu.VMEM((states, block), f32),
        ],
        compiler_params=pltpu.CompilerParams(vmem_limit_bytes=48 << 20),
        cost_estimate=pl.CostEstimate(
            flops=8 * length * width * states,
            transcendentals=length * width * states,
            bytes_accessed=length * width * (2 * states + 10),
        ),
        name="scan_forward",
    )(delta, active, select, rate)


FEW = 4


def backward_body(
    tiles, step, delta, active, d_mixed, select, rate, decay_rate, kept, kept_before,
    d_delta, d_active, d_bc, d_log, push, drive, columns, diagonals, folding, timed, *pairs,
):
    grads, rated = pairs[:2], pairs[2:]
    rows, states = delta.shape[0], rate.shape[0]
    blocks = pl.num_programs(0)
    first = pl.program_id(0) == blocks - 1
    wide = step * states

    @pl.when(pl.program_id(0) == 0)
    def _():
        push[...] = jnp.zeros_like(push)
        d_log[...] = jnp.zeros_like(d_log)

    turned, b_block, _ = selectors(select[...], states)
    columns[...] = turned[states:]
    drive[...] = delta[...] * active[...].astype(f32)
    rates = [rate[:, k * LANES : (k + 1) * LANES] for k in range(tiles)]
    own_rates = [decay_rate[:, k * LANES : (k + 1) * LANES].astype(bf16) for k in range(tiles)]

    place = lax.broadcasted_iota(jnp.int32, (step, wide), 0)
    owner = lax.broadcasted_iota(jnp.int32, (step, wide), 1) // states
    ones_diag = (place == owner).astype(bf16)
    diag = (place == owner).astype(f32)
    diagonals[...] = block_diagonal(b_block, step)

    def sums_of(number):
        held, through_of = number % 2, {}

        def spots(q):
            at = number * GROUP + q * step
            tall = slice(q * wide, (q + 1) * wide)
            return slice(at, at + step), tall

        def through(q):
            spot, tall = spots(q)
            value = jnp.dot(diagonals[spot, :], grads[held][tall, :], preferred_element_type=f32)
            d_active[spot, :] = delta[spot, :] * value
            through_of[q] = active[spot, :].astype(f32) * value

        def summed(q):
            spot, tall = spots(q)
            value = jnp.dot(ones_diag, rated[held][tall, :], preferred_element_type=f32)
            d_delta[spot, :] = value + through_of[q]

        def d_b(q):
            spot, tall = spots(q)
            folding[spot, :wide] = diag * lax.dot_general(
                drive[spot, :].astype(bf16), grads[held][tall, :], NT, preferred_element_type=f32
            )

        def d_c(q):
            spot, _ = spots(q)
            own = slice(spot.start * states, spot.stop * states)
            folding[spot, wide:] = diag * lax.dot_general(
                d_mixed[spot, :].astype(bf16), kept[own, :], NT, preferred_element_type=f32
            )

        return [
            functools.partial(part, q)
            for q in range(GROUP // step)
            for part in (through, summed, d_b, d_c)
        ]

    carry = [push[:, k * LANES : (k + 1) * LANES] for k in range(tiles)]
    waiting = []
    for number in reversed(range(rows // GROUP)):
        pace = GROUP // max(len(waiting), 1)
        sums = [None] * tiles
        held = number % 2
        for j in reversed(range(GROUP)):
            row = number * GROUP + j
            c_wide = jnp.broadcast_to(columns[:, row : row + 1], (states, LANES))
            at = slice(j * states, (j + 1) * states)
            for k in range(tiles):
                lanes = slice(k * LANES, (k + 1) * LANES)
                if row:
                    before = kept[(row - 1) * states : row * states, lanes]
                else:
                    before = jnp.where(first, jnp.zeros((), bf16), kept_before[:, lanes])
                step_size = spread(delta, row, lanes, states)
                grad = spread(d_mixed, row, lanes, states) * c_wide + carry[k]
                carry[k] = jnp.exp2(step_size * rates[k]) * grad
                grads[held][at, lanes] = grad.astype(bf16)
                rated_now = carry[k].astype(bf16) * before * own_rates[k]
                rated[held][at, lanes] = rated_now
                timed_now = rated_now * step_size.astype(bf16)
                sums[k] = timed_now if sums[k] is None else sums[k] + timed_now
                if j % FEW == 0:
                    spot = row // FEW * states
                    timed[spot : spot + states, lanes] = sums[k]
                    sums[k] = None
            if waiting and j % pace == 0:
                waiting.pop(0)()
        while waiting:
            waiting.pop(0)()
        waiting = sums_of(number)
    while waiting:
        waiting.pop(0)()
    for k in range(tiles):
        push[:, k * LANES : (k + 1) * LANES] = carry[k]
    fold = (
        lax.broadcasted_iota(jnp.int32, (wide, states), 0) % states
        == lax.broadcasted_iota(jnp.int32, (wide, states), 1)
    ).astype(bf16)
    for number in range(2):
        value = folding[:, number * wide : (number + 1) * wide]
        high = value.astype(bf16)
        d_bc[:, number * states : (number + 1) * states] = jnp.dot(
            high, fold, preferred_element_type=f32
        )
    span = rows // FEW * states
    pick = (
        lax.broadcasted_iota(jnp.int32, (states, span), 1) % states
        == lax.broadcasted_iota(jnp.int32, (states, span), 0)
    ).astype(bf16)
    d_log[...] += jnp.dot(pick, timed[...], preferred_element_type=f32)


def scan_backward(delta, active, d_mixed, select, rate, decay_rate, kept, block, step):
    length, width = delta.shape
    states = rate.shape[0]
    tiles = width // LANES
    blocks = length // block
    back = lambda i: (blocks - 1 - i, 0)
    return pl.pallas_call(
        functools.partial(backward_body, tiles, step),
        grid=(blocks,),
        in_specs=[
            pl.BlockSpec((block, width), back),
            pl.BlockSpec((block, width), back),
            pl.BlockSpec((block, width), back),
            pl.BlockSpec((block, select.shape[1]), back),
            pl.BlockSpec((states, width), lambda i: (0, 0)),
            pl.BlockSpec((states, width), lambda i: (0, 0)),
            pl.BlockSpec((block * states, width), back),
            pl.BlockSpec(
                (states, width), lambda i: (jnp.maximum((blocks - 1 - i) * block - 1, 0), 0)
            ),
        ],
        out_specs=[
            pl.BlockSpec((block, width), back),
            pl.BlockSpec((block, width), back),
            pl.BlockSpec((block, 2 * states), back),
            pl.BlockSpec((states, width), lambda i: (0, 0)),
        ],
        out_shape=[
            jax.ShapeDtypeStruct((length, width), f32),
            jax.ShapeDtypeStruct((length, width), f32),
            jax.ShapeDtypeStruct((length, 2 * states), f32),
            jax.ShapeDtypeStruct((states, width), f32),
        ],
        scratch_shapes=[
            pltpu.VMEM((states, width), f32),
            pltpu.VMEM((block, width), f32),
            pltpu.VMEM((states, block), f32),
            pltpu.VMEM((block, step * states), bf16),
            pltpu.VMEM((block, 2 * step * states), f32),
            pltpu.VMEM((block // FEW * states, width), bf16),
        ]
        + [pltpu.VMEM((GROUP * states, width), bf16)] * 4,
        compiler_params=pltpu.CompilerParams(vmem_limit_bytes=48 << 20),
        cost_estimate=pl.CostEstimate(
            flops=20 * length * width * states,
            transcendentals=length * width * states,
            bytes_accessed=length * width * (2 * states + 20),
        ),
        name="scan_backward",
    )(delta, active, d_mixed, select, rate, decay_rate, kept, kept)


together = lax.optimization_barrier


def inner_swap(value, axis):
    count = lax.axis_size(axis)
    return lax.ppermute(value, axis, [(i, i ^ 1) for i in range(count)])


def outer_shift(value, axis, steps):
    count = lax.axis_size(axis)
    half = count // 2
    pairs = [(i, (i // 2 + steps) % half * 2 + i % 2) for i in range(count)]
    return lax.ppermute(value, axis, pairs)


def shift_order(half):
    return sorted(range(1, half), key=lambda k: (-min(k, half - k), k))


def pieces_of_all(own, axis):
    count = lax.axis_size(axis)
    place = lax.axis_index(axis)
    half = count // 2
    outer, inner = place // 2, place % 2
    yield place, own
    arrived = {k: outer_shift(own, axis, k) for k in shift_order(half)}
    yield outer * 2 + 1 - inner, inner_swap(own, axis)
    for k, piece in arrived.items():
        origin = (outer - k + half) % half
        yield origin * 2 + inner, piece
    for k, piece in arrived.items():
        origin = (outer - k + half) % half
        yield origin * 2 + 1 - inner, inner_swap(piece, axis)


def gathered(own, axis, dim=0):
    count, size = lax.axis_size(axis), own.shape[dim]
    whole = jnp.zeros(own.shape[:dim] + (count * size,) + own.shape[dim + 1 :], own.dtype)
    for place, piece in pieces_of_all(own, axis):
        whole = lax.dynamic_update_slice_in_dim(whole, piece, place * size, dim)
    return whole


def hop(value, axis, moves):
    pairs = [(a * 2 + i, b * 2 + i) for a, b in moves for i in (0, 1)]
    return lax.ppermute(value, axis, pairs)


def swap_at(value, axis, spots):
    pairs = [(a * 2 + i, a * 2 + 1 - i) for a in spots for i in (0, 1)]
    return lax.ppermute(value, axis, pairs)


UP, DOWN = [(0, 1), (1, 2), (2, 3)], [(1, 0), (2, 1), (3, 2)]


def line_gathered(own, axis):
    if lax.axis_size(axis) != 8:
        return lax.all_gather(own, axis, axis=0, tiled=True)
    place = lax.axis_index(axis)
    z, x = place // 2, place % 2
    rows = own.shape[0]
    upper, edge = z >= 2, (z == 0) | (z == 3)
    across = jnp.where(upper, z - 2, z + 2)
    far = jnp.where(z == 3, 0, 3)

    def put(whole, piece, spot, side):
        return lax.dynamic_update_slice_in_dim(whole, piece, (spot * 2 + side) * rows, 0)

    def put_far(whole, piece, side):
        held = lax.dynamic_slice_in_dim(whole, (far * 2 + side) * rows, rows, 0)
        return put(whole, jnp.where(edge, piece, held), far, side)

    whole = jnp.zeros((8 * rows,) + own.shape[1:], own.dtype)
    up, down, other = hop(own, axis, UP), hop(own, axis, DOWN), swap_at(own, axis, range(4))
    up_two, down_two = hop(up, axis, UP[1:]), hop(down, axis, DOWN[:2])
    other_up, other_down = swap_at(up, axis, (1, 2, 3)), swap_at(down, axis, (0, 1, 2))
    whole = put(put(whole, own, z, x), other, z, 1 - x)
    whole = put(put(whole, up, (z + 3) % 4, x), down, (z + 1) % 4, x)
    two = jnp.where(upper, up_two, down_two)
    three = hop(two, axis, [(2, 3), (1, 0)])
    other_two = swap_at(two, axis, range(4))
    whole = put(put(whole, other_up, (z + 3) % 4, 1 - x), other_down, (z + 1) % 4, 1 - x)
    whole = put(whole, two, across, x)
    other_three = swap_at(three, axis, (0, 3))
    whole = put(whole, other_two, across, 1 - x)
    return put_far(put_far(whole, three, x), other_three, 1 - x)


def line_summed(part_of, axis):
    if lax.axis_size(axis) != 8:
        return (scattered_sum(part_of, axis),)
    place = lax.axis_index(axis)
    z, x = place // 2, place % 2
    upper, edge = z >= 2, (z == 0) | (z == 3)
    across = jnp.where(upper, z - 2, z + 2)
    far = jnp.where(z == 0, 3, 0)
    above, below = jnp.minimum(z + 1, 3), jnp.maximum(z - 1, 0)

    def swapped(spot, spots):
        return swap_at(part_of(spot * 2 + 1 - x), axis, spots)

    def added(spot, given):
        return part_of(spot * 2 + x).astype(f32) + given.astype(f32)

    given_far = swapped(far, (0, 3))
    given_across = swapped(across, range(4))
    given_above, given_below = swapped(above, (0, 1, 2)), swapped(below, (1, 2, 3))
    given_own = swapped(z, range(4))
    three = hop(added(far, given_far).astype(bf16), axis, [(0, 1), (3, 2)])
    three, given_across, given_above, given_below = together(
        (three, given_across, given_above, given_below)
    )
    two = added(across, given_across) + jnp.where(edge, 0.0, three.astype(f32))
    two = two.astype(bf16)
    two_up, two_down, given_own = together(
        (hop(two, axis, UP[:2]), hop(two, axis, DOWN[1:]), given_own)
    )
    one_up = (added(above, given_above) + two_up.astype(f32)).astype(bf16)
    one_down = (added(below, given_below) + two_down.astype(f32)).astype(bf16)
    return added(z, given_own), hop(one_up, axis, UP), hop(one_down, axis, DOWN)


def scattered_sum(part_of, axis):
    count = lax.axis_size(axis)
    place = lax.axis_index(axis)
    half = count // 2
    outer, inner = place // 2, place % 2
    total = None
    for k in shift_order(half) + [0]:
        target = (outer + k) % half
        given = inner_swap(part_of(target * 2 + 1 - inner), axis)
        piece = part_of(target * 2 + inner).astype(f32) + given.astype(f32)
        if k:
            piece = outer_shift(piece.astype(bf16), axis, k).astype(f32)
        total = piece if total is None else total + piece
    return total


def rows_of(value, rows):
    return lambda place: lax.dynamic_slice_in_dim(value, place * rows, rows, 0)


def summed_over_seq(part, change):
    count = lax.axis_size("seq")
    length, columns = part.shape
    part = part.astype(bf16).reshape(count, length // count, columns)
    own = change(jnp.sum(lax.all_to_all(part, "seq", 0, 0).astype(f32), axis=0))
    return shared(own, "seq").reshape(length, own.shape[1])


def two_terms(value):
    high = value.astype(bf16)
    return [high, (value - high.astype(f32)).astype(bf16)]


def shared(own, axis):
    wide = jnp.broadcast_to(own[None], (lax.axis_size(axis),) + own.shape)
    return lax.all_to_all(wide, axis, 0, 0)


def matmul(a, b, dims=(((1,), (0,)), ((), ()))):
    return lax.dot_general(a, b, dims, preferred_element_type=f32)


TN = (((0,), (0,)), ((), ()))


def on_device(
    tokens,
    lengths,
    norm_gain,
    in_proj,
    conv_weight,
    conv_bias,
    x_proj,
    dt_proj,
    dt_bias,
    a_log,
    skip,
    out_proj,
    cotangent,
):
    batch, seq = lax.axis_size("batch"), lax.axis_size("seq")
    place = lax.axis_index("seq")
    span, model = tokens.shape[1:]
    length = span * seq
    in_rows = in_proj.shape[0]
    own = skip.shape[0]
    taps = conv_weight.shape[0]
    rank = dt_proj.shape[0]
    states = a_log.shape[1]
    width = own * batch

    halves = in_proj.reshape(in_rows, 2, batch, seq, own).transpose(1, 3, 0, 2, 4)
    halves = halves.reshape(2, seq, in_rows, width)
    columns = lax.all_to_all(halves[0], "seq", 0, 0)
    small = jnp.concatenate(
        [
            dt_proj,
            x_proj.T,
            a_log.T,
            conv_weight,
            conv_bias[None],
            dt_bias[None],
            skip[None],
            jnp.pad(norm_gain, (0, own - in_rows))[None],
        ],
        axis=0,
    )
    small = gathered(small, "batch", 1)
    cuts = [rank, 2 * rank + 2 * states, 2 * rank + 3 * states]
    cuts = cuts + [cuts[2] + taps + i for i in range(4)]
    delta_weight, select_weight, decay_logs, conv_taps, conv_shift, delta_shift, skip_gain, gain = (
        jnp.split(small, cuts, axis=0)
    )
    conv_taps, conv_shift = conv_taps.astype(f32), conv_shift.astype(f32)
    delta_shift, skip_gain = delta_shift.astype(f32), skip_gain.astype(f32)
    decay = -jnp.exp(decay_logs.astype(f32))
    gain = gain.reshape(batch, own)[:, :in_rows]
    columns, gain = together((columns, gain))
    gain = shared(gain, "seq")
    gate_columns, gain = together((halves[1], gain))
    gate_columns = lax.all_to_all(gate_columns, "seq", 0, 0)
    gain = gain.transpose(1, 0, 2).reshape(model).astype(f32)

    input_weight = gathered(columns.reshape(seq * in_rows, width), "batch")
    output_weight = gathered(out_proj, "batch")

    def normed(rows):
        rows = rows.astype(f32)
        scale = lax.rsqrt(jnp.mean(rows * rows, axis=-1, keepdims=True) + epsilon)
        return (rows * scale * gain).astype(bf16)

    stream = lax.all_gather(tokens[0], "seq", axis=0, tiled=True)
    gate_weight = gathered(gate_columns.reshape(seq * in_rows, width), "batch")
    normalized = normed(stream)
    upstream = line_gathered(cotangent[0], "seq")

    valid = (jnp.arange(length, dtype=jnp.int32) < lengths[0])[:, None]
    inner = matmul(normalized, input_weight).astype(bf16)
    padded = jnp.pad(inner, ((taps - 1, 0), (0, 0)))
    conv_out = conv_shift + jnp.zeros((length, width), f32)
    for tap in range(taps):
        conv_out = conv_out + conv_taps[tap] * padded[tap : tap + length].astype(f32)
    active = jax.nn.silu(conv_out).astype(bf16)
    active_f = active.astype(f32)

    partial, upstream = together((matmul(active, select_weight, NT), upstream))
    select = summed_over_seq(
        partial,
        lambda s: jnp.concatenate([s[:, :rank].astype(bf16)] + two_terms(s[:, rank:]), axis=1),
    )
    gate = matmul(normalized, gate_weight).astype(bf16).astype(f32)
    delta_low = select[:, :rank]
    delta_raw = matmul(delta_low, delta_weight) + delta_shift
    delta = jax.nn.softplus(delta_raw)

    block = min(BLOCK, length)
    step = 256 // states
    rate = decay * LOG2E
    mixed, kept = scan_forward(delta, active, select, rate, block, step)
    mixed = mixed + skip_gain * active_f
    gate_sig = jax.nn.sigmoid(gate)
    gated = (mixed * gate * gate_sig).astype(bf16)
    branch = matmul(gated, output_weight).astype(bf16)
    upstream, branch = together((upstream, branch))
    upstream = jnp.where(valid, upstream, 0).astype(bf16)
    branch = lax.psum_scatter(branch, "seq", scatter_dimension=0, tiled=True)
    own_valid = lax.dynamic_slice_in_dim(valid, place * span, span, 0)
    own_stream = tokens[0].astype(f32)

    d_gated = matmul(upstream, output_weight, NT)
    d_mixed = d_gated * gate * gate_sig
    d_gate = d_gated * mixed * gate_sig * (1.0 + gate * (1.0 - gate_sig))
    grad_skip = jnp.sum(d_mixed * active_f, axis=0, keepdims=True)

    d_gate_low = d_gate.astype(bf16)
    d_delta, d_active, d_bc, grad_log = scan_backward(
        delta, active, d_mixed, select, rate, decay, kept, block, step
    )
    d_raw = d_delta * jax.nn.sigmoid(delta_raw)
    grad_dt_bias = jnp.sum(d_raw, axis=0, keepdims=True)
    d_raw_low = d_raw.astype(bf16)
    grad_dt_proj = matmul(delta_low, d_raw_low, TN)
    partial = jnp.concatenate([matmul(d_raw_low, delta_weight, NT), d_bc], axis=1)
    d_select = summed_over_seq(partial, lambda s: s.astype(bf16))
    grad_gate = scattered_sum(
        rows_of(matmul(normalized, d_gate_low, TN).astype(bf16), model // batch), "batch"
    )
    d_select, grad_gate = together((d_select, grad_gate))
    grad_x_proj = matmul(d_select, active, TN)
    d_active = d_active + d_mixed * skip_gain + matmul(d_select, select_weight)
    conv_sig = jax.nn.sigmoid(conv_out)
    d_conv = (d_active * conv_sig * (1.0 + conv_out * (1.0 - conv_sig))).astype(bf16)
    d_conv_f = d_conv.astype(f32)
    grad_conv_bias = jnp.sum(d_conv_f, axis=0, keepdims=True)
    grad_conv = jnp.stack(
        [
            jnp.sum(d_conv_f * padded[tap : tap + length].astype(f32), axis=0)
            for tap in range(taps)
        ]
    )
    extended = jnp.pad(d_conv, ((0, taps - 1), (0, 0)))
    d_inner = jnp.zeros((length, width), f32)
    for tap in range(taps):
        offset = taps - 1 - tap
        d_inner = d_inner + conv_taps[tap] * extended[offset : offset + length].astype(f32)
    d_inner = d_inner.astype(bf16)
    grad_inner = matmul(normalized, d_inner, TN).astype(bf16)
    d_inner, grad_inner, branch = together((d_inner, grad_inner, branch))
    d_normalized = matmul(
        jnp.concatenate([d_inner, d_gate_low], axis=1),
        jnp.concatenate([input_weight, gate_weight], axis=1),
        NT,
    ).astype(bf16)
    grad_inner = scattered_sum(rows_of(grad_inner, model // batch), "batch")
    grad_gate = grad_gate.astype(bf16).reshape(seq, in_rows, width)
    grad_gate = lax.all_to_all(grad_gate, "seq", 0, 0)
    d_normalized, gated, grad_gate = together((d_normalized, gated, grad_gate))
    grad_output = lax.psum_scatter(
        matmul(gated, upstream, TN).astype(bf16), "batch", scatter_dimension=0, tiled=True
    ).astype(f32)
    d_normalized, *last_terms = line_summed(rows_of(d_normalized, span), "seq")

    block_out = jnp.where(own_valid, own_stream + branch.astype(f32), 0.0)

    def columns_of(part):
        part = part.reshape(seq, in_rows, batch, own).transpose(1, 2, 0, 3)
        return part.reshape(in_rows, batch * seq * own).astype(f32)

    grad_inner = grad_inner.astype(bf16).reshape(seq, in_rows, width)
    grad_inner = lax.all_to_all(grad_inner, "seq", 0, 0)
    grad_input = jnp.concatenate([columns_of(grad_inner), columns_of(grad_gate)], axis=1)

    small_grads = jnp.concatenate(
        [grad_dt_proj, grad_x_proj, grad_log, grad_conv, grad_conv_bias, grad_dt_bias, grad_skip],
        axis=0,
    )
    small_grads = lax.psum_scatter(small_grads, "batch", scatter_dimension=1, tiled=True)
    g_dt_proj, g_x_proj, g_log, g_conv, g_conv_bias, g_dt_bias, g_skip = jnp.split(
        small_grads, cuts[:-1], axis=0
    )

    own_upstream = jnp.where(own_valid, cotangent[0].astype(f32), 0.0)
    own_scale = lax.rsqrt(jnp.mean(own_stream * own_stream, axis=-1, keepdims=True) + epsilon)
    grad_gain = jnp.sum(grad_input * in_proj.astype(f32), axis=1) / norm_gain.astype(f32)
    (
        d_normalized, g_dt_proj, g_x_proj, g_log, g_conv, g_conv_bias, g_dt_bias, g_skip,
        grad_input, grad_gain, grad_output,
    ) = together(
        (
            d_normalized, g_dt_proj, g_x_proj, g_log, g_conv, g_conv_bias, g_dt_bias, g_skip,
            grad_input, grad_gain, grad_output,
        )
    )
    for term in last_terms:
        d_normalized = d_normalized + term.astype(f32)
    d_hat = d_normalized * gain
    grad_tokens = (
        own_scale * d_hat
        - own_stream
        * own_scale
        * own_scale
        * own_scale
        * jnp.mean(d_hat * own_stream, axis=-1, keepdims=True)
        + own_upstream
    )
    return (
        block_out[None],
        grad_tokens[None],
        grad_gain,
        grad_input,
        g_conv,
        g_conv_bias[0],
        g_x_proj.T,
        g_dt_proj,
        g_dt_bias[0],
        g_log.T,
        g_skip[0],
        grad_output,
    )


def solution(mesh):
    placed = (
        P("batch", "seq", None),
        P("batch"),
        P(("batch", "seq")),
        P(("batch", "seq"), None),
        P(None, ("batch", "seq")),
        P(("batch", "seq")),
        P(("batch", "seq"), None),
        P(None, ("batch", "seq")),
        P(("batch", "seq")),
        P(("batch", "seq"), None),
        P(("batch", "seq")),
        P(("batch", "seq"), None),
        P("batch", "seq", None),
    )
    return jax.shard_map(
        on_device,
        mesh=mesh,
        in_specs=placed,
        out_specs=(
            P("batch", "seq", None),
            P("batch", "seq", None),
            P(("batch", "seq")),
            P(("batch", "seq"), None),
            P(None, ("batch", "seq")),
            P(("batch", "seq")),
            P(("batch", "seq"), None),
            P(None, ("batch", "seq")),
            P(("batch", "seq")),
            P(("batch", "seq"), None),
            P(("batch", "seq")),
            P(("batch", "seq"), None),
        ),
        check_vma=False,
    )
```

```python
import functools

import jax
import jax.numpy as jnp
from jax import lax
from jax.experimental import pallas as pl
from jax.experimental.pallas import tpu as pltpu
from jax.sharding import PartitionSpec as P

bf16, f32 = jnp.bfloat16, jnp.float32
NT = (((1,), (1,)), ((), ()))
LANES = 128
GROUP = 32
BLOCK = 128
epsilon = 1e-05
LOG2E = 1.4426950408889634


def spread(tile, row, lanes, states):
    return jnp.broadcast_to(tile[row : row + 1, lanes], (states, LANES))


def selectors(select, states):
    low = select.shape[1] - 4 * states
    middle = low + 2 * states
    block = select[:, low:middle].astype(f32) + select[:, middle:].astype(f32)
    return jnp.transpose(block), block[:, :states], block[:, states:]


def block_diagonal(values, step):
    rows, states = values.shape
    wide = step * states
    spread_out = (
        lax.broadcasted_iota(jnp.int32, (states, wide), 1) % states
        == lax.broadcasted_iota(jnp.int32, (states, wide), 0)
    ).astype(bf16)
    value = jnp.dot(values.astype(bf16), spread_out, preferred_element_type=f32)
    place = lax.broadcasted_iota(jnp.int32, (rows, wide), 0) % step
    owner = lax.broadcasted_iota(jnp.int32, (rows, wide), 1) // states
    return jnp.where(place == owner, value, 0.0).astype(bf16)


def forward_body(tiles, step, delta, active, select, rate, mixed, kept, state, drive, columns):
    rows, states = delta.shape[0], rate.shape[0]
    wide = step * states

    @pl.when(pl.program_id(0) == 0)
    def _():
        state[...] = jnp.zeros_like(state)

    turned, _, c_block = selectors(select[...], states)
    columns[...] = turned[:states]
    drive[...] = delta[...] * active[...].astype(f32)
    rates = [rate[:, k * LANES : (k + 1) * LANES] for k in range(tiles)]

    def group(number, held):
        held = list(held)
        base = pl.multiple_of(number * GROUP, GROUP)
        delta_now, drive_now = delta.at[pl.ds(base, GROUP), :], drive.at[pl.ds(base, GROUP), :]
        b_now = pltpu.roll(columns[...], rows - base, 1)
        for j in range(GROUP):
            b_wide = jnp.broadcast_to(b_now[:, j : j + 1], (states, LANES))
            for k in range(tiles):
                lanes = slice(k * LANES, (k + 1) * LANES)
                decay = jnp.exp2(spread(delta_now, j, lanes, states) * rates[k])
                held[k] = decay * held[k] + spread(drive_now, j, lanes, states) * b_wide
                at = pl.ds(pl.multiple_of((base + j) * states, states), states)
                kept[at, lanes] = held[k].astype(bf16)
        return tuple(held)

    held = lax.fori_loop(
        0,
        rows // GROUP,
        group,
        tuple(state[:, k * LANES : (k + 1) * LANES] for k in range(tiles)),
    )
    for k in range(tiles):
        state[:, k * LANES : (k + 1) * LANES] = held[k]
    c_diag = block_diagonal(c_block, step)
    for q in range(rows // step):
        part = kept[q * wide : (q + 1) * wide, :]
        spot = slice(q * step, (q + 1) * step)
        mixed[spot, :] = jnp.dot(c_diag[spot, :], part, preferred_element_type=f32)


def scan_forward(delta, active, select, rate, block, step):
    length, width = delta.shape
    states = rate.shape[0]
    tiles = width // LANES
    return pl.pallas_call(
        functools.partial(forward_body, tiles, step),
        grid=(length // block,),
        in_specs=[
            pl.BlockSpec((block, width), lambda i: (i, 0)),
            pl.BlockSpec((block, width), lambda i: (i, 0)),
            pl.BlockSpec((block, select.shape[1]), lambda i: (i, 0)),
            pl.BlockSpec((states, width), lambda i: (0, 0)),
        ],
        out_specs=[
            pl.BlockSpec((block, width), lambda i: (i, 0)),
            pl.BlockSpec((block * states, width), lambda i: (i, 0)),
        ],
        out_shape=[
            jax.ShapeDtypeStruct((length, width), f32),
            jax.ShapeDtypeStruct((length * states, width), bf16),
        ],
        scratch_shapes=[
            pltpu.VMEM((states, width), f32),
            pltpu.VMEM((block, width), f32),
            pltpu.VMEM((states, block), f32),
        ],
        compiler_params=pltpu.CompilerParams(vmem_limit_bytes=48 << 20),
        cost_estimate=pl.CostEstimate(
            flops=8 * length * width * states,
            transcendentals=length * width * states,
            bytes_accessed=length * width * (2 * states + 10),
        ),
        name="scan_forward",
    )(delta, active, select, rate)


FEW = 4


def backward_body(
    tiles, step, delta, active, d_mixed, select, rate, decay_rate, kept, kept_before,
    d_delta, d_active, d_bc, d_log, push, drive, columns, diagonals, folding, timed, *pairs,
):
    grads, rated = pairs[:2], pairs[2:]
    rows, states = delta.shape[0], rate.shape[0]
    blocks = pl.num_programs(0)
    first = pl.program_id(0) == blocks - 1
    wide = step * states

    @pl.when(pl.program_id(0) == 0)
    def _():
        push[...] = jnp.zeros_like(push)
        d_log[...] = jnp.zeros_like(d_log)

    turned, b_block, _ = selectors(select[...], states)
    columns[...] = turned[states:]
    drive[...] = delta[...] * active[...].astype(f32)
    rates = [rate[:, k * LANES : (k + 1) * LANES] for k in range(tiles)]
    own_rates = [decay_rate[:, k * LANES : (k + 1) * LANES].astype(bf16) for k in range(tiles)]

    place = lax.broadcasted_iota(jnp.int32, (step, wide), 0)
    owner = lax.broadcasted_iota(jnp.int32, (step, wide), 1) // states
    ones_diag = (place == owner).astype(bf16)
    diag = (place == owner).astype(f32)
    diagonals[...] = block_diagonal(b_block, step)

    def sums_of(number):
        held, through_of = number % 2, {}

        def spots(q):
            at = number * GROUP + q * step
            tall = slice(q * wide, (q + 1) * wide)
            return slice(at, at + step), tall

        def through(q):
            spot, tall = spots(q)
            value = jnp.dot(diagonals[spot, :], grads[held][tall, :], preferred_element_type=f32)
            d_active[spot, :] = delta[spot, :] * value
            through_of[q] = active[spot, :].astype(f32) * value

        def summed(q):
            spot, tall = spots(q)
            value = jnp.dot(ones_diag, rated[held][tall, :], preferred_element_type=f32)
            d_delta[spot, :] = value + through_of[q]

        def d_b(q):
            spot, tall = spots(q)
            folding[spot, :wide] = diag * lax.dot_general(
                drive[spot, :].astype(bf16), grads[held][tall, :], NT, preferred_element_type=f32
            )

        def d_c(q):
            spot, _ = spots(q)
            own = slice(spot.start * states, spot.stop * states)
            folding[spot, wide:] = diag * lax.dot_general(
                d_mixed[spot, :].astype(bf16), kept[own, :], NT, preferred_element_type=f32
            )

        return [
            functools.partial(part, q)
            for q in range(GROUP // step)
            for part in (through, summed, d_b, d_c)
        ]

    carry = [push[:, k * LANES : (k + 1) * LANES] for k in range(tiles)]
    waiting = []
    for number in reversed(range(rows // GROUP)):
        pace = GROUP // max(len(waiting), 1)
        sums = [None] * tiles
        held = number % 2
        for j in reversed(range(GROUP)):
            row = number * GROUP + j
            c_wide = jnp.broadcast_to(columns[:, row : row + 1], (states, LANES))
            at = slice(j * states, (j + 1) * states)
            for k in range(tiles):
                lanes = slice(k * LANES, (k + 1) * LANES)
                if row:
                    before = kept[(row - 1) * states : row * states, lanes]
                else:
                    before = jnp.where(first, jnp.zeros((), bf16), kept_before[:, lanes])
                step_size = spread(delta, row, lanes, states)
                grad = spread(d_mixed, row, lanes, states) * c_wide + carry[k]
                carry[k] = jnp.exp2(step_size * rates[k]) * grad
                grads[held][at, lanes] = grad.astype(bf16)
                rated_now = carry[k].astype(bf16) * before * own_rates[k]
                rated[held][at, lanes] = rated_now
                timed_now = rated_now * step_size.astype(bf16)
                sums[k] = timed_now if sums[k] is None else sums[k] + timed_now
                if j % FEW == 0:
                    spot = row // FEW * states
                    timed[spot : spot + states, lanes] = sums[k]
                    sums[k] = None
            if waiting and j % pace == 0:
                waiting.pop(0)()
        while waiting:
            waiting.pop(0)()
        waiting = sums_of(number)
    while waiting:
        waiting.pop(0)()
    for k in range(tiles):
        push[:, k * LANES : (k + 1) * LANES] = carry[k]
    fold = (
        lax.broadcasted_iota(jnp.int32, (wide, states), 0) % states
        == lax.broadcasted_iota(jnp.int32, (wide, states), 1)
    ).astype(bf16)
    for number in range(2):
        value = folding[:, number * wide : (number + 1) * wide]
        high = value.astype(bf16)
        d_bc[:, number * states : (number + 1) * states] = jnp.dot(
            high, fold, preferred_element_type=f32
        )
    span = rows // FEW * states
    pick = (
        lax.broadcasted_iota(jnp.int32, (states, span), 1) % states
        == lax.broadcasted_iota(jnp.int32, (states, span), 0)
    ).astype(bf16)
    d_log[...] += jnp.dot(pick, timed[...], preferred_element_type=f32)


def scan_backward(delta, active, d_mixed, select, rate, decay_rate, kept, block, step):
    length, width = delta.shape
    states = rate.shape[0]
    tiles = width // LANES
    blocks = length // block
    back = lambda i: (blocks - 1 - i, 0)
    return pl.pallas_call(
        functools.partial(backward_body, tiles, step),
        grid=(blocks,),
        in_specs=[
            pl.BlockSpec((block, width), back),
            pl.BlockSpec((block, width), back),
            pl.BlockSpec((block, width), back),
            pl.BlockSpec((block, select.shape[1]), back),
            pl.BlockSpec((states, width), lambda i: (0, 0)),
            pl.BlockSpec((states, width), lambda i: (0, 0)),
            pl.BlockSpec((block * states, width), back),
            pl.BlockSpec(
                (states, width), lambda i: (jnp.maximum((blocks - 1 - i) * block - 1, 0), 0)
            ),
        ],
        out_specs=[
            pl.BlockSpec((block, width), back),
            pl.BlockSpec((block, width), back),
            pl.BlockSpec((block, 2 * states), back),
            pl.BlockSpec((states, width), lambda i: (0, 0)),
        ],
        out_shape=[
            jax.ShapeDtypeStruct((length, width), f32),
            jax.ShapeDtypeStruct((length, width), f32),
            jax.ShapeDtypeStruct((length, 2 * states), f32),
            jax.ShapeDtypeStruct((states, width), f32),
        ],
        scratch_shapes=[
            pltpu.VMEM((states, width), f32),
            pltpu.VMEM((block, width), f32),
            pltpu.VMEM((states, block), f32),
            pltpu.VMEM((block, step * states), bf16),
            pltpu.VMEM((block, 2 * step * states), f32),
            pltpu.VMEM((block // FEW * states, width), bf16),
        ]
        + [pltpu.VMEM((GROUP * states, width), bf16)] * 4,
        compiler_params=pltpu.CompilerParams(vmem_limit_bytes=48 << 20),
        cost_estimate=pl.CostEstimate(
            flops=20 * length * width * states,
            transcendentals=length * width * states,
            bytes_accessed=length * width * (2 * states + 20),
        ),
        name="scan_backward",
    )(delta, active, d_mixed, select, rate, decay_rate, kept, kept)


together = lax.optimization_barrier


def inner_swap(value, axis):
    count = lax.axis_size(axis)
    return lax.ppermute(value, axis, [(i, i ^ 1) for i in range(count)])


def outer_shift(value, axis, steps):
    count = lax.axis_size(axis)
    half = count // 2
    pairs = [(i, (i // 2 + steps) % half * 2 + i % 2) for i in range(count)]
    return lax.ppermute(value, axis, pairs)


def shift_order(half):
    return sorted(range(1, half), key=lambda k: (-min(k, half - k), k))


def pieces_of_all(own, axis):
    count = lax.axis_size(axis)
    place = lax.axis_index(axis)
    half = count // 2
    outer, inner = place // 2, place % 2
    yield place, own
    arrived = {k: outer_shift(own, axis, k) for k in shift_order(half)}
    yield outer * 2 + 1 - inner, inner_swap(own, axis)
    for k, piece in arrived.items():
        origin = (outer - k + half) % half
        yield origin * 2 + inner, piece
    for k, piece in arrived.items():
        origin = (outer - k + half) % half
        yield origin * 2 + 1 - inner, inner_swap(piece, axis)


def gathered(own, axis, dim=0):
    count, size = lax.axis_size(axis), own.shape[dim]
    whole = jnp.zeros(own.shape[:dim] + (count * size,) + own.shape[dim + 1 :], own.dtype)
    for place, piece in pieces_of_all(own, axis):
        whole = lax.dynamic_update_slice_in_dim(whole, piece, place * size, dim)
    return whole


def hop(value, axis, moves):
    pairs = [(a * 2 + i, b * 2 + i) for a, b in moves for i in (0, 1)]
    return lax.ppermute(value, axis, pairs)


def swap_at(value, axis, spots):
    pairs = [(a * 2 + i, a * 2 + 1 - i) for a in spots for i in (0, 1)]
    return lax.ppermute(value, axis, pairs)


UP, DOWN = [(0, 1), (1, 2), (2, 3)], [(1, 0), (2, 1), (3, 2)]


def line_gathered(own, axis, held):
    if lax.axis_size(axis) != 8:
        return lax.all_gather(own, axis, axis=0, tiled=True), held
    place = lax.axis_index(axis)
    z, x = place // 2, place % 2
    rows = own.shape[0]
    upper, edge = z >= 2, (z == 0) | (z == 3)
    across = jnp.where(upper, z - 2, z + 2)
    far = jnp.where(z == 3, 0, 3)

    def put(whole, piece, spot, side):
        return lax.dynamic_update_slice_in_dim(whole, piece, (spot * 2 + side) * rows, 0)

    def put_far(whole, piece, side):
        held = lax.dynamic_slice_in_dim(whole, (far * 2 + side) * rows, rows, 0)
        return put(whole, jnp.where(edge, piece, held), far, side)

    whole = jnp.zeros((8 * rows,) + own.shape[1:], own.dtype)
    up, down, other, held = together(
        (hop(own, axis, UP), hop(own, axis, DOWN), swap_at(own, axis, range(4)), held)
    )
    up_two, down_two = hop(up, axis, UP[1:]), hop(down, axis, DOWN[:2])
    other_up, other_down = swap_at(up, axis, (1, 2, 3)), swap_at(down, axis, (0, 1, 2))
    whole = put(put(whole, own, z, x), other, z, 1 - x)
    whole = put(put(whole, up, (z + 3) % 4, x), down, (z + 1) % 4, x)
    two = jnp.where(upper, up_two, down_two)
    three = hop(two, axis, [(2, 3), (1, 0)])
    other_two = swap_at(two, axis, range(4))
    whole = put(put(whole, other_up, (z + 3) % 4, 1 - x), other_down, (z + 1) % 4, 1 - x)
    whole = put(whole, two, across, x)
    other_three = swap_at(three, axis, (0, 3))
    whole = put(whole, other_two, across, 1 - x)
    return put_far(put_far(whole, three, x), other_three, 1 - x), held


def line_summed(part_of, axis):
    if lax.axis_size(axis) != 8:
        return (scattered_sum(part_of, axis),)
    place = lax.axis_index(axis)
    z, x = place // 2, place % 2
    upper, edge = z >= 2, (z == 0) | (z == 3)
    across = jnp.where(upper, z - 2, z + 2)
    far = jnp.where(z == 0, 3, 0)
    above, below = jnp.minimum(z + 1, 3), jnp.maximum(z - 1, 0)

    def swapped(spot, spots):
        return swap_at(part_of(spot * 2 + 1 - x), axis, spots)

    def added(spot, given):
        return part_of(spot * 2 + x).astype(f32) + given.astype(f32)

    given_far = swapped(far, (0, 3))
    given_across = swapped(across, range(4))
    given_above, given_below = swapped(above, (0, 1, 2)), swapped(below, (1, 2, 3))
    given_own = swapped(z, range(4))
    three = hop(added(far, given_far).astype(bf16), axis, [(0, 1), (3, 2)])
    three, given_across, given_above, given_below = together(
        (three, given_across, given_above, given_below)
    )
    two = added(across, given_across) + jnp.where(edge, 0.0, three.astype(f32))
    two = two.astype(bf16)
    two_up, two_down, given_own = together(
        (hop(two, axis, UP[:2]), hop(two, axis, DOWN[1:]), given_own)
    )
    one_up = (added(above, given_above) + two_up.astype(f32)).astype(bf16)
    one_down = (added(below, given_below) + two_down.astype(f32)).astype(bf16)
    return added(z, given_own), hop(one_up, axis, UP), hop(one_down, axis, DOWN)


def scattered_sum(part_of, axis):
    count = lax.axis_size(axis)
    place = lax.axis_index(axis)
    half = count // 2
    outer, inner = place // 2, place % 2
    total = None
    for k in shift_order(half) + [0]:
        target = (outer + k) % half
        given = inner_swap(part_of(target * 2 + 1 - inner), axis)
        piece = part_of(target * 2 + inner).astype(f32) + given.astype(f32)
        if k:
            piece = outer_shift(piece.astype(bf16), axis, k).astype(f32)
        total = piece if total is None else total + piece
    return total


def rows_of(value, rows):
    return lambda place: lax.dynamic_slice_in_dim(value, place * rows, rows, 0)


def summed_over_seq(part, change):
    count = lax.axis_size("seq")
    length, columns = part.shape
    part = part.astype(bf16).reshape(count, length // count, columns)
    own = change(jnp.sum(lax.all_to_all(part, "seq", 0, 0).astype(f32), axis=0))
    return shared(own, "seq").reshape(length, own.shape[1])


def two_terms(value):
    high = value.astype(bf16)
    return [high, (value - high.astype(f32)).astype(bf16)]


def shared(own, axis):
    wide = jnp.broadcast_to(own[None], (lax.axis_size(axis),) + own.shape)
    return lax.all_to_all(wide, axis, 0, 0)


def matmul(a, b, dims=(((1,), (0,)), ((), ()))):
    return lax.dot_general(a, b, dims, preferred_element_type=f32)


TN = (((0,), (0,)), ((), ()))


def on_device(
    tokens,
    lengths,
    norm_gain,
    in_proj,
    conv_weight,
    conv_bias,
    x_proj,
    dt_proj,
    dt_bias,
    a_log,
    skip,
    out_proj,
    cotangent,
):
    batch, seq = lax.axis_size("batch"), lax.axis_size("seq")
    place = lax.axis_index("seq")
    span, model = tokens.shape[1:]
    length = span * seq
    in_rows = in_proj.shape[0]
    own = skip.shape[0]
    taps = conv_weight.shape[0]
    rank = dt_proj.shape[0]
    states = a_log.shape[1]
    width = own * batch

    halves = in_proj.reshape(in_rows, 2, batch, seq, own).transpose(1, 3, 0, 2, 4)
    halves = halves.reshape(2, seq, in_rows, width)
    columns = lax.all_to_all(halves[0], "seq", 0, 0)
    columns, gate_columns = together((columns, halves[1]))
    gate_columns = lax.all_to_all(gate_columns, "seq", 0, 0)
    upstream, (dt_proj, x_proj, out_proj) = line_gathered(
        cotangent[0], "seq", (dt_proj, x_proj, out_proj)
    )
    small = jnp.concatenate(
        [
            dt_proj,
            x_proj.T,
            a_log.T,
            conv_weight,
            conv_bias[None],
            dt_bias[None],
            skip[None],
            jnp.pad(norm_gain, (0, own - in_rows))[None],
        ],
        axis=0,
    )
    small = gathered(small, "batch", 1)
    cuts = [rank, 2 * rank + 2 * states, 2 * rank + 3 * states]
    cuts = cuts + [cuts[2] + taps + i for i in range(4)]
    delta_weight, select_weight, decay_logs, conv_taps, conv_shift, delta_shift, skip_gain, gain = (
        jnp.split(small, cuts, axis=0)
    )
    conv_taps, conv_shift = conv_taps.astype(f32), conv_shift.astype(f32)
    delta_shift, skip_gain = delta_shift.astype(f32), skip_gain.astype(f32)
    decay = -jnp.exp(decay_logs.astype(f32))
    gain = gain.reshape(batch, own)[:, :in_rows]
    gate_columns, gain = together((gate_columns, gain))
    gain = shared(gain, "seq").transpose(1, 0, 2).reshape(model).astype(f32)

    input_weight = gathered(columns.reshape(seq * in_rows, width), "batch")

    def normed(rows):
        rows = rows.astype(f32)
        scale = lax.rsqrt(jnp.mean(rows * rows, axis=-1, keepdims=True) + epsilon)
        return (rows * scale * gain).astype(bf16)

    stream = lax.all_gather(tokens[0], "seq", axis=0, tiled=True)
    normalized = normed(stream)
    output_weight = gathered(out_proj, "batch")

    valid = (jnp.arange(length, dtype=jnp.int32) < lengths[0])[:, None]
    inner = matmul(normalized, input_weight).astype(bf16)
    padded = jnp.pad(inner, ((taps - 1, 0), (0, 0)))
    conv_out = conv_shift + jnp.zeros((length, width), f32)
    for tap in range(taps):
        conv_out = conv_out + conv_taps[tap] * padded[tap : tap + length].astype(f32)
    active = jax.nn.silu(conv_out).astype(bf16)
    active_f = active.astype(f32)

    partial, upstream, gate_columns = together(
        (matmul(active, select_weight, NT), upstream, gate_columns)
    )
    gate_weight = gathered(gate_columns.reshape(seq * in_rows, width), "batch")
    select = summed_over_seq(
        partial,
        lambda s: jnp.concatenate([s[:, :rank].astype(bf16)] + two_terms(s[:, rank:]), axis=1),
    )
    upstream = jnp.where(valid, upstream, 0).astype(bf16)
    gate_low = matmul(normalized, gate_weight).astype(bf16)
    d_gated = matmul(upstream, output_weight, NT)
    select, gate_low, d_gated = together((select, gate_low, d_gated))
    gate = gate_low.astype(f32)
    gate_sig = jax.nn.sigmoid(gate)
    delta_low = select[:, :rank]
    delta_raw = matmul(delta_low, delta_weight) + delta_shift
    delta = jax.nn.softplus(delta_raw)

    block = min(BLOCK, length)
    step = 256 // states
    rate = decay * LOG2E
    mixed, kept = scan_forward(delta, active, select, rate, block, step)
    mixed = mixed + skip_gain * active_f
    gated = (mixed * gate * gate_sig).astype(bf16)
    branch = matmul(gated, output_weight).astype(bf16)
    d_gated, branch = together((d_gated, branch))
    branch = lax.psum_scatter(branch, "seq", scatter_dimension=0, tiled=True)
    own_valid = lax.dynamic_slice_in_dim(valid, place * span, span, 0)
    own_stream = tokens[0].astype(f32)

    d_mixed = d_gated * gate * gate_sig
    d_gate = d_gated * mixed * gate_sig * (1.0 + gate * (1.0 - gate_sig))
    grad_skip = jnp.sum(d_mixed * active_f, axis=0, keepdims=True)
    d_gate_low = d_gate.astype(bf16)

    d_delta, d_active, d_bc, grad_log = scan_backward(
        delta, active, d_mixed, select, rate, decay, kept, block, step
    )
    d_raw = d_delta * jax.nn.sigmoid(delta_raw)
    grad_dt_bias = jnp.sum(d_raw, axis=0, keepdims=True)
    d_raw_low = d_raw.astype(bf16)
    grad_dt_proj = matmul(delta_low, d_raw_low, TN)
    partial = jnp.concatenate([matmul(d_raw_low, delta_weight, NT), d_bc], axis=1)
    d_select = summed_over_seq(partial, lambda s: s.astype(bf16))
    grad_gate = scattered_sum(
        rows_of(matmul(normalized, d_gate_low, TN).astype(bf16), model // batch), "batch"
    )
    d_select, grad_gate = together((d_select, grad_gate))
    grad_x_proj = matmul(d_select, active, TN)
    d_active = d_active + d_mixed * skip_gain + matmul(d_select, select_weight)
    conv_sig = jax.nn.sigmoid(conv_out)
    d_conv = (d_active * conv_sig * (1.0 + conv_out * (1.0 - conv_sig))).astype(bf16)
    d_conv_f = d_conv.astype(f32)
    grad_conv_bias = jnp.sum(d_conv_f, axis=0, keepdims=True)
    grad_conv = jnp.stack(
        [
            jnp.sum(d_conv_f * padded[tap : tap + length].astype(f32), axis=0)
            for tap in range(taps)
        ]
    )
    extended = jnp.pad(d_conv, ((0, taps - 1), (0, 0)))
    d_inner = jnp.zeros((length, width), f32)
    for tap in range(taps):
        offset = taps - 1 - tap
        d_inner = d_inner + conv_taps[tap] * extended[offset : offset + length].astype(f32)
    d_inner = d_inner.astype(bf16)
    grad_inner = matmul(normalized, d_inner, TN).astype(bf16)
    d_inner, grad_inner, branch = together((d_inner, grad_inner, branch))
    d_normalized = matmul(
        jnp.concatenate([d_inner, d_gate_low], axis=1),
        jnp.concatenate([input_weight, gate_weight], axis=1),
        NT,
    ).astype(bf16)
    grad_inner = scattered_sum(rows_of(grad_inner, model // batch), "batch")
    grad_gate = grad_gate.astype(bf16).reshape(seq, in_rows, width)
    grad_gate = lax.all_to_all(grad_gate, "seq", 0, 0)
    d_normalized, gated, grad_gate = together((d_normalized, gated, grad_gate))
    grad_output = lax.psum_scatter(
        matmul(gated, upstream, TN).astype(bf16), "batch", scatter_dimension=0, tiled=True
    ).astype(f32)
    d_normalized, *last_terms = line_summed(rows_of(d_normalized, span), "seq")

    block_out = jnp.where(own_valid, own_stream + branch.astype(f32), 0.0)

    def columns_of(part):
        part = part.reshape(seq, in_rows, batch, own).transpose(1, 2, 0, 3)
        return part.reshape(in_rows, batch * seq * own).astype(f32)

    grad_inner = grad_inner.astype(bf16).reshape(seq, in_rows, width)
    grad_inner = lax.all_to_all(grad_inner, "seq", 0, 0)
    grad_input = jnp.concatenate([columns_of(grad_inner), columns_of(grad_gate)], axis=1)

    small_grads = jnp.concatenate(
        [grad_dt_proj, grad_x_proj, grad_log, grad_conv, grad_conv_bias, grad_dt_bias, grad_skip],
        axis=0,
    )
    small_grads = lax.psum_scatter(small_grads, "batch", scatter_dimension=1, tiled=True)
    g_dt_proj, g_x_proj, g_log, g_conv, g_conv_bias, g_dt_bias, g_skip = jnp.split(
        small_grads, cuts[:-1], axis=0
    )

    own_upstream = jnp.where(own_valid, cotangent[0].astype(f32), 0.0)
    own_scale = lax.rsqrt(jnp.mean(own_stream * own_stream, axis=-1, keepdims=True) + epsilon)
    grad_gain = jnp.sum(grad_input * in_proj.astype(f32), axis=1) / norm_gain.astype(f32)
    (
        d_normalized, g_dt_proj, g_x_proj, g_log, g_conv, g_conv_bias, g_dt_bias, g_skip,
        grad_input, grad_gain, grad_output,
    ) = together(
        (
            d_normalized, g_dt_proj, g_x_proj, g_log, g_conv, g_conv_bias, g_dt_bias, g_skip,
            grad_input, grad_gain, grad_output,
        )
    )
    for term in last_terms:
        d_normalized = d_normalized + term.astype(f32)
    d_hat = d_normalized * gain
    grad_tokens = (
        own_scale * d_hat
        - own_stream
        * own_scale
        * own_scale
        * own_scale
        * jnp.mean(d_hat * own_stream, axis=-1, keepdims=True)
        + own_upstream
    )
    return (
        block_out[None],
        grad_tokens[None],
        grad_gain,
        grad_input,
        g_conv,
        g_conv_bias[0],
        g_x_proj.T,
        g_dt_proj,
        g_dt_bias[0],
        g_log.T,
        g_skip[0],
        grad_output,
    )


def solution(mesh):
    placed = (
        P("batch", "seq", None),
        P("batch"),
        P(("batch", "seq")),
        P(("batch", "seq"), None),
        P(None, ("batch", "seq")),
        P(("batch", "seq")),
        P(("batch", "seq"), None),
        P(None, ("batch", "seq")),
        P(("batch", "seq")),
        P(("batch", "seq"), None),
        P(("batch", "seq")),
        P(("batch", "seq"), None),
        P("batch", "seq", None),
    )
    return jax.shard_map(
        on_device,
        mesh=mesh,
        in_specs=placed,
        out_specs=(
            P("batch", "seq", None),
            P("batch", "seq", None),
            P(("batch", "seq")),
            P(("batch", "seq"), None),
            P(None, ("batch", "seq")),
            P(("batch", "seq")),
            P(("batch", "seq"), None),
            P(None, ("batch", "seq")),
            P(("batch", "seq")),
            P(("batch", "seq"), None),
            P(("batch", "seq")),
            P(("batch", "seq"), None),
        ),
        check_vma=False,
    )
```

```python
import functools

import jax
import jax.numpy as jnp
from jax import lax
from jax.experimental import pallas as pl
from jax.experimental.pallas import tpu as pltpu
from jax.sharding import PartitionSpec as P

bf16, f32 = jnp.bfloat16, jnp.float32
NT = (((1,), (1,)), ((), ()))
LANES = 128
GROUP = 32
BLOCK = 128
epsilon = 1e-05
LOG2E = 1.4426950408889634


def spread(tile, row, lanes, states):
    return jnp.broadcast_to(tile[row : row + 1, lanes], (states, LANES))


def selectors(select, states):
    low = select.shape[1] - 4 * states
    middle = low + 2 * states
    block = select[:, low:middle].astype(f32) + select[:, middle:].astype(f32)
    return jnp.transpose(block), block[:, :states], block[:, states:]


def block_diagonal(values, step):
    rows, states = values.shape
    wide = step * states
    spread_out = (
        lax.broadcasted_iota(jnp.int32, (states, wide), 1) % states
        == lax.broadcasted_iota(jnp.int32, (states, wide), 0)
    ).astype(bf16)
    value = jnp.dot(values.astype(bf16), spread_out, preferred_element_type=f32)
    place = lax.broadcasted_iota(jnp.int32, (rows, wide), 0) % step
    owner = lax.broadcasted_iota(jnp.int32, (rows, wide), 1) // states
    return jnp.where(place == owner, value, 0.0).astype(bf16)


def forward_body(tiles, step, delta, active, select, rate, mixed, kept, state, drive, columns):
    rows, states = delta.shape[0], rate.shape[0]
    wide = step * states

    @pl.when(pl.program_id(0) == 0)
    def _():
        state[...] = jnp.zeros_like(state)

    turned, _, c_block = selectors(select[...], states)
    columns[...] = turned[:states]
    drive[...] = delta[...] * active[...].astype(f32)
    rates = [rate[:, k * LANES : (k + 1) * LANES] for k in range(tiles)]

    def group(number, held):
        held = list(held)
        base = pl.multiple_of(number * GROUP, GROUP)
        delta_now, drive_now = delta.at[pl.ds(base, GROUP), :], drive.at[pl.ds(base, GROUP), :]
        b_now = pltpu.roll(columns[...], rows - base, 1)
        for j in range(GROUP):
            b_wide = jnp.broadcast_to(b_now[:, j : j + 1], (states, LANES))
            for k in range(tiles):
                lanes = slice(k * LANES, (k + 1) * LANES)
                decay = jnp.exp2(spread(delta_now, j, lanes, states) * rates[k])
                held[k] = decay * held[k] + spread(drive_now, j, lanes, states) * b_wide
                at = pl.ds(pl.multiple_of((base + j) * states, states), states)
                kept[at, lanes] = held[k].astype(bf16)
        return tuple(held)

    held = lax.fori_loop(
        0,
        rows // GROUP,
        group,
        tuple(state[:, k * LANES : (k + 1) * LANES] for k in range(tiles)),
    )
    for k in range(tiles):
        state[:, k * LANES : (k + 1) * LANES] = held[k]
    c_diag = block_diagonal(c_block, step)
    for q in range(rows // step):
        part = kept[q * wide : (q + 1) * wide, :]
        spot = slice(q * step, (q + 1) * step)
        mixed[spot, :] = jnp.dot(c_diag[spot, :], part, preferred_element_type=f32)


def scan_forward(delta, active, select, rate, block, step):
    length, width = delta.shape
    states = rate.shape[0]
    tiles = width // LANES
    return pl.pallas_call(
        functools.partial(forward_body, tiles, step),
        grid=(length // block,),
        in_specs=[
            pl.BlockSpec((block, width), lambda i: (i, 0)),
            pl.BlockSpec((block, width), lambda i: (i, 0)),
            pl.BlockSpec((block, select.shape[1]), lambda i: (i, 0)),
            pl.BlockSpec((states, width), lambda i: (0, 0)),
        ],
        out_specs=[
            pl.BlockSpec((block, width), lambda i: (i, 0)),
            pl.BlockSpec((block * states, width), lambda i: (i, 0)),
        ],
        out_shape=[
            jax.ShapeDtypeStruct((length, width), f32),
            jax.ShapeDtypeStruct((length * states, width), bf16),
        ],
        scratch_shapes=[
            pltpu.VMEM((states, width), f32),
            pltpu.VMEM((block, width), f32),
            pltpu.VMEM((states, block), f32),
        ],
        compiler_params=pltpu.CompilerParams(vmem_limit_bytes=48 << 20),
        cost_estimate=pl.CostEstimate(
            flops=8 * length * width * states,
            transcendentals=length * width * states,
            bytes_accessed=length * width * (2 * states + 10),
        ),
        name="scan_forward",
    )(delta, active, select, rate)


FEW = 4


def backward_body(
    tiles, step, delta, active, d_mixed, select, rate, decay_rate, kept, kept_before,
    d_delta, d_active, d_bc, d_log, push, drive, columns, diagonals, folding, timed, *pairs,
):
    grads, rated = pairs[:2], pairs[2:]
    rows, states = delta.shape[0], rate.shape[0]
    blocks = pl.num_programs(0)
    first = pl.program_id(0) == blocks - 1
    wide = step * states

    @pl.when(pl.program_id(0) == 0)
    def _():
        push[...] = jnp.zeros_like(push)
        d_log[...] = jnp.zeros_like(d_log)

    turned, b_block, _ = selectors(select[...], states)
    columns[...] = turned[states:]
    drive[...] = delta[...] * active[...].astype(f32)
    rates = [rate[:, k * LANES : (k + 1) * LANES] for k in range(tiles)]
    own_rates = [decay_rate[:, k * LANES : (k + 1) * LANES].astype(bf16) for k in range(tiles)]

    place = lax.broadcasted_iota(jnp.int32, (step, wide), 0)
    owner = lax.broadcasted_iota(jnp.int32, (step, wide), 1) // states
    ones_diag = (place == owner).astype(bf16)
    diag = (place == owner).astype(f32)
    diagonals[...] = block_diagonal(b_block, step)

    def sums_of(number):
        held, through_of = number % 2, {}

        def spots(q):
            at = number * GROUP + q * step
            tall = slice(q * wide, (q + 1) * wide)
            return slice(at, at + step), tall

        def through(q):
            spot, tall = spots(q)
            value = jnp.dot(diagonals[spot, :], grads[held][tall, :], preferred_element_type=f32)
            d_active[spot, :] = delta[spot, :] * value
            through_of[q] = active[spot, :].astype(f32) * value

        def summed(q):
            spot, tall = spots(q)
            value = jnp.dot(ones_diag, rated[held][tall, :], preferred_element_type=f32)
            d_delta[spot, :] = value + through_of[q]

        def d_b(q):
            spot, tall = spots(q)
            folding[spot, :wide] = diag * lax.dot_general(
                drive[spot, :].astype(bf16), grads[held][tall, :], NT, preferred_element_type=f32
            )

        def d_c(q):
            spot, _ = spots(q)
            own = slice(spot.start * states, spot.stop * states)
            folding[spot, wide:] = diag * lax.dot_general(
                d_mixed[spot, :].astype(bf16), kept[own, :], NT, preferred_element_type=f32
            )

        return [
            functools.partial(part, q)
            for q in range(GROUP // step)
            for part in (through, summed, d_b, d_c)
        ]

    carry = [push[:, k * LANES : (k + 1) * LANES] for k in range(tiles)]
    waiting = []
    for number in reversed(range(rows // GROUP)):
        pace = GROUP // max(len(waiting), 1)
        sums = [None] * tiles
        held = number % 2
        for j in reversed(range(GROUP)):
            row = number * GROUP + j
            c_wide = jnp.broadcast_to(columns[:, row : row + 1], (states, LANES))
            at = slice(j * states, (j + 1) * states)
            for k in range(tiles):
                lanes = slice(k * LANES, (k + 1) * LANES)
                if row:
                    before = kept[(row - 1) * states : row * states, lanes]
                else:
                    before = jnp.where(first, jnp.zeros((), bf16), kept_before[:, lanes])
                step_size = spread(delta, row, lanes, states)
                grad = spread(d_mixed, row, lanes, states) * c_wide + carry[k]
                carry[k] = jnp.exp2(step_size * rates[k]) * grad
                grads[held][at, lanes] = grad.astype(bf16)
                rated_now = carry[k].astype(bf16) * before * own_rates[k]
                rated[held][at, lanes] = rated_now
                timed_now = rated_now * step_size.astype(bf16)
                sums[k] = timed_now if sums[k] is None else sums[k] + timed_now
                if j % FEW == 0:
                    spot = row // FEW * states
                    timed[spot : spot + states, lanes] = sums[k]
                    sums[k] = None
            if waiting and j % pace == 0:
                waiting.pop(0)()
        while waiting:
            waiting.pop(0)()
        waiting = sums_of(number)
    while waiting:
        waiting.pop(0)()
    for k in range(tiles):
        push[:, k * LANES : (k + 1) * LANES] = carry[k]
    fold = (
        lax.broadcasted_iota(jnp.int32, (wide, states), 0) % states
        == lax.broadcasted_iota(jnp.int32, (wide, states), 1)
    ).astype(bf16)
    for number in range(2):
        value = folding[:, number * wide : (number + 1) * wide]
        high = value.astype(bf16)
        d_bc[:, number * states : (number + 1) * states] = jnp.dot(
            high, fold, preferred_element_type=f32
        )
    span = rows // FEW * states
    pick = (
        lax.broadcasted_iota(jnp.int32, (states, span), 1) % states
        == lax.broadcasted_iota(jnp.int32, (states, span), 0)
    ).astype(bf16)
    d_log[...] += jnp.dot(pick, timed[...], preferred_element_type=f32)


def scan_backward(delta, active, d_mixed, select, rate, decay_rate, kept, block, step):
    length, width = delta.shape
    states = rate.shape[0]
    tiles = width // LANES
    blocks = length // block
    back = lambda i: (blocks - 1 - i, 0)
    return pl.pallas_call(
        functools.partial(backward_body, tiles, step),
        grid=(blocks,),
        in_specs=[
            pl.BlockSpec((block, width), back),
            pl.BlockSpec((block, width), back),
            pl.BlockSpec((block, width), back),
            pl.BlockSpec((block, select.shape[1]), back),
            pl.BlockSpec((states, width), lambda i: (0, 0)),
            pl.BlockSpec((states, width), lambda i: (0, 0)),
            pl.BlockSpec((block * states, width), back),
            pl.BlockSpec(
                (states, width), lambda i: (jnp.maximum((blocks - 1 - i) * block - 1, 0), 0)
            ),
        ],
        out_specs=[
            pl.BlockSpec((block, width), back),
            pl.BlockSpec((block, width), back),
            pl.BlockSpec((block, 2 * states), back),
            pl.BlockSpec((states, width), lambda i: (0, 0)),
        ],
        out_shape=[
            jax.ShapeDtypeStruct((length, width), f32),
            jax.ShapeDtypeStruct((length, width), f32),
            jax.ShapeDtypeStruct((length, 2 * states), f32),
            jax.ShapeDtypeStruct((states, width), f32),
        ],
        scratch_shapes=[
            pltpu.VMEM((states, width), f32),
            pltpu.VMEM((block, width), f32),
            pltpu.VMEM((states, block), f32),
            pltpu.VMEM((block, step * states), bf16),
            pltpu.VMEM((block, 2 * step * states), f32),
            pltpu.VMEM((block // FEW * states, width), bf16),
        ]
        + [pltpu.VMEM((GROUP * states, width), bf16)] * 4,
        compiler_params=pltpu.CompilerParams(vmem_limit_bytes=48 << 20),
        cost_estimate=pl.CostEstimate(
            flops=20 * length * width * states,
            transcendentals=length * width * states,
            bytes_accessed=length * width * (2 * states + 20),
        ),
        name="scan_backward",
    )(delta, active, d_mixed, select, rate, decay_rate, kept, kept)


together = lax.optimization_barrier


def inner_swap(value, axis):
    count = lax.axis_size(axis)
    return lax.ppermute(value, axis, [(i, i ^ 1) for i in range(count)])


def outer_shift(value, axis, steps):
    count = lax.axis_size(axis)
    half = count // 2
    pairs = [(i, (i // 2 + steps) % half * 2 + i % 2) for i in range(count)]
    return lax.ppermute(value, axis, pairs)


def shift_order(half):
    return sorted(range(1, half), key=lambda k: (-min(k, half - k), k))


def pieces_of_all(own, axis):
    count = lax.axis_size(axis)
    place = lax.axis_index(axis)
    half = count // 2
    outer, inner = place // 2, place % 2
    yield place, own
    arrived = {k: outer_shift(own, axis, k) for k in shift_order(half)}
    yield outer * 2 + 1 - inner, inner_swap(own, axis)
    for k, piece in arrived.items():
        origin = (outer - k + half) % half
        yield origin * 2 + inner, piece
    for k, piece in arrived.items():
        origin = (outer - k + half) % half
        yield origin * 2 + 1 - inner, inner_swap(piece, axis)


def gathered(own, axis, dim=0):
    count, size = lax.axis_size(axis), own.shape[dim]
    whole = jnp.zeros(own.shape[:dim] + (count * size,) + own.shape[dim + 1 :], own.dtype)
    for place, piece in pieces_of_all(own, axis):
        whole = lax.dynamic_update_slice_in_dim(whole, piece, place * size, dim)
    return whole


def hop(value, axis, moves):
    pairs = [(a * 2 + i, b * 2 + i) for a, b in moves for i in (0, 1)]
    return lax.ppermute(value, axis, pairs)


def swap_at(value, axis, spots):
    pairs = [(a * 2 + i, a * 2 + 1 - i) for a in spots for i in (0, 1)]
    return lax.ppermute(value, axis, pairs)


UP, DOWN = [(0, 1), (1, 2), (2, 3)], [(1, 0), (2, 1), (3, 2)]


def line_gathered(own, axis, held):
    if lax.axis_size(axis) != 8:
        return own, lambda own: lax.all_gather(own, axis, axis=0, tiled=True), held
    place = lax.axis_index(axis)
    z, x = place // 2, place % 2
    rows = own.shape[0]
    upper, edge = z >= 2, (z == 0) | (z == 3)
    across = jnp.where(upper, z - 2, z + 2)
    far = jnp.where(z == 3, 0, 3)

    def put(whole, piece, spot, side):
        return lax.dynamic_update_slice_in_dim(whole, piece, (spot * 2 + side) * rows, 0)

    def put_far(whole, piece, side):
        held = lax.dynamic_slice_in_dim(whole, (far * 2 + side) * rows, rows, 0)
        return put(whole, jnp.where(edge, piece, held), far, side)

    whole = jnp.zeros((8 * rows,) + own.shape[1:], own.dtype)
    up, down, other, held = together(
        (hop(own, axis, UP), hop(own, axis, DOWN), swap_at(own, axis, range(4)), held)
    )
    up_two, down_two = hop(up, axis, UP[1:]), hop(down, axis, DOWN[:2])
    other_up, other_down = swap_at(up, axis, (1, 2, 3)), swap_at(down, axis, (0, 1, 2))
    whole = put(put(whole, own, z, x), other, z, 1 - x)
    whole = put(put(whole, up, (z + 3) % 4, x), down, (z + 1) % 4, x)
    two = jnp.where(upper, up_two, down_two)
    three = hop(two, axis, [(2, 3), (1, 0)])
    other_two = swap_at(two, axis, range(4))
    whole = put(put(whole, other_up, (z + 3) % 4, 1 - x), other_down, (z + 1) % 4, 1 - x)
    whole = put(put(whole, two, across, x), other_two, across, 1 - x)

    def end(three):
        other_three = swap_at(three, axis, (0, 3))
        return put_far(put_far(whole, three, x), other_three, 1 - x)

    return three, end, held


def line_summed(part_of, axis):
    if lax.axis_size(axis) != 8:
        return (scattered_sum(part_of, axis),)
    place = lax.axis_index(axis)
    z, x = place // 2, place % 2
    upper, edge = z >= 2, (z == 0) | (z == 3)
    across = jnp.where(upper, z - 2, z + 2)
    far = jnp.where(z == 0, 3, 0)
    above, below = jnp.minimum(z + 1, 3), jnp.maximum(z - 1, 0)

    def swapped(spot, spots):
        return swap_at(part_of(spot * 2 + 1 - x), axis, spots)

    def added(spot, given):
        return part_of(spot * 2 + x).astype(f32) + given.astype(f32)

    given_far = swapped(far, (0, 3))
    given_across = swapped(across, range(4))
    given_above, given_below = swapped(above, (0, 1, 2)), swapped(below, (1, 2, 3))
    given_own = swapped(z, range(4))
    three = hop(added(far, given_far).astype(bf16), axis, [(0, 1), (3, 2)])
    three, given_across = together((three, given_across))
    two = added(across, given_across) + jnp.where(edge, 0.0, three.astype(f32))
    two = two.astype(bf16)
    two_up, two_down, given_above, given_below = together(
        (hop(two, axis, UP[:2]), hop(two, axis, DOWN[1:]), given_above, given_below)
    )
    one_up = (added(above, given_above) + two_up.astype(f32)).astype(bf16)
    one_down = (added(below, given_below) + two_down.astype(f32)).astype(bf16)
    return added(z, given_own), hop(one_up, axis, UP), hop(one_down, axis, DOWN)


def scattered_sum(part_of, axis):
    count = lax.axis_size(axis)
    place = lax.axis_index(axis)
    half = count // 2
    outer, inner = place // 2, place % 2
    total = None
    for k in shift_order(half) + [0]:
        target = (outer + k) % half
        given = inner_swap(part_of(target * 2 + 1 - inner), axis)
        piece = part_of(target * 2 + inner).astype(f32) + given.astype(f32)
        if k:
            piece = outer_shift(piece.astype(bf16), axis, k).astype(f32)
        total = piece if total is None else total + piece
    return total


def rows_of(value, rows):
    return lambda place: lax.dynamic_slice_in_dim(value, place * rows, rows, 0)


def summed_over_seq(part, change):
    count = lax.axis_size("seq")
    length, columns = part.shape
    part = part.astype(bf16).reshape(count, length // count, columns)
    own = change(jnp.sum(lax.all_to_all(part, "seq", 0, 0).astype(f32), axis=0))
    return shared(own, "seq").reshape(length, own.shape[1])


def two_terms(value):
    high = value.astype(bf16)
    return [high, (value - high.astype(f32)).astype(bf16)]


def shared(own, axis):
    wide = jnp.broadcast_to(own[None], (lax.axis_size(axis),) + own.shape)
    return lax.all_to_all(wide, axis, 0, 0)


def matmul(a, b, dims=(((1,), (0,)), ((), ()))):
    return lax.dot_general(a, b, dims, preferred_element_type=f32)


TN = (((0,), (0,)), ((), ()))


def on_device(
    tokens,
    lengths,
    norm_gain,
    in_proj,
    conv_weight,
    conv_bias,
    x_proj,
    dt_proj,
    dt_bias,
    a_log,
    skip,
    out_proj,
    cotangent,
):
    batch, seq = lax.axis_size("batch"), lax.axis_size("seq")
    place = lax.axis_index("seq")
    span, model = tokens.shape[1:]
    length = span * seq
    in_rows = in_proj.shape[0]
    own = skip.shape[0]
    taps = conv_weight.shape[0]
    rank = dt_proj.shape[0]
    states = a_log.shape[1]
    width = own * batch

    halves = in_proj.reshape(in_rows, 2, batch, seq, own).transpose(1, 3, 0, 2, 4)
    halves = halves.reshape(2, seq, in_rows, width)
    columns = lax.all_to_all(halves[0], "seq", 0, 0)
    columns, gate_columns = together((columns, halves[1]))
    gate_columns = lax.all_to_all(gate_columns, "seq", 0, 0)
    last_hop, end_gather, (dt_proj, x_proj, out_proj) = line_gathered(
        cotangent[0], "seq", (dt_proj, x_proj, out_proj)
    )
    small = jnp.concatenate(
        [
            dt_proj,
            x_proj.T,
            a_log.T,
            conv_weight,
            conv_bias[None],
            dt_bias[None],
            skip[None],
            jnp.pad(norm_gain, (0, own - in_rows))[None],
        ],
        axis=0,
    )
    small = gathered(small, "batch", 1)
    cuts = [rank, 2 * rank + 2 * states, 2 * rank + 3 * states]
    cuts = cuts + [cuts[2] + taps + i for i in range(4)]
    delta_weight, select_weight, decay_logs, conv_taps, conv_shift, delta_shift, skip_gain, gain = (
        jnp.split(small, cuts, axis=0)
    )
    conv_taps, conv_shift = conv_taps.astype(f32), conv_shift.astype(f32)
    delta_shift, skip_gain = delta_shift.astype(f32), skip_gain.astype(f32)
    decay = -jnp.exp(decay_logs.astype(f32))
    gain = gain.reshape(batch, own)[:, :in_rows]
    gate_columns, gain = together((gate_columns, gain))
    gain = shared(gain, "seq").transpose(1, 0, 2).reshape(model).astype(f32)

    input_weight = gathered(columns.reshape(seq * in_rows, width), "batch")

    def normed(rows):
        rows = rows.astype(f32)
        scale = lax.rsqrt(jnp.mean(rows * rows, axis=-1, keepdims=True) + epsilon)
        return (rows * scale * gain).astype(bf16)

    stream = lax.all_gather(tokens[0], "seq", axis=0, tiled=True)
    normalized = normed(stream)
    output_weight = gathered(out_proj, "batch")

    valid = (jnp.arange(length, dtype=jnp.int32) < lengths[0])[:, None]
    inner = matmul(normalized, input_weight).astype(bf16)
    padded = jnp.pad(inner, ((taps - 1, 0), (0, 0)))
    conv_out = conv_shift + jnp.zeros((length, width), f32)
    for tap in range(taps):
        conv_out = conv_out + conv_taps[tap] * padded[tap : tap + length].astype(f32)
    active = jax.nn.silu(conv_out).astype(bf16)
    active_f = active.astype(f32)

    partial, last_hop, gate_columns = together(
        (matmul(active, select_weight, NT), last_hop, gate_columns)
    )
    upstream = end_gather(last_hop)
    gate_weight = gathered(gate_columns.reshape(seq * in_rows, width), "batch")
    select = summed_over_seq(
        partial,
        lambda s: jnp.concatenate([s[:, :rank].astype(bf16)] + two_terms(s[:, rank:]), axis=1),
    )
    upstream = jnp.where(valid, upstream, 0).astype(bf16)
    gate_low = matmul(normalized, gate_weight).astype(bf16)
    d_gated = matmul(upstream, output_weight, NT)
    select, gate_low, d_gated = together((select, gate_low, d_gated))
    gate = gate_low.astype(f32)
    gate_sig = jax.nn.sigmoid(gate)
    delta_low = select[:, :rank]
    delta_raw = matmul(delta_low, delta_weight) + delta_shift
    delta = jax.nn.softplus(delta_raw)

    block = min(BLOCK, length)
    step = 256 // states
    rate = decay * LOG2E
    mixed, kept = scan_forward(delta, active, select, rate, block, step)
    mixed = mixed + skip_gain * active_f
    gated = (mixed * gate * gate_sig).astype(bf16)
    branch = matmul(gated, output_weight).astype(bf16)
    d_gated, branch = together((d_gated, branch))
    branch = lax.psum_scatter(branch, "seq", scatter_dimension=0, tiled=True)
    own_valid = lax.dynamic_slice_in_dim(valid, place * span, span, 0)
    own_stream = tokens[0].astype(f32)

    d_mixed = d_gated * gate * gate_sig
    d_gate = d_gated * mixed * gate_sig * (1.0 + gate * (1.0 - gate_sig))
    grad_skip = jnp.sum(d_mixed * active_f, axis=0, keepdims=True)
    d_gate_low = d_gate.astype(bf16)

    d_delta, d_active, d_bc, grad_log = scan_backward(
        delta, active, d_mixed, select, rate, decay, kept, block, step
    )
    d_raw = d_delta * jax.nn.sigmoid(delta_raw)
    grad_dt_bias = jnp.sum(d_raw, axis=0, keepdims=True)
    d_raw_low = d_raw.astype(bf16)
    grad_dt_proj = matmul(delta_low, d_raw_low, TN)
    partial = jnp.concatenate([matmul(d_raw_low, delta_weight, NT), d_bc], axis=1)
    d_select = summed_over_seq(partial, lambda s: s.astype(bf16))
    grad_gate = scattered_sum(
        rows_of(matmul(normalized, d_gate_low, TN).astype(bf16), model // batch), "batch"
    )
    d_select, grad_gate = together((d_select, grad_gate))
    grad_x_proj = matmul(d_select, active, TN)
    d_active = d_active + d_mixed * skip_gain + matmul(d_select, select_weight)
    conv_sig = jax.nn.sigmoid(conv_out)
    d_conv = (d_active * conv_sig * (1.0 + conv_out * (1.0 - conv_sig))).astype(bf16)
    d_conv_f = d_conv.astype(f32)
    grad_conv_bias = jnp.sum(d_conv_f, axis=0, keepdims=True)
    grad_conv = jnp.stack(
        [
            jnp.sum(d_conv_f * padded[tap : tap + length].astype(f32), axis=0)
            for tap in range(taps)
        ]
    )
    extended = jnp.pad(d_conv, ((0, taps - 1), (0, 0)))
    d_inner = jnp.zeros((length, width), f32)
    for tap in range(taps):
        offset = taps - 1 - tap
        d_inner = d_inner + conv_taps[tap] * extended[offset : offset + length].astype(f32)
    d_inner = d_inner.astype(bf16)
    d_normalized = matmul(
        jnp.concatenate([d_inner, d_gate_low], axis=1),
        jnp.concatenate([input_weight, gate_weight], axis=1),
        NT,
    ).astype(bf16)
    grad_gate = grad_gate.astype(bf16).reshape(seq, in_rows, width)
    grad_gate = lax.all_to_all(grad_gate, "seq", 0, 0)
    d_normalized, d_inner, gated, grad_gate, grad_x_proj, branch = together(
        (d_normalized, d_inner, gated, grad_gate, grad_x_proj, branch)
    )
    grad_inner = matmul(normalized, d_inner, TN).astype(bf16)
    grad_inner = scattered_sum(rows_of(grad_inner, model // batch), "batch")
    grad_output = lax.psum_scatter(
        matmul(gated, upstream, TN).astype(bf16), "batch", scatter_dimension=0, tiled=True
    ).astype(f32)
    d_normalized, *last_terms = line_summed(rows_of(d_normalized, span), "seq")

    block_out = jnp.where(own_valid, own_stream + branch.astype(f32), 0.0)

    def columns_of(part):
        part = part.reshape(seq, in_rows, batch, own).transpose(1, 2, 0, 3)
        return part.reshape(in_rows, batch * seq * own).astype(f32)

    grad_inner = grad_inner.astype(bf16).reshape(seq, in_rows, width)
    grad_inner = lax.all_to_all(grad_inner, "seq", 0, 0)
    grad_input = jnp.concatenate([columns_of(grad_inner), columns_of(grad_gate)], axis=1)

    small_grads = jnp.concatenate(
        [grad_dt_proj, grad_x_proj, grad_log, grad_conv, grad_conv_bias, grad_dt_bias, grad_skip],
        axis=0,
    )
    small_grads = lax.psum_scatter(small_grads, "batch", scatter_dimension=1, tiled=True)
    g_dt_proj, g_x_proj, g_log, g_conv, g_conv_bias, g_dt_bias, g_skip = jnp.split(
        small_grads, cuts[:-1], axis=0
    )

    own_upstream = jnp.where(own_valid, cotangent[0].astype(f32), 0.0)
    own_scale = lax.rsqrt(jnp.mean(own_stream * own_stream, axis=-1, keepdims=True) + epsilon)
    grad_gain = jnp.sum(grad_input * in_proj.astype(f32), axis=1) / norm_gain.astype(f32)
    (
        d_normalized, g_dt_proj, g_x_proj, g_log, g_conv, g_conv_bias, g_dt_bias, g_skip,
        grad_input, grad_gain, grad_output,
    ) = together(
        (
            d_normalized, g_dt_proj, g_x_proj, g_log, g_conv, g_conv_bias, g_dt_bias, g_skip,
            grad_input, grad_gain, grad_output,
        )
    )
    for term in last_terms:
        d_normalized = d_normalized + term.astype(f32)
    d_hat = d_normalized * gain
    grad_tokens = (
        own_scale * d_hat
        - own_stream
        * own_scale
        * own_scale
        * own_scale
        * jnp.mean(d_hat * own_stream, axis=-1, keepdims=True)
        + own_upstream
    )
    return (
        block_out[None],
        grad_tokens[None],
        grad_gain,
        grad_input,
        g_conv,
        g_conv_bias[0],
        g_x_proj.T,
        g_dt_proj,
        g_dt_bias[0],
        g_log.T,
        g_skip[0],
        grad_output,
    )


def solution(mesh):
    placed = (
        P("batch", "seq", None),
        P("batch"),
        P(("batch", "seq")),
        P(("batch", "seq"), None),
        P(None, ("batch", "seq")),
        P(("batch", "seq")),
        P(("batch", "seq"), None),
        P(None, ("batch", "seq")),
        P(("batch", "seq")),
        P(("batch", "seq"), None),
        P(("batch", "seq")),
        P(("batch", "seq"), None),
        P("batch", "seq", None),
    )
    return jax.shard_map(
        on_device,
        mesh=mesh,
        in_specs=placed,
        out_specs=(
            P("batch", "seq", None),
            P("batch", "seq", None),
            P(("batch", "seq")),
            P(("batch", "seq"), None),
            P(None, ("batch", "seq")),
            P(("batch", "seq")),
            P(("batch", "seq"), None),
            P(None, ("batch", "seq")),
            P(("batch", "seq")),
            P(("batch", "seq"), None),
            P(("batch", "seq")),
            P(("batch", "seq"), None),
        ),
        check_vma=False,
    )
```

```python
import functools

import jax
import jax.numpy as jnp
from jax import lax
from jax.experimental import pallas as pl
from jax.experimental.pallas import tpu as pltpu
from jax.sharding import PartitionSpec as P

bf16, f32 = jnp.bfloat16, jnp.float32
NT = (((1,), (1,)), ((), ()))
LANES = 128
GROUP = 32
BLOCK = 128
epsilon = 1e-05
LOG2E = 1.4426950408889634


def spread(tile, row, lanes, states):
    return jnp.broadcast_to(tile[row : row + 1, lanes], (states, LANES))


def selectors(select, states):
    low = select.shape[1] - 4 * states
    middle = low + 2 * states
    block = select[:, low:middle].astype(f32) + select[:, middle:].astype(f32)
    return jnp.transpose(block), block[:, :states], block[:, states:]


def block_diagonal(values, step):
    rows, states = values.shape
    wide = step * states
    spread_out = (
        lax.broadcasted_iota(jnp.int32, (states, wide), 1) % states
        == lax.broadcasted_iota(jnp.int32, (states, wide), 0)
    ).astype(bf16)
    value = jnp.dot(values.astype(bf16), spread_out, preferred_element_type=f32)
    place = lax.broadcasted_iota(jnp.int32, (rows, wide), 0) % step
    owner = lax.broadcasted_iota(jnp.int32, (rows, wide), 1) // states
    return jnp.where(place == owner, value, 0.0).astype(bf16)


def forward_body(tiles, step, delta, active, select, rate, mixed, kept, state, drive, columns):
    rows, states = delta.shape[0], rate.shape[0]
    wide = step * states

    @pl.when(pl.program_id(0) == 0)
    def _():
        state[...] = jnp.zeros_like(state)

    turned, _, c_block = selectors(select[...], states)
    columns[...] = turned[:states]
    drive[...] = delta[...] * active[...].astype(f32)
    rates = [rate[:, k * LANES : (k + 1) * LANES] for k in range(tiles)]

    def group(number, held):
        held = list(held)
        base = pl.multiple_of(number * GROUP, GROUP)
        delta_now, drive_now = delta.at[pl.ds(base, GROUP), :], drive.at[pl.ds(base, GROUP), :]
        b_now = pltpu.roll(columns[...], rows - base, 1)
        for j in range(GROUP):
            b_wide = jnp.broadcast_to(b_now[:, j : j + 1], (states, LANES))
            for k in range(tiles):
                lanes = slice(k * LANES, (k + 1) * LANES)
                decay = jnp.exp2(spread(delta_now, j, lanes, states) * rates[k])
                held[k] = decay * held[k] + spread(drive_now, j, lanes, states) * b_wide
                at = pl.ds(pl.multiple_of((base + j) * states, states), states)
                kept[at, lanes] = held[k].astype(bf16)
        return tuple(held)

    held = lax.fori_loop(
        0,
        rows // GROUP,
        group,
        tuple(state[:, k * LANES : (k + 1) * LANES] for k in range(tiles)),
    )
    for k in range(tiles):
        state[:, k * LANES : (k + 1) * LANES] = held[k]
    c_diag = block_diagonal(c_block, step)
    for q in range(rows // step):
        part = kept[q * wide : (q + 1) * wide, :]
        spot = slice(q * step, (q + 1) * step)
        mixed[spot, :] = jnp.dot(c_diag[spot, :], part, preferred_element_type=f32)


def scan_forward(delta, active, select, rate, block, step):
    length, width = delta.shape
    states = rate.shape[0]
    tiles = width // LANES
    return pl.pallas_call(
        functools.partial(forward_body, tiles, step),
        grid=(length // block,),
        in_specs=[
            pl.BlockSpec((block, width), lambda i: (i, 0)),
            pl.BlockSpec((block, width), lambda i: (i, 0)),
            pl.BlockSpec((block, select.shape[1]), lambda i: (i, 0)),
            pl.BlockSpec((states, width), lambda i: (0, 0)),
        ],
        out_specs=[
            pl.BlockSpec((block, width), lambda i: (i, 0)),
            pl.BlockSpec((block * states, width), lambda i: (i, 0)),
        ],
        out_shape=[
            jax.ShapeDtypeStruct((length, width), f32),
            jax.ShapeDtypeStruct((length * states, width), bf16),
        ],
        scratch_shapes=[
            pltpu.VMEM((states, width), f32),
            pltpu.VMEM((block, width), f32),
            pltpu.VMEM((states, block), f32),
        ],
        compiler_params=pltpu.CompilerParams(vmem_limit_bytes=48 << 20),
        cost_estimate=pl.CostEstimate(
            flops=8 * length * width * states,
            transcendentals=length * width * states,
            bytes_accessed=length * width * (2 * states + 10),
        ),
        name="scan_forward",
    )(delta, active, select, rate)


FEW = 4


def backward_body(
    tiles, step, delta, active, d_mixed, select, rate, decay_rate, kept, kept_before,
    d_delta, d_active, d_bc, d_log, push, drive, columns, diagonals, folding, timed, *pairs,
):
    grads, rated = pairs[:2], pairs[2:]
    rows, states = delta.shape[0], rate.shape[0]
    blocks = pl.num_programs(0)
    first = pl.program_id(0) == blocks - 1
    wide = step * states

    @pl.when(pl.program_id(0) == 0)
    def _():
        push[...] = jnp.zeros_like(push)
        d_log[...] = jnp.zeros_like(d_log)

    turned, b_block, _ = selectors(select[...], states)
    columns[...] = turned[states:]
    drive[...] = delta[...] * active[...].astype(f32)
    rates = [rate[:, k * LANES : (k + 1) * LANES] for k in range(tiles)]
    own_rates = [decay_rate[:, k * LANES : (k + 1) * LANES].astype(bf16) for k in range(tiles)]

    place = lax.broadcasted_iota(jnp.int32, (step, wide), 0)
    owner = lax.broadcasted_iota(jnp.int32, (step, wide), 1) // states
    ones_diag = (place == owner).astype(bf16)
    diag = (place == owner).astype(f32)
    diagonals[...] = block_diagonal(b_block, step)

    def sums_of(number):
        held, through_of = number % 2, {}

        def spots(q):
            at = number * GROUP + q * step
            tall = slice(q * wide, (q + 1) * wide)
            return slice(at, at + step), tall

        def through(q):
            spot, tall = spots(q)
            value = jnp.dot(diagonals[spot, :], grads[held][tall, :], preferred_element_type=f32)
            d_active[spot, :] = delta[spot, :] * value
            through_of[q] = active[spot, :].astype(f32) * value

        def summed(q):
            spot, tall = spots(q)
            value = jnp.dot(ones_diag, rated[held][tall, :], preferred_element_type=f32)
            d_delta[spot, :] = value + through_of[q]

        def d_b(q):
            spot, tall = spots(q)
            folding[spot, :wide] = diag * lax.dot_general(
                drive[spot, :].astype(bf16), grads[held][tall, :], NT, preferred_element_type=f32
            )

        def d_c(q):
            spot, _ = spots(q)
            own = slice(spot.start * states, spot.stop * states)
            folding[spot, wide:] = diag * lax.dot_general(
                d_mixed[spot, :].astype(bf16), kept[own, :], NT, preferred_element_type=f32
            )

        return [
            functools.partial(part, q)
            for q in range(GROUP // step)
            for part in (through, summed, d_b, d_c)
        ]

    carry = [push[:, k * LANES : (k + 1) * LANES] for k in range(tiles)]
    waiting = []
    for number in reversed(range(rows // GROUP)):
        pace = GROUP // max(len(waiting), 1)
        sums = [None] * tiles
        held = number % 2
        for j in reversed(range(GROUP)):
            row = number * GROUP + j
            c_wide = jnp.broadcast_to(columns[:, row : row + 1], (states, LANES))
            at = slice(j * states, (j + 1) * states)
            for k in range(tiles):
                lanes = slice(k * LANES, (k + 1) * LANES)
                if row:
                    before = kept[(row - 1) * states : row * states, lanes]
                else:
                    before = jnp.where(first, jnp.zeros((), bf16), kept_before[:, lanes])
                step_size = spread(delta, row, lanes, states)
                grad = spread(d_mixed, row, lanes, states) * c_wide + carry[k]
                carry[k] = jnp.exp2(step_size * rates[k]) * grad
                grads[held][at, lanes] = grad.astype(bf16)
                rated_now = carry[k].astype(bf16) * before * own_rates[k]
                rated[held][at, lanes] = rated_now
                timed_now = rated_now * step_size.astype(bf16)
                sums[k] = timed_now if sums[k] is None else sums[k] + timed_now
                if j % FEW == 0:
                    spot = row // FEW * states
                    timed[spot : spot + states, lanes] = sums[k]
                    sums[k] = None
            if waiting and j % pace == 0:
                waiting.pop(0)()
        while waiting:
            waiting.pop(0)()
        waiting = sums_of(number)
    while waiting:
        waiting.pop(0)()
    for k in range(tiles):
        push[:, k * LANES : (k + 1) * LANES] = carry[k]
    fold = (
        lax.broadcasted_iota(jnp.int32, (wide, states), 0) % states
        == lax.broadcasted_iota(jnp.int32, (wide, states), 1)
    ).astype(bf16)
    for number in range(2):
        value = folding[:, number * wide : (number + 1) * wide]
        high = value.astype(bf16)
        d_bc[:, number * states : (number + 1) * states] = jnp.dot(
            high, fold, preferred_element_type=f32
        )
    span = rows // FEW * states
    pick = (
        lax.broadcasted_iota(jnp.int32, (states, span), 1) % states
        == lax.broadcasted_iota(jnp.int32, (states, span), 0)
    ).astype(bf16)
    d_log[...] += jnp.dot(pick, timed[...], preferred_element_type=f32)


def scan_backward(delta, active, d_mixed, select, rate, decay_rate, kept, block, step):
    length, width = delta.shape
    states = rate.shape[0]
    tiles = width // LANES
    blocks = length // block
    back = lambda i: (blocks - 1 - i, 0)
    return pl.pallas_call(
        functools.partial(backward_body, tiles, step),
        grid=(blocks,),
        in_specs=[
            pl.BlockSpec((block, width), back),
            pl.BlockSpec((block, width), back),
            pl.BlockSpec((block, width), back),
            pl.BlockSpec((block, select.shape[1]), back),
            pl.BlockSpec((states, width), lambda i: (0, 0)),
            pl.BlockSpec((states, width), lambda i: (0, 0)),
            pl.BlockSpec((block * states, width), back),
            pl.BlockSpec(
                (states, width), lambda i: (jnp.maximum((blocks - 1 - i) * block - 1, 0), 0)
            ),
        ],
        out_specs=[
            pl.BlockSpec((block, width), back),
            pl.BlockSpec((block, width), back),
            pl.BlockSpec((block, 2 * states), back),
            pl.BlockSpec((states, width), lambda i: (0, 0)),
        ],
        out_shape=[
            jax.ShapeDtypeStruct((length, width), f32),
            jax.ShapeDtypeStruct((length, width), f32),
            jax.ShapeDtypeStruct((length, 2 * states), f32),
            jax.ShapeDtypeStruct((states, width), f32),
        ],
        scratch_shapes=[
            pltpu.VMEM((states, width), f32),
            pltpu.VMEM((block, width), f32),
            pltpu.VMEM((states, block), f32),
            pltpu.VMEM((block, step * states), bf16),
            pltpu.VMEM((block, 2 * step * states), f32),
            pltpu.VMEM((block // FEW * states, width), bf16),
        ]
        + [pltpu.VMEM((GROUP * states, width), bf16)] * 4,
        compiler_params=pltpu.CompilerParams(vmem_limit_bytes=48 << 20),
        cost_estimate=pl.CostEstimate(
            flops=20 * length * width * states,
            transcendentals=length * width * states,
            bytes_accessed=length * width * (2 * states + 20),
        ),
        name="scan_backward",
    )(delta, active, d_mixed, select, rate, decay_rate, kept, kept)


together = lax.optimization_barrier


def inner_swap(value, axis):
    count = lax.axis_size(axis)
    return lax.ppermute(value, axis, [(i, i ^ 1) for i in range(count)])


def outer_shift(value, axis, steps):
    count = lax.axis_size(axis)
    half = count // 2
    pairs = [(i, (i // 2 + steps) % half * 2 + i % 2) for i in range(count)]
    return lax.ppermute(value, axis, pairs)


def shift_order(half):
    return sorted(range(1, half), key=lambda k: (-min(k, half - k), k))


def pieces_of_all(own, axis):
    count = lax.axis_size(axis)
    place = lax.axis_index(axis)
    half = count // 2
    outer, inner = place // 2, place % 2
    yield place, own
    arrived = {k: outer_shift(own, axis, k) for k in shift_order(half)}
    yield outer * 2 + 1 - inner, inner_swap(own, axis)
    for k, piece in arrived.items():
        origin = (outer - k + half) % half
        yield origin * 2 + inner, piece
    for k, piece in arrived.items():
        origin = (outer - k + half) % half
        yield origin * 2 + 1 - inner, inner_swap(piece, axis)


def gathered(own, axis, dim=0):
    count, size = lax.axis_size(axis), own.shape[dim]
    whole = jnp.zeros(own.shape[:dim] + (count * size,) + own.shape[dim + 1 :], own.dtype)
    for place, piece in pieces_of_all(own, axis):
        whole = lax.dynamic_update_slice_in_dim(whole, piece, place * size, dim)
    return whole


def hop(value, axis, moves):
    pairs = [(a * 2 + i, b * 2 + i) for a, b in moves for i in (0, 1)]
    return lax.ppermute(value, axis, pairs)


def swap_at(value, axis, spots):
    pairs = [(a * 2 + i, a * 2 + 1 - i) for a in spots for i in (0, 1)]
    return lax.ppermute(value, axis, pairs)


UP, DOWN = [(0, 1), (1, 2), (2, 3)], [(1, 0), (2, 1), (3, 2)]


def line_gathered(own, axis, held):
    if lax.axis_size(axis) != 8:
        return own, lambda own: own, lambda own, _: lax.all_gather(own, axis, axis=0, tiled=True), held
    place = lax.axis_index(axis)
    z, x = place // 2, place % 2
    rows = own.shape[0]
    upper, edge = z >= 2, (z == 0) | (z == 3)
    across = jnp.where(upper, z - 2, z + 2)
    far = jnp.where(z == 3, 0, 3)

    def put(whole, piece, spot, side):
        return lax.dynamic_update_slice_in_dim(whole, piece, (spot * 2 + side) * rows, 0)

    def put_far(whole, piece, side):
        held = lax.dynamic_slice_in_dim(whole, (far * 2 + side) * rows, rows, 0)
        return put(whole, jnp.where(edge, piece, held), far, side)

    whole = jnp.zeros((8 * rows,) + own.shape[1:], own.dtype)
    up, down, other, held = together(
        (hop(own, axis, UP), hop(own, axis, DOWN), swap_at(own, axis, range(4)), held)
    )
    up_two, down_two = hop(up, axis, UP[1:]), hop(down, axis, DOWN[:2])
    other_up, other_down = swap_at(up, axis, (1, 2, 3)), swap_at(down, axis, (0, 1, 2))
    whole = put(put(whole, own, z, x), other, z, 1 - x)
    whole = put(put(whole, up, (z + 3) % 4, x), down, (z + 1) % 4, x)
    two = jnp.where(upper, up_two, down_two)
    three = hop(two, axis, [(2, 3), (1, 0)])
    other_two = swap_at(two, axis, range(4))
    whole = put(put(whole, other_up, (z + 3) % 4, 1 - x), other_down, (z + 1) % 4, 1 - x)
    whole = put(put(whole, two, across, x), other_two, across, 1 - x)

    def end(three, other_three):
        return put_far(put_far(whole, three, x), other_three, 1 - x)

    return three, lambda three: swap_at(three, axis, (0, 3)), end, held


def line_summed(part_of, axis):
    if lax.axis_size(axis) != 8:
        return (scattered_sum(part_of, axis),)
    place = lax.axis_index(axis)
    z, x = place // 2, place % 2
    upper, edge = z >= 2, (z == 0) | (z == 3)
    across = jnp.where(upper, z - 2, z + 2)
    far = jnp.where(z == 0, 3, 0)
    above, below = jnp.minimum(z + 1, 3), jnp.maximum(z - 1, 0)

    def swapped(spot, spots):
        return swap_at(part_of(spot * 2 + 1 - x), axis, spots)

    def added(spot, given):
        return part_of(spot * 2 + x).astype(f32) + given.astype(f32)

    given_far = swapped(far, (0, 3))
    given_across = swapped(across, range(4))
    given_above, given_below = swapped(above, (0, 1, 2)), swapped(below, (1, 2, 3))
    given_own = swapped(z, range(4))
    three = hop(added(far, given_far).astype(bf16), axis, [(0, 1), (3, 2)])
    three, given_across = together((three, given_across))
    two = added(across, given_across) + jnp.where(edge, 0.0, three.astype(f32))
    two = two.astype(bf16)
    two_up, two_down, given_above, given_below = together(
        (hop(two, axis, UP[:2]), hop(two, axis, DOWN[1:]), given_above, given_below)
    )
    one_up = (added(above, given_above) + two_up.astype(f32)).astype(bf16)
    one_down = (added(below, given_below) + two_down.astype(f32)).astype(bf16)
    return added(z, given_own), hop(one_up, axis, UP), hop(one_down, axis, DOWN)


def scattered_sum(part_of, axis):
    count = lax.axis_size(axis)
    place = lax.axis_index(axis)
    half = count // 2
    outer, inner = place // 2, place % 2
    total = None
    for k in shift_order(half) + [0]:
        target = (outer + k) % half
        given = inner_swap(part_of(target * 2 + 1 - inner), axis)
        piece = part_of(target * 2 + inner).astype(f32) + given.astype(f32)
        if k:
            piece = outer_shift(piece.astype(bf16), axis, k).astype(f32)
        total = piece if total is None else total + piece
    return total


def rows_of(value, rows):
    return lambda place: lax.dynamic_slice_in_dim(value, place * rows, rows, 0)


def summed_over_seq(part, change, held):
    count = lax.axis_size("seq")
    length, columns = part.shape
    part = part.astype(bf16).reshape(count, length // count, columns)
    own = change(jnp.sum(lax.all_to_all(part, "seq", 0, 0).astype(f32), axis=0))
    own, held = together((own, held))
    return shared(own, "seq").reshape(length, own.shape[1]), held


def two_terms(value):
    high = value.astype(bf16)
    return [high, (value - high.astype(f32)).astype(bf16)]


def shared(own, axis):
    wide = jnp.broadcast_to(own[None], (lax.axis_size(axis),) + own.shape)
    return lax.all_to_all(wide, axis, 0, 0)


def matmul(a, b, dims=(((1,), (0,)), ((), ()))):
    return lax.dot_general(a, b, dims, preferred_element_type=f32)


TN = (((0,), (0,)), ((), ()))


def on_device(
    tokens,
    lengths,
    norm_gain,
    in_proj,
    conv_weight,
    conv_bias,
    x_proj,
    dt_proj,
    dt_bias,
    a_log,
    skip,
    out_proj,
    cotangent,
):
    batch, seq = lax.axis_size("batch"), lax.axis_size("seq")
    place = lax.axis_index("seq")
    span, model = tokens.shape[1:]
    length = span * seq
    in_rows = in_proj.shape[0]
    own = skip.shape[0]
    taps = conv_weight.shape[0]
    rank = dt_proj.shape[0]
    states = a_log.shape[1]
    width = own * batch

    halves = in_proj.reshape(in_rows, 2, batch, seq, own).transpose(1, 3, 0, 2, 4)
    halves = halves.reshape(2, seq, in_rows, width)
    columns = lax.all_to_all(halves[0], "seq", 0, 0)
    columns, gate_columns = together((columns, halves[1]))
    gate_columns = lax.all_to_all(gate_columns, "seq", 0, 0)
    last_hop, last_swap, end_gather, (dt_proj, x_proj, out_proj) = line_gathered(
        cotangent[0], "seq", (dt_proj, x_proj, out_proj)
    )
    small = jnp.concatenate(
        [
            dt_proj,
            x_proj.T,
            a_log.T,
            conv_weight,
            conv_bias[None],
            dt_bias[None],
            skip[None],
            jnp.pad(norm_gain, (0, own - in_rows))[None],
        ],
        axis=0,
    )
    small = gathered(small, "batch", 1)
    cuts = [rank, 2 * rank + 2 * states, 2 * rank + 3 * states]
    cuts = cuts + [cuts[2] + taps + i for i in range(4)]
    delta_weight, select_weight, decay_logs, conv_taps, conv_shift, delta_shift, skip_gain, gain = (
        jnp.split(small, cuts, axis=0)
    )
    conv_taps, conv_shift = conv_taps.astype(f32), conv_shift.astype(f32)
    delta_shift, skip_gain = delta_shift.astype(f32), skip_gain.astype(f32)
    decay = -jnp.exp(decay_logs.astype(f32))
    gain = gain.reshape(batch, own)[:, :in_rows]
    gate_columns, gain = together((gate_columns, gain))
    gain = shared(gain, "seq").transpose(1, 0, 2).reshape(model).astype(f32)

    input_weight = gathered(columns.reshape(seq * in_rows, width), "batch")

    def normed(rows):
        rows = rows.astype(f32)
        scale = lax.rsqrt(jnp.mean(rows * rows, axis=-1, keepdims=True) + epsilon)
        return (rows * scale * gain).astype(bf16)

    stream = lax.all_gather(tokens[0], "seq", axis=0, tiled=True)
    normalized = normed(stream)
    output_weight = gathered(out_proj, "batch")

    valid = (jnp.arange(length, dtype=jnp.int32) < lengths[0])[:, None]
    inner = matmul(normalized, input_weight).astype(bf16)
    padded = jnp.pad(inner, ((taps - 1, 0), (0, 0)))
    conv_out = conv_shift + jnp.zeros((length, width), f32)
    for tap in range(taps):
        conv_out = conv_out + conv_taps[tap] * padded[tap : tap + length].astype(f32)
    active = jax.nn.silu(conv_out).astype(bf16)
    active_f = active.astype(f32)

    partial, last_hop, gate_columns = together(
        (matmul(active, select_weight, NT), last_hop, gate_columns)
    )
    partial, last = together((partial, last_swap(last_hop)))
    gate_weight = gathered(gate_columns.reshape(seq * in_rows, width), "batch")
    select, (last_hop, last) = summed_over_seq(
        partial,
        lambda s: jnp.concatenate([s[:, :rank].astype(bf16)] + two_terms(s[:, rank:]), axis=1),
        (last_hop, last),
    )
    upstream = end_gather(last_hop, last)
    upstream = jnp.where(valid, upstream, 0).astype(bf16)
    gate_low = matmul(normalized, gate_weight).astype(bf16)
    d_gated = matmul(upstream, output_weight, NT)
    select, gate_low, d_gated = together((select, gate_low, d_gated))
    gate = gate_low.astype(f32)
    gate_sig = jax.nn.sigmoid(gate)
    delta_low = select[:, :rank]
    delta_raw = matmul(delta_low, delta_weight) + delta_shift
    delta = jax.nn.softplus(delta_raw)

    block = min(BLOCK, length)
    step = 256 // states
    rate = decay * LOG2E
    mixed, kept = scan_forward(delta, active, select, rate, block, step)
    mixed = mixed + skip_gain * active_f
    gated = (mixed * gate * gate_sig).astype(bf16)
    branch = matmul(gated, output_weight).astype(bf16)
    d_gated, branch = together((d_gated, branch))
    branch = lax.psum_scatter(branch, "seq", scatter_dimension=0, tiled=True)
    own_valid = lax.dynamic_slice_in_dim(valid, place * span, span, 0)
    own_stream = tokens[0].astype(f32)

    d_mixed = d_gated * gate * gate_sig
    d_gate = d_gated * mixed * gate_sig * (1.0 + gate * (1.0 - gate_sig))
    grad_skip = jnp.sum(d_mixed * active_f, axis=0, keepdims=True)
    d_gate_low = d_gate.astype(bf16)

    d_delta, d_active, d_bc, grad_log = scan_backward(
        delta, active, d_mixed, select, rate, decay, kept, block, step
    )
    d_raw = d_delta * jax.nn.sigmoid(delta_raw)
    grad_dt_bias = jnp.sum(d_raw, axis=0, keepdims=True)
    d_raw_low = d_raw.astype(bf16)
    grad_dt_proj = matmul(delta_low, d_raw_low, TN)
    partial = jnp.concatenate([matmul(d_raw_low, delta_weight, NT), d_bc], axis=1)
    d_select, _ = summed_over_seq(partial, lambda s: s.astype(bf16), ())
    grad_gate = scattered_sum(
        rows_of(matmul(normalized, d_gate_low, TN).astype(bf16), model // batch), "batch"
    )
    d_select, grad_gate = together((d_select, grad_gate))
    grad_x_proj = matmul(d_select, active, TN)
    d_active = d_active + d_mixed * skip_gain + matmul(d_select, select_weight)
    conv_sig = jax.nn.sigmoid(conv_out)
    d_conv = (d_active * conv_sig * (1.0 + conv_out * (1.0 - conv_sig))).astype(bf16)
    d_conv_f = d_conv.astype(f32)
    grad_conv_bias = jnp.sum(d_conv_f, axis=0, keepdims=True)
    grad_conv = jnp.stack(
        [
            jnp.sum(d_conv_f * padded[tap : tap + length].astype(f32), axis=0)
            for tap in range(taps)
        ]
    )
    extended = jnp.pad(d_conv, ((0, taps - 1), (0, 0)))
    d_inner = jnp.zeros((length, width), f32)
    for tap in range(taps):
        offset = taps - 1 - tap
        d_inner = d_inner + conv_taps[tap] * extended[offset : offset + length].astype(f32)
    d_inner = d_inner.astype(bf16)
    d_normalized = matmul(
        jnp.concatenate([d_inner, d_gate_low], axis=1),
        jnp.concatenate([input_weight, gate_weight], axis=1),
        NT,
    ).astype(bf16)
    grad_gate = grad_gate.astype(bf16).reshape(seq, in_rows, width)
    grad_gate = lax.all_to_all(grad_gate, "seq", 0, 0)
    d_normalized, d_inner, gated, grad_gate, grad_x_proj, branch = together(
        (d_normalized, d_inner, gated, grad_gate, grad_x_proj, branch)
    )
    grad_inner = matmul(normalized, d_inner, TN).astype(bf16)
    grad_inner = scattered_sum(rows_of(grad_inner, model // batch), "batch")
    grad_output = lax.psum_scatter(
        matmul(gated, upstream, TN).astype(bf16), "batch", scatter_dimension=0, tiled=True
    ).astype(f32)
    d_normalized, *last_terms = line_summed(rows_of(d_normalized, span), "seq")

    block_out = jnp.where(own_valid, own_stream + branch.astype(f32), 0.0)

    def columns_of(part):
        part = part.reshape(seq, in_rows, batch, own).transpose(1, 2, 0, 3)
        return part.reshape(in_rows, batch * seq * own).astype(f32)

    grad_inner = grad_inner.astype(bf16).reshape(seq, in_rows, width)
    grad_inner = lax.all_to_all(grad_inner, "seq", 0, 0)
    grad_input = jnp.concatenate([columns_of(grad_inner), columns_of(grad_gate)], axis=1)

    small_grads = jnp.concatenate(
        [grad_dt_proj, grad_x_proj, grad_log, grad_conv, grad_conv_bias, grad_dt_bias, grad_skip],
        axis=0,
    )
    small_grads = lax.psum_scatter(small_grads, "batch", scatter_dimension=1, tiled=True)
    g_dt_proj, g_x_proj, g_log, g_conv, g_conv_bias, g_dt_bias, g_skip = jnp.split(
        small_grads, cuts[:-1], axis=0
    )

    own_upstream = jnp.where(own_valid, cotangent[0].astype(f32), 0.0)
    own_scale = lax.rsqrt(jnp.mean(own_stream * own_stream, axis=-1, keepdims=True) + epsilon)
    grad_gain = jnp.sum(grad_input * in_proj.astype(f32), axis=1) / norm_gain.astype(f32)
    (
        d_normalized, g_dt_proj, g_x_proj, g_log, g_conv, g_conv_bias, g_dt_bias, g_skip,
        grad_input, grad_gain, grad_output,
    ) = together(
        (
            d_normalized, g_dt_proj, g_x_proj, g_log, g_conv, g_conv_bias, g_dt_bias, g_skip,
            grad_input, grad_gain, grad_output,
        )
    )
    for term in last_terms:
        d_normalized = d_normalized + term.astype(f32)
    d_hat = d_normalized * gain
    grad_tokens = (
        own_scale * d_hat
        - own_stream
        * own_scale
        * own_scale
        * own_scale
        * jnp.mean(d_hat * own_stream, axis=-1, keepdims=True)
        + own_upstream
    )
    return (
        block_out[None],
        grad_tokens[None],
        grad_gain,
        grad_input,
        g_conv,
        g_conv_bias[0],
        g_x_proj.T,
        g_dt_proj,
        g_dt_bias[0],
        g_log.T,
        g_skip[0],
        grad_output,
    )


def solution(mesh):
    placed = (
        P("batch", "seq", None),
        P("batch"),
        P(("batch", "seq")),
        P(("batch", "seq"), None),
        P(None, ("batch", "seq")),
        P(("batch", "seq")),
        P(("batch", "seq"), None),
        P(None, ("batch", "seq")),
        P(("batch", "seq")),
        P(("batch", "seq"), None),
        P(("batch", "seq")),
        P(("batch", "seq"), None),
        P("batch", "seq", None),
    )
    return jax.shard_map(
        on_device,
        mesh=mesh,
        in_specs=placed,
        out_specs=(
            P("batch", "seq", None),
            P("batch", "seq", None),
            P(("batch", "seq")),
            P(("batch", "seq"), None),
            P(None, ("batch", "seq")),
            P(("batch", "seq")),
            P(("batch", "seq"), None),
            P(None, ("batch", "seq")),
            P(("batch", "seq")),
            P(("batch", "seq"), None),
            P(("batch", "seq")),
            P(("batch", "seq"), None),
        ),
        check_vma=False,
    )
```

```python
import functools

import jax
import jax.numpy as jnp
from jax import lax
from jax.experimental import pallas as pl
from jax.experimental.pallas import tpu as pltpu
from jax.sharding import PartitionSpec as P

bf16, f32 = jnp.bfloat16, jnp.float32
NT = (((1,), (1,)), ((), ()))
LANES = 128
GROUP = 32
BLOCK = 128
epsilon = 1e-05
LOG2E = 1.4426950408889634


def spread(tile, row, lanes, states):
    return jnp.broadcast_to(tile[row : row + 1, lanes], (states, LANES))


def selectors(select, states):
    low = select.shape[1] - 4 * states
    middle = low + 2 * states
    block = select[:, low:middle].astype(f32) + select[:, middle:].astype(f32)
    return jnp.transpose(block), block[:, :states], block[:, states:]


def block_diagonal(values, step):
    rows, states = values.shape
    wide = step * states
    spread_out = (
        lax.broadcasted_iota(jnp.int32, (states, wide), 1) % states
        == lax.broadcasted_iota(jnp.int32, (states, wide), 0)
    ).astype(bf16)
    value = jnp.dot(values.astype(bf16), spread_out, preferred_element_type=f32)
    place = lax.broadcasted_iota(jnp.int32, (rows, wide), 0) % step
    owner = lax.broadcasted_iota(jnp.int32, (rows, wide), 1) // states
    return jnp.where(place == owner, value, 0.0).astype(bf16)


def forward_body(tiles, step, delta, active, select, rate, mixed, kept, state, drive, columns):
    rows, states = delta.shape[0], rate.shape[0]
    wide = step * states

    @pl.when(pl.program_id(0) == 0)
    def _():
        state[...] = jnp.zeros_like(state)

    turned, _, c_block = selectors(select[...], states)
    columns[...] = turned[:states]
    drive[...] = delta[...] * active[...].astype(f32)
    rates = [rate[:, k * LANES : (k + 1) * LANES] for k in range(tiles)]

    def group(number, held):
        held = list(held)
        base = pl.multiple_of(number * GROUP, GROUP)
        delta_now, drive_now = delta.at[pl.ds(base, GROUP), :], drive.at[pl.ds(base, GROUP), :]
        b_now = pltpu.roll(columns[...], rows - base, 1)
        for j in range(GROUP):
            b_wide = jnp.broadcast_to(b_now[:, j : j + 1], (states, LANES))
            for k in range(tiles):
                lanes = slice(k * LANES, (k + 1) * LANES)
                decay = jnp.exp2(spread(delta_now, j, lanes, states) * rates[k])
                held[k] = decay * held[k] + spread(drive_now, j, lanes, states) * b_wide
                at = pl.ds(pl.multiple_of((base + j) * states, states), states)
                kept[at, lanes] = held[k].astype(bf16)
        return tuple(held)

    held = lax.fori_loop(
        0,
        rows // GROUP,
        group,
        tuple(state[:, k * LANES : (k + 1) * LANES] for k in range(tiles)),
    )
    for k in range(tiles):
        state[:, k * LANES : (k + 1) * LANES] = held[k]
    c_diag = block_diagonal(c_block, step)
    for q in range(rows // step):
        part = kept[q * wide : (q + 1) * wide, :]
        spot = slice(q * step, (q + 1) * step)
        mixed[spot, :] = jnp.dot(c_diag[spot, :], part, preferred_element_type=f32)


def scan_forward(delta, active, select, rate, block, step):
    length, width = delta.shape
    states = rate.shape[0]
    tiles = width // LANES
    return pl.pallas_call(
        functools.partial(forward_body, tiles, step),
        grid=(length // block,),
        in_specs=[
            pl.BlockSpec((block, width), lambda i: (i, 0)),
            pl.BlockSpec((block, width), lambda i: (i, 0)),
            pl.BlockSpec((block, select.shape[1]), lambda i: (i, 0)),
            pl.BlockSpec((states, width), lambda i: (0, 0)),
        ],
        out_specs=[
            pl.BlockSpec((block, width), lambda i: (i, 0)),
            pl.BlockSpec((block * states, width), lambda i: (i, 0)),
        ],
        out_shape=[
            jax.ShapeDtypeStruct((length, width), f32),
            jax.ShapeDtypeStruct((length * states, width), bf16),
        ],
        scratch_shapes=[
            pltpu.VMEM((states, width), f32),
            pltpu.VMEM((block, width), f32),
            pltpu.VMEM((states, block), f32),
        ],
        compiler_params=pltpu.CompilerParams(vmem_limit_bytes=48 << 20),
        cost_estimate=pl.CostEstimate(
            flops=8 * length * width * states,
            transcendentals=length * width * states,
            bytes_accessed=length * width * (2 * states + 10),
        ),
        name="scan_forward",
    )(delta, active, select, rate)


FEW = 4


def backward_body(
    tiles, step, delta, active, d_mixed, select, rate, decay_rate, kept, kept_before,
    d_delta, d_active, d_bc, d_log, push, drive, columns, diagonals, folding, timed, *pairs,
):
    grads, rated = pairs[:2], pairs[2:]
    rows, states = delta.shape[0], rate.shape[0]
    blocks = pl.num_programs(0)
    first = pl.program_id(0) == blocks - 1
    wide = step * states

    @pl.when(pl.program_id(0) == 0)
    def _():
        push[...] = jnp.zeros_like(push)
        d_log[...] = jnp.zeros_like(d_log)

    turned, b_block, _ = selectors(select[...], states)
    columns[...] = turned[states:]
    drive[...] = delta[...] * active[...].astype(f32)
    rates = [rate[:, k * LANES : (k + 1) * LANES] for k in range(tiles)]
    own_rates = [decay_rate[:, k * LANES : (k + 1) * LANES].astype(bf16) for k in range(tiles)]

    place = lax.broadcasted_iota(jnp.int32, (step, wide), 0)
    owner = lax.broadcasted_iota(jnp.int32, (step, wide), 1) // states
    ones_diag = (place == owner).astype(bf16)
    diag = (place == owner).astype(f32)
    diagonals[...] = block_diagonal(b_block, step)

    def sums_of(number):
        held, through_of = number % 2, {}

        def spots(q):
            at = number * GROUP + q * step
            tall = slice(q * wide, (q + 1) * wide)
            return slice(at, at + step), tall

        def through(q):
            spot, tall = spots(q)
            value = jnp.dot(diagonals[spot, :], grads[held][tall, :], preferred_element_type=f32)
            d_active[spot, :] = delta[spot, :] * value
            through_of[q] = active[spot, :].astype(f32) * value

        def summed(q):
            spot, tall = spots(q)
            value = jnp.dot(ones_diag, rated[held][tall, :], preferred_element_type=f32)
            d_delta[spot, :] = value + through_of[q]

        def d_b(q):
            spot, tall = spots(q)
            folding[spot, :wide] = diag * lax.dot_general(
                drive[spot, :].astype(bf16), grads[held][tall, :], NT, preferred_element_type=f32
            )

        def d_c(q):
            spot, _ = spots(q)
            own = slice(spot.start * states, spot.stop * states)
            folding[spot, wide:] = diag * lax.dot_general(
                d_mixed[spot, :].astype(bf16), kept[own, :], NT, preferred_element_type=f32
            )

        return [
            functools.partial(part, q)
            for q in range(GROUP // step)
            for part in (through, summed, d_b, d_c)
        ]

    carry = [push[:, k * LANES : (k + 1) * LANES] for k in range(tiles)]
    waiting = []
    for number in reversed(range(rows // GROUP)):
        pace = GROUP // max(len(waiting), 1)
        sums = [None] * tiles
        held = number % 2
        for j in reversed(range(GROUP)):
            row = number * GROUP + j
            c_wide = jnp.broadcast_to(columns[:, row : row + 1], (states, LANES))
            at = slice(j * states, (j + 1) * states)
            for k in range(tiles):
                lanes = slice(k * LANES, (k + 1) * LANES)
                if row:
                    before = kept[(row - 1) * states : row * states, lanes]
                else:
                    before = jnp.where(first, jnp.zeros((), bf16), kept_before[:, lanes])
                step_size = spread(delta, row, lanes, states)
                grad = spread(d_mixed, row, lanes, states) * c_wide + carry[k]
                carry[k] = jnp.exp2(step_size * rates[k]) * grad
                grads[held][at, lanes] = grad.astype(bf16)
                rated_now = carry[k].astype(bf16) * before * own_rates[k]
                rated[held][at, lanes] = rated_now
                timed_now = rated_now * step_size.astype(bf16)
                sums[k] = timed_now if sums[k] is None else sums[k] + timed_now
                if j % FEW == 0:
                    spot = row // FEW * states
                    timed[spot : spot + states, lanes] = sums[k]
                    sums[k] = None
            if waiting and j % pace == 0:
                waiting.pop(0)()
        while waiting:
            waiting.pop(0)()
        waiting = sums_of(number)
    while waiting:
        waiting.pop(0)()
    for k in range(tiles):
        push[:, k * LANES : (k + 1) * LANES] = carry[k]
    fold = (
        lax.broadcasted_iota(jnp.int32, (wide, states), 0) % states
        == lax.broadcasted_iota(jnp.int32, (wide, states), 1)
    ).astype(bf16)
    for number in range(2):
        value = folding[:, number * wide : (number + 1) * wide]
        high = value.astype(bf16)
        d_bc[:, number * states : (number + 1) * states] = jnp.dot(
            high, fold, preferred_element_type=f32
        )
    span = rows // FEW * states
    pick = (
        lax.broadcasted_iota(jnp.int32, (states, span), 1) % states
        == lax.broadcasted_iota(jnp.int32, (states, span), 0)
    ).astype(bf16)
    d_log[...] += jnp.dot(pick, timed[...], preferred_element_type=f32)


def scan_backward(delta, active, d_mixed, select, rate, decay_rate, kept, block, step):
    length, width = delta.shape
    states = rate.shape[0]
    tiles = width // LANES
    blocks = length // block
    back = lambda i: (blocks - 1 - i, 0)
    return pl.pallas_call(
        functools.partial(backward_body, tiles, step),
        grid=(blocks,),
        in_specs=[
            pl.BlockSpec((block, width), back),
            pl.BlockSpec((block, width), back),
            pl.BlockSpec((block, width), back),
            pl.BlockSpec((block, select.shape[1]), back),
            pl.BlockSpec((states, width), lambda i: (0, 0)),
            pl.BlockSpec((states, width), lambda i: (0, 0)),
            pl.BlockSpec((block * states, width), back),
            pl.BlockSpec(
                (states, width), lambda i: (jnp.maximum((blocks - 1 - i) * block - 1, 0), 0)
            ),
        ],
        out_specs=[
            pl.BlockSpec((block, width), back),
            pl.BlockSpec((block, width), back),
            pl.BlockSpec((block, 2 * states), back),
            pl.BlockSpec((states, width), lambda i: (0, 0)),
        ],
        out_shape=[
            jax.ShapeDtypeStruct((length, width), f32),
            jax.ShapeDtypeStruct((length, width), f32),
            jax.ShapeDtypeStruct((length, 2 * states), f32),
            jax.ShapeDtypeStruct((states, width), f32),
        ],
        scratch_shapes=[
            pltpu.VMEM((states, width), f32),
            pltpu.VMEM((block, width), f32),
            pltpu.VMEM((states, block), f32),
            pltpu.VMEM((block, step * states), bf16),
            pltpu.VMEM((block, 2 * step * states), f32),
            pltpu.VMEM((block // FEW * states, width), bf16),
        ]
        + [pltpu.VMEM((GROUP * states, width), bf16)] * 4,
        compiler_params=pltpu.CompilerParams(vmem_limit_bytes=48 << 20),
        cost_estimate=pl.CostEstimate(
            flops=20 * length * width * states,
            transcendentals=length * width * states,
            bytes_accessed=length * width * (2 * states + 20),
        ),
        name="scan_backward",
    )(delta, active, d_mixed, select, rate, decay_rate, kept, kept)


together = lax.optimization_barrier


def inner_swap(value, axis):
    count = lax.axis_size(axis)
    return lax.ppermute(value, axis, [(i, i ^ 1) for i in range(count)])


def outer_shift(value, axis, steps):
    count = lax.axis_size(axis)
    half = count // 2
    pairs = [(i, (i // 2 + steps) % half * 2 + i % 2) for i in range(count)]
    return lax.ppermute(value, axis, pairs)


def shift_order(half):
    return sorted(range(1, half), key=lambda k: (-min(k, half - k), k))


def pieces_of_all(own, axis):
    count = lax.axis_size(axis)
    place = lax.axis_index(axis)
    half = count // 2
    outer, inner = place // 2, place % 2
    yield place, own
    arrived = {k: outer_shift(own, axis, k) for k in shift_order(half)}
    yield outer * 2 + 1 - inner, inner_swap(own, axis)
    for k, piece in arrived.items():
        origin = (outer - k + half) % half
        yield origin * 2 + inner, piece
    for k, piece in arrived.items():
        origin = (outer - k + half) % half
        yield origin * 2 + 1 - inner, inner_swap(piece, axis)


def gathered(own, axis, dim=0):
    count, size = lax.axis_size(axis), own.shape[dim]
    whole = jnp.zeros(own.shape[:dim] + (count * size,) + own.shape[dim + 1 :], own.dtype)
    for place, piece in pieces_of_all(own, axis):
        whole = lax.dynamic_update_slice_in_dim(whole, piece, place * size, dim)
    return whole


def hop(value, axis, moves):
    pairs = [(a * 2 + i, b * 2 + i) for a, b in moves for i in (0, 1)]
    return lax.ppermute(value, axis, pairs)


def swap_at(value, axis, spots):
    pairs = [(a * 2 + i, a * 2 + 1 - i) for a in spots for i in (0, 1)]
    return lax.ppermute(value, axis, pairs)


UP, DOWN = [(0, 1), (1, 2), (2, 3)], [(1, 0), (2, 1), (3, 2)]


def line_gathered(own, axis, held):
    if lax.axis_size(axis) != 8:
        return own, lambda own: own, lambda own, _: lax.all_gather(own, axis, axis=0, tiled=True), held
    place = lax.axis_index(axis)
    z, x = place // 2, place % 2
    rows = own.shape[0]
    upper, edge = z >= 2, (z == 0) | (z == 3)
    across = jnp.where(upper, z - 2, z + 2)
    far = jnp.where(z == 3, 0, 3)

    def put(whole, piece, spot, side):
        return lax.dynamic_update_slice_in_dim(whole, piece, (spot * 2 + side) * rows, 0)

    def put_far(whole, piece, side):
        held = lax.dynamic_slice_in_dim(whole, (far * 2 + side) * rows, rows, 0)
        return put(whole, jnp.where(edge, piece, held), far, side)

    whole = jnp.zeros((8 * rows,) + own.shape[1:], own.dtype)
    up, down, other, held = together(
        (hop(own, axis, UP), hop(own, axis, DOWN), swap_at(own, axis, range(4)), held)
    )
    up_two, down_two = hop(up, axis, UP[1:]), hop(down, axis, DOWN[:2])
    other_up, other_down = swap_at(up, axis, (1, 2, 3)), swap_at(down, axis, (0, 1, 2))
    whole = put(put(whole, own, z, x), other, z, 1 - x)
    whole = put(put(whole, up, (z + 3) % 4, x), down, (z + 1) % 4, x)
    two = jnp.where(upper, up_two, down_two)
    three = hop(two, axis, [(2, 3), (1, 0)])
    other_two = swap_at(two, axis, range(4))
    whole = put(put(whole, other_up, (z + 3) % 4, 1 - x), other_down, (z + 1) % 4, 1 - x)
    whole = put(put(whole, two, across, x), other_two, across, 1 - x)

    def end(three, other_three):
        return put_far(put_far(whole, three, x), other_three, 1 - x)

    return three, lambda three: swap_at(three, axis, (0, 3)), end, held


def line_summed(part_of, axis):
    if lax.axis_size(axis) != 8:
        return (scattered_sum(part_of, axis),)
    place = lax.axis_index(axis)
    z, x = place // 2, place % 2
    upper, edge = z >= 2, (z == 0) | (z == 3)
    across = jnp.where(upper, z - 2, z + 2)
    far = jnp.where(z == 0, 3, 0)
    above, below = jnp.minimum(z + 1, 3), jnp.maximum(z - 1, 0)

    def swapped(spot, spots):
        return swap_at(part_of(spot * 2 + 1 - x), axis, spots)

    def added(spot, given):
        return part_of(spot * 2 + x).astype(f32) + given.astype(f32)

    given_far = swapped(far, (0, 3))
    given_across = swapped(across, range(4))
    given_above, given_below = swapped(above, (0, 1, 2)), swapped(below, (1, 2, 3))
    given_own = swapped(z, range(4))
    three = hop(added(far, given_far).astype(bf16), axis, [(0, 1), (3, 2)])
    three, given_across = together((three, given_across))
    two = added(across, given_across) + jnp.where(edge, 0.0, three.astype(f32))
    two = two.astype(bf16)
    two_up, two_down, given_above, given_below = together(
        (hop(two, axis, UP[:2]), hop(two, axis, DOWN[1:]), given_above, given_below)
    )
    one_up = (added(above, given_above) + two_up.astype(f32)).astype(bf16)
    one_down = (added(below, given_below) + two_down.astype(f32)).astype(bf16)
    return added(z, given_own), hop(one_up, axis, UP), hop(one_down, axis, DOWN)


def scattered_sum(part_of, axis):
    count = lax.axis_size(axis)
    place = lax.axis_index(axis)
    half = count // 2
    outer, inner = place // 2, place % 2
    total = None
    for k in shift_order(half) + [0]:
        target = (outer + k) % half
        given = inner_swap(part_of(target * 2 + 1 - inner), axis)
        piece = part_of(target * 2 + inner).astype(f32) + given.astype(f32)
        if k:
            piece = outer_shift(piece.astype(bf16), axis, k).astype(f32)
        total = piece if total is None else total + piece
    return total


def rows_of(value, rows):
    return lambda place: lax.dynamic_slice_in_dim(value, place * rows, rows, 0)


def summed_over_seq(part, change, held):
    count = lax.axis_size("seq")
    length, columns = part.shape
    part = part.astype(bf16).reshape(count, length // count, columns)
    own = change(jnp.sum(lax.all_to_all(part, "seq", 0, 0).astype(f32), axis=0))
    own, held = together((own, held))
    return shared(own, "seq").reshape(length, own.shape[1]), held


def two_terms(value):
    high = value.astype(bf16)
    return [high, (value - high.astype(f32)).astype(bf16)]


def shared(own, axis):
    wide = jnp.broadcast_to(own[None], (lax.axis_size(axis),) + own.shape)
    return lax.all_to_all(wide, axis, 0, 0)


def matmul(a, b, dims=(((1,), (0,)), ((), ()))):
    return lax.dot_general(a, b, dims, preferred_element_type=f32)


TN = (((0,), (0,)), ((), ()))


def on_device(
    tokens,
    lengths,
    norm_gain,
    in_proj,
    conv_weight,
    conv_bias,
    x_proj,
    dt_proj,
    dt_bias,
    a_log,
    skip,
    out_proj,
    cotangent,
):
    batch, seq = lax.axis_size("batch"), lax.axis_size("seq")
    place = lax.axis_index("seq")
    span, model = tokens.shape[1:]
    length = span * seq
    in_rows = in_proj.shape[0]
    own = skip.shape[0]
    taps = conv_weight.shape[0]
    rank = dt_proj.shape[0]
    states = a_log.shape[1]
    width = own * batch

    halves = in_proj.reshape(in_rows, 2, batch, seq, own).transpose(1, 3, 0, 2, 4)
    halves = halves.reshape(2, seq, in_rows, width)
    beside = jnp.broadcast_to(norm_gain[None, :, None], (seq, in_rows, LANES))
    columns = lax.all_to_all(jnp.concatenate([halves[0], beside], axis=2), "seq", 0, 0)
    columns, gate_columns = together((columns, halves[1]))
    gate_columns = lax.all_to_all(gate_columns, "seq", 0, 0)
    last_hop, last_swap, end_gather, (dt_proj, x_proj, out_proj) = line_gathered(
        cotangent[0], "seq", (dt_proj, x_proj, out_proj)
    )
    small = jnp.concatenate(
        [
            dt_proj,
            x_proj.T,
            a_log.T,
            conv_weight,
            conv_bias[None],
            dt_bias[None],
            skip[None],
        ],
        axis=0,
    )
    small = gathered(small, "batch", 1)
    cuts = [rank, 2 * rank + 2 * states, 2 * rank + 3 * states]
    cuts = cuts + [cuts[2] + taps + i for i in range(3)]
    delta_weight, select_weight, decay_logs, conv_taps, conv_shift, delta_shift, skip_gain = (
        jnp.split(small, cuts, axis=0)
    )
    conv_taps, conv_shift = conv_taps.astype(f32), conv_shift.astype(f32)
    delta_shift, skip_gain = delta_shift.astype(f32), skip_gain.astype(f32)
    decay = -jnp.exp(decay_logs.astype(f32))
    input_weight = gathered(columns.reshape(seq * in_rows, width + LANES), "batch")
    one = (jnp.arange(LANES) == 0).astype(bf16)[None]
    gain = matmul(one, input_weight[:, width:], NT)
    input_weight = input_weight[:, :width]
    gate_weight = gathered(gate_columns.reshape(seq * in_rows, width), "batch")

    def normed(rows):
        rows = rows.astype(f32)
        scale = lax.rsqrt(jnp.mean(rows * rows, axis=-1, keepdims=True) + epsilon)
        return (rows * scale * gain).astype(bf16)

    stream = lax.all_gather(tokens[0], "seq", axis=0, tiled=True)
    normalized = normed(stream)
    output_weight = gathered(out_proj, "batch")

    valid = (jnp.arange(length, dtype=jnp.int32) < lengths[0])[:, None]
    inner = matmul(normalized, input_weight).astype(bf16)
    padded = jnp.pad(inner, ((taps - 1, 0), (0, 0)))
    conv_out = conv_shift + jnp.zeros((length, width), f32)
    for tap in range(taps):
        conv_out = conv_out + conv_taps[tap] * padded[tap : tap + length].astype(f32)
    active = jax.nn.silu(conv_out).astype(bf16)
    active_f = active.astype(f32)

    partial, last_hop = together((matmul(active, select_weight, NT), last_hop))
    partial, last, gate_weight = together((partial, last_swap(last_hop), gate_weight))
    select, (last_hop, last) = summed_over_seq(
        partial,
        lambda s: jnp.concatenate([s[:, :rank].astype(bf16)] + two_terms(s[:, rank:]), axis=1),
        (last_hop, last),
    )
    upstream = end_gather(last_hop, last)
    upstream = jnp.where(valid, upstream, 0).astype(bf16)
    gate_low = matmul(normalized, gate_weight).astype(bf16)
    d_gated = matmul(upstream, output_weight, NT)
    select, gate_low, d_gated = together((select, gate_low, d_gated))
    gate = gate_low.astype(f32)
    gate_sig = jax.nn.sigmoid(gate)
    delta_low = select[:, :rank]
    delta_raw = matmul(delta_low, delta_weight) + delta_shift
    delta = jax.nn.softplus(delta_raw)

    block = min(BLOCK, length)
    step = 256 // states
    rate = decay * LOG2E
    mixed, kept = scan_forward(delta, active, select, rate, block, step)
    mixed = mixed + skip_gain * active_f
    gated = (mixed * gate * gate_sig).astype(bf16)
    branch = matmul(gated, output_weight).astype(bf16)
    d_gated, branch = together((d_gated, branch))
    branch = lax.psum_scatter(branch, "seq", scatter_dimension=0, tiled=True)
    own_valid = lax.dynamic_slice_in_dim(valid, place * span, span, 0)
    own_stream = tokens[0].astype(f32)

    d_mixed = d_gated * gate * gate_sig
    d_gate = d_gated * mixed * gate_sig * (1.0 + gate * (1.0 - gate_sig))
    grad_skip = jnp.sum(d_mixed * active_f, axis=0, keepdims=True)
    d_gate_low = d_gate.astype(bf16)

    d_delta, d_active, d_bc, grad_log = scan_backward(
        delta, active, d_mixed, select, rate, decay, kept, block, step
    )
    d_raw = d_delta * jax.nn.sigmoid(delta_raw)
    grad_dt_bias = jnp.sum(d_raw, axis=0, keepdims=True)
    d_raw_low = d_raw.astype(bf16)
    grad_dt_proj = matmul(delta_low, d_raw_low, TN)
    partial = jnp.concatenate([matmul(d_raw_low, delta_weight, NT), d_bc], axis=1)
    d_select, _ = summed_over_seq(partial, lambda s: s.astype(bf16), ())
    grad_gate = scattered_sum(
        rows_of(matmul(normalized, d_gate_low, TN).astype(bf16), model // batch), "batch"
    )
    d_select, grad_gate = together((d_select, grad_gate))
    grad_x_proj = matmul(d_select, active, TN)
    d_active = d_active + d_mixed * skip_gain + matmul(d_select, select_weight)
    conv_sig = jax.nn.sigmoid(conv_out)
    d_conv = (d_active * conv_sig * (1.0 + conv_out * (1.0 - conv_sig))).astype(bf16)
    d_conv_f = d_conv.astype(f32)
    grad_conv_bias = jnp.sum(d_conv_f, axis=0, keepdims=True)
    grad_conv = jnp.stack(
        [
            jnp.sum(d_conv_f * padded[tap : tap + length].astype(f32), axis=0)
            for tap in range(taps)
        ]
    )
    extended = jnp.pad(d_conv, ((0, taps - 1), (0, 0)))
    d_inner = jnp.zeros((length, width), f32)
    for tap in range(taps):
        offset = taps - 1 - tap
        d_inner = d_inner + conv_taps[tap] * extended[offset : offset + length].astype(f32)
    d_inner = d_inner.astype(bf16)
    d_normalized = matmul(
        jnp.concatenate([d_inner, d_gate_low], axis=1),
        jnp.concatenate([input_weight, gate_weight], axis=1),
        NT,
    ).astype(bf16)
    grad_gate = grad_gate.astype(bf16).reshape(seq, in_rows, width)
    grad_gate = lax.all_to_all(grad_gate, "seq", 0, 0)
    d_normalized, d_inner, gated, grad_gate, grad_x_proj, branch = together(
        (d_normalized, d_inner, gated, grad_gate, grad_x_proj, branch)
    )
    grad_inner = matmul(normalized, d_inner, TN).astype(bf16)
    grad_inner = scattered_sum(rows_of(grad_inner, model // batch), "batch")
    grad_output = lax.psum_scatter(
        matmul(gated, upstream, TN).astype(bf16), "batch", scatter_dimension=0, tiled=True
    ).astype(f32)
    d_normalized, *last_terms = line_summed(rows_of(d_normalized, span), "seq")

    block_out = jnp.where(own_valid, own_stream + branch.astype(f32), 0.0)

    def columns_of(part):
        part = part.reshape(seq, in_rows, batch, own).transpose(1, 2, 0, 3)
        return part.reshape(in_rows, batch * seq * own).astype(f32)

    grad_inner = grad_inner.astype(bf16).reshape(seq, in_rows, width)
    grad_inner = lax.all_to_all(grad_inner, "seq", 0, 0)
    grad_input = jnp.concatenate([columns_of(grad_inner), columns_of(grad_gate)], axis=1)

    small_grads = jnp.concatenate(
        [grad_dt_proj, grad_x_proj, grad_log, grad_conv, grad_conv_bias, grad_dt_bias, grad_skip],
        axis=0,
    )
    small_grads = lax.psum_scatter(small_grads, "batch", scatter_dimension=1, tiled=True)
    g_dt_proj, g_x_proj, g_log, g_conv, g_conv_bias, g_dt_bias, g_skip = jnp.split(
        small_grads, cuts, axis=0
    )

    own_upstream = jnp.where(own_valid, cotangent[0].astype(f32), 0.0)
    own_scale = lax.rsqrt(jnp.mean(own_stream * own_stream, axis=-1, keepdims=True) + epsilon)
    grad_gain = jnp.sum(grad_input * in_proj.astype(f32), axis=1) / norm_gain.astype(f32)
    (
        d_normalized, g_dt_proj, g_x_proj, g_log, g_conv, g_conv_bias, g_dt_bias, g_skip,
        grad_input, grad_gain, grad_output,
    ) = together(
        (
            d_normalized, g_dt_proj, g_x_proj, g_log, g_conv, g_conv_bias, g_dt_bias, g_skip,
            grad_input, grad_gain, grad_output,
        )
    )
    for term in last_terms:
        d_normalized = d_normalized + term.astype(f32)
    d_hat = d_normalized * gain
    grad_tokens = (
        own_scale * d_hat
        - own_stream
        * own_scale
        * own_scale
        * own_scale
        * jnp.mean(d_hat * own_stream, axis=-1, keepdims=True)
        + own_upstream
    )
    return (
        block_out[None],
        grad_tokens[None],
        grad_gain,
        grad_input,
        g_conv,
        g_conv_bias[0],
        g_x_proj.T,
        g_dt_proj,
        g_dt_bias[0],
        g_log.T,
        g_skip[0],
        grad_output,
    )


def solution(mesh):
    placed = (
        P("batch", "seq", None),
        P("batch"),
        P(("batch", "seq")),
        P(("batch", "seq"), None),
        P(None, ("batch", "seq")),
        P(("batch", "seq")),
        P(("batch", "seq"), None),
        P(None, ("batch", "seq")),
        P(("batch", "seq")),
        P(("batch", "seq"), None),
        P(("batch", "seq")),
        P(("batch", "seq"), None),
        P("batch", "seq", None),
    )
    return jax.shard_map(
        on_device,
        mesh=mesh,
        in_specs=placed,
        out_specs=(
            P("batch", "seq", None),
            P("batch", "seq", None),
            P(("batch", "seq")),
            P(("batch", "seq"), None),
            P(None, ("batch", "seq")),
            P(("batch", "seq")),
            P(("batch", "seq"), None),
            P(None, ("batch", "seq")),
            P(("batch", "seq")),
            P(("batch", "seq"), None),
            P(("batch", "seq")),
            P(("batch", "seq"), None),
        ),
        check_vma=False,
    )
```

```python
import functools

import jax
import jax.numpy as jnp
from jax import lax
from jax.experimental import pallas as pl
from jax.experimental.pallas import tpu as pltpu
from jax.sharding import PartitionSpec as P

bf16, f32 = jnp.bfloat16, jnp.float32
NT = (((1,), (1,)), ((), ()))
LANES = 128
GROUP = 32
BLOCK = 128
epsilon = 1e-05
LOG2E = 1.4426950408889634


def spread(tile, row, lanes, states):
    return jnp.broadcast_to(tile[row : row + 1, lanes], (states, LANES))


def selectors(select, states):
    low = select.shape[1] - 4 * states
    middle = low + 2 * states
    block = select[:, low:middle].astype(f32) + select[:, middle:].astype(f32)
    return jnp.transpose(block), block[:, :states], block[:, states:]


def block_diagonal(values, step):
    rows, states = values.shape
    wide = step * states
    spread_out = (
        lax.broadcasted_iota(jnp.int32, (states, wide), 1) % states
        == lax.broadcasted_iota(jnp.int32, (states, wide), 0)
    ).astype(bf16)
    value = jnp.dot(values.astype(bf16), spread_out, preferred_element_type=f32)
    place = lax.broadcasted_iota(jnp.int32, (rows, wide), 0) % step
    owner = lax.broadcasted_iota(jnp.int32, (rows, wide), 1) // states
    return jnp.where(place == owner, value, 0.0).astype(bf16)


def forward_body(tiles, step, delta, active, select, rate, mixed, kept, state, drive, columns):
    rows, states = delta.shape[0], rate.shape[0]
    wide = step * states

    @pl.when(pl.program_id(0) == 0)
    def _():
        state[...] = jnp.zeros_like(state)

    turned, _, c_block = selectors(select[...], states)
    columns[...] = turned[:states]
    drive[...] = delta[...] * active[...].astype(f32)
    rates = [rate[:, k * LANES : (k + 1) * LANES] for k in range(tiles)]

    def group(number, held):
        held = list(held)
        base = pl.multiple_of(number * GROUP, GROUP)
        delta_now, drive_now = delta.at[pl.ds(base, GROUP), :], drive.at[pl.ds(base, GROUP), :]
        b_now = pltpu.roll(columns[...], rows - base, 1)
        for j in range(GROUP):
            b_wide = jnp.broadcast_to(b_now[:, j : j + 1], (states, LANES))
            for k in range(tiles):
                lanes = slice(k * LANES, (k + 1) * LANES)
                decay = jnp.exp2(spread(delta_now, j, lanes, states) * rates[k])
                held[k] = decay * held[k] + spread(drive_now, j, lanes, states) * b_wide
                at = pl.ds(pl.multiple_of((base + j) * states, states), states)
                kept[at, lanes] = held[k].astype(bf16)
        return tuple(held)

    held = lax.fori_loop(
        0,
        rows // GROUP,
        group,
        tuple(state[:, k * LANES : (k + 1) * LANES] for k in range(tiles)),
    )
    for k in range(tiles):
        state[:, k * LANES : (k + 1) * LANES] = held[k]
    c_diag = block_diagonal(c_block, step)
    for q in range(rows // step):
        part = kept[q * wide : (q + 1) * wide, :]
        spot = slice(q * step, (q + 1) * step)
        mixed[spot, :] = jnp.dot(c_diag[spot, :], part, preferred_element_type=f32)


def scan_forward(delta, active, select, rate, block, step):
    length, width = delta.shape
    states = rate.shape[0]
    tiles = width // LANES
    return pl.pallas_call(
        functools.partial(forward_body, tiles, step),
        grid=(length // block,),
        in_specs=[
            pl.BlockSpec((block, width), lambda i: (i, 0)),
            pl.BlockSpec((block, width), lambda i: (i, 0)),
            pl.BlockSpec((block, select.shape[1]), lambda i: (i, 0)),
            pl.BlockSpec((states, width), lambda i: (0, 0)),
        ],
        out_specs=[
            pl.BlockSpec((block, width), lambda i: (i, 0)),
            pl.BlockSpec((block * states, width), lambda i: (i, 0)),
        ],
        out_shape=[
            jax.ShapeDtypeStruct((length, width), f32),
            jax.ShapeDtypeStruct((length * states, width), bf16),
        ],
        scratch_shapes=[
            pltpu.VMEM((states, width), f32),
            pltpu.VMEM((block, width), f32),
            pltpu.VMEM((states, block), f32),
        ],
        compiler_params=pltpu.CompilerParams(vmem_limit_bytes=48 << 20),
        cost_estimate=pl.CostEstimate(
            flops=8 * length * width * states,
            transcendentals=length * width * states,
            bytes_accessed=length * width * (2 * states + 10),
        ),
        name="scan_forward",
    )(delta, active, select, rate)


FEW = 4


def backward_body(
    tiles, step, delta, active, d_mixed, select, rate, decay_rate, kept, kept_before,
    d_delta, d_active, d_bc, d_log, push, drive, columns, diagonals, folding, timed, *pairs,
):
    grads, rated = pairs[:2], pairs[2:]
    rows, states = delta.shape[0], rate.shape[0]
    blocks = pl.num_programs(0)
    first = pl.program_id(0) == blocks - 1
    wide = step * states

    @pl.when(pl.program_id(0) == 0)
    def _():
        push[...] = jnp.zeros_like(push)
        d_log[...] = jnp.zeros_like(d_log)

    turned, b_block, _ = selectors(select[...], states)
    columns[...] = turned[states:]
    drive[...] = delta[...] * active[...].astype(f32)
    rates = [rate[:, k * LANES : (k + 1) * LANES] for k in range(tiles)]
    own_rates = [decay_rate[:, k * LANES : (k + 1) * LANES].astype(bf16) for k in range(tiles)]

    place = lax.broadcasted_iota(jnp.int32, (step, wide), 0)
    owner = lax.broadcasted_iota(jnp.int32, (step, wide), 1) // states
    ones_diag = (place == owner).astype(bf16)
    diag = (place == owner).astype(f32)
    diagonals[...] = block_diagonal(b_block, step)

    def sums_of(number):
        held, through_of = number % 2, {}

        def spots(q):
            at = number * GROUP + q * step
            tall = slice(q * wide, (q + 1) * wide)
            return slice(at, at + step), tall

        def through(q):
            spot, tall = spots(q)
            value = jnp.dot(diagonals[spot, :], grads[held][tall, :], preferred_element_type=f32)
            d_active[spot, :] = delta[spot, :] * value
            through_of[q] = active[spot, :].astype(f32) * value

        def summed(q):
            spot, tall = spots(q)
            value = jnp.dot(ones_diag, rated[held][tall, :], preferred_element_type=f32)
            d_delta[spot, :] = value + through_of[q]

        def d_b(q):
            spot, tall = spots(q)
            folding[spot, :wide] = diag * lax.dot_general(
                drive[spot, :].astype(bf16), grads[held][tall, :], NT, preferred_element_type=f32
            )

        def d_c(q):
            spot, _ = spots(q)
            own = slice(spot.start * states, spot.stop * states)
            folding[spot, wide:] = diag * lax.dot_general(
                d_mixed[spot, :].astype(bf16), kept[own, :], NT, preferred_element_type=f32
            )

        return [
            functools.partial(part, q)
            for q in range(GROUP // step)
            for part in (through, summed, d_b, d_c)
        ]

    carry = [push[:, k * LANES : (k + 1) * LANES] for k in range(tiles)]
    waiting = []
    for number in reversed(range(rows // GROUP)):
        pace = GROUP // max(len(waiting), 1)
        sums = [None] * tiles
        held = number % 2
        for j in reversed(range(GROUP)):
            row = number * GROUP + j
            c_wide = jnp.broadcast_to(columns[:, row : row + 1], (states, LANES))
            at = slice(j * states, (j + 1) * states)
            for k in range(tiles):
                lanes = slice(k * LANES, (k + 1) * LANES)
                if row:
                    before = kept[(row - 1) * states : row * states, lanes]
                else:
                    before = jnp.where(first, jnp.zeros((), bf16), kept_before[:, lanes])
                step_size = spread(delta, row, lanes, states)
                grad = spread(d_mixed, row, lanes, states) * c_wide + carry[k]
                carry[k] = jnp.exp2(step_size * rates[k]) * grad
                grads[held][at, lanes] = grad.astype(bf16)
                rated_now = carry[k].astype(bf16) * before * own_rates[k]
                rated[held][at, lanes] = rated_now
                timed_now = rated_now * step_size.astype(bf16)
                sums[k] = timed_now if sums[k] is None else sums[k] + timed_now
                if j % FEW == 0:
                    spot = row // FEW * states
                    timed[spot : spot + states, lanes] = sums[k]
                    sums[k] = None
            if waiting and j % pace == 0:
                waiting.pop(0)()
        while waiting:
            waiting.pop(0)()
        waiting = sums_of(number)
    while waiting:
        waiting.pop(0)()
    for k in range(tiles):
        push[:, k * LANES : (k + 1) * LANES] = carry[k]
    fold = (
        lax.broadcasted_iota(jnp.int32, (wide, states), 0) % states
        == lax.broadcasted_iota(jnp.int32, (wide, states), 1)
    ).astype(bf16)
    for number in range(2):
        value = folding[:, number * wide : (number + 1) * wide]
        high = value.astype(bf16)
        d_bc[:, number * states : (number + 1) * states] = jnp.dot(
            high, fold, preferred_element_type=f32
        )
    span = rows // FEW * states
    pick = (
        lax.broadcasted_iota(jnp.int32, (states, span), 1) % states
        == lax.broadcasted_iota(jnp.int32, (states, span), 0)
    ).astype(bf16)
    d_log[...] += jnp.dot(pick, timed[...], preferred_element_type=f32)


def scan_backward(delta, active, d_mixed, select, rate, decay_rate, kept, block, step):
    length, width = delta.shape
    states = rate.shape[0]
    tiles = width // LANES
    blocks = length // block
    back = lambda i: (blocks - 1 - i, 0)
    return pl.pallas_call(
        functools.partial(backward_body, tiles, step),
        grid=(blocks,),
        in_specs=[
            pl.BlockSpec((block, width), back),
            pl.BlockSpec((block, width), back),
            pl.BlockSpec((block, width), back),
            pl.BlockSpec((block, select.shape[1]), back),
            pl.BlockSpec((states, width), lambda i: (0, 0)),
            pl.BlockSpec((states, width), lambda i: (0, 0)),
            pl.BlockSpec((block * states, width), back),
            pl.BlockSpec(
                (states, width), lambda i: (jnp.maximum((blocks - 1 - i) * block - 1, 0), 0)
            ),
        ],
        out_specs=[
            pl.BlockSpec((block, width), back),
            pl.BlockSpec((block, width), back),
            pl.BlockSpec((block, 2 * states), back),
            pl.BlockSpec((states, width), lambda i: (0, 0)),
        ],
        out_shape=[
            jax.ShapeDtypeStruct((length, width), f32),
            jax.ShapeDtypeStruct((length, width), f32),
            jax.ShapeDtypeStruct((length, 2 * states), f32),
            jax.ShapeDtypeStruct((states, width), f32),
        ],
        scratch_shapes=[
            pltpu.VMEM((states, width), f32),
            pltpu.VMEM((block, width), f32),
            pltpu.VMEM((states, block), f32),
            pltpu.VMEM((block, step * states), bf16),
            pltpu.VMEM((block, 2 * step * states), f32),
            pltpu.VMEM((block // FEW * states, width), bf16),
        ]
        + [pltpu.VMEM((GROUP * states, width), bf16)] * 4,
        compiler_params=pltpu.CompilerParams(vmem_limit_bytes=48 << 20),
        cost_estimate=pl.CostEstimate(
            flops=20 * length * width * states,
            transcendentals=length * width * states,
            bytes_accessed=length * width * (2 * states + 20),
        ),
        name="scan_backward",
    )(delta, active, d_mixed, select, rate, decay_rate, kept, kept)


together = lax.optimization_barrier


def inner_swap(value, axis):
    count = lax.axis_size(axis)
    return lax.ppermute(value, axis, [(i, i ^ 1) for i in range(count)])


def outer_shift(value, axis, steps):
    count = lax.axis_size(axis)
    half = count // 2
    pairs = [(i, (i // 2 + steps) % half * 2 + i % 2) for i in range(count)]
    return lax.ppermute(value, axis, pairs)


def shift_order(half):
    return sorted(range(1, half), key=lambda k: (-min(k, half - k), k))


def pieces_of_all(own, axis):
    count = lax.axis_size(axis)
    place = lax.axis_index(axis)
    half = count // 2
    outer, inner = place // 2, place % 2
    yield place, own
    arrived = {k: outer_shift(own, axis, k) for k in shift_order(half)}
    yield outer * 2 + 1 - inner, inner_swap(own, axis)
    for k, piece in arrived.items():
        origin = (outer - k + half) % half
        yield origin * 2 + inner, piece
    for k, piece in arrived.items():
        origin = (outer - k + half) % half
        yield origin * 2 + 1 - inner, inner_swap(piece, axis)


def gathered(own, axis, dim=0):
    count, size = lax.axis_size(axis), own.shape[dim]
    whole = jnp.zeros(own.shape[:dim] + (count * size,) + own.shape[dim + 1 :], own.dtype)
    for place, piece in pieces_of_all(own, axis):
        whole = lax.dynamic_update_slice_in_dim(whole, piece, place * size, dim)
    return whole


def hop(value, axis, moves):
    pairs = [(a * 2 + i, b * 2 + i) for a, b in moves for i in (0, 1)]
    return lax.ppermute(value, axis, pairs)


def swap_at(value, axis, spots):
    pairs = [(a * 2 + i, a * 2 + 1 - i) for a in spots for i in (0, 1)]
    return lax.ppermute(value, axis, pairs)


UP, DOWN = [(0, 1), (1, 2), (2, 3)], [(1, 0), (2, 1), (3, 2)]


def line_gathered(own, axis, held):
    if lax.axis_size(axis) != 8:
        return own, lambda own: own, lambda own, _: lax.all_gather(own, axis, axis=0, tiled=True), held
    place = lax.axis_index(axis)
    z, x = place // 2, place % 2
    rows = own.shape[0]
    upper, edge = z >= 2, (z == 0) | (z == 3)
    across = jnp.where(upper, z - 2, z + 2)
    far = jnp.where(z == 3, 0, 3)

    def put(whole, piece, spot, side):
        return lax.dynamic_update_slice_in_dim(whole, piece, (spot * 2 + side) * rows, 0)

    def put_far(whole, piece, side):
        held = lax.dynamic_slice_in_dim(whole, (far * 2 + side) * rows, rows, 0)
        return put(whole, jnp.where(edge, piece, held), far, side)

    whole = jnp.zeros((8 * rows,) + own.shape[1:], own.dtype)
    up, down, other, held = together(
        (hop(own, axis, UP), hop(own, axis, DOWN), swap_at(own, axis, range(4)), held)
    )
    up_two, down_two = hop(up, axis, UP[1:]), hop(down, axis, DOWN[:2])
    other_up, other_down = swap_at(up, axis, (1, 2, 3)), swap_at(down, axis, (0, 1, 2))
    whole = put(put(whole, own, z, x), other, z, 1 - x)
    whole = put(put(whole, up, (z + 3) % 4, x), down, (z + 1) % 4, x)
    two = jnp.where(upper, up_two, down_two)
    three = hop(two, axis, [(2, 3), (1, 0)])
    other_two = swap_at(two, axis, range(4))
    whole = put(put(whole, other_up, (z + 3) % 4, 1 - x), other_down, (z + 1) % 4, 1 - x)
    whole = put(whole, two, across, x)

    def end(last, other_three):
        three, other_two = last
        ended = put(whole, other_two, across, 1 - x)
        return put_far(put_far(ended, three, x), other_three, 1 - x)

    return (three, other_two), lambda last: swap_at(last[0], axis, (0, 3)), end, held


def line_summed(part_of, axis):
    if lax.axis_size(axis) != 8:
        return (scattered_sum(part_of, axis),)
    place = lax.axis_index(axis)
    z, x = place // 2, place % 2
    upper, edge = z >= 2, (z == 0) | (z == 3)
    across = jnp.where(upper, z - 2, z + 2)
    far = jnp.where(z == 0, 3, 0)
    above, below = jnp.minimum(z + 1, 3), jnp.maximum(z - 1, 0)

    def swapped(spot, spots):
        return swap_at(part_of(spot * 2 + 1 - x), axis, spots)

    def added(spot, given):
        return part_of(spot * 2 + x).astype(f32) + given.astype(f32)

    given_far = swapped(far, (0, 3))
    given_across = swapped(across, range(4))
    given_above, given_below = swapped(above, (0, 1, 2)), swapped(below, (1, 2, 3))
    given_own = swapped(z, range(4))
    three = hop(added(far, given_far).astype(bf16), axis, [(0, 1), (3, 2)])
    three, given_across = together((three, given_across))
    two = added(across, given_across) + jnp.where(edge, 0.0, three.astype(f32))
    two = two.astype(bf16)
    two_up, two_down, given_above, given_below = together(
        (hop(two, axis, UP[:2]), hop(two, axis, DOWN[1:]), given_above, given_below)
    )
    one_up = (added(above, given_above) + two_up.astype(f32)).astype(bf16)
    one_down = (added(below, given_below) + two_down.astype(f32)).astype(bf16)
    return added(z, given_own), hop(one_up, axis, UP), hop(one_down, axis, DOWN)


def scattered_sum(part_of, axis):
    count = lax.axis_size(axis)
    place = lax.axis_index(axis)
    half = count // 2
    outer, inner = place // 2, place % 2
    total = None
    for k in shift_order(half) + [0]:
        target = (outer + k) % half
        given = inner_swap(part_of(target * 2 + 1 - inner), axis)
        piece = part_of(target * 2 + inner).astype(f32) + given.astype(f32)
        if k:
            piece = outer_shift(piece.astype(bf16), axis, k).astype(f32)
        total = piece if total is None else total + piece
    return total


def rows_of(value, rows):
    return lambda place: lax.dynamic_slice_in_dim(value, place * rows, rows, 0)


def summed_over_seq(part, change):
    count = lax.axis_size("seq")
    length, columns = part.shape
    part = part.astype(bf16).reshape(count, length // count, columns)
    own = change(jnp.sum(lax.all_to_all(part, "seq", 0, 0).astype(f32), axis=0))
    return shared(own, "seq").reshape(length, own.shape[1])


def two_terms(value):
    high = value.astype(bf16)
    return [high, (value - high.astype(f32)).astype(bf16)]


def shared(own, axis):
    wide = jnp.broadcast_to(own[None], (lax.axis_size(axis),) + own.shape)
    return lax.all_to_all(wide, axis, 0, 0)


def matmul(a, b, dims=(((1,), (0,)), ((), ()))):
    return lax.dot_general(a, b, dims, preferred_element_type=f32)


TN = (((0,), (0,)), ((), ()))


def on_device(
    tokens,
    lengths,
    norm_gain,
    in_proj,
    conv_weight,
    conv_bias,
    x_proj,
    dt_proj,
    dt_bias,
    a_log,
    skip,
    out_proj,
    cotangent,
):
    batch, seq = lax.axis_size("batch"), lax.axis_size("seq")
    place = lax.axis_index("seq")
    span, model = tokens.shape[1:]
    length = span * seq
    in_rows = in_proj.shape[0]
    own = skip.shape[0]
    taps = conv_weight.shape[0]
    rank = dt_proj.shape[0]
    states = a_log.shape[1]
    width = own * batch

    halves = in_proj.reshape(in_rows, 2, batch, seq, own).transpose(1, 3, 0, 2, 4)
    halves = halves.reshape(2, seq, in_rows, width)
    beside = jnp.broadcast_to(norm_gain[None, :, None], (seq, in_rows, LANES))
    columns = lax.all_to_all(jnp.concatenate([halves[0], beside], axis=2), "seq", 0, 0)
    columns, gate_columns = together((columns, halves[1]))
    gate_columns = lax.all_to_all(gate_columns, "seq", 0, 0)
    last_hop, last_swap, end_gather, (dt_proj, x_proj, out_proj) = line_gathered(
        cotangent[0], "seq", (dt_proj, x_proj, out_proj)
    )
    small = jnp.concatenate(
        [
            dt_proj,
            x_proj.T,
            a_log.T,
            conv_weight,
            conv_bias[None],
            dt_bias[None],
            skip[None],
        ],
        axis=0,
    )
    small = gathered(small, "batch", 1)
    cuts = [rank, 2 * rank + 2 * states, 2 * rank + 3 * states]
    cuts = cuts + [cuts[2] + taps + i for i in range(3)]
    delta_weight, select_weight, decay_logs, conv_taps, conv_shift, delta_shift, skip_gain = (
        jnp.split(small, cuts, axis=0)
    )
    conv_taps, conv_shift = conv_taps.astype(f32), conv_shift.astype(f32)
    delta_shift, skip_gain = delta_shift.astype(f32), skip_gain.astype(f32)
    decay = -jnp.exp(decay_logs.astype(f32))
    input_weight = gathered(columns.reshape(seq * in_rows, width + LANES), "batch")
    one = (jnp.arange(LANES) == 0).astype(bf16)[None]
    gain = matmul(one, input_weight[:, width:], NT)
    input_weight = input_weight[:, :width]
    gate_weight = gathered(gate_columns.reshape(seq * in_rows, width), "batch")

    def normed(rows):
        rows = rows.astype(f32)
        scale = lax.rsqrt(jnp.mean(rows * rows, axis=-1, keepdims=True) + epsilon)
        return (rows * scale * gain).astype(bf16)

    stream = lax.all_gather(tokens[0], "seq", axis=0, tiled=True)
    normalized = normed(stream)
    output_weight = gathered(out_proj, "batch")

    valid = (jnp.arange(length, dtype=jnp.int32) < lengths[0])[:, None]
    inner = matmul(normalized, input_weight).astype(bf16)
    padded = jnp.pad(inner, ((taps - 1, 0), (0, 0)))
    conv_out = conv_shift + jnp.zeros((length, width), f32)
    for tap in range(taps):
        conv_out = conv_out + conv_taps[tap] * padded[tap : tap + length].astype(f32)
    active = jax.nn.silu(conv_out).astype(bf16)
    active_f = active.astype(f32)

    partial, last_hop, gate_weight = together(
        (matmul(active, select_weight, NT), last_hop, gate_weight)
    )
    select = summed_over_seq(
        partial,
        lambda s: jnp.concatenate([s[:, :rank].astype(bf16)] + two_terms(s[:, rank:]), axis=1),
    )
    gate_low = matmul(normalized, gate_weight).astype(bf16)
    select, gate_low, last_hop = together((select, gate_low, last_hop))
    last = last_swap(last_hop)
    gate = gate_low.astype(f32)
    gate_sig = jax.nn.sigmoid(gate)
    delta_low = select[:, :rank]
    delta_raw = matmul(delta_low, delta_weight) + delta_shift
    delta = jax.nn.softplus(delta_raw)

    block = min(BLOCK, length)
    step = 256 // states
    rate = decay * LOG2E
    mixed, kept = scan_forward(delta, active, select, rate, block, step)
    mixed = mixed + skip_gain * active_f
    gated = (mixed * gate * gate_sig).astype(bf16)
    branch = matmul(gated, output_weight).astype(bf16)
    branch, last_hop, last = together((branch, last_hop, last))
    branch = lax.psum_scatter(branch, "seq", scatter_dimension=0, tiled=True)
    own_valid = lax.dynamic_slice_in_dim(valid, place * span, span, 0)
    own_stream = tokens[0].astype(f32)

    upstream = jnp.where(valid, end_gather(last_hop, last), 0).astype(bf16)
    d_gated = matmul(upstream, output_weight, NT)
    d_mixed = d_gated * gate * gate_sig
    d_gate = d_gated * mixed * gate_sig * (1.0 + gate * (1.0 - gate_sig))
    grad_skip = jnp.sum(d_mixed * active_f, axis=0, keepdims=True)
    d_gate_low = d_gate.astype(bf16)

    d_delta, d_active, d_bc, grad_log = scan_backward(
        delta, active, d_mixed, select, rate, decay, kept, block, step
    )
    d_raw = d_delta * jax.nn.sigmoid(delta_raw)
    grad_dt_bias = jnp.sum(d_raw, axis=0, keepdims=True)
    d_raw_low = d_raw.astype(bf16)
    grad_dt_proj = matmul(delta_low, d_raw_low, TN)
    partial = jnp.concatenate([matmul(d_raw_low, delta_weight, NT), d_bc], axis=1)
    d_select = summed_over_seq(partial, lambda s: s.astype(bf16))
    grad_gate = scattered_sum(
        rows_of(matmul(normalized, d_gate_low, TN).astype(bf16), model // batch), "batch"
    )
    d_select, grad_gate = together((d_select, grad_gate))
    grad_x_proj = matmul(d_select, active, TN)
    d_active = d_active + d_mixed * skip_gain + matmul(d_select, select_weight)
    conv_sig = jax.nn.sigmoid(conv_out)
    d_conv = (d_active * conv_sig * (1.0 + conv_out * (1.0 - conv_sig))).astype(bf16)
    d_conv_f = d_conv.astype(f32)
    grad_conv_bias = jnp.sum(d_conv_f, axis=0, keepdims=True)
    grad_conv = jnp.stack(
        [
            jnp.sum(d_conv_f * padded[tap : tap + length].astype(f32), axis=0)
            for tap in range(taps)
        ]
    )
    extended = jnp.pad(d_conv, ((0, taps - 1), (0, 0)))
    d_inner = jnp.zeros((length, width), f32)
    for tap in range(taps):
        offset = taps - 1 - tap
        d_inner = d_inner + conv_taps[tap] * extended[offset : offset + length].astype(f32)
    d_inner = d_inner.astype(bf16)
    d_normalized = matmul(
        jnp.concatenate([d_inner, d_gate_low], axis=1),
        jnp.concatenate([input_weight, gate_weight], axis=1),
        NT,
    ).astype(bf16)
    grad_gate = grad_gate.astype(bf16).reshape(seq, in_rows, width)
    grad_gate = lax.all_to_all(grad_gate, "seq", 0, 0)
    d_normalized, d_inner, gated, grad_gate, grad_x_proj, branch = together(
        (d_normalized, d_inner, gated, grad_gate, grad_x_proj, branch)
    )
    grad_inner = matmul(normalized, d_inner, TN).astype(bf16)
    grad_inner = scattered_sum(rows_of(grad_inner, model // batch), "batch")
    grad_output = lax.psum_scatter(
        matmul(gated, upstream, TN).astype(bf16), "batch", scatter_dimension=0, tiled=True
    ).astype(f32)
    d_normalized, *last_terms = line_summed(rows_of(d_normalized, span), "seq")

    block_out = jnp.where(own_valid, own_stream + branch.astype(f32), 0.0)

    def columns_of(part):
        part = part.reshape(seq, in_rows, batch, own).transpose(1, 2, 0, 3)
        return part.reshape(in_rows, batch * seq * own).astype(f32)

    grad_inner = grad_inner.astype(bf16).reshape(seq, in_rows, width)
    grad_inner = lax.all_to_all(grad_inner, "seq", 0, 0)
    grad_input = jnp.concatenate([columns_of(grad_inner), columns_of(grad_gate)], axis=1)

    small_grads = jnp.concatenate(
        [grad_dt_proj, grad_x_proj, grad_log, grad_conv, grad_conv_bias, grad_dt_bias, grad_skip],
        axis=0,
    )
    small_grads = lax.psum_scatter(small_grads, "batch", scatter_dimension=1, tiled=True)
    g_dt_proj, g_x_proj, g_log, g_conv, g_conv_bias, g_dt_bias, g_skip = jnp.split(
        small_grads, cuts, axis=0
    )

    own_upstream = jnp.where(own_valid, cotangent[0].astype(f32), 0.0)
    own_scale = lax.rsqrt(jnp.mean(own_stream * own_stream, axis=-1, keepdims=True) + epsilon)
    grad_gain = jnp.sum(grad_input * in_proj.astype(f32), axis=1) / norm_gain.astype(f32)
    (
        d_normalized, g_dt_proj, g_x_proj, g_log, g_conv, g_conv_bias, g_dt_bias, g_skip,
        grad_input, grad_gain, grad_output,
    ) = together(
        (
            d_normalized, g_dt_proj, g_x_proj, g_log, g_conv, g_conv_bias, g_dt_bias, g_skip,
            grad_input, grad_gain, grad_output,
        )
    )
    for term in last_terms:
        d_normalized = d_normalized + term.astype(f32)
    d_hat = d_normalized * gain
    grad_tokens = (
        own_scale * d_hat
        - own_stream
        * own_scale
        * own_scale
        * own_scale
        * jnp.mean(d_hat * own_stream, axis=-1, keepdims=True)
        + own_upstream
    )
    return (
        block_out[None],
        grad_tokens[None],
        grad_gain,
        grad_input,
        g_conv,
        g_conv_bias[0],
        g_x_proj.T,
        g_dt_proj,
        g_dt_bias[0],
        g_log.T,
        g_skip[0],
        grad_output,
    )


def solution(mesh):
    placed = (
        P("batch", "seq", None),
        P("batch"),
        P(("batch", "seq")),
        P(("batch", "seq"), None),
        P(None, ("batch", "seq")),
        P(("batch", "seq")),
        P(("batch", "seq"), None),
        P(None, ("batch", "seq")),
        P(("batch", "seq")),
        P(("batch", "seq"), None),
        P(("batch", "seq")),
        P(("batch", "seq"), None),
        P("batch", "seq", None),
    )
    return jax.shard_map(
        on_device,
        mesh=mesh,
        in_specs=placed,
        out_specs=(
            P("batch", "seq", None),
            P("batch", "seq", None),
            P(("batch", "seq")),
            P(("batch", "seq"), None),
            P(None, ("batch", "seq")),
            P(("batch", "seq")),
            P(("batch", "seq"), None),
            P(None, ("batch", "seq")),
            P(("batch", "seq")),
            P(("batch", "seq"), None),
            P(("batch", "seq")),
            P(("batch", "seq"), None),
        ),
        check_vma=False,
    )
```

```python
import functools

import jax
import jax.numpy as jnp
from jax import lax
from jax.experimental import pallas as pl
from jax.experimental.pallas import tpu as pltpu
from jax.sharding import PartitionSpec as P

bf16, f32 = jnp.bfloat16, jnp.float32
NT = (((1,), (1,)), ((), ()))
LANES = 128
GROUP = 32
BLOCK = 128
epsilon = 1e-05
LOG2E = 1.4426950408889634


def spread(tile, row, lanes, states):
    return jnp.broadcast_to(tile[row : row + 1, lanes], (states, LANES))


def selectors(select, states):
    low = select.shape[1] - 4 * states
    middle = low + 2 * states
    block = select[:, low:middle].astype(f32) + select[:, middle:].astype(f32)
    return jnp.transpose(block), block[:, :states], block[:, states:]


def block_diagonal(values, step):
    rows, states = values.shape
    wide = step * states
    spread_out = (
        lax.broadcasted_iota(jnp.int32, (states, wide), 1) % states
        == lax.broadcasted_iota(jnp.int32, (states, wide), 0)
    ).astype(bf16)
    value = jnp.dot(values.astype(bf16), spread_out, preferred_element_type=f32)
    place = lax.broadcasted_iota(jnp.int32, (rows, wide), 0) % step
    owner = lax.broadcasted_iota(jnp.int32, (rows, wide), 1) // states
    return jnp.where(place == owner, value, 0.0).astype(bf16)


def forward_body(tiles, step, delta, active, select, rate, mixed, kept, state, drive, columns):
    rows, states = delta.shape[0], rate.shape[0]
    wide = step * states

    @pl.when(pl.program_id(0) == 0)
    def _():
        state[...] = jnp.zeros_like(state)

    turned, _, c_block = selectors(select[...], states)
    columns[...] = turned[:states]
    drive[...] = delta[...] * active[...].astype(f32)
    rates = [rate[:, k * LANES : (k + 1) * LANES] for k in range(tiles)]

    def group(number, held):
        held = list(held)
        base = pl.multiple_of(number * GROUP, GROUP)
        delta_now, drive_now = delta.at[pl.ds(base, GROUP), :], drive.at[pl.ds(base, GROUP), :]
        b_now = pltpu.roll(columns[...], rows - base, 1)
        for j in range(GROUP):
            b_wide = jnp.broadcast_to(b_now[:, j : j + 1], (states, LANES))
            for k in range(tiles):
                lanes = slice(k * LANES, (k + 1) * LANES)
                decay = jnp.exp2(spread(delta_now, j, lanes, states) * rates[k])
                held[k] = decay * held[k] + spread(drive_now, j, lanes, states) * b_wide
                at = pl.ds(pl.multiple_of((base + j) * states, states), states)
                kept[at, lanes] = held[k].astype(bf16)
        return tuple(held)

    held = lax.fori_loop(
        0,
        rows // GROUP,
        group,
        tuple(state[:, k * LANES : (k + 1) * LANES] for k in range(tiles)),
    )
    for k in range(tiles):
        state[:, k * LANES : (k + 1) * LANES] = held[k]
    c_diag = block_diagonal(c_block, step)
    for q in range(rows // step):
        part = kept[q * wide : (q + 1) * wide, :]
        spot = slice(q * step, (q + 1) * step)
        mixed[spot, :] = jnp.dot(c_diag[spot, :], part, preferred_element_type=f32)


def scan_forward(delta, active, select, rate, block, step):
    length, width = delta.shape
    states = rate.shape[0]
    tiles = width // LANES
    return pl.pallas_call(
        functools.partial(forward_body, tiles, step),
        grid=(length // block,),
        in_specs=[
            pl.BlockSpec((block, width), lambda i: (i, 0)),
            pl.BlockSpec((block, width), lambda i: (i, 0)),
            pl.BlockSpec((block, select.shape[1]), lambda i: (i, 0)),
            pl.BlockSpec((states, width), lambda i: (0, 0)),
        ],
        out_specs=[
            pl.BlockSpec((block, width), lambda i: (i, 0)),
            pl.BlockSpec((block * states, width), lambda i: (i, 0)),
        ],
        out_shape=[
            jax.ShapeDtypeStruct((length, width), f32),
            jax.ShapeDtypeStruct((length * states, width), bf16),
        ],
        scratch_shapes=[
            pltpu.VMEM((states, width), f32),
            pltpu.VMEM((block, width), f32),
            pltpu.VMEM((states, block), f32),
        ],
        compiler_params=pltpu.CompilerParams(vmem_limit_bytes=48 << 20),
        cost_estimate=pl.CostEstimate(
            flops=8 * length * width * states,
            transcendentals=length * width * states,
            bytes_accessed=length * width * (2 * states + 10),
        ),
        name="scan_forward",
    )(delta, active, select, rate)


FEW = 4


def backward_body(
    tiles, step, delta, active, d_mixed, select, rate, decay_rate, kept, kept_before,
    d_delta, d_active, d_bc, d_log, push, drive, columns, diagonals, folding, timed, *pairs,
):
    grads, rated = pairs[:2], pairs[2:]
    rows, states = delta.shape[0], rate.shape[0]
    blocks = pl.num_programs(0)
    first = pl.program_id(0) == blocks - 1
    wide = step * states

    @pl.when(pl.program_id(0) == 0)
    def _():
        push[...] = jnp.zeros_like(push)
        d_log[...] = jnp.zeros_like(d_log)

    turned, b_block, _ = selectors(select[...], states)
    columns[...] = turned[states:]
    drive[...] = delta[...] * active[...].astype(f32)
    rates = [rate[:, k * LANES : (k + 1) * LANES] for k in range(tiles)]
    own_rates = [decay_rate[:, k * LANES : (k + 1) * LANES].astype(bf16) for k in range(tiles)]

    place = lax.broadcasted_iota(jnp.int32, (step, wide), 0)
    owner = lax.broadcasted_iota(jnp.int32, (step, wide), 1) // states
    ones_diag = (place == owner).astype(bf16)
    diag = (place == owner).astype(f32)
    diagonals[...] = block_diagonal(b_block, step)

    def sums_of(number):
        held, through_of = number % 2, {}

        def spots(q):
            at = number * GROUP + q * step
            tall = slice(q * wide, (q + 1) * wide)
            return slice(at, at + step), tall

        def through(q):
            spot, tall = spots(q)
            value = jnp.dot(diagonals[spot, :], grads[held][tall, :], preferred_element_type=f32)
            d_active[spot, :] = delta[spot, :] * value
            through_of[q] = active[spot, :].astype(f32) * value

        def summed(q):
            spot, tall = spots(q)
            value = jnp.dot(ones_diag, rated[held][tall, :], preferred_element_type=f32)
            d_delta[spot, :] = value + through_of[q]

        def d_b(q):
            spot, tall = spots(q)
            folding[spot, :wide] = diag * lax.dot_general(
                drive[spot, :].astype(bf16), grads[held][tall, :], NT, preferred_element_type=f32
            )

        def d_c(q):
            spot, _ = spots(q)
            own = slice(spot.start * states, spot.stop * states)
            folding[spot, wide:] = diag * lax.dot_general(
                d_mixed[spot, :].astype(bf16), kept[own, :], NT, preferred_element_type=f32
            )

        return [
            functools.partial(part, q)
            for q in range(GROUP // step)
            for part in (through, summed, d_b, d_c)
        ]

    carry = [push[:, k * LANES : (k + 1) * LANES] for k in range(tiles)]
    waiting = []
    for number in reversed(range(rows // GROUP)):
        pace = GROUP // max(len(waiting), 1)
        sums = [None] * tiles
        held = number % 2
        for j in reversed(range(GROUP)):
            row = number * GROUP + j
            c_wide = jnp.broadcast_to(columns[:, row : row + 1], (states, LANES))
            at = slice(j * states, (j + 1) * states)
            for k in range(tiles):
                lanes = slice(k * LANES, (k + 1) * LANES)
                if row:
                    before = kept[(row - 1) * states : row * states, lanes]
                else:
                    before = jnp.where(first, jnp.zeros((), bf16), kept_before[:, lanes])
                step_size = spread(delta, row, lanes, states)
                grad = spread(d_mixed, row, lanes, states) * c_wide + carry[k]
                carry[k] = jnp.exp2(step_size * rates[k]) * grad
                grads[held][at, lanes] = grad.astype(bf16)
                rated_now = carry[k].astype(bf16) * before * own_rates[k]
                rated[held][at, lanes] = rated_now
                timed_now = rated_now * step_size.astype(bf16)
                sums[k] = timed_now if sums[k] is None else sums[k] + timed_now
                if j % FEW == 0:
                    spot = row // FEW * states
                    timed[spot : spot + states, lanes] = sums[k]
                    sums[k] = None
            if waiting and j % pace == 0:
                waiting.pop(0)()
        while waiting:
            waiting.pop(0)()
        waiting = sums_of(number)
    while waiting:
        waiting.pop(0)()
    for k in range(tiles):
        push[:, k * LANES : (k + 1) * LANES] = carry[k]
    fold = (
        lax.broadcasted_iota(jnp.int32, (wide, states), 0) % states
        == lax.broadcasted_iota(jnp.int32, (wide, states), 1)
    ).astype(bf16)
    for number in range(2):
        value = folding[:, number * wide : (number + 1) * wide]
        high = value.astype(bf16)
        d_bc[:, number * states : (number + 1) * states] = jnp.dot(
            high, fold, preferred_element_type=f32
        )
    span = rows // FEW * states
    pick = (
        lax.broadcasted_iota(jnp.int32, (states, span), 1) % states
        == lax.broadcasted_iota(jnp.int32, (states, span), 0)
    ).astype(bf16)
    d_log[...] += jnp.dot(pick, timed[...], preferred_element_type=f32)


def scan_backward(delta, active, d_mixed, select, rate, decay_rate, kept, block, step):
    length, width = delta.shape
    states = rate.shape[0]
    tiles = width // LANES
    blocks = length // block
    back = lambda i: (blocks - 1 - i, 0)
    return pl.pallas_call(
        functools.partial(backward_body, tiles, step),
        grid=(blocks,),
        in_specs=[
            pl.BlockSpec((block, width), back),
            pl.BlockSpec((block, width), back),
            pl.BlockSpec((block, width), back),
            pl.BlockSpec((block, select.shape[1]), back),
            pl.BlockSpec((states, width), lambda i: (0, 0)),
            pl.BlockSpec((states, width), lambda i: (0, 0)),
            pl.BlockSpec((block * states, width), back),
            pl.BlockSpec(
                (states, width), lambda i: (jnp.maximum((blocks - 1 - i) * block - 1, 0), 0)
            ),
        ],
        out_specs=[
            pl.BlockSpec((block, width), back),
            pl.BlockSpec((block, width), back),
            pl.BlockSpec((block, 2 * states), back),
            pl.BlockSpec((states, width), lambda i: (0, 0)),
        ],
        out_shape=[
            jax.ShapeDtypeStruct((length, width), f32),
            jax.ShapeDtypeStruct((length, width), f32),
            jax.ShapeDtypeStruct((length, 2 * states), f32),
            jax.ShapeDtypeStruct((states, width), f32),
        ],
        scratch_shapes=[
            pltpu.VMEM((states, width), f32),
            pltpu.VMEM((block, width), f32),
            pltpu.VMEM((states, block), f32),
            pltpu.VMEM((block, step * states), bf16),
            pltpu.VMEM((block, 2 * step * states), f32),
            pltpu.VMEM((block // FEW * states, width), bf16),
        ]
        + [pltpu.VMEM((GROUP * states, width), bf16)] * 4,
        compiler_params=pltpu.CompilerParams(vmem_limit_bytes=48 << 20),
        cost_estimate=pl.CostEstimate(
            flops=20 * length * width * states,
            transcendentals=length * width * states,
            bytes_accessed=length * width * (2 * states + 20),
        ),
        name="scan_backward",
    )(delta, active, d_mixed, select, rate, decay_rate, kept, kept)


together = lax.optimization_barrier


def inner_swap(value, axis):
    count = lax.axis_size(axis)
    return lax.ppermute(value, axis, [(i, i ^ 1) for i in range(count)])


def outer_shift(value, axis, steps):
    count = lax.axis_size(axis)
    half = count // 2
    pairs = [(i, (i // 2 + steps) % half * 2 + i % 2) for i in range(count)]
    return lax.ppermute(value, axis, pairs)


def shift_order(half):
    return sorted(range(1, half), key=lambda k: (-min(k, half - k), k))


def pieces_of_all(own, axis):
    count = lax.axis_size(axis)
    place = lax.axis_index(axis)
    half = count // 2
    outer, inner = place // 2, place % 2
    yield place, own
    arrived = {k: outer_shift(own, axis, k) for k in shift_order(half)}
    yield outer * 2 + 1 - inner, inner_swap(own, axis)
    for k, piece in arrived.items():
        origin = (outer - k + half) % half
        yield origin * 2 + inner, piece
    for k, piece in arrived.items():
        origin = (outer - k + half) % half
        yield origin * 2 + 1 - inner, inner_swap(piece, axis)


def gathered(own, axis, dim=0):
    count, size = lax.axis_size(axis), own.shape[dim]
    whole = jnp.zeros(own.shape[:dim] + (count * size,) + own.shape[dim + 1 :], own.dtype)
    for place, piece in pieces_of_all(own, axis):
        whole = lax.dynamic_update_slice_in_dim(whole, piece, place * size, dim)
    return whole


def hop(value, axis, moves):
    pairs = [(a * 2 + i, b * 2 + i) for a, b in moves for i in (0, 1)]
    return lax.ppermute(value, axis, pairs)


def swap_at(value, axis, spots):
    pairs = [(a * 2 + i, a * 2 + 1 - i) for a in spots for i in (0, 1)]
    return lax.ppermute(value, axis, pairs)


UP, DOWN = [(0, 1), (1, 2), (2, 3)], [(1, 0), (2, 1), (3, 2)]


def line_gathered(own, axis, held):
    if lax.axis_size(axis) != 8:
        return own, lambda own: own, lambda own, _: lax.all_gather(own, axis, axis=0, tiled=True), held
    place = lax.axis_index(axis)
    z, x = place // 2, place % 2
    rows = own.shape[0]
    upper, edge = z >= 2, (z == 0) | (z == 3)
    across = jnp.where(upper, z - 2, z + 2)
    far = jnp.where(z == 3, 0, 3)

    def put(whole, piece, spot, side):
        return lax.dynamic_update_slice_in_dim(whole, piece, (spot * 2 + side) * rows, 0)

    def put_far(whole, piece, side):
        held = lax.dynamic_slice_in_dim(whole, (far * 2 + side) * rows, rows, 0)
        return put(whole, jnp.where(edge, piece, held), far, side)

    whole = jnp.zeros((8 * rows,) + own.shape[1:], own.dtype)
    up, down, other, held = together(
        (hop(own, axis, UP), hop(own, axis, DOWN), swap_at(own, axis, range(4)), held)
    )
    up_two, down_two = hop(up, axis, UP[1:]), hop(down, axis, DOWN[:2])
    other_up, other_down = swap_at(up, axis, (1, 2, 3)), swap_at(down, axis, (0, 1, 2))
    whole = put(put(whole, own, z, x), other, z, 1 - x)
    whole = put(put(whole, up, (z + 3) % 4, x), down, (z + 1) % 4, x)
    two = jnp.where(upper, up_two, down_two)
    three = hop(two, axis, [(2, 3), (1, 0)])
    other_two = swap_at(two, axis, range(4))
    whole = put(put(whole, other_up, (z + 3) % 4, 1 - x), other_down, (z + 1) % 4, 1 - x)
    whole = put(whole, two, across, x)

    def end(last, other_three):
        three, other_two = last
        ended = put(whole, other_two, across, 1 - x)
        return put_far(put_far(ended, three, x), other_three, 1 - x)

    return (three, other_two), lambda last: swap_at(last[0], axis, (0, 3)), end, held


def line_summed(part_of, axis):
    if lax.axis_size(axis) != 8:
        return (scattered_sum(part_of, axis),)
    place = lax.axis_index(axis)
    z, x = place // 2, place % 2
    upper, edge = z >= 2, (z == 0) | (z == 3)
    across = jnp.where(upper, z - 2, z + 2)
    far = jnp.where(z == 0, 3, 0)
    above, below = jnp.minimum(z + 1, 3), jnp.maximum(z - 1, 0)

    def swapped(spot, spots):
        return swap_at(part_of(spot * 2 + 1 - x), axis, spots)

    def added(spot, given):
        return part_of(spot * 2 + x).astype(f32) + given.astype(f32)

    given_far = swapped(far, (0, 3))
    given_across = swapped(across, range(4))
    given_above, given_below = swapped(above, (0, 1, 2)), swapped(below, (1, 2, 3))
    given_own = swapped(z, range(4))
    three = hop(added(far, given_far).astype(bf16), axis, [(0, 1), (3, 2)])
    three, given_across = together((three, given_across))
    two = added(across, given_across) + jnp.where(edge, 0.0, three.astype(f32))
    two = two.astype(bf16)
    two_up, two_down, given_above, given_below = together(
        (hop(two, axis, UP[:2]), hop(two, axis, DOWN[1:]), given_above, given_below)
    )
    one_up = (added(above, given_above) + two_up.astype(f32)).astype(bf16)
    one_down = (added(below, given_below) + two_down.astype(f32)).astype(bf16)
    return added(z, given_own), hop(one_up, axis, UP), hop(one_down, axis, DOWN)


def scattered_sum(part_of, axis):
    count = lax.axis_size(axis)
    place = lax.axis_index(axis)
    half = count // 2
    outer, inner = place // 2, place % 2
    total = None
    for k in shift_order(half) + [0]:
        target = (outer + k) % half
        given = inner_swap(part_of(target * 2 + 1 - inner), axis)
        piece = part_of(target * 2 + inner).astype(f32) + given.astype(f32)
        if k:
            piece = outer_shift(piece.astype(bf16), axis, k).astype(f32)
        total = piece if total is None else total + piece
    return total


def rows_of(value, rows):
    return lambda place: lax.dynamic_slice_in_dim(value, place * rows, rows, 0)


def summed_over_seq(part, change, held=()):
    count = lax.axis_size("seq")
    length, columns = part.shape
    part = part.astype(bf16).reshape(count, length // count, columns)
    own = change(jnp.sum(lax.all_to_all(part, "seq", 0, 0).astype(f32), axis=0))
    own, held = together((own, held))
    return shared(own, "seq").reshape(length, own.shape[1]), held


def two_terms(value):
    high = value.astype(bf16)
    return [high, (value - high.astype(f32)).astype(bf16)]


def shared(own, axis):
    wide = jnp.broadcast_to(own[None], (lax.axis_size(axis),) + own.shape)
    return lax.all_to_all(wide, axis, 0, 0)


def matmul(a, b, dims=(((1,), (0,)), ((), ()))):
    return lax.dot_general(a, b, dims, preferred_element_type=f32)


TN = (((0,), (0,)), ((), ()))


def on_device(
    tokens,
    lengths,
    norm_gain,
    in_proj,
    conv_weight,
    conv_bias,
    x_proj,
    dt_proj,
    dt_bias,
    a_log,
    skip,
    out_proj,
    cotangent,
):
    batch, seq = lax.axis_size("batch"), lax.axis_size("seq")
    place = lax.axis_index("seq")
    span, model = tokens.shape[1:]
    length = span * seq
    in_rows = in_proj.shape[0]
    own = skip.shape[0]
    taps = conv_weight.shape[0]
    rank = dt_proj.shape[0]
    states = a_log.shape[1]
    width = own * batch

    halves = in_proj.reshape(in_rows, 2, batch, seq, own).transpose(1, 3, 0, 2, 4)
    halves = halves.reshape(2, seq, in_rows, width)
    beside = jnp.broadcast_to(norm_gain[None, :, None], (seq, in_rows, LANES))
    columns = lax.all_to_all(jnp.concatenate([halves[0], beside], axis=2), "seq", 0, 0)
    columns, gate_columns = together((columns, halves[1]))
    gate_columns = lax.all_to_all(gate_columns, "seq", 0, 0)
    last_hop, last_swap, end_gather, (dt_proj, x_proj, out_proj) = line_gathered(
        cotangent[0], "seq", (dt_proj, x_proj, out_proj)
    )
    small = jnp.concatenate(
        [
            dt_proj,
            x_proj.T,
            a_log.T,
            conv_weight,
            conv_bias[None],
            dt_bias[None],
            skip[None],
        ],
        axis=0,
    )
    small = gathered(small, "batch", 1)
    cuts = [rank, 2 * rank + 2 * states, 2 * rank + 3 * states]
    cuts = cuts + [cuts[2] + taps + i for i in range(3)]
    delta_weight, select_weight, decay_logs, conv_taps, conv_shift, delta_shift, skip_gain = (
        jnp.split(small, cuts, axis=0)
    )
    conv_taps, conv_shift = conv_taps.astype(f32), conv_shift.astype(f32)
    delta_shift, skip_gain = delta_shift.astype(f32), skip_gain.astype(f32)
    decay = -jnp.exp(decay_logs.astype(f32))
    input_weight = gathered(columns.reshape(seq * in_rows, width + LANES), "batch")
    one = (jnp.arange(LANES) == 0).astype(bf16)[None]
    gain = matmul(one, input_weight[:, width:], NT)
    input_weight = input_weight[:, :width]
    gate_weight = gathered(gate_columns.reshape(seq * in_rows, width), "batch")

    def normed(rows):
        rows = rows.astype(f32)
        scale = lax.rsqrt(jnp.mean(rows * rows, axis=-1, keepdims=True) + epsilon)
        return (rows * scale * gain).astype(bf16)

    stream = lax.all_gather(tokens[0], "seq", axis=0, tiled=True)
    normalized = normed(stream)
    output_weight = gathered(out_proj, "batch")

    valid = (jnp.arange(length, dtype=jnp.int32) < lengths[0])[:, None]
    inner = matmul(normalized, input_weight).astype(bf16)
    padded = jnp.pad(inner, ((taps - 1, 0), (0, 0)))
    conv_out = conv_shift + jnp.zeros((length, width), f32)
    for tap in range(taps):
        conv_out = conv_out + conv_taps[tap] * padded[tap : tap + length].astype(f32)
    active = jax.nn.silu(conv_out).astype(bf16)
    active_f = active.astype(f32)

    partial, last_hop, gate_weight = together(
        (matmul(active, select_weight, NT), last_hop, gate_weight)
    )
    select, _ = summed_over_seq(
        partial,
        lambda s: jnp.concatenate([s[:, :rank].astype(bf16)] + two_terms(s[:, rank:]), axis=1),
    )
    gate_low = matmul(normalized, gate_weight).astype(bf16)
    select, gate_low, last_hop = together((select, gate_low, last_hop))
    last = last_swap(last_hop)
    gate = gate_low.astype(f32)
    gate_sig = jax.nn.sigmoid(gate)
    delta_low = select[:, :rank]
    delta_raw = matmul(delta_low, delta_weight) + delta_shift
    delta = jax.nn.softplus(delta_raw)

    block = min(BLOCK, length)
    step = 256 // states
    rate = decay * LOG2E
    mixed, kept = scan_forward(delta, active, select, rate, block, step)
    mixed = mixed + skip_gain * active_f
    gated = (mixed * gate * gate_sig).astype(bf16)
    branch = matmul(gated, output_weight).astype(bf16)
    branch, last_hop, last = together((branch, last_hop, last))
    branch = lax.psum_scatter(branch, "seq", scatter_dimension=0, tiled=True)
    own_valid = lax.dynamic_slice_in_dim(valid, place * span, span, 0)
    own_stream = tokens[0].astype(f32)

    upstream = jnp.where(valid, end_gather(last_hop, last), 0).astype(bf16)
    d_gated = matmul(upstream, output_weight, NT)
    d_mixed = d_gated * gate * gate_sig
    d_gate = d_gated * mixed * gate_sig * (1.0 + gate * (1.0 - gate_sig))
    grad_skip = jnp.sum(d_mixed * active_f, axis=0, keepdims=True)
    d_gate_low = d_gate.astype(bf16)

    d_delta, d_active, d_bc, grad_log = scan_backward(
        delta, active, d_mixed, select, rate, decay, kept, block, step
    )
    d_raw = d_delta * jax.nn.sigmoid(delta_raw)
    grad_dt_bias = jnp.sum(d_raw, axis=0, keepdims=True)
    d_raw_low = d_raw.astype(bf16)
    grad_dt_proj = matmul(delta_low, d_raw_low, TN)
    partial = jnp.concatenate([matmul(d_raw_low, delta_weight, NT), d_bc], axis=1)
    d_select, gated = summed_over_seq(partial, lambda s: s.astype(bf16), gated)
    grad_output = matmul(gated, upstream, TN).astype(bf16)
    grad_gate = scattered_sum(
        rows_of(matmul(normalized, d_gate_low, TN).astype(bf16), model // batch), "batch"
    )
    d_select, grad_gate, grad_output = together((d_select, grad_gate, grad_output))
    grad_output = lax.psum_scatter(grad_output, "batch", scatter_dimension=0, tiled=True)
    grad_output = grad_output.astype(f32)
    grad_x_proj = matmul(d_select, active, TN)
    d_active = d_active + d_mixed * skip_gain + matmul(d_select, select_weight)
    conv_sig = jax.nn.sigmoid(conv_out)
    d_conv = (d_active * conv_sig * (1.0 + conv_out * (1.0 - conv_sig))).astype(bf16)
    d_conv_f = d_conv.astype(f32)
    grad_conv_bias = jnp.sum(d_conv_f, axis=0, keepdims=True)
    grad_conv = jnp.stack(
        [
            jnp.sum(d_conv_f * padded[tap : tap + length].astype(f32), axis=0)
            for tap in range(taps)
        ]
    )
    extended = jnp.pad(d_conv, ((0, taps - 1), (0, 0)))
    d_inner = jnp.zeros((length, width), f32)
    for tap in range(taps):
        offset = taps - 1 - tap
        d_inner = d_inner + conv_taps[tap] * extended[offset : offset + length].astype(f32)
    d_inner = d_inner.astype(bf16)
    d_normalized = matmul(
        jnp.concatenate([d_inner, d_gate_low], axis=1),
        jnp.concatenate([input_weight, gate_weight], axis=1),
        NT,
    ).astype(bf16)
    grad_gate = grad_gate.astype(bf16).reshape(seq, in_rows, width)
    grad_gate = lax.all_to_all(grad_gate, "seq", 0, 0)
    d_normalized, d_inner, grad_gate, grad_x_proj, branch = together(
        (d_normalized, d_inner, grad_gate, grad_x_proj, branch)
    )
    grad_inner = matmul(normalized, d_inner, TN).astype(bf16)
    grad_inner = scattered_sum(rows_of(grad_inner, model // batch), "batch")
    d_normalized, *last_terms = line_summed(rows_of(d_normalized, span), "seq")

    block_out = jnp.where(own_valid, own_stream + branch.astype(f32), 0.0)

    def columns_of(part):
        part = part.reshape(seq, in_rows, batch, own).transpose(1, 2, 0, 3)
        return part.reshape(in_rows, batch * seq * own).astype(f32)

    grad_inner = grad_inner.astype(bf16).reshape(seq, in_rows, width)
    grad_inner = lax.all_to_all(grad_inner, "seq", 0, 0)
    grad_input = jnp.concatenate([columns_of(grad_inner), columns_of(grad_gate)], axis=1)

    small_grads = jnp.concatenate(
        [grad_dt_proj, grad_x_proj, grad_log, grad_conv, grad_conv_bias, grad_dt_bias, grad_skip],
        axis=0,
    )
    small_grads = lax.psum_scatter(small_grads, "batch", scatter_dimension=1, tiled=True)
    g_dt_proj, g_x_proj, g_log, g_conv, g_conv_bias, g_dt_bias, g_skip = jnp.split(
        small_grads, cuts, axis=0
    )

    own_upstream = jnp.where(own_valid, cotangent[0].astype(f32), 0.0)
    own_scale = lax.rsqrt(jnp.mean(own_stream * own_stream, axis=-1, keepdims=True) + epsilon)
    grad_gain = jnp.sum(grad_input * in_proj.astype(f32), axis=1) / norm_gain.astype(f32)
    (
        d_normalized, g_dt_proj, g_x_proj, g_log, g_conv, g_conv_bias, g_dt_bias, g_skip,
        grad_input, grad_gain, grad_output,
    ) = together(
        (
            d_normalized, g_dt_proj, g_x_proj, g_log, g_conv, g_conv_bias, g_dt_bias, g_skip,
            grad_input, grad_gain, grad_output,
        )
    )
    for term in last_terms:
        d_normalized = d_normalized + term.astype(f32)
    d_hat = d_normalized * gain
    grad_tokens = (
        own_scale * d_hat
        - own_stream
        * own_scale
        * own_scale
        * own_scale
        * jnp.mean(d_hat * own_stream, axis=-1, keepdims=True)
        + own_upstream
    )
    return (
        block_out[None],
        grad_tokens[None],
        grad_gain,
        grad_input,
        g_conv,
        g_conv_bias[0],
        g_x_proj.T,
        g_dt_proj,
        g_dt_bias[0],
        g_log.T,
        g_skip[0],
        grad_output,
    )


def solution(mesh):
    placed = (
        P("batch", "seq", None),
        P("batch"),
        P(("batch", "seq")),
        P(("batch", "seq"), None),
        P(None, ("batch", "seq")),
        P(("batch", "seq")),
        P(("batch", "seq"), None),
        P(None, ("batch", "seq")),
        P(("batch", "seq")),
        P(("batch", "seq"), None),
        P(("batch", "seq")),
        P(("batch", "seq"), None),
        P("batch", "seq", None),
    )
    return jax.shard_map(
        on_device,
        mesh=mesh,
        in_specs=placed,
        out_specs=(
            P("batch", "seq", None),
            P("batch", "seq", None),
            P(("batch", "seq")),
            P(("batch", "seq"), None),
            P(None, ("batch", "seq")),
            P(("batch", "seq")),
            P(("batch", "seq"), None),
            P(None, ("batch", "seq")),
            P(("batch", "seq")),
            P(("batch", "seq"), None),
            P(("batch", "seq")),
            P(("batch", "seq"), None),
        ),
        check_vma=False,
    )
```

```python
import functools

import jax
import jax.numpy as jnp
from jax import lax
from jax.experimental import pallas as pl
from jax.experimental.pallas import tpu as pltpu
from jax.sharding import PartitionSpec as P

bf16, f32 = jnp.bfloat16, jnp.float32
NT = (((1,), (1,)), ((), ()))
LANES = 128
GROUP = 32
BLOCK = 128
epsilon = 1e-05
LOG2E = 1.4426950408889634


def spread(tile, row, lanes, states):
    return jnp.broadcast_to(tile[row : row + 1, lanes], (states, LANES))


def selectors(select, states):
    low = select.shape[1] - 4 * states
    middle = low + 2 * states
    block = select[:, low:middle].astype(f32) + select[:, middle:].astype(f32)
    return jnp.transpose(block), block[:, :states], block[:, states:]


def block_diagonal(values, step):
    rows, states = values.shape
    wide = step * states
    spread_out = (
        lax.broadcasted_iota(jnp.int32, (states, wide), 1) % states
        == lax.broadcasted_iota(jnp.int32, (states, wide), 0)
    ).astype(bf16)
    value = jnp.dot(values.astype(bf16), spread_out, preferred_element_type=f32)
    place = lax.broadcasted_iota(jnp.int32, (rows, wide), 0) % step
    owner = lax.broadcasted_iota(jnp.int32, (rows, wide), 1) // states
    return jnp.where(place == owner, value, 0.0).astype(bf16)


def forward_body(tiles, step, delta, active, select, rate, mixed, kept, state, drive, columns):
    rows, states = delta.shape[0], rate.shape[0]
    wide = step * states

    @pl.when(pl.program_id(0) == 0)
    def _():
        state[...] = jnp.zeros_like(state)

    turned, _, c_block = selectors(select[...], states)
    columns[...] = turned[:states]
    drive[...] = delta[...] * active[...].astype(f32)
    rates = [rate[:, k * LANES : (k + 1) * LANES] for k in range(tiles)]

    def group(number, held):
        held = list(held)
        base = pl.multiple_of(number * GROUP, GROUP)
        delta_now, drive_now = delta.at[pl.ds(base, GROUP), :], drive.at[pl.ds(base, GROUP), :]
        b_now = pltpu.roll(columns[...], rows - base, 1)
        for j in range(GROUP):
            b_wide = jnp.broadcast_to(b_now[:, j : j + 1], (states, LANES))
            for k in range(tiles):
                lanes = slice(k * LANES, (k + 1) * LANES)
                decay = jnp.exp2(spread(delta_now, j, lanes, states) * rates[k])
                held[k] = decay * held[k] + spread(drive_now, j, lanes, states) * b_wide
                at = pl.ds(pl.multiple_of((base + j) * states, states), states)
                kept[at, lanes] = held[k].astype(bf16)
        return tuple(held)

    held = lax.fori_loop(
        0,
        rows // GROUP,
        group,
        tuple(state[:, k * LANES : (k + 1) * LANES] for k in range(tiles)),
    )
    for k in range(tiles):
        state[:, k * LANES : (k + 1) * LANES] = held[k]
    c_diag = block_diagonal(c_block, step)
    for q in range(rows // step):
        part = kept[q * wide : (q + 1) * wide, :]
        spot = slice(q * step, (q + 1) * step)
        mixed[spot, :] = jnp.dot(c_diag[spot, :], part, preferred_element_type=f32)


def scan_forward(delta, active, select, rate, block, step):
    length, width = delta.shape
    states = rate.shape[0]
    tiles = width // LANES
    return pl.pallas_call(
        functools.partial(forward_body, tiles, step),
        grid=(length // block,),
        in_specs=[
            pl.BlockSpec((block, width), lambda i: (i, 0)),
            pl.BlockSpec((block, width), lambda i: (i, 0)),
            pl.BlockSpec((block, select.shape[1]), lambda i: (i, 0)),
            pl.BlockSpec((states, width), lambda i: (0, 0)),
        ],
        out_specs=[
            pl.BlockSpec((block, width), lambda i: (i, 0)),
            pl.BlockSpec((block * states, width), lambda i: (i, 0)),
        ],
        out_shape=[
            jax.ShapeDtypeStruct((length, width), f32),
            jax.ShapeDtypeStruct((length * states, width), bf16),
        ],
        scratch_shapes=[
            pltpu.VMEM((states, width), f32),
            pltpu.VMEM((block, width), f32),
            pltpu.VMEM((states, block), f32),
        ],
        compiler_params=pltpu.CompilerParams(vmem_limit_bytes=48 << 20),
        cost_estimate=pl.CostEstimate(
            flops=8 * length * width * states,
            transcendentals=length * width * states,
            bytes_accessed=length * width * (2 * states + 10),
        ),
        name="scan_forward",
    )(delta, active, select, rate)


FEW = 4


def backward_body(
    tiles, step, delta, active, d_mixed, select, rate, decay_rate, kept, kept_before,
    d_delta, d_active, d_bc, d_log, push, drive, columns, diagonals, folding, timed, *pairs,
):
    grads, rated = pairs[:2], pairs[2:]
    rows, states = delta.shape[0], rate.shape[0]
    blocks = pl.num_programs(0)
    first = pl.program_id(0) == blocks - 1
    wide = step * states

    @pl.when(pl.program_id(0) == 0)
    def _():
        push[...] = jnp.zeros_like(push)
        d_log[...] = jnp.zeros_like(d_log)

    turned, b_block, _ = selectors(select[...], states)
    columns[...] = turned[states:]
    drive[...] = delta[...] * active[...].astype(f32)
    rates = [rate[:, k * LANES : (k + 1) * LANES] for k in range(tiles)]
    own_rates = [decay_rate[:, k * LANES : (k + 1) * LANES].astype(bf16) for k in range(tiles)]

    place = lax.broadcasted_iota(jnp.int32, (step, wide), 0)
    owner = lax.broadcasted_iota(jnp.int32, (step, wide), 1) // states
    ones_diag = (place == owner).astype(bf16)
    diag = (place == owner).astype(f32)
    diagonals[...] = block_diagonal(b_block, step)

    def sums_of(number):
        held, through_of = number % 2, {}

        def spots(q):
            at = number * GROUP + q * step
            tall = slice(q * wide, (q + 1) * wide)
            return slice(at, at + step), tall

        def through(q):
            spot, tall = spots(q)
            value = jnp.dot(diagonals[spot, :], grads[held][tall, :], preferred_element_type=f32)
            d_active[spot, :] = delta[spot, :] * value
            through_of[q] = active[spot, :].astype(f32) * value

        def summed(q):
            spot, tall = spots(q)
            value = jnp.dot(ones_diag, rated[held][tall, :], preferred_element_type=f32)
            d_delta[spot, :] = value + through_of[q]

        def d_b(q):
            spot, tall = spots(q)
            folding[spot, :wide] = diag * lax.dot_general(
                drive[spot, :].astype(bf16), grads[held][tall, :], NT, preferred_element_type=f32
            )

        def d_c(q):
            spot, _ = spots(q)
            own = slice(spot.start * states, spot.stop * states)
            folding[spot, wide:] = diag * lax.dot_general(
                d_mixed[spot, :].astype(bf16), kept[own, :], NT, preferred_element_type=f32
            )

        return [
            functools.partial(part, q)
            for q in range(GROUP // step)
            for part in (through, summed, d_b, d_c)
        ]

    carry = [push[:, k * LANES : (k + 1) * LANES] for k in range(tiles)]
    waiting = []
    for number in reversed(range(rows // GROUP)):
        pace = GROUP // max(len(waiting), 1)
        sums = [None] * tiles
        held = number % 2
        for j in reversed(range(GROUP)):
            row = number * GROUP + j
            c_wide = jnp.broadcast_to(columns[:, row : row + 1], (states, LANES))
            at = slice(j * states, (j + 1) * states)
            for k in range(tiles):
                lanes = slice(k * LANES, (k + 1) * LANES)
                if row:
                    before = kept[(row - 1) * states : row * states, lanes]
                else:
                    before = jnp.where(first, jnp.zeros((), bf16), kept_before[:, lanes])
                step_size = spread(delta, row, lanes, states)
                grad = spread(d_mixed, row, lanes, states) * c_wide + carry[k]
                carry[k] = jnp.exp2(step_size * rates[k]) * grad
                grads[held][at, lanes] = grad.astype(bf16)
                rated_now = carry[k].astype(bf16) * before * own_rates[k]
                rated[held][at, lanes] = rated_now
                timed_now = rated_now * step_size.astype(bf16)
                sums[k] = timed_now if sums[k] is None else sums[k] + timed_now
                if j % FEW == 0:
                    spot = row // FEW * states
                    timed[spot : spot + states, lanes] = sums[k]
                    sums[k] = None
            if waiting and j % pace == 0:
                waiting.pop(0)()
        while waiting:
            waiting.pop(0)()
        waiting = sums_of(number)
    while waiting:
        waiting.pop(0)()
    for k in range(tiles):
        push[:, k * LANES : (k + 1) * LANES] = carry[k]
    fold = (
        lax.broadcasted_iota(jnp.int32, (wide, states), 0) % states
        == lax.broadcasted_iota(jnp.int32, (wide, states), 1)
    ).astype(bf16)
    for number in range(2):
        value = folding[:, number * wide : (number + 1) * wide]
        high = value.astype(bf16)
        d_bc[:, number * states : (number + 1) * states] = jnp.dot(
            high, fold, preferred_element_type=f32
        )
    span = rows // FEW * states
    pick = (
        lax.broadcasted_iota(jnp.int32, (states, span), 1) % states
        == lax.broadcasted_iota(jnp.int32, (states, span), 0)
    ).astype(bf16)
    d_log[...] += jnp.dot(pick, timed[...], preferred_element_type=f32)


def scan_backward(delta, active, d_mixed, select, rate, decay_rate, kept, block, step):
    length, width = delta.shape
    states = rate.shape[0]
    tiles = width // LANES
    blocks = length // block
    back = lambda i: (blocks - 1 - i, 0)
    return pl.pallas_call(
        functools.partial(backward_body, tiles, step),
        grid=(blocks,),
        in_specs=[
            pl.BlockSpec((block, width), back),
            pl.BlockSpec((block, width), back),
            pl.BlockSpec((block, width), back),
            pl.BlockSpec((block, select.shape[1]), back),
            pl.BlockSpec((states, width), lambda i: (0, 0)),
            pl.BlockSpec((states, width), lambda i: (0, 0)),
            pl.BlockSpec((block * states, width), back),
            pl.BlockSpec(
                (states, width), lambda i: (jnp.maximum((blocks - 1 - i) * block - 1, 0), 0)
            ),
        ],
        out_specs=[
            pl.BlockSpec((block, width), back),
            pl.BlockSpec((block, width), back),
            pl.BlockSpec((block, 2 * states), back),
            pl.BlockSpec((states, width), lambda i: (0, 0)),
        ],
        out_shape=[
            jax.ShapeDtypeStruct((length, width), f32),
            jax.ShapeDtypeStruct((length, width), f32),
            jax.ShapeDtypeStruct((length, 2 * states), f32),
            jax.ShapeDtypeStruct((states, width), f32),
        ],
        scratch_shapes=[
            pltpu.VMEM((states, width), f32),
            pltpu.VMEM((block, width), f32),
            pltpu.VMEM((states, block), f32),
            pltpu.VMEM((block, step * states), bf16),
            pltpu.VMEM((block, 2 * step * states), f32),
            pltpu.VMEM((block // FEW * states, width), bf16),
        ]
        + [pltpu.VMEM((GROUP * states, width), bf16)] * 4,
        compiler_params=pltpu.CompilerParams(vmem_limit_bytes=48 << 20),
        cost_estimate=pl.CostEstimate(
            flops=20 * length * width * states,
            transcendentals=length * width * states,
            bytes_accessed=length * width * (2 * states + 20),
        ),
        name="scan_backward",
    )(delta, active, d_mixed, select, rate, decay_rate, kept, kept)


together = lax.optimization_barrier


def inner_swap(value, axis):
    count = lax.axis_size(axis)
    return lax.ppermute(value, axis, [(i, i ^ 1) for i in range(count)])


def outer_shift(value, axis, steps):
    count = lax.axis_size(axis)
    half = count // 2
    pairs = [(i, (i // 2 + steps) % half * 2 + i % 2) for i in range(count)]
    return lax.ppermute(value, axis, pairs)


def shift_order(half):
    return sorted(range(1, half), key=lambda k: (-min(k, half - k), k))


def pieces_of_all(own, axis):
    count = lax.axis_size(axis)
    place = lax.axis_index(axis)
    half = count // 2
    outer, inner = place // 2, place % 2
    yield place, own
    arrived = {k: outer_shift(own, axis, k) for k in shift_order(half)}
    yield outer * 2 + 1 - inner, inner_swap(own, axis)
    for k, piece in arrived.items():
        origin = (outer - k + half) % half
        yield origin * 2 + inner, piece
    for k, piece in arrived.items():
        origin = (outer - k + half) % half
        yield origin * 2 + 1 - inner, inner_swap(piece, axis)


def gathered(own, axis, dim=0):
    count, size = lax.axis_size(axis), own.shape[dim]
    whole = jnp.zeros(own.shape[:dim] + (count * size,) + own.shape[dim + 1 :], own.dtype)
    for place, piece in pieces_of_all(own, axis):
        whole = lax.dynamic_update_slice_in_dim(whole, piece, place * size, dim)
    return whole


def hop(value, axis, moves):
    pairs = [(a * 2 + i, b * 2 + i) for a, b in moves for i in (0, 1)]
    return lax.ppermute(value, axis, pairs)


def swap_at(value, axis, spots):
    pairs = [(a * 2 + i, a * 2 + 1 - i) for a in spots for i in (0, 1)]
    return lax.ppermute(value, axis, pairs)


UP, DOWN = [(0, 1), (1, 2), (2, 3)], [(1, 0), (2, 1), (3, 2)]


def line_gathered(own, axis, held):
    if lax.axis_size(axis) != 8:
        same = lambda own: own
        return own, same, same, lambda own, _: lax.all_gather(own, axis, axis=0, tiled=True), held
    place = lax.axis_index(axis)
    z, x = place // 2, place % 2
    rows = own.shape[0]
    upper, edge = z >= 2, (z == 0) | (z == 3)
    across = jnp.where(upper, z - 2, z + 2)
    far = jnp.where(z == 3, 0, 3)

    def put(whole, piece, spot, side):
        return lax.dynamic_update_slice_in_dim(whole, piece, (spot * 2 + side) * rows, 0)

    def put_far(whole, piece, side):
        held = lax.dynamic_slice_in_dim(whole, (far * 2 + side) * rows, rows, 0)
        return put(whole, jnp.where(edge, piece, held), far, side)

    whole = jnp.zeros((8 * rows,) + own.shape[1:], own.dtype)
    up, down, other, held = together(
        (hop(own, axis, UP), hop(own, axis, DOWN), swap_at(own, axis, range(4)), held)
    )
    up_two, down_two = hop(up, axis, UP[1:]), hop(down, axis, DOWN[:2])
    other_up, other_down = swap_at(up, axis, (1, 2, 3)), swap_at(down, axis, (0, 1, 2))
    whole = put(put(whole, own, z, x), other, z, 1 - x)
    whole = put(put(whole, up, (z + 3) % 4, x), down, (z + 1) % 4, x)
    two = jnp.where(upper, up_two, down_two)
    three = hop(two, axis, [(2, 3), (1, 0)])
    other_two = swap_at(two, axis, range(4))
    whole = put(put(whole, other_up, (z + 3) % 4, 1 - x), other_down, (z + 1) % 4, 1 - x)
    whole = put(whole, two, across, x)

    def collect(last):
        three, other_two = last
        return put_far(put(whole, other_two, across, 1 - x), three, x)

    def end(collected, other_three):
        return put_far(collected, other_three, 1 - x)

    swap = lambda last: swap_at(last[0], axis, (0, 3))
    return (three, other_two), swap, collect, end, held


def line_summed(part_of, axis):
    if lax.axis_size(axis) != 8:
        return (scattered_sum(part_of, axis),)
    place = lax.axis_index(axis)
    z, x = place // 2, place % 2
    upper, edge = z >= 2, (z == 0) | (z == 3)
    across = jnp.where(upper, z - 2, z + 2)
    far = jnp.where(z == 0, 3, 0)
    above, below = jnp.minimum(z + 1, 3), jnp.maximum(z - 1, 0)

    def swapped(spot, spots):
        return swap_at(part_of(spot * 2 + 1 - x), axis, spots)

    def added(spot, given):
        return part_of(spot * 2 + x).astype(f32) + given.astype(f32)

    given_far = swapped(far, (0, 3))
    given_across = swapped(across, range(4))
    given_above, given_below = swapped(above, (0, 1, 2)), swapped(below, (1, 2, 3))
    given_own = swapped(z, range(4))
    three = hop(added(far, given_far).astype(bf16), axis, [(0, 1), (3, 2)])
    three, given_across = together((three, given_across))
    two = added(across, given_across) + jnp.where(edge, 0.0, three.astype(f32))
    two = two.astype(bf16)
    two_up, two_down, given_above, given_below = together(
        (hop(two, axis, UP[:2]), hop(two, axis, DOWN[1:]), given_above, given_below)
    )
    one_up = (added(above, given_above) + two_up.astype(f32)).astype(bf16)
    one_down = (added(below, given_below) + two_down.astype(f32)).astype(bf16)
    return added(z, given_own), hop(one_up, axis, UP), hop(one_down, axis, DOWN)


def scattered_sum(part_of, axis):
    count = lax.axis_size(axis)
    place = lax.axis_index(axis)
    half = count // 2
    outer, inner = place // 2, place % 2
    total = None
    for k in shift_order(half) + [0]:
        target = (outer + k) % half
        given = inner_swap(part_of(target * 2 + 1 - inner), axis)
        piece = part_of(target * 2 + inner).astype(f32) + given.astype(f32)
        if k:
            piece = outer_shift(piece.astype(bf16), axis, k).astype(f32)
        total = piece if total is None else total + piece
    return total


def rows_of(value, rows):
    return lambda place: lax.dynamic_slice_in_dim(value, place * rows, rows, 0)


def summed_over_seq(part, change, held=()):
    count = lax.axis_size("seq")
    length, columns = part.shape
    part = part.astype(bf16).reshape(count, length // count, columns)
    own = change(jnp.sum(lax.all_to_all(part, "seq", 0, 0).astype(f32), axis=0))
    own, held = together((own, held))
    return shared(own, "seq").reshape(length, own.shape[1]), held


def two_terms(value):
    high = value.astype(bf16)
    return [high, (value - high.astype(f32)).astype(bf16)]


def shared(own, axis):
    wide = jnp.broadcast_to(own[None], (lax.axis_size(axis),) + own.shape)
    return lax.all_to_all(wide, axis, 0, 0)


def matmul(a, b, dims=(((1,), (0,)), ((), ()))):
    return lax.dot_general(a, b, dims, preferred_element_type=f32)


TN = (((0,), (0,)), ((), ()))


def on_device(
    tokens,
    lengths,
    norm_gain,
    in_proj,
    conv_weight,
    conv_bias,
    x_proj,
    dt_proj,
    dt_bias,
    a_log,
    skip,
    out_proj,
    cotangent,
):
    batch, seq = lax.axis_size("batch"), lax.axis_size("seq")
    place = lax.axis_index("seq")
    span, model = tokens.shape[1:]
    length = span * seq
    in_rows = in_proj.shape[0]
    own = skip.shape[0]
    taps = conv_weight.shape[0]
    rank = dt_proj.shape[0]
    states = a_log.shape[1]
    width = own * batch

    halves = in_proj.reshape(in_rows, 2, batch, seq, own).transpose(1, 3, 0, 2, 4)
    halves = halves.reshape(2, seq, in_rows, width)
    beside = jnp.broadcast_to(norm_gain[None, :, None], (seq, in_rows, LANES))
    columns = lax.all_to_all(jnp.concatenate([halves[0], beside], axis=2), "seq", 0, 0)
    columns, gate_columns = together((columns, halves[1]))
    gate_columns = lax.all_to_all(gate_columns, "seq", 0, 0)
    last_hop, last_swap, collect, end_gather, (dt_proj, x_proj, out_proj) = line_gathered(
        cotangent[0], "seq", (dt_proj, x_proj, out_proj)
    )
    small = jnp.concatenate(
        [
            dt_proj,
            x_proj.T,
            a_log.T,
            conv_weight,
            conv_bias[None],
            dt_bias[None],
            skip[None],
        ],
        axis=0,
    )
    small = gathered(small, "batch", 1)
    cuts = [rank, 2 * rank + 2 * states, 2 * rank + 3 * states]
    cuts = cuts + [cuts[2] + taps + i for i in range(3)]
    delta_weight, select_weight, decay_logs, conv_taps, conv_shift, delta_shift, skip_gain = (
        jnp.split(small, cuts, axis=0)
    )
    conv_taps, conv_shift = conv_taps.astype(f32), conv_shift.astype(f32)
    delta_shift, skip_gain = delta_shift.astype(f32), skip_gain.astype(f32)
    decay = -jnp.exp(decay_logs.astype(f32))
    input_weight = gathered(columns.reshape(seq * in_rows, width + LANES), "batch")
    one = (jnp.arange(LANES) == 0).astype(bf16)[None]
    gain = matmul(one, input_weight[:, width:], NT)
    input_weight = input_weight[:, :width]
    gate_weight = gathered(gate_columns.reshape(seq * in_rows, width), "batch")

    def normed(rows):
        rows = rows.astype(f32)
        scale = lax.rsqrt(jnp.mean(rows * rows, axis=-1, keepdims=True) + epsilon)
        return (rows * scale * gain).astype(bf16)

    stream = lax.all_gather(tokens[0], "seq", axis=0, tiled=True)
    normalized = normed(stream)
    output_weight = gathered(out_proj, "batch")

    valid = (jnp.arange(length, dtype=jnp.int32) < lengths[0])[:, None]
    inner = matmul(normalized, input_weight).astype(bf16)
    padded = jnp.pad(inner, ((taps - 1, 0), (0, 0)))
    conv_out = conv_shift + jnp.zeros((length, width), f32)
    for tap in range(taps):
        conv_out = conv_out + conv_taps[tap] * padded[tap : tap + length].astype(f32)
    active = jax.nn.silu(conv_out).astype(bf16)
    active_f = active.astype(f32)

    partial, last_hop, gate_weight = together(
        (matmul(active, select_weight, NT), last_hop, gate_weight)
    )
    select, _ = summed_over_seq(
        partial,
        lambda s: jnp.concatenate([s[:, :rank].astype(bf16)] + two_terms(s[:, rank:]), axis=1),
    )
    gate_low = matmul(normalized, gate_weight).astype(bf16)
    select, gate_low, last_hop, collected = together(
        (select, gate_low, last_hop, collect(last_hop))
    )
    last = last_swap(last_hop)
    gate = gate_low.astype(f32)
    gate_sig = jax.nn.sigmoid(gate)
    delta_low = select[:, :rank]
    delta_raw = matmul(delta_low, delta_weight) + delta_shift
    delta = jax.nn.softplus(delta_raw)

    block = min(BLOCK, length)
    step = 256 // states
    rate = decay * LOG2E
    mixed, kept = scan_forward(delta, active, select, rate, block, step)
    mixed = mixed + skip_gain * active_f
    gated = (mixed * gate * gate_sig).astype(bf16)
    branch = matmul(gated, output_weight).astype(bf16)
    branch, collected, last = together((branch, collected, last))
    branch = lax.psum_scatter(branch, "seq", scatter_dimension=0, tiled=True)
    own_valid = lax.dynamic_slice_in_dim(valid, place * span, span, 0)
    own_stream = tokens[0].astype(f32)

    upstream = jnp.where(valid, end_gather(collected, last), 0).astype(bf16)
    d_gated = matmul(upstream, output_weight, NT)
    d_mixed = d_gated * gate * gate_sig
    d_gate = d_gated * mixed * gate_sig * (1.0 + gate * (1.0 - gate_sig))
    grad_skip = jnp.sum(d_mixed * active_f, axis=0, keepdims=True)
    d_gate_low = d_gate.astype(bf16)

    d_delta, d_active, d_bc, grad_log = scan_backward(
        delta, active, d_mixed, select, rate, decay, kept, block, step
    )
    d_raw = d_delta * jax.nn.sigmoid(delta_raw)
    grad_dt_bias = jnp.sum(d_raw, axis=0, keepdims=True)
    d_raw_low = d_raw.astype(bf16)
    grad_dt_proj = matmul(delta_low, d_raw_low, TN)
    partial = jnp.concatenate([matmul(d_raw_low, delta_weight, NT), d_bc], axis=1)
    d_select, gated = summed_over_seq(partial, lambda s: s.astype(bf16), gated)
    grad_output = matmul(gated, upstream, TN).astype(bf16)
    grad_gate = scattered_sum(
        rows_of(matmul(normalized, d_gate_low, TN).astype(bf16), model // batch), "batch"
    )
    weight = jnp.concatenate([input_weight, gate_weight], axis=1)
    d_select, grad_gate, grad_output, weight = together(
        (d_select, grad_gate, grad_output, weight)
    )
    grad_output = lax.psum_scatter(grad_output, "batch", scatter_dimension=0, tiled=True)
    grad_output = grad_output.astype(f32)
    grad_x_proj = matmul(d_select, active, TN)
    d_active = d_active + d_mixed * skip_gain + matmul(d_select, select_weight)
    conv_sig = jax.nn.sigmoid(conv_out)
    d_conv = (d_active * conv_sig * (1.0 + conv_out * (1.0 - conv_sig))).astype(bf16)
    d_conv_f = d_conv.astype(f32)
    grad_conv_bias = jnp.sum(d_conv_f, axis=0, keepdims=True)
    grad_conv = jnp.stack(
        [
            jnp.sum(d_conv_f * padded[tap : tap + length].astype(f32), axis=0)
            for tap in range(taps)
        ]
    )
    extended = jnp.pad(d_conv, ((0, taps - 1), (0, 0)))
    d_inner = jnp.zeros((length, width), f32)
    for tap in range(taps):
        offset = taps - 1 - tap
        d_inner = d_inner + conv_taps[tap] * extended[offset : offset + length].astype(f32)
    d_inner = d_inner.astype(bf16)
    d_normalized = matmul(
        jnp.concatenate([d_inner, d_gate_low], axis=1),
        weight,
        NT,
    ).astype(bf16)
    grad_gate = grad_gate.astype(bf16).reshape(seq, in_rows, width)
    grad_gate = lax.all_to_all(grad_gate, "seq", 0, 0)
    d_normalized, d_inner, grad_gate, grad_x_proj, branch = together(
        (d_normalized, d_inner, grad_gate, grad_x_proj, branch)
    )
    grad_inner = matmul(normalized, d_inner, TN).astype(bf16)
    grad_inner = scattered_sum(rows_of(grad_inner, model // batch), "batch")
    d_normalized, *last_terms = line_summed(rows_of(d_normalized, span), "seq")

    block_out = jnp.where(own_valid, own_stream + branch.astype(f32), 0.0)

    def columns_of(part):
        part = part.reshape(seq, in_rows, batch, own).transpose(1, 2, 0, 3)
        return part.reshape(in_rows, batch * seq * own).astype(f32)

    grad_inner = grad_inner.astype(bf16).reshape(seq, in_rows, width)
    grad_inner = lax.all_to_all(grad_inner, "seq", 0, 0)
    grad_input = jnp.concatenate([columns_of(grad_inner), columns_of(grad_gate)], axis=1)

    small_grads = jnp.concatenate(
        [grad_dt_proj, grad_x_proj, grad_log, grad_conv, grad_conv_bias, grad_dt_bias, grad_skip],
        axis=0,
    )
    small_grads = lax.psum_scatter(small_grads, "batch", scatter_dimension=1, tiled=True)
    g_dt_proj, g_x_proj, g_log, g_conv, g_conv_bias, g_dt_bias, g_skip = jnp.split(
        small_grads, cuts, axis=0
    )

    own_upstream = jnp.where(own_valid, cotangent[0].astype(f32), 0.0)
    own_scale = lax.rsqrt(jnp.mean(own_stream * own_stream, axis=-1, keepdims=True) + epsilon)
    grad_gain = jnp.sum(grad_input * in_proj.astype(f32), axis=1) / norm_gain.astype(f32)
    (
        d_normalized, g_dt_proj, g_x_proj, g_log, g_conv, g_conv_bias, g_dt_bias, g_skip,
        grad_input, grad_gain, grad_output,
    ) = together(
        (
            d_normalized, g_dt_proj, g_x_proj, g_log, g_conv, g_conv_bias, g_dt_bias, g_skip,
            grad_input, grad_gain, grad_output,
        )
    )
    for term in last_terms:
        d_normalized = d_normalized + term.astype(f32)
    d_hat = d_normalized * gain
    grad_tokens = (
        own_scale * d_hat
        - own_stream
        * own_scale
        * own_scale
        * own_scale
        * jnp.mean(d_hat * own_stream, axis=-1, keepdims=True)
        + own_upstream
    )
    return (
        block_out[None],
        grad_tokens[None],
        grad_gain,
        grad_input,
        g_conv,
        g_conv_bias[0],
        g_x_proj.T,
        g_dt_proj,
        g_dt_bias[0],
        g_log.T,
        g_skip[0],
        grad_output,
    )


def solution(mesh):
    placed = (
        P("batch", "seq", None),
        P("batch"),
        P(("batch", "seq")),
        P(("batch", "seq"), None),
        P(None, ("batch", "seq")),
        P(("batch", "seq")),
        P(("batch", "seq"), None),
        P(None, ("batch", "seq")),
        P(("batch", "seq")),
        P(("batch", "seq"), None),
        P(("batch", "seq")),
        P(("batch", "seq"), None),
        P("batch", "seq", None),
    )
    return jax.shard_map(
        on_device,
        mesh=mesh,
        in_specs=placed,
        out_specs=(
            P("batch", "seq", None),
            P("batch", "seq", None),
            P(("batch", "seq")),
            P(("batch", "seq"), None),
            P(None, ("batch", "seq")),
            P(("batch", "seq")),
            P(("batch", "seq"), None),
            P(None, ("batch", "seq")),
            P(("batch", "seq")),
            P(("batch", "seq"), None),
            P(("batch", "seq")),
            P(("batch", "seq"), None),
        ),
        check_vma=False,
    )
```

```python
import functools

import jax
import jax.numpy as jnp
from jax import lax
from jax.experimental import pallas as pl
from jax.experimental.pallas import tpu as pltpu
from jax.sharding import PartitionSpec as P

bf16, f32 = jnp.bfloat16, jnp.float32
NT = (((1,), (1,)), ((), ()))
LANES = 128
GROUP = 32
BLOCK = 128
epsilon = 1e-05
LOG2E = 1.4426950408889634


def spread(tile, row, lanes, states):
    return jnp.broadcast_to(tile[row : row + 1, lanes], (states, LANES))


def selectors(select, states):
    low = select.shape[1] - 4 * states
    middle = low + 2 * states
    block = select[:, low:middle].astype(f32) + select[:, middle:].astype(f32)
    return jnp.transpose(block), block[:, :states], block[:, states:]


def block_diagonal(values, step):
    rows, states = values.shape
    wide = step * states
    spread_out = (
        lax.broadcasted_iota(jnp.int32, (states, wide), 1) % states
        == lax.broadcasted_iota(jnp.int32, (states, wide), 0)
    ).astype(bf16)
    value = jnp.dot(values.astype(bf16), spread_out, preferred_element_type=f32)
    place = lax.broadcasted_iota(jnp.int32, (rows, wide), 0) % step
    owner = lax.broadcasted_iota(jnp.int32, (rows, wide), 1) // states
    return jnp.where(place == owner, value, 0.0).astype(bf16)


def forward_body(tiles, step, delta, active, select, rate, mixed, kept, state, drive, columns):
    rows, states = delta.shape[0], rate.shape[0]
    wide = step * states

    @pl.when(pl.program_id(0) == 0)
    def _():
        state[...] = jnp.zeros_like(state)

    turned, _, c_block = selectors(select[...], states)
    columns[...] = turned[:states]
    drive[...] = delta[...] * active[...].astype(f32)
    rates = [rate[:, k * LANES : (k + 1) * LANES] for k in range(tiles)]

    def group(number, held):
        held = list(held)
        base = pl.multiple_of(number * GROUP, GROUP)
        delta_now, drive_now = delta.at[pl.ds(base, GROUP), :], drive.at[pl.ds(base, GROUP), :]
        b_now = pltpu.roll(columns[...], rows - base, 1)
        for j in range(GROUP):
            b_wide = jnp.broadcast_to(b_now[:, j : j + 1], (states, LANES))
            for k in range(tiles):
                lanes = slice(k * LANES, (k + 1) * LANES)
                decay = jnp.exp2(spread(delta_now, j, lanes, states) * rates[k])
                held[k] = decay * held[k] + spread(drive_now, j, lanes, states) * b_wide
                at = pl.ds(pl.multiple_of((base + j) * states, states), states)
                kept[at, lanes] = held[k].astype(bf16)
        return tuple(held)

    held = lax.fori_loop(
        0,
        rows // GROUP,
        group,
        tuple(state[:, k * LANES : (k + 1) * LANES] for k in range(tiles)),
    )
    for k in range(tiles):
        state[:, k * LANES : (k + 1) * LANES] = held[k]
    c_diag = block_diagonal(c_block, step)
    for q in range(rows // step):
        part = kept[q * wide : (q + 1) * wide, :]
        spot = slice(q * step, (q + 1) * step)
        mixed[spot, :] = jnp.dot(c_diag[spot, :], part, preferred_element_type=f32)


def scan_forward(delta, active, select, rate, block, step):
    length, width = delta.shape
    states = rate.shape[0]
    tiles = width // LANES
    return pl.pallas_call(
        functools.partial(forward_body, tiles, step),
        grid=(length // block,),
        in_specs=[
            pl.BlockSpec((block, width), lambda i: (i, 0)),
            pl.BlockSpec((block, width), lambda i: (i, 0)),
            pl.BlockSpec((block, select.shape[1]), lambda i: (i, 0)),
            pl.BlockSpec((states, width), lambda i: (0, 0)),
        ],
        out_specs=[
            pl.BlockSpec((block, width), lambda i: (i, 0)),
            pl.BlockSpec((block * states, width), lambda i: (i, 0)),
        ],
        out_shape=[
            jax.ShapeDtypeStruct((length, width), f32),
            jax.ShapeDtypeStruct((length * states, width), bf16),
        ],
        scratch_shapes=[
            pltpu.VMEM((states, width), f32),
            pltpu.VMEM((block, width), f32),
            pltpu.VMEM((states, block), f32),
        ],
        compiler_params=pltpu.CompilerParams(vmem_limit_bytes=48 << 20),
        cost_estimate=pl.CostEstimate(
            flops=8 * length * width * states,
            transcendentals=length * width * states,
            bytes_accessed=length * width * (2 * states + 10),
        ),
        name="scan_forward",
    )(delta, active, select, rate)


FEW = 4


def backward_body(
    tiles, step, delta, active, d_mixed, select, rate, decay_rate, kept, kept_before,
    d_delta, d_active, d_bc, d_log, push, drive, columns, diagonals, folding, timed, *pairs,
):
    grads, rated = pairs[:2], pairs[2:]
    rows, states = delta.shape[0], rate.shape[0]
    blocks = pl.num_programs(0)
    first = pl.program_id(0) == blocks - 1
    wide = step * states

    @pl.when(pl.program_id(0) == 0)
    def _():
        push[...] = jnp.zeros_like(push)
        d_log[...] = jnp.zeros_like(d_log)

    turned, b_block, _ = selectors(select[...], states)
    columns[...] = turned[states:]
    drive[...] = delta[...] * active[...].astype(f32)
    rates = [rate[:, k * LANES : (k + 1) * LANES] for k in range(tiles)]
    own_rates = [decay_rate[:, k * LANES : (k + 1) * LANES].astype(bf16) for k in range(tiles)]

    place = lax.broadcasted_iota(jnp.int32, (step, wide), 0)
    owner = lax.broadcasted_iota(jnp.int32, (step, wide), 1) // states
    ones_diag = (place == owner).astype(bf16)
    diag = (place == owner).astype(f32)
    diagonals[...] = block_diagonal(b_block, step)

    def sums_of(number):
        held, through_of = number % 2, {}

        def spots(q):
            at = number * GROUP + q * step
            tall = slice(q * wide, (q + 1) * wide)
            return slice(at, at + step), tall

        def through(q):
            spot, tall = spots(q)
            value = jnp.dot(diagonals[spot, :], grads[held][tall, :], preferred_element_type=f32)
            d_active[spot, :] = delta[spot, :] * value
            through_of[q] = active[spot, :].astype(f32) * value

        def summed(q):
            spot, tall = spots(q)
            value = jnp.dot(ones_diag, rated[held][tall, :], preferred_element_type=f32)
            d_delta[spot, :] = value + through_of[q]

        def d_b(q):
            spot, tall = spots(q)
            folding[spot, :wide] = diag * lax.dot_general(
                drive[spot, :].astype(bf16), grads[held][tall, :], NT, preferred_element_type=f32
            )

        def d_c(q):
            spot, _ = spots(q)
            own = slice(spot.start * states, spot.stop * states)
            folding[spot, wide:] = diag * lax.dot_general(
                d_mixed[spot, :].astype(bf16), kept[own, :], NT, preferred_element_type=f32
            )

        return [
            functools.partial(part, q)
            for q in range(GROUP // step)
            for part in (through, summed, d_b, d_c)
        ]

    carry = [push[:, k * LANES : (k + 1) * LANES] for k in range(tiles)]
    waiting = []
    for number in reversed(range(rows // GROUP)):
        pace = GROUP // max(len(waiting), 1)
        sums = [None] * tiles
        held = number % 2
        for j in reversed(range(GROUP)):
            row = number * GROUP + j
            c_wide = jnp.broadcast_to(columns[:, row : row + 1], (states, LANES))
            at = slice(j * states, (j + 1) * states)
            for k in range(tiles):
                lanes = slice(k * LANES, (k + 1) * LANES)
                if row:
                    before = kept[(row - 1) * states : row * states, lanes]
                else:
                    before = jnp.where(first, jnp.zeros((), bf16), kept_before[:, lanes])
                step_size = spread(delta, row, lanes, states)
                grad = spread(d_mixed, row, lanes, states) * c_wide + carry[k]
                carry[k] = jnp.exp2(step_size * rates[k]) * grad
                grads[held][at, lanes] = grad.astype(bf16)
                rated_now = carry[k].astype(bf16) * before * own_rates[k]
                rated[held][at, lanes] = rated_now
                timed_now = rated_now * step_size.astype(bf16)
                sums[k] = timed_now if sums[k] is None else sums[k] + timed_now
                if j % FEW == 0:
                    spot = row // FEW * states
                    timed[spot : spot + states, lanes] = sums[k]
                    sums[k] = None
            if waiting and j % pace == 0:
                waiting.pop(0)()
        while waiting:
            waiting.pop(0)()
        waiting = sums_of(number)
    while waiting:
        waiting.pop(0)()
    for k in range(tiles):
        push[:, k * LANES : (k + 1) * LANES] = carry[k]
    fold = (
        lax.broadcasted_iota(jnp.int32, (wide, states), 0) % states
        == lax.broadcasted_iota(jnp.int32, (wide, states), 1)
    ).astype(bf16)
    for number in range(2):
        value = folding[:, number * wide : (number + 1) * wide]
        high = value.astype(bf16)
        d_bc[:, number * states : (number + 1) * states] = jnp.dot(
            high, fold, preferred_element_type=f32
        )
    span = rows // FEW * states
    pick = (
        lax.broadcasted_iota(jnp.int32, (states, span), 1) % states
        == lax.broadcasted_iota(jnp.int32, (states, span), 0)
    ).astype(bf16)
    d_log[...] += jnp.dot(pick, timed[...], preferred_element_type=f32)


def scan_backward(delta, active, d_mixed, select, rate, decay_rate, kept, block, step):
    length, width = delta.shape
    states = rate.shape[0]
    tiles = width // LANES
    blocks = length // block
    back = lambda i: (blocks - 1 - i, 0)
    return pl.pallas_call(
        functools.partial(backward_body, tiles, step),
        grid=(blocks,),
        in_specs=[
            pl.BlockSpec((block, width), back),
            pl.BlockSpec((block, width), back),
            pl.BlockSpec((block, width), back),
            pl.BlockSpec((block, select.shape[1]), back),
            pl.BlockSpec((states, width), lambda i: (0, 0)),
            pl.BlockSpec((states, width), lambda i: (0, 0)),
            pl.BlockSpec((block * states, width), back),
            pl.BlockSpec(
                (states, width), lambda i: (jnp.maximum((blocks - 1 - i) * block - 1, 0), 0)
            ),
        ],
        out_specs=[
            pl.BlockSpec((block, width), back),
            pl.BlockSpec((block, width), back),
            pl.BlockSpec((block, 2 * states), back),
            pl.BlockSpec((states, width), lambda i: (0, 0)),
        ],
        out_shape=[
            jax.ShapeDtypeStruct((length, width), f32),
            jax.ShapeDtypeStruct((length, width), f32),
            jax.ShapeDtypeStruct((length, 2 * states), f32),
            jax.ShapeDtypeStruct((states, width), f32),
        ],
        scratch_shapes=[
            pltpu.VMEM((states, width), f32),
            pltpu.VMEM((block, width), f32),
            pltpu.VMEM((states, block), f32),
            pltpu.VMEM((block, step * states), bf16),
            pltpu.VMEM((block, 2 * step * states), f32),
            pltpu.VMEM((block // FEW * states, width), bf16),
        ]
        + [pltpu.VMEM((GROUP * states, width), bf16)] * 4,
        compiler_params=pltpu.CompilerParams(vmem_limit_bytes=48 << 20),
        cost_estimate=pl.CostEstimate(
            flops=20 * length * width * states,
            transcendentals=length * width * states,
            bytes_accessed=length * width * (2 * states + 20),
        ),
        name="scan_backward",
    )(delta, active, d_mixed, select, rate, decay_rate, kept, kept)


together = lax.optimization_barrier


def inner_swap(value, axis):
    count = lax.axis_size(axis)
    return lax.ppermute(value, axis, [(i, i ^ 1) for i in range(count)])


def outer_shift(value, axis, steps):
    count = lax.axis_size(axis)
    half = count // 2
    pairs = [(i, (i // 2 + steps) % half * 2 + i % 2) for i in range(count)]
    return lax.ppermute(value, axis, pairs)


def shift_order(half):
    return sorted(range(1, half), key=lambda k: (-min(k, half - k), k))


def pieces_of_all(own, axis):
    count = lax.axis_size(axis)
    place = lax.axis_index(axis)
    half = count // 2
    outer, inner = place // 2, place % 2
    yield place, own
    arrived = {k: outer_shift(own, axis, k) for k in shift_order(half)}
    yield outer * 2 + 1 - inner, inner_swap(own, axis)
    for k, piece in arrived.items():
        origin = (outer - k + half) % half
        yield origin * 2 + inner, piece
    for k, piece in arrived.items():
        origin = (outer - k + half) % half
        yield origin * 2 + 1 - inner, inner_swap(piece, axis)


def gathered(own, axis, dim=0):
    count, size = lax.axis_size(axis), own.shape[dim]
    whole = jnp.zeros(own.shape[:dim] + (count * size,) + own.shape[dim + 1 :], own.dtype)
    for place, piece in pieces_of_all(own, axis):
        whole = lax.dynamic_update_slice_in_dim(whole, piece, place * size, dim)
    return whole


def hop(value, axis, moves):
    pairs = [(a * 2 + i, b * 2 + i) for a, b in moves for i in (0, 1)]
    return lax.ppermute(value, axis, pairs)


def swap_at(value, axis, spots):
    pairs = [(a * 2 + i, a * 2 + 1 - i) for a in spots for i in (0, 1)]
    return lax.ppermute(value, axis, pairs)


UP, DOWN = [(0, 1), (1, 2), (2, 3)], [(1, 0), (2, 1), (3, 2)]


def line_gathered(own, axis, held):
    if lax.axis_size(axis) != 8:
        return own, lambda own: own, lambda own, _: lax.all_gather(own, axis, axis=0, tiled=True), held
    place = lax.axis_index(axis)
    z, x = place // 2, place % 2
    rows = own.shape[0]
    upper, edge = z >= 2, (z == 0) | (z == 3)
    across = jnp.where(upper, z - 2, z + 2)
    far = jnp.where(z == 3, 0, 3)

    def put(whole, piece, spot, side):
        return lax.dynamic_update_slice_in_dim(whole, piece, (spot * 2 + side) * rows, 0)

    def put_far(whole, piece, side):
        held = lax.dynamic_slice_in_dim(whole, (far * 2 + side) * rows, rows, 0)
        return put(whole, jnp.where(edge, piece, held), far, side)

    whole = jnp.zeros((8 * rows,) + own.shape[1:], own.dtype)
    up, down, other, held = together(
        (hop(own, axis, UP), hop(own, axis, DOWN), swap_at(own, axis, range(4)), held)
    )
    up_two, down_two = hop(up, axis, UP[1:]), hop(down, axis, DOWN[:2])
    other_up, other_down = swap_at(up, axis, (1, 2, 3)), swap_at(down, axis, (0, 1, 2))
    whole = put(put(whole, own, z, x), other, z, 1 - x)
    whole = put(put(whole, up, (z + 3) % 4, x), down, (z + 1) % 4, x)
    two = jnp.where(upper, up_two, down_two)
    three = hop(two, axis, [(2, 3), (1, 0)])
    other_two = swap_at(two, axis, range(4))
    whole = put(put(whole, other_up, (z + 3) % 4, 1 - x), other_down, (z + 1) % 4, 1 - x)
    whole = put(whole, two, across, x)

    def end(last, other_three):
        three, other_two = last
        ended = put(whole, other_two, across, 1 - x)
        return put_far(put_far(ended, three, x), other_three, 1 - x)

    return (three, other_two), lambda last: swap_at(last[0], axis, (0, 3)), end, held


def line_summed(part_of, axis):
    if lax.axis_size(axis) != 8:
        return (scattered_sum(part_of, axis),)
    place = lax.axis_index(axis)
    z, x = place // 2, place % 2
    upper, edge = z >= 2, (z == 0) | (z == 3)
    across = jnp.where(upper, z - 2, z + 2)
    far = jnp.where(z == 0, 3, 0)
    above, below = jnp.minimum(z + 1, 3), jnp.maximum(z - 1, 0)

    def swapped(spot, spots):
        return swap_at(part_of(spot * 2 + 1 - x), axis, spots)

    def added(spot, given):
        return part_of(spot * 2 + x).astype(f32) + given.astype(f32)

    given_far = swapped(far, (0, 3))
    given_across = swapped(across, range(4))
    given_above, given_below = swapped(above, (0, 1, 2)), swapped(below, (1, 2, 3))
    given_own = swapped(z, range(4))
    three = hop(added(far, given_far).astype(bf16), axis, [(0, 1), (3, 2)])
    three, given_across = together((three, given_across))
    two = added(across, given_across) + jnp.where(edge, 0.0, three.astype(f32))
    two = two.astype(bf16)
    two_up, two_down, given_above, given_below = together(
        (hop(two, axis, UP[:2]), hop(two, axis, DOWN[1:]), given_above, given_below)
    )
    one_up = (added(above, given_above) + two_up.astype(f32)).astype(bf16)
    one_down = (added(below, given_below) + two_down.astype(f32)).astype(bf16)
    return added(z, given_own), hop(one_up, axis, UP), hop(one_down, axis, DOWN)


def scattered_sum(part_of, axis):
    count = lax.axis_size(axis)
    place = lax.axis_index(axis)
    half = count // 2
    outer, inner = place // 2, place % 2
    total = None
    for k in shift_order(half) + [0]:
        target = (outer + k) % half
        given = inner_swap(part_of(target * 2 + 1 - inner), axis)
        piece = part_of(target * 2 + inner).astype(f32) + given.astype(f32)
        if k:
            piece = outer_shift(piece.astype(bf16), axis, k).astype(f32)
        total = piece if total is None else total + piece
    return total


def rows_of(value, rows):
    return lambda place: lax.dynamic_slice_in_dim(value, place * rows, rows, 0)


def summed_over_seq(part, change, held=()):
    count = lax.axis_size("seq")
    length, columns = part.shape
    part = part.astype(bf16).reshape(count, length // count, columns)
    own = change(jnp.sum(lax.all_to_all(part, "seq", 0, 0).astype(f32), axis=0))
    own, held = together((own, held))
    return shared(own, "seq").reshape(length, own.shape[1]), held


def two_terms(value):
    high = value.astype(bf16)
    return [high, (value - high.astype(f32)).astype(bf16)]


def shared(own, axis):
    wide = jnp.broadcast_to(own[None], (lax.axis_size(axis),) + own.shape)
    return lax.all_to_all(wide, axis, 0, 0)


def matmul(a, b, dims=(((1,), (0,)), ((), ()))):
    return lax.dot_general(a, b, dims, preferred_element_type=f32)


TN = (((0,), (0,)), ((), ()))


def on_device(
    tokens,
    lengths,
    norm_gain,
    in_proj,
    conv_weight,
    conv_bias,
    x_proj,
    dt_proj,
    dt_bias,
    a_log,
    skip,
    out_proj,
    cotangent,
):
    batch, seq = lax.axis_size("batch"), lax.axis_size("seq")
    place = lax.axis_index("seq")
    span, model = tokens.shape[1:]
    length = span * seq
    in_rows = in_proj.shape[0]
    own = skip.shape[0]
    taps = conv_weight.shape[0]
    rank = dt_proj.shape[0]
    states = a_log.shape[1]
    width = own * batch

    halves = in_proj.reshape(in_rows, 2, batch, seq, own).transpose(1, 3, 0, 2, 4)
    halves = halves.reshape(2, seq, in_rows, width)
    beside = jnp.broadcast_to(norm_gain[None, :, None], (seq, in_rows, LANES))
    columns = lax.all_to_all(jnp.concatenate([halves[0], beside], axis=2), "seq", 0, 0)
    columns, gate_columns = together((columns, halves[1]))
    gate_columns = lax.all_to_all(gate_columns, "seq", 0, 0)
    last_hop, last_swap, end_gather, (dt_proj, x_proj, out_proj) = line_gathered(
        cotangent[0], "seq", (dt_proj, x_proj, out_proj)
    )
    small = jnp.concatenate(
        [
            dt_proj,
            x_proj.T,
            a_log.T,
            conv_weight,
            conv_bias[None],
            dt_bias[None],
            skip[None],
        ],
        axis=0,
    )
    small = gathered(small, "batch", 1)
    cuts = [rank, 2 * rank + 2 * states, 2 * rank + 3 * states]
    cuts = cuts + [cuts[2] + taps + i for i in range(3)]
    delta_weight, select_weight, decay_logs, conv_taps, conv_shift, delta_shift, skip_gain = (
        jnp.split(small, cuts, axis=0)
    )
    conv_taps, conv_shift = conv_taps.astype(f32), conv_shift.astype(f32)
    delta_shift, skip_gain = delta_shift.astype(f32), skip_gain.astype(f32)
    decay = -jnp.exp(decay_logs.astype(f32))
    input_weight = gathered(columns.reshape(seq * in_rows, width + LANES), "batch")
    one = (jnp.arange(LANES) == 0).astype(bf16)[None]
    gain = matmul(one, input_weight[:, width:], NT)
    gate_weight = gathered(gate_columns.reshape(seq * in_rows, width), "batch")

    def normed(rows):
        rows = rows.astype(f32)
        scale = lax.rsqrt(jnp.mean(rows * rows, axis=-1, keepdims=True) + epsilon)
        return (rows * scale * gain).astype(bf16)

    stream = lax.all_gather(tokens[0], "seq", axis=0, tiled=True)
    normalized = normed(stream)
    output_weight = gathered(out_proj, "batch")

    valid = (jnp.arange(length, dtype=jnp.int32) < lengths[0])[:, None]
    inner = matmul(normalized, input_weight[:, :width]).astype(bf16)
    padded = jnp.pad(inner, ((taps - 1, 0), (0, 0)))
    conv_out = conv_shift + jnp.zeros((length, width), f32)
    for tap in range(taps):
        conv_out = conv_out + conv_taps[tap] * padded[tap : tap + length].astype(f32)
    active = jax.nn.silu(conv_out).astype(bf16)
    active_f = active.astype(f32)

    partial, last_hop, gate_weight = together(
        (matmul(active, select_weight, NT), last_hop, gate_weight)
    )
    select, _ = summed_over_seq(
        partial,
        lambda s: jnp.concatenate([s[:, :rank].astype(bf16)] + two_terms(s[:, rank:]), axis=1),
    )
    gate_low = matmul(normalized, gate_weight).astype(bf16)
    select, gate_low, last_hop = together((select, gate_low, last_hop))
    last = last_swap(last_hop)
    gate = gate_low.astype(f32)
    gate_sig = jax.nn.sigmoid(gate)
    delta_low = select[:, :rank]
    delta_raw = matmul(delta_low, delta_weight) + delta_shift
    delta = jax.nn.softplus(delta_raw)

    block = min(BLOCK, length)
    step = 256 // states
    rate = decay * LOG2E
    mixed, kept = scan_forward(delta, active, select, rate, block, step)
    mixed = mixed + skip_gain * active_f
    gated = (mixed * gate * gate_sig).astype(bf16)
    branch = matmul(gated, output_weight).astype(bf16)
    branch, last_hop, last = together((branch, last_hop, last))
    branch = lax.psum_scatter(branch, "seq", scatter_dimension=0, tiled=True)
    own_valid = lax.dynamic_slice_in_dim(valid, place * span, span, 0)
    own_stream = tokens[0].astype(f32)

    upstream = jnp.where(valid, end_gather(last_hop, last), 0).astype(bf16)
    d_gated = matmul(upstream, output_weight, NT)
    d_mixed = d_gated * gate * gate_sig
    d_gate = d_gated * mixed * gate_sig * (1.0 + gate * (1.0 - gate_sig))
    grad_skip = jnp.sum(d_mixed * active_f, axis=0, keepdims=True)
    d_gate_low = d_gate.astype(bf16)

    d_delta, d_active, d_bc, grad_log = scan_backward(
        delta, active, d_mixed, select, rate, decay, kept, block, step
    )
    d_raw = d_delta * jax.nn.sigmoid(delta_raw)
    grad_dt_bias = jnp.sum(d_raw, axis=0, keepdims=True)
    d_raw_low = d_raw.astype(bf16)
    grad_dt_proj = matmul(delta_low, d_raw_low, TN)
    partial = jnp.concatenate([matmul(d_raw_low, delta_weight, NT), d_bc], axis=1)
    d_select, gated = summed_over_seq(partial, lambda s: s.astype(bf16), gated)
    grad_output = matmul(gated, upstream, TN).astype(bf16)
    grad_gate = scattered_sum(
        rows_of(matmul(normalized, d_gate_low, TN).astype(bf16), model // batch), "batch"
    )
    d_select, grad_gate, grad_output = together((d_select, grad_gate, grad_output))
    grad_output = lax.psum_scatter(grad_output, "batch", scatter_dimension=0, tiled=True)
    grad_output = grad_output.astype(f32)
    grad_x_proj = matmul(d_select, active, TN)
    d_active = d_active + d_mixed * skip_gain + matmul(d_select, select_weight)
    conv_sig = jax.nn.sigmoid(conv_out)
    d_conv = (d_active * conv_sig * (1.0 + conv_out * (1.0 - conv_sig))).astype(bf16)
    d_conv_f = d_conv.astype(f32)
    grad_conv_bias = jnp.sum(d_conv_f, axis=0, keepdims=True)
    grad_conv = jnp.stack(
        [
            jnp.sum(d_conv_f * padded[tap : tap + length].astype(f32), axis=0)
            for tap in range(taps)
        ]
    )
    extended = jnp.pad(d_conv, ((0, taps - 1), (0, 0)))
    d_inner = jnp.zeros((length, width), f32)
    for tap in range(taps):
        offset = taps - 1 - tap
        d_inner = d_inner + conv_taps[tap] * extended[offset : offset + length].astype(f32)
    d_inner = d_inner.astype(bf16)
    d_normalized = matmul(
        jnp.concatenate([d_inner, jnp.zeros((length, LANES), bf16), d_gate_low], axis=1),
        jnp.concatenate([input_weight, gate_weight], axis=1),
        NT,
    ).astype(bf16)
    grad_gate = grad_gate.astype(bf16).reshape(seq, in_rows, width)
    grad_gate = lax.all_to_all(grad_gate, "seq", 0, 0)
    d_normalized, d_inner, grad_gate, grad_x_proj, branch = together(
        (d_normalized, d_inner, grad_gate, grad_x_proj, branch)
    )
    grad_inner = matmul(normalized, d_inner, TN).astype(bf16)
    grad_inner = scattered_sum(rows_of(grad_inner, model // batch), "batch")
    d_normalized, *last_terms = line_summed(rows_of(d_normalized, span), "seq")

    block_out = jnp.where(own_valid, own_stream + branch.astype(f32), 0.0)

    def columns_of(part):
        part = part.reshape(seq, in_rows, batch, own).transpose(1, 2, 0, 3)
        return part.reshape(in_rows, batch * seq * own).astype(f32)

    grad_inner = grad_inner.astype(bf16).reshape(seq, in_rows, width)
    grad_inner = lax.all_to_all(grad_inner, "seq", 0, 0)
    grad_input = jnp.concatenate([columns_of(grad_inner), columns_of(grad_gate)], axis=1)

    small_grads = jnp.concatenate(
        [grad_dt_proj, grad_x_proj, grad_log, grad_conv, grad_conv_bias, grad_dt_bias, grad_skip],
        axis=0,
    )
    small_grads = lax.psum_scatter(small_grads, "batch", scatter_dimension=1, tiled=True)
    g_dt_proj, g_x_proj, g_log, g_conv, g_conv_bias, g_dt_bias, g_skip = jnp.split(
        small_grads, cuts, axis=0
    )

    own_upstream = jnp.where(own_valid, cotangent[0].astype(f32), 0.0)
    own_scale = lax.rsqrt(jnp.mean(own_stream * own_stream, axis=-1, keepdims=True) + epsilon)
    grad_gain = jnp.sum(grad_input * in_proj.astype(f32), axis=1) / norm_gain.astype(f32)
    (
        d_normalized, g_dt_proj, g_x_proj, g_log, g_conv, g_conv_bias, g_dt_bias, g_skip,
        grad_input, grad_gain, grad_output,
    ) = together(
        (
            d_normalized, g_dt_proj, g_x_proj, g_log, g_conv, g_conv_bias, g_dt_bias, g_skip,
            grad_input, grad_gain, grad_output,
        )
    )
    for term in last_terms:
        d_normalized = d_normalized + term.astype(f32)
    d_hat = d_normalized * gain
    grad_tokens = (
        own_scale * d_hat
        - own_stream
        * own_scale
        * own_scale
        * own_scale
        * jnp.mean(d_hat * own_stream, axis=-1, keepdims=True)
        + own_upstream
    )
    return (
        block_out[None],
        grad_tokens[None],
        grad_gain,
        grad_input,
        g_conv,
        g_conv_bias[0],
        g_x_proj.T,
        g_dt_proj,
        g_dt_bias[0],
        g_log.T,
        g_skip[0],
        grad_output,
    )


def solution(mesh):
    placed = (
        P("batch", "seq", None),
        P("batch"),
        P(("batch", "seq")),
        P(("batch", "seq"), None),
        P(None, ("batch", "seq")),
        P(("batch", "seq")),
        P(("batch", "seq"), None),
        P(None, ("batch", "seq")),
        P(("batch", "seq")),
        P(("batch", "seq"), None),
        P(("batch", "seq")),
        P(("batch", "seq"), None),
        P("batch", "seq", None),
    )
    return jax.shard_map(
        on_device,
        mesh=mesh,
        in_specs=placed,
        out_specs=(
            P("batch", "seq", None),
            P("batch", "seq", None),
            P(("batch", "seq")),
            P(("batch", "seq"), None),
            P(None, ("batch", "seq")),
            P(("batch", "seq")),
            P(("batch", "seq"), None),
            P(None, ("batch", "seq")),
            P(("batch", "seq")),
            P(("batch", "seq"), None),
            P(("batch", "seq")),
            P(("batch", "seq"), None),
        ),
        check_vma=False,
    )
```
